32 devices in a mesh: rep: 4 (over y, x), grp: 8 (over z, core).
Axes of the slice: x: 2, y: 2, z: 4, core: 2. Of those that a mesh axis runs over, the one named last changes fastest.
Arguments:
- tokens: bfloat16 [8, 4096, 384], P('rep', 'grp'), may hold values from -6 to 6
- segment_ids: int32 [8, 4096], P('rep', 'grp'), may hold values from 0 to 7, never falling along the last dimension, each value on 1 to 2048 neighbouring positions
- out_grad: bfloat16 [8, 4096, 384], P('rep', 'grp'), may hold values from -6 to 6
- query_weight: bfloat16 [384, 384], P('grp'), may hold values from -0.3125 to 0.3125
- key_weight: bfloat16 [384, 384], P('grp'), may hold values from -0.3125 to 0.3125
- value_weight: bfloat16 [384, 384], P('grp'), may hold values from -0.3125 to 0.3125
- output_weight: bfloat16 [384, 384], P('grp'), may hold values from -3.5 to 3.5
- inner_weight: bfloat16 [384, 1536], P('grp'), may hold values from -0.3125 to 0.3125
- outer_weight: bfloat16 [1536, 384], P('grp'), may hold values from -0.15625 to 0.15625
- query_bias: bfloat16 [384], P('grp'), may hold values from -3 to 3
- value_bias: bfloat16 [384], P('grp'), may hold values from -3 to 3
- output_bias: bfloat16 [384], P('grp'), may hold values from -3 to 3
- inner_bias: bfloat16 [1536], P('grp'), may hold values from -3 to 3
- outer_bias: bfloat16 [384], P('grp'), may hold values from -3 to 3
- first_gain: bfloat16 [384], P('grp'), may hold values from 0.25 to 1.75
- first_shift: bfloat16 [384], P('grp'), may hold values from -3 to 3
- second_gain: bfloat16 [384], P('grp'), may hold values from 0.25 to 1.75
- second_shift: bfloat16 [384], P('grp'), may hold values from -3 to 3
Outputs:
- layer_out: bfloat16 [8, 4096, 384], P('rep', 'grp')
- input_grad: bfloat16 [8, 4096, 384], P('rep', 'grp')
- grad_query_weight: float32 [384, 384], P('grp')
- grad_key_weight: float32 [384, 384], P('grp')
- grad_value_weight: float32 [384, 384], P('grp')
- grad_output_weight: float32 [384, 384], P('grp')
- grad_inner_weight: float32 [384, 1536], P('grp')
- grad_outer_weight: float32 [1536, 384], P('grp')
- grad_query_bias: float32 [384], P('grp')
- grad_value_bias: float32 [384], P('grp')
- grad_output_bias: float32 [384], P('grp')
- grad_inner_bias: float32 [1536], P('grp')
- grad_outer_bias: float32 [384], P('grp')
- grad_first_gain: float32 [384], P('grp')
- grad_first_shift: float32 [384], P('grp')
- grad_second_gain: float32 [384], P('grp')
- grad_second_shift: float32 [384], P('grp')
The draws below stay inside these ranges and needn't reach their ends.
Inputs may be any that keep to these rules, and one draw needn't show every extreme that they name: `segment_ids`: along each sequence the ids never fall; each of the 8 ids marks one document of 1 to 2048 tokens, and one document of each sequence holds exactly 2048 tokens.
All inputs are finite; a program needn't handle non-finite values.
Results may differ from the reference program's by a relative error of at most 0.015.
Values may be sent and summed in bfloat16 or wider, within the bound.
A program may use at most 320 MiB of HBM per device.

```python
import math
import jax
import jax.numpy as jnp
import numpy as np
from jax import lax

D = 384
H = 12
HD = 32
FF = 1536
LEN = 4096
DOCS = 8
SEQS = 8


def raised(array, key, source, target, blocks, factor):
    def block_of(axis_at):
        return (jnp.arange(array.shape[axis_at]) // (array.shape[axis_at] // blocks)).reshape((-1,) + (1,) * (array.ndim - 1 - axis_at))

    one_side = jax.random.permutation(key, blocks)[block_of(target)]
    other_side = (block_of(target) + blocks // 2) % blocks
    return jnp.where((block_of(source) == one_side) | (block_of(source) == other_side), factor * array, array)


def block_levels(rng, extent, split, smallest, largest):
    def one(position, shards_of):
        draws = jax.random.uniform(jax.random.fold_in(jax.random.fold_in(rng, 6), position), (shards_of,), jnp.float32, smallest / len(split), largest / len(split))
        return jnp.repeat(jnp.exp(draws), extent[position] // shards_of).reshape((-1,) + (1,) * (len(extent) - position - 1))

    gain = one(*split[0])
    for cut in split[1:]:
        gain = gain * one(*cut)
    return gain


def length_profile(count, total, reach, skew):
    portions = [(1 << 20) // math.isqrt(standing ** skew) + 1 for standing in range(2, count + 1)]
    surplus, counts = total - reach - (count - 1), [1] * (count - 1)
    while surplus > 0:
        candidates = [i for i in range(count - 1) if counts[i] < reach]
        mass, budget = sum([portions[i] for i in candidates]), surplus
        for i in candidates:
            addition = min(reach - counts[i], max(1, budget * portions[i] // mass), surplus)
            counts[i] = counts[i] + addition
            surplus = surplus - addition
    return np.array([reach] + counts)


def ragged_sizes(stream_key, count, total, limit, skew):
    if count == 2:
        one = jax.random.randint(stream_key, (), max(1, total - limit), min(limit, total - 1) + 1)
        return jnp.stack([one, total - one])
    tallies = jnp.asarray(length_profile(count, total, limit, skew), jnp.int32)
    couples = (count - 1) // 2
    giver, sink = tallies[1:1 + 2 * couples:2], tallies[2:2 + 2 * couples:2]
    room = jnp.minimum(giver - 1, limit - sink)
    passed = jax.random.randint(jax.random.fold_in(stream_key, 1), (couples,), 0, 1 << 20) % (room + 1)
    tallies = tallies.at[1:1 + 2 * couples:2].set(giver - passed).at[2:2 + 2 * couples:2].set(sink + passed)
    return tallies[jax.random.permutation(jax.random.fold_in(stream_key, 2), count)]


def bell_draw(rng, dims, scale, reach, split=(), held_as=jnp.bfloat16):
    entries = jax.random.normal(rng, dims, jnp.float32) * scale
    if len(split) > 0:
        entries = block_levels(rng, dims, split, -0.22, 0.18) * entries
    return jnp.clip(entries, min=-reach, max=reach).astype(held_as)


def gaussian_with(rng, extent, deviation, bound, cuts, heavy, held_as=jnp.bfloat16):
    drawn = deviation * jax.random.normal(rng, extent, jnp.float32)
    if cuts:
        drawn = drawn * block_levels(rng, extent, cuts, -0.22, 0.18)
    return jnp.clip(raised(drawn, jax.random.fold_in(rng, 3), *heavy), -bound, bound).astype(held_as)


def setup_inputs(seed: int = 0) -> dict:
    key_list = jax.random.split(jax.random.key(seed), 19)
    tokens = bell_draw(key_list[0], (SEQS, LEN, D), 1.0, 6.0, ((0, 4), (1, 8)))
    segment_ids = jax.vmap(lambda own: jnp.searchsorted(jnp.cumsum(ragged_sizes(own, DOCS, LEN, LEN // 2, 1)), jnp.arange(LEN), side="right"))(jax.random.split(key_list[1], SEQS)).reshape((SEQS, LEN)).astype(jnp.int32)
    out_grad = gaussian_with(key_list[2], (SEQS, LEN, D), 1.0, 6.0, ((0, 4), (1, 8)), (1, 2, 8, 2.0))
    query_weight = bell_draw(key_list[3], (D, D), D ** -0.5, 0.3125, ((0, 8),))
    key_weight = bell_draw(key_list[4], (D, D), D ** -0.5, 0.3125, ((0, 8),))
    value_weight = bell_draw(key_list[5], (D, D), D ** -0.5, 0.3125, ((0, 8),))
    output_weight = bell_draw(key_list[6], (D, D), (max(1, D // 128)) ** -0.5, 3.5, ((0, 8),))
    inner_weight = bell_draw(key_list[7], (D, FF), D ** -0.5, 0.3125, ((0, 8),))
    outer_weight = bell_draw(key_list[8], (FF, D), FF ** -0.5, 0.15625, ((0, 8),))
    query_bias = bell_draw(key_list[9], (D,), 0.5, 3.0, ((0, 8),))
    value_bias = bell_draw(key_list[10], (D,), 0.5, 3.0, ((0, 8),))
    output_bias = bell_draw(key_list[11], (D,), 0.5, 3.0, ((0, 8),))
    inner_bias = bell_draw(key_list[12], (FF,), 0.5, 3.0, ((0, 8),))
    outer_bias = bell_draw(key_list[13], (D,), 0.5, 3.0, ((0, 8),))
    first_gain = jnp.clip(1.0 + 0.15 * jax.random.normal(key_list[14], (D,), jnp.float32), 0.25, 1.75).astype(jnp.bfloat16)
    first_shift = bell_draw(key_list[15], (D,), 0.5, 3.0, ((0, 8),))
    second_gain = jnp.clip(1.0 + 0.15 * jax.random.normal(key_list[16], (D,), jnp.float32), 0.25, 1.75).astype(jnp.bfloat16)
    second_shift = bell_draw(key_list[17], (D,), 0.5, 3.0, ((0, 8),))
    return {"tokens": tokens, "segment_ids": segment_ids, "out_grad": out_grad, "query_weight": query_weight, "key_weight": key_weight, "value_weight": value_weight, "output_weight": output_weight, "inner_weight": inner_weight, "outer_weight": outer_weight, "query_bias": query_bias, "value_bias": value_bias, "output_bias": output_bias, "inner_bias": inner_bias, "outer_bias": outer_bias, "first_gain": first_gain, "first_shift": first_shift, "second_gain": second_gain, "second_shift": second_shift}


highest_precision = lax.Precision.HIGHEST
norm_epsilon = 1e-05
masked_score = -1000000000.0

@jax.custom_vjp
def low(v):
    return lax.optimization_barrier(v.astype(jnp.bfloat16)).astype(jnp.float32)

@jax.custom_vjp
def low_back(v):
    return v

def low_keep(v):
    return (low(v), None)

def low_pass(kept, grad):
    return (grad,)

def back_keep(v):
    return (v, None)

def back_low(kept, grad):
    return (low(grad),)
low.defvjp(low_keep, low_pass)
low_back.defvjp(back_keep, back_low)

def rounded(inputs):
    return low(low_back(inputs))

def layer_norm(inputs, norm_gain, norm_shift):
    center = inputs - lax.optimization_barrier(jnp.mean(inputs, axis=-1, keepdims=True))
    spread = lax.optimization_barrier(jnp.mean(center * center, axis=-1, keepdims=True))
    return center * lax.rsqrt(spread + norm_epsilon) * norm_gain + norm_shift

def attend_block(query_block, segment_block, key_rows, value_rows, key_segments):
    count_rows = query_block.shape[0]
    query_heads = query_block.reshape(count_rows, H, HD)
    key_heads = key_rows.reshape(key_rows.shape[0], H, HD)
    value_heads = value_rows.reshape(value_rows.shape[0], H, HD)
    scores = jnp.einsum('qhd,khd->hqk', query_heads, key_heads, precision=highest_precision) * HD ** (-0.5)
    scores = low_back(scores)
    same_doc = segment_block[:, None] == key_segments[None, :]
    scores = jnp.where(same_doc[None], scores, masked_score)
    attn_probs = low(jax.nn.softmax(scores, axis=-1))
    context = jnp.einsum('hqk,khd->qhd', attn_probs, value_heads, precision=highest_precision)
    return context.reshape(count_rows, H * HD)
checked_block = jax.checkpoint(attend_block)

def sequence_layer(weights, sequence_tokens, sequence_segments):
    query_weight, key_weight, value_weight, output_weight, inner_weight, outer_weight, query_bias, value_bias, output_bias, inner_bias, outer_bias, first_gain, first_shift, second_gain, second_shift = weights
    length = sequence_tokens.shape[0]
    model_width = sequence_tokens.shape[1]
    queries = rounded(jnp.dot(sequence_tokens, query_weight, precision=highest_precision) + query_bias)
    key_rows = rounded(jnp.dot(sequence_tokens, key_weight, precision=highest_precision))
    value_rows = rounded(jnp.dot(sequence_tokens, value_weight, precision=highest_precision) + value_bias)
    block_rows = min(512, length)
    block_count = length // block_rows
    query_blocks = queries.reshape(block_count, block_rows, model_width)
    segment_blocks = sequence_segments.reshape(block_count, block_rows)

    def one_block(pieces):
        return checked_block(pieces[0], pieces[1], key_rows, value_rows, sequence_segments)
    context = lax.map(one_block, (query_blocks, segment_blocks)).reshape(length, model_width)
    context = rounded(context)
    attention = low_back(jnp.dot(context, output_weight, precision=highest_precision) + output_bias)
    hidden_one = layer_norm(sequence_tokens + attention, first_gain, first_shift)
    inner = low_back(jnp.dot(low(hidden_one), inner_weight, precision=highest_precision) + inner_bias)
    active = low(jax.nn.gelu(inner, approximate=False))
    feed = low_back(jnp.dot(active, outer_weight, precision=highest_precision) + outer_bias)
    return layer_norm(hidden_one + feed, second_gain, second_shift)

def reference(tokens, segment_ids, out_grad, query_weight, key_weight, value_weight, output_weight, inner_weight, outer_weight, query_bias, value_bias, output_bias, inner_bias, outer_bias, first_gain, first_shift, second_gain, second_shift):
    weights = tuple((parameter.astype(jnp.float32) for parameter in (query_weight, key_weight, value_weight, output_weight, inner_weight, outer_weight, query_bias, value_bias, output_bias, inner_bias, outer_bias, first_gain, first_shift, second_gain, second_shift)))

    def one_sequence(totals, inputs):
        sequence_tokens, sequence_segments, sequence_grad = inputs

        def forward_one(layer_weights, layer_tokens):
            return sequence_layer(layer_weights, layer_tokens, sequence_segments)
        result, pullback = jax.vjp(forward_one, weights, sequence_tokens.astype(jnp.float32))
        grad_weights, grad_tokens = pullback(sequence_grad.astype(jnp.float32))
        totals = jax.tree.map(jnp.add, totals, grad_weights)
        return (totals, (result.astype(jnp.bfloat16), grad_tokens.astype(jnp.bfloat16)))
    starting = tuple((jnp.zeros(parameter.shape, jnp.float32) for parameter in weights))
    totals, (layer_out, input_grad) = lax.scan(one_sequence, starting, (tokens, segment_ids, out_grad))
    return (layer_out, input_grad, totals[0], totals[1], totals[2], totals[3], totals[4], totals[5], totals[6], totals[7], totals[8], totals[9], totals[10], totals[11], totals[12], totals[13], totals[14])
```

```python
from functools import reduce

import jax
import jax.numpy as jnp
from jax import lax
from jax.experimental import pallas as pl
from jax.experimental.pallas import tpu as pltpu
from jax.sharding import PartitionSpec as P

H = 12
MICRO = 2
SEQ_MB = 1


norm_epsilon = 1e-05
masked_score = -1000000000.0


def layer_norm(inputs, norm_gain, norm_shift):
    center = inputs - jnp.mean(inputs, axis=-1, keepdims=True)
    spread = jnp.mean(center * center, axis=-1, keepdims=True)
    return center * lax.rsqrt(spread + norm_epsilon) * norm_gain + norm_shift


def exact_gelu(inputs):
    return jax.nn.gelu(inputs, approximate=False)


def times_transpose(left, right):
    return lax.dot_general(
        left, right, (((1,), (1,)), ((), ())), preferred_element_type=jnp.float32
    )


def transpose_times(left, right):
    return lax.dot_general(
        left, right, (((0,), (0,)), ((), ())), preferred_element_type=jnp.float32
    )


def column_total(inputs):
    return jnp.sum(inputs.astype(jnp.float32), axis=0)


def masked_scores(query_group, key_group, same_doc, score_scale):
    scores = (
        jnp.einsum("bqhd,bkhd->bhqk", query_group, key_group, preferred_element_type=jnp.float32)
        * score_scale
    )
    return jnp.where(same_doc[:, None], scores, masked_score)


def group_forward(query_group, key_group, value_group, same_doc, score_scale):
    scores = masked_scores(query_group, key_group, same_doc, score_scale)
    highest = jnp.max(scores, axis=-1, keepdims=True)
    log_total = highest + jnp.log(jnp.sum(jnp.exp(scores - highest), axis=-1, keepdims=True))
    weights_low = jnp.exp(scores - log_total).astype(jnp.bfloat16)
    context = jnp.einsum(
        "bhqk,bkhd->bqhd", weights_low, value_group, preferred_element_type=jnp.float32
    )
    return (context.astype(jnp.bfloat16), log_total)


def group_backward(
    query_group, key_group, value_group, same_doc, log_total, grad_context, score_scale
):
    attn_weights = jnp.exp(masked_scores(query_group, key_group, same_doc, score_scale) - log_total)
    weights_low = attn_weights.astype(jnp.bfloat16)
    grad_weights = jnp.einsum(
        "bqhd,bkhd->bhqk", grad_context, value_group, preferred_element_type=jnp.float32
    )
    centre = jnp.sum(attn_weights * grad_weights, axis=-1, keepdims=True)
    grad_scores = (attn_weights * (grad_weights - centre)).astype(jnp.bfloat16)
    grad_query = jnp.einsum(
        "bhqk,bkhd->bqhd", grad_scores, key_group, preferred_element_type=jnp.float32
    )
    grad_query = (grad_query * score_scale).astype(jnp.bfloat16)
    grad_key = (
        jnp.einsum("bhqk,bqhd->bkhd", grad_scores, query_group, preferred_element_type=jnp.float32)
        * score_scale
    )
    grad_value = jnp.einsum(
        "bhqk,bqhd->bkhd", weights_low, grad_context, preferred_element_type=jnp.float32
    )
    return (grad_query, grad_key, grad_value)


def merge_groups(stacked, row_total, model_width):
    return jnp.moveaxis(stacked, 0, 2).reshape(row_total, model_width)


def gradient_terms(
    token_rows,
    context_rows,
    hidden_rows,
    active_rows,
    grad_queries,
    grad_keys,
    grad_values,
    grad_attention,
    grad_inner,
    grad_feed,
    norm_grads,
):
    return (
        transpose_times(token_rows, grad_queries),
        transpose_times(token_rows, grad_keys),
        transpose_times(token_rows, grad_values),
        transpose_times(context_rows, grad_attention),
        transpose_times(hidden_rows, grad_inner),
        transpose_times(active_rows, grad_feed),
        column_total(grad_queries),
        column_total(grad_values),
        column_total(grad_attention),
        column_total(grad_inner),
        column_total(grad_feed),
        norm_grads[0],
        norm_grads[1],
        norm_grads[2],
        norm_grads[3],
    )


def on_device(
    tokens,
    segment_ids,
    out_grad,
    query_weight,
    key_weight,
    value_weight,
    output_weight,
    inner_weight,
    outer_weight,
    query_bias,
    value_bias,
    output_bias,
    inner_bias,
    outer_bias,
    first_gain,
    first_shift,
    second_gain,
    second_shift,
):
    row_count = tokens.shape[1]
    model_width = tokens.shape[2]
    head_count = H
    head_size = model_width // head_count
    per_group = max(1, min(head_count, 128 // head_size))
    group_width = per_group * head_size
    group_count = head_count // per_group
    score_scale = head_size ** (-0.5)
    seq_count = SEQ_MB
    flat_rows = seq_count * row_count
    all_segments = lax.all_gather(segment_ids, "grp", axis=1, tiled=True)
    outputs = []
    input_grads = []
    shares_list = []
    for batch_index in range(MICRO):
        offset = batch_index * seq_count
        local_tokens = tokens[offset : offset + seq_count]
        flat_tokens = local_tokens.reshape(flat_rows, model_width)
        gathered = (
            lax.all_gather(query_weight, "grp", axis=0, tiled=True),
            lax.all_gather(key_weight, "grp", axis=0, tiled=True),
            lax.all_gather(value_weight, "grp", axis=0, tiled=True),
            lax.all_gather(output_weight, "grp", axis=0, tiled=True),
            lax.all_gather(inner_weight, "grp", axis=0, tiled=True),
            lax.all_gather(outer_weight, "grp", axis=0, tiled=True),
            lax.all_gather(query_bias, "grp", axis=0, tiled=True),
            lax.all_gather(value_bias, "grp", axis=0, tiled=True),
            lax.all_gather(output_bias, "grp", axis=0, tiled=True),
            lax.all_gather(inner_bias, "grp", axis=0, tiled=True),
            lax.all_gather(outer_bias, "grp", axis=0, tiled=True),
            lax.all_gather(first_gain, "grp", axis=0, tiled=True),
            lax.all_gather(first_shift, "grp", axis=0, tiled=True),
            lax.all_gather(second_gain, "grp", axis=0, tiled=True),
            lax.all_gather(second_shift, "grp", axis=0, tiled=True),
        )
        full_query, full_key, full_value, full_output, full_inner, full_outer = gathered[:6]
        (
            bias_query,
            bias_value,
            bias_output,
            bias_inner,
            bias_outer,
            gain_first,
            shift_first,
            gain_second,
            shift_second,
        ) = [vector.astype(jnp.float32) for vector in gathered[6:]]
        queries = (
            jnp.dot(flat_tokens, full_query, preferred_element_type=jnp.float32) + bias_query
        ).astype(jnp.bfloat16)
        key_rows = jnp.dot(flat_tokens, full_key, preferred_element_type=jnp.float32).astype(
            jnp.bfloat16
        )
        value_rows = (
            jnp.dot(flat_tokens, full_value, preferred_element_type=jnp.float32) + bias_value
        ).astype(jnp.bfloat16)
        key_split = key_rows.reshape(seq_count, row_count, model_width)
        value_split = value_rows.reshape(seq_count, row_count, model_width)
        key_all, value_all = (
            lax.all_gather(key_split, "grp", axis=1, tiled=True),
            lax.all_gather(value_split, "grp", axis=1, tiled=True),
        )
        length = key_all.shape[1]
        local_segments = segment_ids[offset : offset + seq_count]
        far_segments = all_segments[offset : offset + seq_count]
        same_doc = local_segments[:, :, None] == far_segments[:, None, :]
        query_split = queries.reshape(seq_count, row_count, model_width)

        def slice_group(array, group_index):
            piece = lax.dynamic_slice_in_dim(array, group_index * group_width, group_width, 2)
            return piece.reshape(array.shape[0], array.shape[1], per_group, head_size)

        def forward_group(group_index):
            context, log_total = group_forward(
                slice_group(query_split, group_index),
                slice_group(key_all, group_index),
                slice_group(value_all, group_index),
                same_doc,
                score_scale,
            )
            return (context.reshape(seq_count, row_count, group_width), log_total)

        context_groups, log_totals = lax.map(forward_group, jnp.arange(group_count))
        context_rows = merge_groups(context_groups, flat_rows, model_width)
        attention = (
            jnp.dot(context_rows, full_output, preferred_element_type=jnp.float32) + bias_output
        )
        residual_one = flat_tokens.astype(jnp.float32) + attention
        hidden_one, norm_one_pullback = jax.vjp(layer_norm, residual_one, gain_first, shift_first)
        hidden_low = hidden_one.astype(jnp.bfloat16)
        inner_pre = jnp.dot(hidden_low, full_inner, preferred_element_type=jnp.float32) + bias_inner
        activation, gelu_pullback = jax.vjp(exact_gelu, inner_pre)
        active_low = activation.astype(jnp.bfloat16)
        feed = jnp.dot(active_low, full_outer, preferred_element_type=jnp.float32) + bias_outer
        output_rows, norm_two_pullback = jax.vjp(
            layer_norm, hidden_one + feed, gain_second, shift_second
        )
        outputs.append(output_rows.astype(jnp.bfloat16).reshape(seq_count, row_count, model_width))
        cotangent = (
            out_grad[offset : offset + seq_count]
            .reshape(flat_rows, model_width)
            .astype(jnp.float32)
        )
        grad_two, grad_gain_two, grad_shift_two = norm_two_pullback(cotangent)
        grad_feed = grad_two.astype(jnp.bfloat16)
        grad_active = times_transpose(grad_feed, full_outer)
        grad_inner = gelu_pullback(grad_active)[0].astype(jnp.bfloat16)
        grad_hidden = grad_two + times_transpose(grad_inner, full_inner)
        grad_one, grad_gain_one, grad_shift_one = norm_one_pullback(grad_hidden)
        grad_attention = grad_one.astype(jnp.bfloat16)
        grad_context = times_transpose(grad_attention, full_output).astype(jnp.bfloat16)
        grad_context = grad_context.reshape(seq_count, row_count, model_width)

        def backward_group(pieces):
            group_index, log_total = pieces
            grad_query, grad_key, grad_value = group_backward(
                slice_group(query_split, group_index),
                slice_group(key_all, group_index),
                slice_group(value_all, group_index),
                same_doc,
                log_total,
                slice_group(grad_context, group_index),
                score_scale,
            )
            return (
                grad_query.reshape(seq_count, row_count, group_width),
                grad_key.reshape(seq_count, length, group_width),
                grad_value.reshape(seq_count, length, group_width),
            )

        query_groups, key_groups, value_groups = lax.map(
            backward_group, (jnp.arange(group_count), log_totals)
        )
        key_owned, value_owned = (
            lax.psum_scatter(key_groups, "grp", scatter_dimension=2, tiled=True),
            lax.psum_scatter(value_groups, "grp", scatter_dimension=2, tiled=True),
        )
        grad_keys = merge_groups(key_owned, flat_rows, model_width).astype(jnp.bfloat16)
        grad_values = merge_groups(value_owned, flat_rows, model_width).astype(jnp.bfloat16)
        grad_queries = merge_groups(query_groups, flat_rows, model_width)
        grad_tokens = (
            grad_one
            + times_transpose(grad_queries, full_query)
            + times_transpose(grad_keys, full_key)
            + times_transpose(grad_values, full_value)
        )
        input_grads.append(
            grad_tokens.astype(jnp.bfloat16).reshape(seq_count, row_count, model_width)
        )
        norm_grads = (grad_gain_one, grad_shift_one, grad_gain_two, grad_shift_two)
        terms = gradient_terms(
            flat_tokens,
            context_rows,
            hidden_low,
            active_low,
            grad_queries,
            grad_keys,
            grad_values,
            grad_attention,
            grad_inner,
            grad_feed,
            norm_grads,
        )
        shares = (
            lax.psum_scatter(terms[0], "grp", scatter_dimension=0, tiled=True),
            lax.psum_scatter(terms[1], "grp", scatter_dimension=0, tiled=True),
            lax.psum_scatter(terms[2], "grp", scatter_dimension=0, tiled=True),
            lax.psum_scatter(terms[3], "grp", scatter_dimension=0, tiled=True),
            lax.psum_scatter(terms[4], "grp", scatter_dimension=0, tiled=True),
            lax.psum_scatter(terms[5], "grp", scatter_dimension=0, tiled=True),
            lax.psum_scatter(terms[6], "grp", scatter_dimension=0, tiled=True),
            lax.psum_scatter(terms[7], "grp", scatter_dimension=0, tiled=True),
            lax.psum_scatter(terms[8], "grp", scatter_dimension=0, tiled=True),
            lax.psum_scatter(terms[9], "grp", scatter_dimension=0, tiled=True),
            lax.psum_scatter(terms[10], "grp", scatter_dimension=0, tiled=True),
            lax.psum_scatter(terms[11], "grp", scatter_dimension=0, tiled=True),
            lax.psum_scatter(terms[12], "grp", scatter_dimension=0, tiled=True),
            lax.psum_scatter(terms[13], "grp", scatter_dimension=0, tiled=True),
            lax.psum_scatter(terms[14], "grp", scatter_dimension=0, tiled=True),
        )
        shares_list.append(shares)
    owned = reduce(
        lambda left_part, right_part: jax.tree.map(jnp.add, left_part, right_part), shares_list
    )
    summed = (
        lax.psum(owned[0].astype(jnp.bfloat16), "rep").astype(jnp.float32),
        lax.psum(owned[1].astype(jnp.bfloat16), "rep").astype(jnp.float32),
        lax.psum(owned[2].astype(jnp.bfloat16), "rep").astype(jnp.float32),
        lax.psum(owned[3].astype(jnp.bfloat16), "rep").astype(jnp.float32),
        lax.psum(owned[4].astype(jnp.bfloat16), "rep").astype(jnp.float32),
        lax.psum(owned[5].astype(jnp.bfloat16), "rep").astype(jnp.float32),
        lax.psum(owned[6].astype(jnp.bfloat16), "rep").astype(jnp.float32),
        lax.psum(owned[7].astype(jnp.bfloat16), "rep").astype(jnp.float32),
        lax.psum(owned[8].astype(jnp.bfloat16), "rep").astype(jnp.float32),
        lax.psum(owned[9].astype(jnp.bfloat16), "rep").astype(jnp.float32),
        lax.psum(owned[10].astype(jnp.bfloat16), "rep").astype(jnp.float32),
        lax.psum(owned[11].astype(jnp.bfloat16), "rep").astype(jnp.float32),
        lax.psum(owned[12].astype(jnp.bfloat16), "rep").astype(jnp.float32),
        lax.psum(owned[13].astype(jnp.bfloat16), "rep").astype(jnp.float32),
        lax.psum(owned[14].astype(jnp.bfloat16), "rep").astype(jnp.float32),
    )
    return (
        jnp.concatenate(outputs, axis=0),
        jnp.concatenate(input_grads, axis=0),
        summed[0],
        summed[1],
        summed[2],
        summed[3],
        summed[4],
        summed[5],
        summed[6],
        summed[7],
        summed[8],
        summed[9],
        summed[10],
        summed[11],
        summed[12],
        summed[13],
        summed[14],
    )


HEAD = 32
LANES = 128
QB = 256
KB = 256
AWAY = 2.0 ** 100
MESH = pl.DeviceIdType.MESH
BIG = 100 * 1024 * 1024 // 2
LOG2E = 1.4426950408889634


def halves(value):
    first = value.astype(jnp.bfloat16).astype(jnp.float32)
    rest = value - first
    second = rest.astype(jnp.bfloat16).astype(jnp.float32)
    third = (rest - second).astype(jnp.bfloat16).astype(jnp.float32)
    return first, second, third


def dot(left, right):
    return jnp.dot(left, right, preferred_element_type=jnp.float32)


def iota(shape, dim):
    return lax.broadcasted_iota(jnp.int32, shape, dim)


def where_am_i():
    r = lax.axis_index("rep")
    g = lax.axis_index("grp")
    return r, g, lax.div(g, 2), lax.rem(g, 2)


def remote(src, dst, send, recv, r, g):
    return pltpu.make_async_remote_copy(
        src_ref=src, dst_ref=dst, send_sem=send, recv_sem=recv, device_id=(r, g), device_id_type=MESH
    )


def greet(r, g, reps, group):
    barrier = pltpu.get_barrier_semaphore()
    for d in range(1, group):
        pl.semaphore_signal(barrier, inc=1, device_id=(r, lax.rem(g + d, group)), device_id_type=MESH)
    for d in range(1, reps):
        pl.semaphore_signal(barrier, inc=1, device_id=(lax.rem(r + d, reps), g), device_id_type=MESH)
    pl.semaphore_wait(barrier, group + reps - 2)


def gather_kernel(
    tok, wp, small, x_out, w_out, s_out,
    lsem, tsend, trecv, psend, wsend1, wrecv1, wsend2, wrecv2, wsend3, wrecv3, ssend, srecv,
):
    r, g, z, c = where_am_i()
    reps, chips = 4, 4
    p = 2 * z + 1 - c
    greet(r, g, reps, 2 * chips)
    own_w = pltpu.make_async_copy(wp.at[r], w_out.at[r, c, z], lsem.at[1])
    own_w.start()
    own_x = pltpu.make_async_copy(tok.at[c], x_out.at[g], lsem.at[0])
    own_x.start()
    own_s = pltpu.make_async_copy(small, s_out.at[g], lsem.at[2])
    own_s.start()
    swap = remote(tok.at[1 - c], x_out.at[g], psend, trecv.at[g], r, p)
    swap.start()

    first = []
    for d in range(1, chips):
        zz = lax.rem(z + d, chips)
        copy = remote(wp.at[r], w_out.at[r, c, z], wsend1.at[d - 1], wrecv1.at[z], r, 2 * zz + c)
        copy.start()
        first.append(copy)
    smalls = []
    for d in range(1, 2 * chips):
        copy = remote(small, s_out.at[g], ssend.at[d - 1], srecv.at[g], r, lax.rem(g + d, 2 * chips))
        copy.start()
        smalls.append(copy)

    def pass_on(b, src, way):
        to = g + 2 if way == 0 else g - 2
        return remote(src, x_out.at[b], tsend.at[way, b], trecv.at[b], r, to)

    def forward(b, src, way):
        ok = z < chips - 1 if way == 0 else z > 0

        @pl.when(ok)
        def _():
            pass_on(b, src, way).start()

    def arrived(b):
        remote(x_out.at[b], x_out.at[b], tsend.at[0, b], trecv.at[b], r, p).wait_recv()

    forward(g, tok.at[c], 0)
    forward(g, tok.at[c], 1)
    arrived(p)
    forward(p, x_out.at[p], 0)
    forward(p, x_out.at[p], 1)

    def tokens_from(d):
        for k in range(2):
            @pl.when(z >= d)
            def _():
                b = 2 * (z - d) + (c if k == 0 else 1 - c)
                arrived(b)
                forward(b, x_out.at[b], 0)

            @pl.when(z + d < chips)
            def _():
                b = 2 * (z + d) + (c if k == 0 else 1 - c)
                arrived(b)
                forward(b, x_out.at[b], 1)

    tokens_from(1)
    own_w.wait()
    for d in range(1, chips):
        zz = lax.rem(z + d, chips)
        remote(wp.at[r], w_out.at[r, c, zz], wsend1.at[0], wrecv1.at[zz], r, g).wait_recv()
    second = []
    for d in range(1, reps):
        copy = remote(
            w_out.at[r, c], w_out.at[r, c], wsend2.at[d - 1], wrecv2.at[r], lax.rem(r + d, reps), g
        )
        copy.start()
        second.append(copy)
    third = [remote(w_out.at[r, c], w_out.at[r, c], wsend3.at[r], wrecv3.at[r], r, p)]
    third[0].start()
    tokens_from(2)
    for d in range(1, reps):
        q = lax.rem(r + d, reps)
        remote(w_out.at[q, c], w_out.at[q, c], wsend2.at[0], wrecv2.at[q], r, p).wait_recv()
        copy = remote(w_out.at[q, c], w_out.at[q, c], wsend3.at[q], wrecv3.at[q], r, p)
        copy.start()
        third.append(copy)
    tokens_from(3)
    for q in range(reps):
        remote(w_out.at[q, 1 - c], w_out.at[q, 1 - c], wsend3.at[q], wrecv3.at[q], r, p).wait_recv()
    for d in range(1, 2 * chips):
        b = lax.rem(g + d, 2 * chips)
        remote(small, s_out.at[b], ssend.at[0], srecv.at[b], r, p).wait_recv()
    own_x.wait()
    own_s.wait()
    swap.wait_send()
    for copy in first + smalls + second + third:
        copy.wait_send()
    for b in range(2 * chips):
        @pl.when((z < chips - 1) & (b < 2 * z + 2))
        def _():
            pass_on(b, x_out.at[b], 0).wait_send()

        @pl.when((z > 0) & (b >= 2 * z))
        def _():
            pass_on(b, x_out.at[b], 1).wait_send()


def gather(tokens, wp, small):
    dma = pltpu.SemaphoreType.DMA
    anywhere = pl.BlockSpec(memory_space=pl.ANY)
    rows, width = tokens.shape[1:]
    return pl.pallas_call(
        gather_kernel,
        name="gather",
        out_shape=(
            jax.ShapeDtypeStruct((8, rows, width), jnp.bfloat16),
            jax.ShapeDtypeStruct((4, 2, 4) + wp.shape[1:], jnp.bfloat16),
            jax.ShapeDtypeStruct((8,) + small.shape, jnp.bfloat16),
        ),
        in_specs=[anywhere] * 3,
        out_specs=[anywhere] * 3,
        scratch_shapes=[
            dma((3,)), dma((2, 8)), dma((8,)), dma, dma((3,)), dma((4,)), dma((3,)), dma((4,)),
            dma((4,)), dma((4,)), dma((7,)), dma((8,)),
        ],
        compiler_params=pltpu.CompilerParams(collective_id=1, has_side_effects=True),
    )(tokens, wp, small)


def span_of(starts, q0, docs):
    low = jnp.int32(0)
    high = starts[docs]
    for d in range(docs):
        low = jnp.where(starts[d] <= q0, jnp.maximum(low, starts[d]), low)
        high = jnp.where(starts[d + 1] >= q0 + QB, jnp.minimum(high, starts[d + 1]), high)
    first = lax.div(low, LANES)
    last = lax.div(high + LANES - 1, LANES)
    steps = lax.div(last - first + KB // LANES - 1, KB // LANES)
    total = lax.div(starts[docs], LANES)
    first = jnp.minimum(first, total - steps * (KB // LANES))
    return first, steps


def attend_kernel(
    place, x, w, bias, seg, kv, qt, kt, qr, ctx, ctx32, spans, wrow, wtr, vt, acc, starts,
):
    heads = kv.shape[0]
    length, width = x.shape
    blocks, hw, rows = ctx.shape
    docs = 8
    z = place[0]
    c = place[1]
    span = heads * HEAD

    full = [
        jnp.concatenate([w[g % 2, g // 2, 48 * i : 48 * i + 48, :] for g in range(8)], axis=0)
        for i in range(3)
    ]
    lane = iota((width, heads * LANES), 1)
    head, inner = lax.div(lane, LANES), lax.rem(lane, LANES)
    column = span * z + head * HEAD + lax.rem(inner, HEAD)
    hit = iota((width, heads * LANES), 0) == column
    pick_k = jnp.where(hit & (inner < 64), 1.0, 0.0).astype(jnp.bfloat16)
    pick_v = jnp.where(hit & (inner >= 64) & (inner < 96), 1.0, 0.0).astype(jnp.bfloat16)
    pick_q = jnp.where(hit & (inner >= 32) & (inner < 64), 1.0, 0.0).astype(jnp.bfloat16)
    wrow[0] = (dot(full[1], pick_k) + dot(full[2], pick_v)).astype(jnp.bfloat16)
    wrow[1] = dot(full[0], pick_q).astype(jnp.bfloat16)
    row_kv = dot(bias[1:2, :], pick_v)
    row_q = dot(bias[0:1, :], pick_q)
    pick_t = jnp.where(
        iota((span, width), 1) == span * z + iota((span, width), 0), 1.0, 0.0
    ).astype(jnp.bfloat16)
    for i in range(3):
        wtr[i] = lax.dot_general(
            pick_t, full[i], (((1,), (1,)), ((), ())), preferred_element_type=jnp.float32
        ).astype(jnp.bfloat16)
    column_bias = lax.dot_general(
        pick_t, bias[...], (((1,), (1,)), ((), ())), preferred_element_type=jnp.float32
    )
    col_q, col_v = column_bias[:, 0:1], column_bias[:, 1:2]

    ids = seg[...]
    starts[0] = jnp.int32(0)
    for d in range(1, docs):
        starts[d] = jnp.sum(jnp.where(ids < d, 1.0, 0.0)).astype(jnp.int32)
    starts[docs] = jnp.int32(length)

    scale = (HEAD ** -0.5) * LOG2E
    one_lane = lax.rem(iota((1, heads * LANES), 1), LANES)
    ones_row = jnp.where((one_lane >= 104) & (one_lane < 107), 1.0, 0.0)

    def project(b, carry):
        r0 = pl.multiple_of(b * rows, rows)
        xb = x[pl.ds(r0, rows), :]
        idrow = seg[pl.ds(b, 1), :]
        same = jnp.where(iota((8, rows), 0) == idrow, 1.0, 0.0)
        hot = jnp.concatenate(
            [jnp.zeros((96, rows), jnp.float32), same, jnp.zeros((24, rows), jnp.float32)], axis=0
        ).T
        flat = dot(xb, wrow[0]) + (row_kv + ones_row)
        for h in range(heads):
            kv[h, pl.ds(r0, rows), :] = (flat[:, h * LANES : (h + 1) * LANES] + hot).astype(
                jnp.bfloat16
            )
        flat = (dot(xb, wrow[1]) + row_q).astype(jnp.bfloat16)
        for h in range(heads):
            qr[h, pl.ds(r0, rows), :] = flat[:, h * LANES : (h + 1) * LANES]

        def turned(i):
            return lax.dot_general(
                wtr[i], xb, (((1,), (1,)), ((), ())), preferred_element_type=jnp.float32
            )

        q_t = (turned(0) + col_q).astype(jnp.bfloat16).astype(jnp.float32) * scale
        q_hi = q_t.astype(jnp.bfloat16)
        q_lo = (q_t - q_hi.astype(jnp.float32)).astype(jnp.bfloat16)
        k_t = turned(1).astype(jnp.bfloat16)
        v_t = (turned(2) + col_v).astype(jnp.bfloat16)
        far = jnp.concatenate([(same - 1.0) * AWAY, jnp.zeros((8, rows), jnp.float32)], axis=0)
        far = far.astype(jnp.bfloat16)
        one = jnp.where(iota((16, rows), 0) == 0, 1.0, 0.0).astype(jnp.bfloat16)
        cols = pl.ds(r0, rows)
        for h in range(heads):
            part = slice(h * HEAD, (h + 1) * HEAD)
            qt[h, 0:32, cols] = q_hi[part]
            qt[h, 32:64, cols] = q_lo[part]
            qt[h, 64:96, cols] = jnp.zeros((32, rows), jnp.bfloat16)
            qt[h, 96:112, cols] = far
            qt[h, 112:128, cols] = jnp.zeros((16, rows), jnp.bfloat16)
            kt[h, :, cols] = k_t[part]
            vt[h, 0:32, cols] = v_t[part]
            vt[h, 32:48, cols] = one
        return carry

    lax.fori_loop(0, blocks, project, 0)

    per = rows // QB

    def query_block(b, carry):
        q0 = pl.multiple_of(b * QB, QB)
        first, steps = span_of(starts, q0, docs)
        spans[0, b] = first
        spans[1, b] = steps
        acc[...] = jnp.zeros_like(acc)

        def key_block(i, tops):
            k0 = pl.multiple_of((first + i * (KB // LANES)) * LANES, LANES)
            new = []
            for h in range(heads):
                s = dot(kv[h, pl.ds(k0, KB), :], qt[h, :, pl.ds(q0, QB)])
                top = jnp.maximum(tops[h], jnp.max(s, axis=0, keepdims=True))
                p = jnp.exp2(s - top).astype(jnp.bfloat16)
                acc[h] = acc[h] * jnp.exp2(tops[h] - top) + dot(vt[h, :, pl.ds(k0, KB)], p)
                new.append(top)
            return tuple(new)

        lowest = jnp.full((1, QB), -3e38, jnp.float32)
        tops = lax.fori_loop(0, steps, key_block, (lowest,) * heads)
        g = lax.div(b, per)
        off = pl.multiple_of(lax.rem(b, per) * QB, QB)
        same = jnp.where(iota((8, QB), 0) == seg[pl.ds(g, 1), pl.ds(off, QB)], 1.0, 0.0)
        for h in range(heads):
            total = acc[h, 32:33, :]
            out = acc[h, 0:32, :] / total
            ctx[g, h * HEAD : (h + 1) * HEAD, pl.ds(off, QB)] = out.astype(jnp.bfloat16)
            ctx32[g, h * HEAD : (h + 1) * HEAD, pl.ds(off, QB)] = out
            parts = halves(-(tops[h] + jnp.log2(total)))
            tail = jnp.concatenate(
                [(same - 1.0) * AWAY, *parts, jnp.zeros((5, QB), jnp.float32)], axis=0
            )
            qt[h, 96:112, pl.ds(q0, QB)] = tail.astype(jnp.bfloat16)
        return carry

    lax.fori_loop(0, length // QB, query_block, 0)


def attend(place, x, w, bias, seg):
    blocks, rows, width = x.shape
    length = blocks * rows
    heads = 3
    vm = pl.BlockSpec(memory_space=pltpu.VMEM)
    sm = pl.BlockSpec(memory_space=pltpu.SMEM)
    bf, f4 = jnp.bfloat16, jnp.float32
    return pl.pallas_call(
        attend_kernel,
        name="attend",
        out_shape=(
            jax.ShapeDtypeStruct((heads, length, LANES), bf),
            jax.ShapeDtypeStruct((heads, LANES, length), bf),
            jax.ShapeDtypeStruct((heads, HEAD, length), bf),
            jax.ShapeDtypeStruct((heads, length, LANES), bf),
            jax.ShapeDtypeStruct((blocks, heads * HEAD, rows), bf),
            jax.ShapeDtypeStruct((blocks, heads * HEAD, rows), f4),
            jax.ShapeDtypeStruct((2, length // QB), jnp.int32),
        ),
        in_specs=[sm, vm, vm, vm, vm],
        out_specs=[vm] * 6 + [sm],
        scratch_shapes=[
            pltpu.VMEM((2, width, heads * LANES), bf),
            pltpu.VMEM((3, heads * HEAD, width), bf),
            pltpu.VMEM((heads, 48, length), bf),
            pltpu.VMEM((heads, 48, QB), f4),
            pltpu.SMEM((16,), jnp.int32),
        ],
        compiler_params=pltpu.CompilerParams(vmem_limit_bytes=BIG),
    )(place, x.reshape(length, width), w, bias, seg)


def context_kernel(src, dst, lsem, send, recv):
    r, g, z, c = where_am_i()
    greet(r, g, 1, 8)
    own = pltpu.make_async_copy(src.at[g], dst.at[c, z], lsem)
    own.start()
    copies = []
    for d in range(1, 8):
        to = lax.rem(g + d, 8)
        copy = remote(src.at[to], dst.at[c, z], send.at[d - 1], recv.at[g], r, to)
        copy.start()
        copies.append(copy)
    for d in range(1, 8):
        b = lax.rem(g + d, 8)
        remote(src.at[g], dst.at[lax.rem(b, 2), lax.div(b, 2)], send.at[0], recv.at[b], r, b).wait_recv()
    for copy in copies:
        copy.wait_send()
    own.wait()


def exchange_context(ctx):
    dma = pltpu.SemaphoreType.DMA
    anywhere = pl.BlockSpec(memory_space=pl.ANY)
    return pl.pallas_call(
        context_kernel,
        name="exchange_context",
        out_shape=jax.ShapeDtypeStruct((2, 4) + ctx.shape[1:], ctx.dtype),
        in_specs=[anywhere],
        out_specs=anywhere,
        scratch_shapes=[dma, dma((7,)), dma((8,))],
        compiler_params=pltpu.CompilerParams(collective_id=2, has_side_effects=True),
    )(ctx)


def cotangent_kernel(src, pg, dst, pg_out, lsem, send, recv, psend, precv):
    r, g, z, c = where_am_i()
    greet(r, g, 1, 8)
    pair = remote(pg.at[1 - c], pg_out, psend, precv, r, 2 * z + 1 - c)
    pair.start()
    own = pltpu.make_async_copy(src.at[c, z], dst.at[g], lsem)
    own.start()
    copies = []
    for d in range(1, 8):
        to = lax.rem(g + d, 8)
        copy = remote(
            src.at[lax.rem(to, 2), lax.div(to, 2)], dst.at[g], send.at[d - 1], recv.at[g], r, to
        )
        copy.start()
        copies.append(copy)
    for d in range(1, 8):
        b = lax.rem(g + d, 8)
        remote(src.at[c, z], dst.at[b], send.at[0], recv.at[b], r, b).wait_recv()
    for copy in copies:
        copy.wait_send()
    pair.wait()
    own.wait()


def exchange_cotangent(src, pg):
    dma = pltpu.SemaphoreType.DMA
    anywhere = pl.BlockSpec(memory_space=pl.ANY)
    return pl.pallas_call(
        cotangent_kernel,
        name="exchange_cotangent",
        out_shape=(
            jax.ShapeDtypeStruct((8,) + src.shape[2:], src.dtype),
            jax.ShapeDtypeStruct(pg.shape[1:], pg.dtype),
        ),
        in_specs=[anywhere] * 2,
        out_specs=[anywhere] * 2,
        scratch_shapes=[dma, dma((7,)), dma((8,)), dma, dma],
        compiler_params=pltpu.CompilerParams(collective_id=3, has_side_effects=True),
    )(src, pg)


def dense_kernel(
    tok, og, ctx, w, vec, inner_bias,
    layer_out, grad_one_out, gctx, pg, wo, wi, wu, gwo, gwi, gwu, sums, inner_sum,
):
    seqs, rows, width = tok.shape
    slabs = wi.shape[0]
    block = 256
    per = rows // block
    for g in range(8):
        c, z = g % 2, g // 2
        wo[48 * g : 48 * g + 48, :] = w[1, c, z, 0:48, :]
        wi[0, 48 * g : 48 * g + 48, :] = w[1, c, z, 48:96, :]
        wi[1, 48 * g : 48 * g + 48, :] = w[1, c, z, 96:144, :]
        wi[2, 48 * g : 48 * g + 48, :] = w[2, c, z, 0:48, :]
        wi[3, 48 * g : 48 * g + 48, :] = w[2, c, z, 48:96, :]
        wu[g // 2, 192 * c : 192 * c + 48, :] = w[2, c, z, 96:144, :]
        wu[g // 2, 192 * c + 48 : 192 * c + 192, :] = w[3, c, z, :, :]
    for ref in (gwo, gwi, gwu, sums, inner_sum):
        ref[...] = jnp.zeros_like(ref)

    out_bias, outer_bias = vec[2:3, :], vec[3:4, :]
    gain_one, shift_one = vec[4:5, :], vec[5:6, :]
    gain_two, shift_two = vec[6:7, :], vec[7:8, :]

    def normal(value):
        centre = value - jnp.mean(value, axis=-1, keepdims=True)
        rate = lax.rsqrt(jnp.mean(centre * centre, axis=-1, keepdims=True) + norm_epsilon)
        return centre * rate, rate

    def normal_back(grad, gain, n, rate):
        u = grad * gain
        return rate * (
            u - jnp.mean(u, axis=-1, keepdims=True) - n * jnp.mean(u * n, axis=-1, keepdims=True)
        )

    def total(value):
        return jnp.sum(value, axis=0, keepdims=True)

    def turn_dot(left, right):
        return lax.dot_general(
            left, right, (((0,), (0,)), ((), ())), preferred_element_type=jnp.float32
        )

    def dot_turn(left, right):
        return lax.dot_general(
            left, right, (((1,), (1,)), ((), ())), preferred_element_type=jnp.float32
        )

    def one(b, carry):
        s = lax.div(b, per)
        r0 = pl.multiple_of(lax.rem(b, per) * block, block)
        here = pl.ds(r0, block)
        ctx_t = ctx[s, :, here]
        context = ctx_t.astype(jnp.float32).T.astype(jnp.bfloat16)
        x = tok[s, here, :].astype(jnp.float32)
        n_one, rate_one = normal(x + (dot(context, wo[...]) + out_bias))
        hidden = n_one * gain_one + shift_one
        low = hidden.astype(jnp.bfloat16)
        low_t = hidden.T.astype(jnp.bfloat16)
        feed = jnp.zeros((block, width), jnp.float32)
        slopes, actives = [], []
        for j in range(slabs):
            inner = dot(low, wi[j]) + inner_bias[:, j * width : (j + 1) * width]
            cdf = 0.5 + 0.5 * lax.erf(inner * (0.5 ** 0.5))
            pdf = jnp.exp(inner * inner * -0.5) * 0.3989422804014327
            slopes.append(cdf + inner * pdf)
            active = inner * cdf
            actives.append(active)
            feed = feed + dot(active.astype(jnp.bfloat16), wu[j])
        n_two, rate_two = normal(hidden + (feed + outer_bias))
        layer_out[s, here, :] = (n_two * gain_two + shift_two).astype(jnp.bfloat16)
        grad = og[s, here, :].astype(jnp.float32)
        grad_two = normal_back(grad, gain_two, n_two, rate_two)
        grad_feed = grad_two.astype(jnp.bfloat16)
        grad_hidden = grad_two
        for j in range(slabs):
            grad_inner = (dot_turn(grad_feed, wu[j]) * slopes[j]).astype(jnp.bfloat16)
            inner_sum[:, j * width : (j + 1) * width] += total(grad_inner.astype(jnp.float32))
            grad_hidden = grad_hidden + dot_turn(grad_inner, wi[j])
            gwi[j] += dot(low_t, grad_inner)
            gwu[j] += dot(actives[j].T.astype(jnp.bfloat16), grad_feed)
        grad_one = normal_back(grad_hidden, gain_one, n_one, rate_one)
        grad_one_out[s, here, :] = grad_one
        grad_att = grad_one.astype(jnp.bfloat16)
        gctx[s, :, here] = dot_turn(wo[...], grad_att).astype(jnp.bfloat16)
        gwo[...] += dot(ctx_t, grad_att)
        sums[0:1, :] += total(grad_att.astype(jnp.float32))
        sums[1:2, :] += total(grad_feed.astype(jnp.float32))
        sums[2:3, :] += total(grad_hidden * n_one)
        sums[3:4, :] += total(grad_hidden)
        sums[4:5, :] += total(grad * n_two)
        sums[5:6, :] += total(grad)
        return carry

    lax.fori_loop(0, seqs * per, one, 0)
    for g in range(8):
        c, z = g % 2, g // 2
        mine = slice(48 * g, 48 * g + 48)
        pg[c, 0, z, 0:48, :] = gwo[mine, :].astype(jnp.bfloat16)
        pg[c, 0, z, 48:96, :] = gwi[0, mine, :].astype(jnp.bfloat16)
        pg[c, 1, z, 0:48, :] = gwi[1, mine, :].astype(jnp.bfloat16)
        pg[c, 1, z, 48:96, :] = gwi[2, mine, :].astype(jnp.bfloat16)
        pg[c, 2, z, 0:48, :] = gwi[3, mine, :].astype(jnp.bfloat16)
        base = 192 * c
        pg[c, 0, z, 96:112, :] = gwu[z, base : base + 16, :].astype(jnp.bfloat16)
        pg[c, 1, z, 96:112, :] = gwu[z, base + 16 : base + 32, :].astype(jnp.bfloat16)
        pg[c, 2, z, 48:112, :] = gwu[z, base + 32 : base + 96, :].astype(jnp.bfloat16)
        pg[c, 3, z, 0:96, :] = gwu[z, base + 96 : base + 192, :].astype(jnp.bfloat16)
        pg[c, 3, z, 96:112, :] = jnp.concatenate(
            [sums[...]]
            + [inner_sum[:, j * width : (j + 1) * width] for j in range(slabs)]
            + [jnp.zeros((6, width), jnp.float32)],
            axis=0,
        ).astype(jnp.bfloat16)


def dense(tok, og, ctx, w, vec, inner_bias):
    seqs, rows, width = tok.shape
    vm = pl.BlockSpec(memory_space=pltpu.VMEM)
    bf, f4 = jnp.bfloat16, jnp.float32
    return pl.pallas_call(
        dense_kernel,
        name="dense",
        out_shape=(
            jax.ShapeDtypeStruct((seqs, rows, width), bf),
            jax.ShapeDtypeStruct((seqs, rows, width), f4),
            jax.ShapeDtypeStruct((seqs, width, rows), bf),
            jax.ShapeDtypeStruct((2, 4, 4, 112, width), bf),
        ),
        in_specs=[vm] * 6,
        out_specs=[vm] * 4,
        scratch_shapes=[
            pltpu.VMEM((width, width), bf),
            pltpu.VMEM((4, width, width), bf),
            pltpu.VMEM((4, width, width), bf),
            pltpu.VMEM((width, width), f4),
            pltpu.VMEM((4, width, width), f4),
            pltpu.VMEM((4, width, width), f4),
            pltpu.VMEM((6, width), f4),
            pltpu.VMEM((1, 4 * width), f4),
        ],
        compiler_params=pltpu.CompilerParams(vmem_limit_bytes=BIG),
    )(tok, og, ctx, w, vec, inner_bias)


def attend_back_kernel(
    place, spans, x, kv, qt, kt, qr, gctx, ctx32, pg, pg_in, out, gq, pr, dt, do, acc, dq,
):
    heads = kv.shape[0]
    length, width = x.shape
    blocks, _, rows = gctx.shape
    z = place[0]
    c = place[1]
    scale = HEAD ** -0.5

    def prepare(g, carry):
        r0 = pl.multiple_of(g * rows, rows)
        cols = pl.ds(r0, rows)
        for h in range(heads):
            part = slice(h * HEAD, (h + 1) * HEAD)
            grad = gctx[g, part, :]
            wide = grad.astype(jnp.float32)
            delta = -jnp.sum(wide * ctx32[g, part, :], axis=0, keepdims=True)
            dt[h, 0:64, cols] = jnp.zeros((64, rows), jnp.bfloat16)
            dt[h, 64:96, cols] = grad
            tail = jnp.concatenate(
                [jnp.zeros((8, rows), jnp.float32), *halves(delta), jnp.zeros((21, rows), jnp.float32)],
                axis=0,
            )
            dt[h, 96:128, cols] = tail.astype(jnp.bfloat16)
            do[h, cols, :] = jnp.concatenate(
                [wide, jnp.zeros((96, rows), jnp.float32)], axis=0
            ).T.astype(jnp.bfloat16)
        return carry

    lax.fori_loop(0, blocks, prepare, 0)
    for s in range(4):
        pr[s] = (pg[c, s].astype(jnp.float32) + pg_in[s].astype(jnp.float32)).astype(jnp.bfloat16)
    acc[...] = jnp.zeros_like(acc)
    per = rows // QB

    def query_block(b, carry):
        q0 = pl.multiple_of(b * QB, QB)
        first = spans[0, b]
        dq[...] = jnp.zeros_like(dq)

        def key_block(i, inner):
            k0 = pl.multiple_of((first + i * (KB // LANES)) * LANES, LANES)
            keys = pl.ds(k0, KB)
            for h in range(heads):
                rows_k = kv[h, keys, :]
                p = jnp.exp2(dot(rows_k, qt[h, :, pl.ds(q0, QB)]))
                ds = (p * dot(rows_k, dt[h, :, pl.ds(q0, QB)])).astype(jnp.bfloat16)
                acc[h, keys, :] += dot(p.astype(jnp.bfloat16), do[h, pl.ds(q0, QB), :]) + dot(
                    ds, qr[h, pl.ds(q0, QB), :]
                )
                dq[h] += dot(kt[h, :, keys], ds)
            return inner

        lax.fori_loop(0, spans[1, b], key_block, 0)
        g = lax.div(b, per)
        off = pl.multiple_of(lax.rem(b, per) * QB, QB)
        for h in range(heads):
            out[g, h * HEAD : (h + 1) * HEAD, pl.ds(off, QB)] = (dq[h] * scale).astype(jnp.bfloat16)
        return carry

    lax.fori_loop(0, length // QB, query_block, 0)

    gq[...] = jnp.zeros_like(gq)
    span = heads * HEAD

    def finish(g, totals):
        r0 = pl.multiple_of(g * rows, rows)
        cols = pl.ds(r0, rows)
        for h in range(heads):
            both = acc[h, cols, :].T
            out[g, 2 * span + h * HEAD : 2 * span + (h + 1) * HEAD, :] = both[0:32].astype(jnp.bfloat16)
            out[g, span + h * HEAD : span + (h + 1) * HEAD, :] = (both[32:64] * scale).astype(
                jnp.bfloat16
            )
        piece = out[g]
        grad = dot(piece, x[cols, :])
        summed = jnp.sum(piece.astype(jnp.float32), axis=1, keepdims=True)
        return totals[0] + grad, totals[1] + summed

    grads, summed = lax.fori_loop(
        0,
        blocks,
        finish,
        (jnp.zeros((3 * span, width), jnp.float32), jnp.zeros((3 * span, 1), jnp.float32)),
    )
    grads_t = grads.T
    for g in range(8):
        cc, zz = g % 2, g // 2
        gq[cc, zz, :, 0 : 3 * span] = grads_t[48 * g : 48 * g + 48, :].astype(jnp.bfloat16)
    for cc in range(2):
        mine = jnp.concatenate(
            [
                summed[48 * cc : 48 * cc + 48, :],
                summed[2 * span + 48 * cc : 2 * span + 48 * cc + 48, :],
                jnp.zeros((48, 94), jnp.float32),
            ],
            axis=1,
        )
        gq[cc, z, :, 3 * span :] = mine.astype(jnp.bfloat16)


def attend_back(place, spans, x, kv, qt, kt, qr, gctx, ctx32, pg, pg_in):
    blocks, rows, width = x.shape
    length = blocks * rows
    heads = kv.shape[0]
    vm = pl.BlockSpec(memory_space=pltpu.VMEM)
    sm = pl.BlockSpec(memory_space=pltpu.SMEM)
    bf, f4 = jnp.bfloat16, jnp.float32
    return pl.pallas_call(
        attend_back_kernel,
        name="attend_back",
        out_shape=(
            jax.ShapeDtypeStruct((blocks, 3 * heads * HEAD, rows), bf),
            jax.ShapeDtypeStruct((2, 4, 48, width), bf),
            jax.ShapeDtypeStruct(pg_in.shape, bf),
        ),
        in_specs=[sm, sm] + [vm] * 9,
        out_specs=[vm] * 3,
        scratch_shapes=[
            pltpu.VMEM((heads, LANES, length), bf),
            pltpu.VMEM((heads, length, LANES), bf),
            pltpu.VMEM((heads, length, LANES), f4),
            pltpu.VMEM((heads, HEAD, QB), f4),
        ],
        compiler_params=pltpu.CompilerParams(vmem_limit_bytes=BIG),
    )(place, spans, x.reshape(length, width), kv, qt, kt, qr, gctx, ctx32, pg, pg_in)


def reduce_kernel(
    src, gq, pr, dst, p_out, q_out,
    gq_in, gq_sum, qa_in, qa_sum, qb_in, pa_in, pa_sum, pb_in, p_own, gq_own, pr_own,
    lsem, send, recv, gsend, grecv, qasend, qarecv, qbsend, qbrecv, qcsend, qcrecv,
    pasend, parecv, pbsend, pbrecv, pcsend, pcrecv,
):
    r, g, z, c = where_am_i()
    greet(r, g, 4, 8)
    pair = remote(gq.at[1 - c], gq_in, gsend, grecv, r, 2 * z + 1 - c)
    pair.start()
    waits = []
    for d in range(1, 4):
        rr = lax.rem(r + d, 4)
        copy = remote(pr.at[rr], pa_in.at[r], pasend.at[d - 1], parecv.at[r], rr, g)
        copy.start()
        waits.append(copy)
    own = pltpu.make_async_copy(src.at[g], dst.at[c, z], lsem.at[0])
    own.start()
    load_g = pltpu.make_async_copy(gq.at[c], gq_own, lsem.at[1])
    load_g.start()
    load_p = pltpu.make_async_copy(pr.at[r], pr_own, lsem.at[2])
    load_p.start()
    for d in range(1, 8):
        to = lax.rem(g + d, 8)
        copy = remote(src.at[to], dst.at[c, z], send.at[d - 1], recv.at[g], r, to)
        copy.start()
        waits.append(copy)

    def f32(value):
        return value.astype(jnp.float32)

    load_g.wait()
    pair.wait_recv()
    gq_sum[...] = (f32(gq_own[...]) + f32(gq_in[...])).astype(jnp.bfloat16)
    for d in range(1, 4):
        rr = lax.rem(r + d, 4)
        copy = remote(gq_sum.at[rr], qa_in.at[r], qasend.at[d - 1], qarecv.at[r], rr, g)
        copy.start()
        waits.append(copy)
    load_p.wait()
    for d in range(1, 4):
        b = lax.rem(r + d, 4)
        remote(pr.at[r], pa_in.at[b], pasend.at[0], parecv.at[b], b, g).wait_recv()
    total = f32(pr_own[...])
    for d in range(1, 4):
        total = total + f32(pa_in[lax.rem(r + d, 4)])
    pa_sum[...] = total.astype(jnp.bfloat16)
    for d in range(1, 4):
        zz = lax.rem(z + d, 4)
        copy = remote(pa_sum.at[zz], pb_in.at[z], pbsend.at[d - 1], pbrecv.at[z], r, 2 * zz + c)
        copy.start()
        waits.append(copy)
    for d in range(1, 4):
        b = lax.rem(r + d, 4)
        remote(gq_sum.at[r], qa_in.at[b], qasend.at[0], qarecv.at[b], b, g).wait_recv()
    total = f32(gq_sum[r])
    for d in range(1, 4):
        total = total + f32(qa_in[lax.rem(r + d, 4)])
    qa_sum[...] = total.astype(jnp.bfloat16)

    @pl.when(z != r)
    def _():
        remote(qa_sum, qb_in.at[z], qbsend, qbrecv.at[z], r, 2 * r + c).start()

    for d in range(1, 4):
        b = lax.rem(z + d, 4)
        remote(pa_sum.at[z], pb_in.at[b], pbsend.at[0], pbrecv.at[b], r, g).wait_recv()
    total = f32(pa_sum[z])
    for d in range(1, 4):
        total = total + f32(pb_in[lax.rem(z + d, 4)])
    p_own[...] = total.astype(jnp.bfloat16)
    keep_p = pltpu.make_async_copy(p_own, p_out.at[r], lsem.at[3])
    keep_p.start()
    for d in range(1, 4):
        rr = lax.rem(r + d, 4)
        copy = remote(p_own, p_out.at[r], pcsend.at[d - 1], pcrecv.at[r], rr, g)
        copy.start()
        waits.append(copy)

    @pl.when(z == r)
    def _():
        for d in range(1, 4):
            b = lax.rem(z + d, 4)
            remote(qa_sum, qb_in.at[b], qbsend, qbrecv.at[b], r, g).wait_recv()
        qb_in[z] = qa_sum[...]
        keep = pltpu.make_async_copy(qb_in, q_out, lsem.at[4])
        keep.start()
        for d in range(1, 4):
            remote(qb_in, q_out, qcsend.at[d - 1], qcrecv, lax.rem(r + d, 4), g).start()
        keep.wait()
        for d in range(1, 4):
            remote(qb_in, q_out, qcsend.at[d - 1], qcrecv, lax.rem(r + d, 4), g).wait_send()

    @pl.when(z != r)
    def _():
        remote(qb_in, q_out, qcsend.at[0], qcrecv, r, g).wait_recv()
        remote(qa_sum, qb_in.at[z], qbsend, qbrecv.at[z], r, 2 * r + c).wait_send()

    for d in range(1, 4):
        b = lax.rem(r + d, 4)
        remote(p_own, p_out.at[b], pcsend.at[0], pcrecv.at[b], b, g).wait_recv()
    for d in range(1, 8):
        b = lax.rem(g + d, 8)
        remote(src.at[g], dst.at[lax.rem(b, 2), lax.div(b, 2)], send.at[0], recv.at[b], r, b).wait_recv()
    pair.wait_send()
    for copy in waits:
        copy.wait_send()
    keep_p.wait()
    own.wait()


def reduce_all(src, gq, pr):
    dma = pltpu.SemaphoreType.DMA
    anywhere = pl.BlockSpec(memory_space=pl.ANY)
    bf = jnp.bfloat16
    width = gq.shape[-1]
    return pl.pallas_call(
        reduce_kernel,
        name="reduce",
        out_shape=(
            jax.ShapeDtypeStruct((2, 4) + src.shape[1:], bf),
            jax.ShapeDtypeStruct((4, 112, width), bf),
            jax.ShapeDtypeStruct((4, 48, width), bf),
        ),
        in_specs=[anywhere] * 3,
        out_specs=[anywhere] * 3,
        scratch_shapes=[
            pltpu.VMEM((4, 48, width), bf),
            pltpu.VMEM((4, 48, width), bf),
            pltpu.VMEM((4, 48, width), bf),
            pltpu.VMEM((48, width), bf),
            pltpu.VMEM((4, 48, width), bf),
            pltpu.VMEM((4, 4, 112, width), bf),
            pltpu.VMEM((4, 112, width), bf),
            pltpu.VMEM((4, 112, width), bf),
            pltpu.VMEM((112, width), bf),
            pltpu.VMEM((4, 48, width), bf),
            pltpu.VMEM((4, 112, width), bf),
            dma((5,)), dma((7,)), dma((8,)), dma, dma, dma((3,)), dma((4,)), dma, dma((4,)),
            dma((3,)), dma, dma((3,)), dma((4,)), dma((3,)), dma((4,)), dma((3,)), dma((4,)),
        ],
        compiler_params=pltpu.CompilerParams(
            collective_id=4, has_side_effects=True, vmem_limit_bytes=BIG // 2
        ),
    )(src, gq, pr)


def finish_kernel(
    place, parts, grad_one, w, p_in, q_in,
    out, g_q, g_k, g_v, g_o, g_in, g_up, rows_out, wq,
):
    seqs, rows, width = grad_one.shape
    span = 96
    for i in range(3):
        for g in range(8):
            wq[i, 48 * g : 48 * g + 48, :] = w[g % 2, g // 2, 48 * i : 48 * i + 48, :]
    for s in range(seqs):
        total = grad_one[s]
        for i in range(3):
            turned = jnp.concatenate(
                [parts[s, z, i * span : (i + 1) * span, :] for z in range(4)], axis=0
            )
            back = turned.astype(jnp.float32).T.astype(jnp.bfloat16)
            total = total + lax.dot_general(
                back, wq[i], (((1,), (1,)), ((), ())), preferred_element_type=jnp.float32
            )
        out[s] = total.astype(jnp.bfloat16)
    wide = [q_in[z].astype(jnp.float32) for z in range(4)]
    for i, ref in enumerate((g_q, g_k, g_v)):
        ref[...] = jnp.concatenate([v[:, i * span : (i + 1) * span] for v in wide], axis=1)
    z = place[0]
    mine = q_in[z].astype(jnp.float32)[:, 3 * span :]
    rows_out[0:48, 0:96] = mine
    rows_out[0:48, 96:384] = jnp.zeros((48, 288), jnp.float32)
    rows_out[48:64, :] = p_in[3, 96:112, :].astype(jnp.float32)
    g_o[...] = p_in[0, 0:48, :].astype(jnp.float32)
    g_in[:, 0:384] = p_in[0, 48:96, :].astype(jnp.float32)
    g_in[:, 384:768] = p_in[1, 0:48, :].astype(jnp.float32)
    g_in[:, 768:1152] = p_in[1, 48:96, :].astype(jnp.float32)
    g_in[:, 1152:1536] = p_in[2, 0:48, :].astype(jnp.float32)
    g_up[0:16, :] = p_in[0, 96:112, :].astype(jnp.float32)
    g_up[16:32, :] = p_in[1, 96:112, :].astype(jnp.float32)
    g_up[32:96, :] = p_in[2, 48:112, :].astype(jnp.float32)
    g_up[96:192, :] = p_in[3, 0:96, :].astype(jnp.float32)


def finish(place, parts, grad_one, w, p_in, q_in):
    seqs, rows, width = grad_one.shape
    vm = pl.BlockSpec(memory_space=pltpu.VMEM)
    sm = pl.BlockSpec(memory_space=pltpu.SMEM)
    bf, f4 = jnp.bfloat16, jnp.float32
    return pl.pallas_call(
        finish_kernel,
        name="finish",
        out_shape=(
            jax.ShapeDtypeStruct((seqs, rows, width), bf),
            jax.ShapeDtypeStruct((48, width), f4),
            jax.ShapeDtypeStruct((48, width), f4),
            jax.ShapeDtypeStruct((48, width), f4),
            jax.ShapeDtypeStruct((48, width), f4),
            jax.ShapeDtypeStruct((48, 4 * width), f4),
            jax.ShapeDtypeStruct((192, width), f4),
            jax.ShapeDtypeStruct((64, width), f4),
        ),
        in_specs=[sm] + [vm] * 5,
        out_specs=[vm] * 8,
        scratch_shapes=[pltpu.VMEM((3, width, width), bf)],
        compiler_params=pltpu.CompilerParams(vmem_limit_bytes=BIG),
    )(place, parts, grad_one, w, p_in, q_in)


def line_of_chips(
    tokens, segment_ids, out_grad, query_weight, key_weight, value_weight, output_weight,
    inner_weight, outer_weight, query_bias, value_bias, output_bias, inner_bias, outer_bias,
    first_gain, first_shift, second_gain, second_shift,
):
    bf = jnp.bfloat16
    width = tokens.shape[2]
    g = lax.axis_index("grp")
    z, c = lax.div(g, 2), lax.rem(g, 2)
    place = jnp.stack([z, c]).astype(jnp.int32)
    wp = jnp.concatenate(
        [query_weight, key_weight, value_weight, output_weight]
        + [inner_weight[:, j * width : (j + 1) * width] for j in range(4)]
        + [outer_weight],
        axis=0,
    ).reshape(4, 144, width)
    vectors = jnp.concatenate(
        [query_bias, value_bias, output_bias, outer_bias, first_gain, first_shift, second_gain, second_shift]
    )
    small = jnp.concatenate(
        [
            jnp.pad(vectors, (0, 128))[None],
            jnp.pad(inner_bias, (0, 320))[None],
            segment_ids.astype(bf),
            jnp.zeros((12, 512), bf),
        ],
        axis=0,
    )
    x, w, s = gather(tokens, wp, small)
    vec = s[:, 0, :width].reshape(8, 8, 48).transpose(1, 0, 2).reshape(8, width)
    inner_vec = s[:, 1, :192].reshape(1, 4 * width).astype(jnp.float32)
    seg = jnp.where(c == 0, s[:, 2], s[:, 3]).astype(jnp.int32)
    kv, qt, kt, qr, ctx, ctx32, spans = attend(place, x, w[0], vec, seg)
    mine = exchange_context(ctx).reshape(2, width, -1)
    layer_out, grad_one, gctx, pg = dense(
        tokens, out_grad, mine, w, vec.astype(jnp.float32), inner_vec
    )
    gctx_in, pg_in = exchange_cotangent(gctx.reshape(2, 4, 96, -1), pg)
    parts, gq, pr = attend_back(place, spans, x, kv, qt, kt, qr, gctx_in, ctx32, pg, pg_in)
    parts_in, p_in, q_in = reduce_all(parts, gq, pr)
    (input_grad, g_q, g_k, g_v, g_o, g_in, g_up, rows) = finish(
        place, parts_in, grad_one, w[0], p_in, q_in
    )
    cols = lax.dynamic_slice_in_dim(rows[48:54], 48 * g, 48, 1)
    inner_rows = rows[54:58].reshape(-1)
    g_inner_bias = lax.dynamic_slice_in_dim(inner_rows, 192 * g, 192, 0)
    return (
        layer_out, input_grad, g_q, g_k, g_v, g_o, g_in, g_up,
        rows[0:48, 0], rows[0:48, 1], cols[0], g_inner_bias, cols[1],
        cols[2], cols[3], cols[4], cols[5],
    )


def solution(mesh):
    in_specs = (
        P("rep", "grp", None),
        P("rep", "grp"),
        P("rep", "grp", None),
        P("grp", None),
        P("grp", None),
        P("grp", None),
        P("grp", None),
        P("grp", None),
        P("grp", None),
        P("grp"),
        P("grp"),
        P("grp"),
        P("grp"),
        P("grp"),
        P("grp"),
        P("grp"),
        P("grp"),
        P("grp"),
    )
    out_specs = (
        P("rep", "grp", None),
        P("rep", "grp", None),
        P("grp", None),
        P("grp", None),
        P("grp", None),
        P("grp", None),
        P("grp", None),
        P("grp", None),
        P("grp"),
        P("grp"),
        P("grp"),
        P("grp"),
        P("grp"),
        P("grp"),
        P("grp"),
        P("grp"),
        P("grp"),
    )
    whole_line = mesh.shape["grp"] == 8 and mesh.shape["rep"] == 4
    return jax.shard_map(
        line_of_chips if whole_line else on_device, mesh=mesh, in_specs=in_specs, out_specs=out_specs, check_vma=False
    )
```

```python
import functools
from functools import reduce

import jax
import jax.numpy as jnp
from jax import lax
from jax.experimental import pallas as pl
from jax.experimental.pallas import tpu as pltpu
from jax.sharding import PartitionSpec as P

H = 12
MICRO = 2
SEQ_MB = 1


norm_epsilon = 1e-05
masked_score = -1000000000.0


def layer_norm(inputs, norm_gain, norm_shift):
    center = inputs - jnp.mean(inputs, axis=-1, keepdims=True)
    spread = jnp.mean(center * center, axis=-1, keepdims=True)
    return center * lax.rsqrt(spread + norm_epsilon) * norm_gain + norm_shift


def exact_gelu(inputs):
    return jax.nn.gelu(inputs, approximate=False)


def times_transpose(left, right):
    return lax.dot_general(
        left, right, (((1,), (1,)), ((), ())), preferred_element_type=jnp.float32
    )


def transpose_times(left, right):
    return lax.dot_general(
        left, right, (((0,), (0,)), ((), ())), preferred_element_type=jnp.float32
    )


def column_total(inputs):
    return jnp.sum(inputs.astype(jnp.float32), axis=0)


def masked_scores(query_group, key_group, same_doc, score_scale):
    scores = (
        jnp.einsum("bqhd,bkhd->bhqk", query_group, key_group, preferred_element_type=jnp.float32)
        * score_scale
    )
    return jnp.where(same_doc[:, None], scores, masked_score)


def group_forward(query_group, key_group, value_group, same_doc, score_scale):
    scores = masked_scores(query_group, key_group, same_doc, score_scale)
    highest = jnp.max(scores, axis=-1, keepdims=True)
    log_total = highest + jnp.log(jnp.sum(jnp.exp(scores - highest), axis=-1, keepdims=True))
    weights_low = jnp.exp(scores - log_total).astype(jnp.bfloat16)
    context = jnp.einsum(
        "bhqk,bkhd->bqhd", weights_low, value_group, preferred_element_type=jnp.float32
    )
    return (context.astype(jnp.bfloat16), log_total)


def group_backward(
    query_group, key_group, value_group, same_doc, log_total, grad_context, score_scale
):
    attn_weights = jnp.exp(masked_scores(query_group, key_group, same_doc, score_scale) - log_total)
    weights_low = attn_weights.astype(jnp.bfloat16)
    grad_weights = jnp.einsum(
        "bqhd,bkhd->bhqk", grad_context, value_group, preferred_element_type=jnp.float32
    )
    centre = jnp.sum(attn_weights * grad_weights, axis=-1, keepdims=True)
    grad_scores = (attn_weights * (grad_weights - centre)).astype(jnp.bfloat16)
    grad_query = jnp.einsum(
        "bhqk,bkhd->bqhd", grad_scores, key_group, preferred_element_type=jnp.float32
    )
    grad_query = (grad_query * score_scale).astype(jnp.bfloat16)
    grad_key = (
        jnp.einsum("bhqk,bqhd->bkhd", grad_scores, query_group, preferred_element_type=jnp.float32)
        * score_scale
    )
    grad_value = jnp.einsum(
        "bhqk,bqhd->bkhd", weights_low, grad_context, preferred_element_type=jnp.float32
    )
    return (grad_query, grad_key, grad_value)


def merge_groups(stacked, row_total, model_width):
    return jnp.moveaxis(stacked, 0, 2).reshape(row_total, model_width)


def gradient_terms(
    token_rows,
    context_rows,
    hidden_rows,
    active_rows,
    grad_queries,
    grad_keys,
    grad_values,
    grad_attention,
    grad_inner,
    grad_feed,
    norm_grads,
):
    return (
        transpose_times(token_rows, grad_queries),
        transpose_times(token_rows, grad_keys),
        transpose_times(token_rows, grad_values),
        transpose_times(context_rows, grad_attention),
        transpose_times(hidden_rows, grad_inner),
        transpose_times(active_rows, grad_feed),
        column_total(grad_queries),
        column_total(grad_values),
        column_total(grad_attention),
        column_total(grad_inner),
        column_total(grad_feed),
        norm_grads[0],
        norm_grads[1],
        norm_grads[2],
        norm_grads[3],
    )


def on_device(
    tokens,
    segment_ids,
    out_grad,
    query_weight,
    key_weight,
    value_weight,
    output_weight,
    inner_weight,
    outer_weight,
    query_bias,
    value_bias,
    output_bias,
    inner_bias,
    outer_bias,
    first_gain,
    first_shift,
    second_gain,
    second_shift,
):
    row_count = tokens.shape[1]
    model_width = tokens.shape[2]
    head_count = H
    head_size = model_width // head_count
    per_group = max(1, min(head_count, 128 // head_size))
    group_width = per_group * head_size
    group_count = head_count // per_group
    score_scale = head_size ** (-0.5)
    seq_count = SEQ_MB
    flat_rows = seq_count * row_count
    all_segments = lax.all_gather(segment_ids, "grp", axis=1, tiled=True)
    outputs = []
    input_grads = []
    shares_list = []
    for batch_index in range(MICRO):
        offset = batch_index * seq_count
        local_tokens = tokens[offset : offset + seq_count]
        flat_tokens = local_tokens.reshape(flat_rows, model_width)
        gathered = (
            lax.all_gather(query_weight, "grp", axis=0, tiled=True),
            lax.all_gather(key_weight, "grp", axis=0, tiled=True),
            lax.all_gather(value_weight, "grp", axis=0, tiled=True),
            lax.all_gather(output_weight, "grp", axis=0, tiled=True),
            lax.all_gather(inner_weight, "grp", axis=0, tiled=True),
            lax.all_gather(outer_weight, "grp", axis=0, tiled=True),
            lax.all_gather(query_bias, "grp", axis=0, tiled=True),
            lax.all_gather(value_bias, "grp", axis=0, tiled=True),
            lax.all_gather(output_bias, "grp", axis=0, tiled=True),
            lax.all_gather(inner_bias, "grp", axis=0, tiled=True),
            lax.all_gather(outer_bias, "grp", axis=0, tiled=True),
            lax.all_gather(first_gain, "grp", axis=0, tiled=True),
            lax.all_gather(first_shift, "grp", axis=0, tiled=True),
            lax.all_gather(second_gain, "grp", axis=0, tiled=True),
            lax.all_gather(second_shift, "grp", axis=0, tiled=True),
        )
        full_query, full_key, full_value, full_output, full_inner, full_outer = gathered[:6]
        (
            bias_query,
            bias_value,
            bias_output,
            bias_inner,
            bias_outer,
            gain_first,
            shift_first,
            gain_second,
            shift_second,
        ) = [vector.astype(jnp.float32) for vector in gathered[6:]]
        queries = (
            jnp.dot(flat_tokens, full_query, preferred_element_type=jnp.float32) + bias_query
        ).astype(jnp.bfloat16)
        key_rows = jnp.dot(flat_tokens, full_key, preferred_element_type=jnp.float32).astype(
            jnp.bfloat16
        )
        value_rows = (
            jnp.dot(flat_tokens, full_value, preferred_element_type=jnp.float32) + bias_value
        ).astype(jnp.bfloat16)
        key_split = key_rows.reshape(seq_count, row_count, model_width)
        value_split = value_rows.reshape(seq_count, row_count, model_width)
        key_all, value_all = (
            lax.all_gather(key_split, "grp", axis=1, tiled=True),
            lax.all_gather(value_split, "grp", axis=1, tiled=True),
        )
        length = key_all.shape[1]
        local_segments = segment_ids[offset : offset + seq_count]
        far_segments = all_segments[offset : offset + seq_count]
        same_doc = local_segments[:, :, None] == far_segments[:, None, :]
        query_split = queries.reshape(seq_count, row_count, model_width)

        def slice_group(array, group_index):
            piece = lax.dynamic_slice_in_dim(array, group_index * group_width, group_width, 2)
            return piece.reshape(array.shape[0], array.shape[1], per_group, head_size)

        def forward_group(group_index):
            context, log_total = group_forward(
                slice_group(query_split, group_index),
                slice_group(key_all, group_index),
                slice_group(value_all, group_index),
                same_doc,
                score_scale,
            )
            return (context.reshape(seq_count, row_count, group_width), log_total)

        context_groups, log_totals = lax.map(forward_group, jnp.arange(group_count))
        context_rows = merge_groups(context_groups, flat_rows, model_width)
        attention = (
            jnp.dot(context_rows, full_output, preferred_element_type=jnp.float32) + bias_output
        )
        residual_one = flat_tokens.astype(jnp.float32) + attention
        hidden_one, norm_one_pullback = jax.vjp(layer_norm, residual_one, gain_first, shift_first)
        hidden_low = hidden_one.astype(jnp.bfloat16)
        inner_pre = jnp.dot(hidden_low, full_inner, preferred_element_type=jnp.float32) + bias_inner
        activation, gelu_pullback = jax.vjp(exact_gelu, inner_pre)
        active_low = activation.astype(jnp.bfloat16)
        feed = jnp.dot(active_low, full_outer, preferred_element_type=jnp.float32) + bias_outer
        output_rows, norm_two_pullback = jax.vjp(
            layer_norm, hidden_one + feed, gain_second, shift_second
        )
        outputs.append(output_rows.astype(jnp.bfloat16).reshape(seq_count, row_count, model_width))
        cotangent = (
            out_grad[offset : offset + seq_count]
            .reshape(flat_rows, model_width)
            .astype(jnp.float32)
        )
        grad_two, grad_gain_two, grad_shift_two = norm_two_pullback(cotangent)
        grad_feed = grad_two.astype(jnp.bfloat16)
        grad_active = times_transpose(grad_feed, full_outer)
        grad_inner = gelu_pullback(grad_active)[0].astype(jnp.bfloat16)
        grad_hidden = grad_two + times_transpose(grad_inner, full_inner)
        grad_one, grad_gain_one, grad_shift_one = norm_one_pullback(grad_hidden)
        grad_attention = grad_one.astype(jnp.bfloat16)
        grad_context = times_transpose(grad_attention, full_output).astype(jnp.bfloat16)
        grad_context = grad_context.reshape(seq_count, row_count, model_width)

        def backward_group(pieces):
            group_index, log_total = pieces
            grad_query, grad_key, grad_value = group_backward(
                slice_group(query_split, group_index),
                slice_group(key_all, group_index),
                slice_group(value_all, group_index),
                same_doc,
                log_total,
                slice_group(grad_context, group_index),
                score_scale,
            )
            return (
                grad_query.reshape(seq_count, row_count, group_width),
                grad_key.reshape(seq_count, length, group_width),
                grad_value.reshape(seq_count, length, group_width),
            )

        query_groups, key_groups, value_groups = lax.map(
            backward_group, (jnp.arange(group_count), log_totals)
        )
        key_owned, value_owned = (
            lax.psum_scatter(key_groups, "grp", scatter_dimension=2, tiled=True),
            lax.psum_scatter(value_groups, "grp", scatter_dimension=2, tiled=True),
        )
        grad_keys = merge_groups(key_owned, flat_rows, model_width).astype(jnp.bfloat16)
        grad_values = merge_groups(value_owned, flat_rows, model_width).astype(jnp.bfloat16)
        grad_queries = merge_groups(query_groups, flat_rows, model_width)
        grad_tokens = (
            grad_one
            + times_transpose(grad_queries, full_query)
            + times_transpose(grad_keys, full_key)
            + times_transpose(grad_values, full_value)
        )
        input_grads.append(
            grad_tokens.astype(jnp.bfloat16).reshape(seq_count, row_count, model_width)
        )
        norm_grads = (grad_gain_one, grad_shift_one, grad_gain_two, grad_shift_two)
        terms = gradient_terms(
            flat_tokens,
            context_rows,
            hidden_low,
            active_low,
            grad_queries,
            grad_keys,
            grad_values,
            grad_attention,
            grad_inner,
            grad_feed,
            norm_grads,
        )
        shares = (
            lax.psum_scatter(terms[0], "grp", scatter_dimension=0, tiled=True),
            lax.psum_scatter(terms[1], "grp", scatter_dimension=0, tiled=True),
            lax.psum_scatter(terms[2], "grp", scatter_dimension=0, tiled=True),
            lax.psum_scatter(terms[3], "grp", scatter_dimension=0, tiled=True),
            lax.psum_scatter(terms[4], "grp", scatter_dimension=0, tiled=True),
            lax.psum_scatter(terms[5], "grp", scatter_dimension=0, tiled=True),
            lax.psum_scatter(terms[6], "grp", scatter_dimension=0, tiled=True),
            lax.psum_scatter(terms[7], "grp", scatter_dimension=0, tiled=True),
            lax.psum_scatter(terms[8], "grp", scatter_dimension=0, tiled=True),
            lax.psum_scatter(terms[9], "grp", scatter_dimension=0, tiled=True),
            lax.psum_scatter(terms[10], "grp", scatter_dimension=0, tiled=True),
            lax.psum_scatter(terms[11], "grp", scatter_dimension=0, tiled=True),
            lax.psum_scatter(terms[12], "grp", scatter_dimension=0, tiled=True),
            lax.psum_scatter(terms[13], "grp", scatter_dimension=0, tiled=True),
            lax.psum_scatter(terms[14], "grp", scatter_dimension=0, tiled=True),
        )
        shares_list.append(shares)
    owned = reduce(
        lambda left_part, right_part: jax.tree.map(jnp.add, left_part, right_part), shares_list
    )
    summed = (
        lax.psum(owned[0].astype(jnp.bfloat16), "rep").astype(jnp.float32),
        lax.psum(owned[1].astype(jnp.bfloat16), "rep").astype(jnp.float32),
        lax.psum(owned[2].astype(jnp.bfloat16), "rep").astype(jnp.float32),
        lax.psum(owned[3].astype(jnp.bfloat16), "rep").astype(jnp.float32),
        lax.psum(owned[4].astype(jnp.bfloat16), "rep").astype(jnp.float32),
        lax.psum(owned[5].astype(jnp.bfloat16), "rep").astype(jnp.float32),
        lax.psum(owned[6].astype(jnp.bfloat16), "rep").astype(jnp.float32),
        lax.psum(owned[7].astype(jnp.bfloat16), "rep").astype(jnp.float32),
        lax.psum(owned[8].astype(jnp.bfloat16), "rep").astype(jnp.float32),
        lax.psum(owned[9].astype(jnp.bfloat16), "rep").astype(jnp.float32),
        lax.psum(owned[10].astype(jnp.bfloat16), "rep").astype(jnp.float32),
        lax.psum(owned[11].astype(jnp.bfloat16), "rep").astype(jnp.float32),
        lax.psum(owned[12].astype(jnp.bfloat16), "rep").astype(jnp.float32),
        lax.psum(owned[13].astype(jnp.bfloat16), "rep").astype(jnp.float32),
        lax.psum(owned[14].astype(jnp.bfloat16), "rep").astype(jnp.float32),
    )
    return (
        jnp.concatenate(outputs, axis=0),
        jnp.concatenate(input_grads, axis=0),
        summed[0],
        summed[1],
        summed[2],
        summed[3],
        summed[4],
        summed[5],
        summed[6],
        summed[7],
        summed[8],
        summed[9],
        summed[10],
        summed[11],
        summed[12],
        summed[13],
        summed[14],
    )


HEAD = 32
LANES = 128
QB = 256
KB = 256
AWAY = 2.0 ** 100
LIMIT = 100.0
MESH = pl.DeviceIdType.MESH
BIG = 100 * 1024 * 1024 // 2
LOG2E = 1.4426950408889634


def halves(value):
    first = value.astype(jnp.bfloat16).astype(jnp.float32)
    rest = value - first
    second = rest.astype(jnp.bfloat16).astype(jnp.float32)
    third = (rest - second).astype(jnp.bfloat16).astype(jnp.float32)
    return first, second, third


def dot(left, right):
    return jnp.dot(left, right, preferred_element_type=jnp.float32)


def zeros_for(rank, *grid):
    return (0,) * rank


def whole_spec(array):
    return pl.BlockSpec(array.shape, functools.partial(zeros_for, array.ndim), pipeline_mode=pl.Buffered(1))


def quarter_spec(w, i):
    return pl.BlockSpec((1,) + w.shape[1:], lambda *grid: (i, 0, 0, 0, 0), pipeline_mode=pl.Buffered(1))


def iota(shape, dim):
    return lax.broadcasted_iota(jnp.int32, shape, dim)


def where_am_i():
    r = lax.axis_index("rep")
    g = lax.axis_index("grp")
    return r, g, lax.div(g, 2), lax.rem(g, 2)


def remote(src, dst, send, recv, r, g):
    return pltpu.make_async_remote_copy(
        src_ref=src, dst_ref=dst, send_sem=send, recv_sem=recv, device_id=(r, g), device_id_type=MESH
    )


def greet(r, g, reps, group):
    barrier = pltpu.get_barrier_semaphore()
    for d in range(1, group):
        pl.semaphore_signal(barrier, inc=1, device_id=(r, lax.rem(g + d, group)), device_id_type=MESH)
    for d in range(1, reps):
        pl.semaphore_signal(barrier, inc=1, device_id=(lax.rem(r + d, reps), g), device_id_type=MESH)
    pl.semaphore_wait(barrier, group + reps - 2)


def gather_kernel(
    tok, wq, wk, wv, wo, wi, wu, small, x_out, w_out, s_out,
    lsem, tsend, trecv, psend, wsend1, wrecv1, wsend2, wrecv2, wsend3, wrecv3, ssend, srecv,
):
    r, g, z, c = where_am_i()
    reps, chips = 4, 4
    p = 2 * z + 1 - c
    greet(r, g, reps, 2 * chips)
    width = wq.shape[1]
    slab = [wi.at[:, pl.ds(j * width, width)] for j in range(4)]
    first_part = pl.ds(0, 48)
    quarters = (
        ((wq, 0, 48), (wk, 48, 48), (wv, 96, 48)),
        ((wo, 0, 48), (slab[0], 48, 48), (slab[1], 96, 48)),
        ((slab[2], 0, 48), (slab[3], 48, 48), (wu.at[first_part, :], 96, 48)),
        ((wu.at[pl.ds(48, 144), :], 0, 144),),
    )
    for i, pieces in enumerate(quarters):
        @pl.when(r == i)
        def _():
            copies = [
                pltpu.make_async_copy(
                    ref, w_out.at[i, c, z, pl.ds(row, count), :], lsem.at[3 + k]
                )
                for k, (ref, row, count) in enumerate(pieces)
            ]
            for copy in copies:
                copy.start()
            for copy in copies:
                copy.wait()

    mine = w_out.at[r, c, z]
    own_x = pltpu.make_async_copy(tok.at[c], x_out.at[g], lsem.at[0])
    own_x.start()
    own_s = pltpu.make_async_copy(small, s_out.at[g], lsem.at[2])
    own_s.start()
    swap = remote(tok.at[1 - c], x_out.at[g], psend, trecv.at[g], r, p)
    swap.start()

    first = []
    for d in range(1, chips):
        zz = lax.rem(z + d, chips)
        copy = remote(mine, mine, wsend1.at[d - 1], wrecv1.at[z], r, 2 * zz + c)
        copy.start()
        first.append(copy)
    smalls = []
    for d in range(1, 2 * chips):
        copy = remote(small, s_out.at[g], ssend.at[d - 1], srecv.at[g], r, lax.rem(g + d, 2 * chips))
        copy.start()
        smalls.append(copy)

    def pass_on(b, src, way):
        to = g + 2 if way == 0 else g - 2
        return remote(src, x_out.at[b], tsend.at[way, b], trecv.at[b], r, to)

    def forward(b, src, way):
        ok = z < chips - 1 if way == 0 else z > 0

        @pl.when(ok)
        def _():
            pass_on(b, src, way).start()

    def arrived(b):
        remote(x_out.at[b], x_out.at[b], tsend.at[0, b], trecv.at[b], r, p).wait_recv()

    forward(g, tok.at[c], 0)
    forward(g, tok.at[c], 1)
    arrived(p)
    forward(p, x_out.at[p], 0)
    forward(p, x_out.at[p], 1)

    def tokens_from(d):
        for k in range(2):
            @pl.when(z >= d)
            def _():
                b = 2 * (z - d) + (c if k == 0 else 1 - c)
                arrived(b)
                forward(b, x_out.at[b], 0)

            @pl.when(z + d < chips)
            def _():
                b = 2 * (z + d) + (c if k == 0 else 1 - c)
                arrived(b)
                forward(b, x_out.at[b], 1)

    tokens_from(1)
    for d in range(1, chips):
        zz = lax.rem(z + d, chips)
        remote(mine, w_out.at[r, c, zz], wsend1.at[0], wrecv1.at[zz], r, p).wait_recv()
    second = []
    for d in range(1, reps):
        copy = remote(
            w_out.at[r, c], w_out.at[r, c], wsend2.at[d - 1], wrecv2.at[r], lax.rem(r + d, reps), g
        )
        copy.start()
        second.append(copy)
    third = [remote(w_out.at[r, c], w_out.at[r, c], wsend3.at[r], wrecv3.at[r], r, p)]
    third[0].start()
    tokens_from(2)
    for d in range(1, reps):
        q = lax.rem(r + d, reps)
        remote(w_out.at[q, c], w_out.at[q, c], wsend2.at[0], wrecv2.at[q], r, p).wait_recv()
        copy = remote(w_out.at[q, c], w_out.at[q, c], wsend3.at[q], wrecv3.at[q], r, p)
        copy.start()
        third.append(copy)
    tokens_from(3)
    for q in range(reps):
        remote(w_out.at[q, 1 - c], w_out.at[q, 1 - c], wsend3.at[q], wrecv3.at[q], r, p).wait_recv()
    for d in range(1, 2 * chips):
        b = lax.rem(g + d, 2 * chips)
        remote(small, s_out.at[b], ssend.at[0], srecv.at[b], r, p).wait_recv()
    own_x.wait()
    own_s.wait()
    swap.wait_send()
    for copy in first + smalls + second + third:
        copy.wait_send()
    for b in range(2 * chips):
        @pl.when((z < chips - 1) & (b < 2 * z + 2))
        def _():
            pass_on(b, x_out.at[b], 0).wait_send()

        @pl.when((z > 0) & (b >= 2 * z))
        def _():
            pass_on(b, x_out.at[b], 1).wait_send()


def gather(tokens, weights, small):
    dma = pltpu.SemaphoreType.DMA
    anywhere = pl.BlockSpec(memory_space=pl.ANY)
    rows, width = tokens.shape[1:]
    return pl.pallas_call(
        gather_kernel,
        name="gather",
        out_shape=(
            jax.ShapeDtypeStruct((8, rows, width), jnp.bfloat16),
            jax.ShapeDtypeStruct((4, 2, 4, 144, width), jnp.bfloat16),
            jax.ShapeDtypeStruct((8,) + small.shape, jnp.bfloat16),
        ),
        in_specs=[anywhere] * 8,
        out_specs=[anywhere] * 3,
        scratch_shapes=[
            dma((6,)), dma((2, 8)), dma((8,)), dma, dma((3,)), dma((4,)), dma((3,)), dma((4,)),
            dma((4,)), dma((4,)), dma((7,)), dma((8,)),
        ],
        compiler_params=pltpu.CompilerParams(collective_id=1, has_side_effects=True),
    )(tokens, *weights, small)


def span_of(starts, q0, docs):
    low = jnp.int32(0)
    high = starts[docs]
    for d in range(docs):
        low = jnp.where(starts[d] <= q0, jnp.maximum(low, starts[d]), low)
        high = jnp.where(starts[d + 1] >= q0 + QB, jnp.minimum(high, starts[d + 1]), high)
    first = lax.div(low, LANES)
    last = lax.div(high + LANES - 1, LANES)
    steps = lax.div(last - first + KB // LANES - 1, KB // LANES)
    total = lax.div(starts[docs], LANES)
    first = jnp.minimum(first, total - steps * (KB // LANES))
    return first, steps


def vectors_of(small):
    return jnp.concatenate([small[g, 0:8, 0:48].astype(jnp.float32) for g in range(8)], axis=1)


def in_pairs(first, steps, body):
    double = lax.div(steps, 2)

    def two(i, none):
        body(pl.ds(pl.multiple_of((first + i * (2 * KB // LANES)) * LANES, LANES), 2 * KB))
        return none

    lax.fori_loop(0, double, two, 0)

    @pl.when(steps > 2 * double)
    def _():
        body(pl.ds(pl.multiple_of((first + double * (2 * KB // LANES)) * LANES, LANES), KB))


def attend_kernel(
    place, x, w, small, kv, qt, kt, qr, ctx, ctx32, spans, wrow, wtr, vt, acc, tall, seg, starts,
):
    heads = kv.shape[0]
    length, width = x.shape
    blocks, hw, rows = ctx.shape
    docs = 8
    z = place[0]
    c = place[1]
    span = heads * HEAD
    bias = vectors_of(small).astype(jnp.bfloat16)
    for g in range(8):
        two = small[g, 8:16, :].astype(jnp.float32)
        seg[g : g + 1, :] = jnp.where(c == 0, two[1:2], two[2:3]).astype(jnp.int32)

    full = [
        jnp.concatenate([w[0, g % 2, g // 2, 48 * i : 48 * i + 48, :] for g in range(8)], axis=0)
        for i in range(3)
    ]
    lane = iota((width, heads * LANES), 1)
    head, inner = lax.div(lane, LANES), lax.rem(lane, LANES)
    column = span * z + head * HEAD + lax.rem(inner, HEAD)
    hit = iota((width, heads * LANES), 0) == column
    pick_k = jnp.where(hit & (inner < 64), 1.0, 0.0).astype(jnp.bfloat16)
    pick_v = jnp.where(hit & (inner >= 64) & (inner < 96), 1.0, 0.0).astype(jnp.bfloat16)
    pick_q = jnp.where(hit & (inner >= 32) & (inner < 64), 1.0, 0.0).astype(jnp.bfloat16)
    wrow[0] = (dot(full[1], pick_k) + dot(full[2], pick_v)).astype(jnp.bfloat16)
    wrow[1] = dot(full[0], pick_q).astype(jnp.bfloat16)
    row_kv = dot(bias[1:2, :], pick_v)
    row_q = dot(bias[0:1, :], pick_q)
    pick_t = jnp.where(
        iota((span, width), 1) == span * z + iota((span, width), 0), 1.0, 0.0
    ).astype(jnp.bfloat16)
    for i in range(3):
        wtr[i] = lax.dot_general(
            pick_t, full[i], (((1,), (1,)), ((), ())), preferred_element_type=jnp.float32
        ).astype(jnp.bfloat16)
    column_bias = lax.dot_general(
        pick_t, bias, (((1,), (1,)), ((), ())), preferred_element_type=jnp.float32
    )
    col_q, col_v = column_bias[:, 0:1], column_bias[:, 1:2]

    ids = seg[...]
    starts[0] = jnp.int32(0)
    for d in range(1, docs):
        starts[d] = jnp.sum(jnp.where(ids < d, 1.0, 0.0)).astype(jnp.int32)
    starts[docs] = jnp.int32(length)

    scale = (HEAD ** -0.5) * LOG2E
    one_lane = lax.rem(iota((1, heads * LANES), 1), LANES)
    ones_row = jnp.where((one_lane >= 104) & (one_lane < 107), 1.0, 0.0)

    def project(b, carry):
        r0 = pl.multiple_of(b * rows, rows)
        xb = x[pl.ds(r0, rows), :]
        idrow = seg[pl.ds(b, 1), :]
        same = jnp.where(iota((8, rows), 0) == idrow, 1.0, 0.0)
        hot = jnp.concatenate(
            [jnp.zeros((96, rows), jnp.float32), same, jnp.zeros((24, rows), jnp.float32)], axis=0
        ).T
        flat = dot(xb, wrow[0]) + (row_kv + ones_row)
        for h in range(heads):
            kv[h, pl.ds(r0, rows), :] = (flat[:, h * LANES : (h + 1) * LANES] + hot).astype(
                jnp.bfloat16
            )
        flat = (dot(xb, wrow[1]) + row_q).astype(jnp.bfloat16)
        for h in range(heads):
            qr[h, pl.ds(r0, rows), :] = flat[:, h * LANES : (h + 1) * LANES]

        def turned(i):
            return lax.dot_general(
                wtr[i], xb, (((1,), (1,)), ((), ())), preferred_element_type=jnp.float32
            )

        q_t = (turned(0) + col_q).astype(jnp.bfloat16).astype(jnp.float32) * scale
        k_t = turned(1).astype(jnp.bfloat16)
        k_wide = k_t.astype(jnp.float32)
        norms = [
            jnp.maximum(
                carry[i],
                functools.reduce(
                    jnp.maximum,
                    [
                        jnp.sum(v[h * HEAD : (h + 1) * HEAD] ** 2, axis=0, keepdims=True)
                        for h in range(heads)
                    ],
                ),
            )
            for i, v in enumerate((q_t, k_wide))
        ]
        q_hi = q_t.astype(jnp.bfloat16)
        q_lo = (q_t - q_hi.astype(jnp.float32)).astype(jnp.bfloat16)
        v_t = (turned(2) + col_v).astype(jnp.bfloat16)
        far = jnp.concatenate([(same - 1.0) * AWAY, jnp.zeros((8, rows), jnp.float32)], axis=0)
        far = far.astype(jnp.bfloat16)
        one = jnp.where(iota((16, rows), 0) == 0, 1.0, 0.0).astype(jnp.bfloat16)
        cols = pl.ds(r0, rows)
        for h in range(heads):
            part = slice(h * HEAD, (h + 1) * HEAD)
            qt[h, 0:32, cols] = q_hi[part]
            qt[h, 32:64, cols] = q_lo[part]
            qt[h, 64:96, cols] = jnp.zeros((32, rows), jnp.bfloat16)
            qt[h, 96:112, cols] = far
            qt[h, 112:128, cols] = jnp.zeros((16, rows), jnp.bfloat16)
            kt[h, :, cols] = k_t[part]
            vt[h, 0:32, cols] = v_t[part]
            vt[h, 32:48, cols] = one
        return tuple(norms)

    zero = jnp.zeros((1, rows), jnp.float32)
    q_norm, k_norm = lax.fori_loop(0, blocks, project, (zero, zero))
    bounded = jnp.max(q_norm) * jnp.max(k_norm) < LIMIT * LIMIT

    per = rows // QB

    def query_block(b, carry):
        q0 = pl.multiple_of(b * QB, QB)
        first, steps = span_of(starts, q0, docs)
        spans[0, b] = first
        spans[1, b] = steps
        acc[...] = jnp.zeros_like(acc)

        def key_block(i, tops):
            k0 = pl.multiple_of((first + i * (KB // LANES)) * LANES, LANES)
            s = [dot(kv[h, pl.ds(k0, KB), :], qt[h, :, pl.ds(q0, QB)]) for h in range(heads)]
            new = [jnp.maximum(tops[h], jnp.max(s[h], axis=0, keepdims=True)) for h in range(heads)]
            p = [jnp.exp2(s[h] - new[h]).astype(jnp.bfloat16) for h in range(heads)]
            for h in range(heads):
                acc[h] = acc[h] * jnp.exp2(tops[h] - new[h]) + dot(vt[h, :, pl.ds(k0, KB)], p[h])
            return tuple(new)

        def plain_block(keys):
            s = [dot(kv[h, keys, :], qt[h, :, pl.ds(q0, QB)]) for h in range(heads)]
            p = [jnp.exp2(v).astype(jnp.bfloat16) for v in s]
            for h in range(heads):
                acc[h] += dot(vt[h, :, keys], p[h])

        @pl.when(bounded)
        def _():
            in_pairs(first, steps, plain_block)
            tall[...] = jnp.zeros_like(tall)

        @pl.when(jnp.logical_not(bounded))
        def _():
            lowest = jnp.full((1, QB), -3e38, jnp.float32)
            tops = lax.fori_loop(0, steps, key_block, (lowest,) * heads)
            for h in range(heads):
                tall[h] = tops[h]

        g = lax.div(b, per)
        off = pl.multiple_of(lax.rem(b, per) * QB, QB)
        same = jnp.where(iota((8, QB), 0) == seg[pl.ds(g, 1), pl.ds(off, QB)], 1.0, 0.0)
        for h in range(heads):
            total = acc[h, 32:33, :]
            out = acc[h, 0:32, :] / total
            ctx[g, h * HEAD : (h + 1) * HEAD, pl.ds(off, QB)] = out.astype(jnp.bfloat16)
            ctx32[g, h * HEAD : (h + 1) * HEAD, pl.ds(off, QB)] = out
            parts = halves(-(tall[h] + jnp.log2(total)))
            tail = jnp.concatenate(
                [(same - 1.0) * AWAY, *parts, jnp.zeros((5, QB), jnp.float32)], axis=0
            )
            qt[h, 96:112, pl.ds(q0, QB)] = tail.astype(jnp.bfloat16)
        return carry

    lax.fori_loop(0, length // QB, query_block, 0)


def attend(place, x, w, small):
    blocks, rows, width = x.shape
    length = blocks * rows
    heads = 3
    vm = pl.BlockSpec(memory_space=pltpu.VMEM)
    sm = pl.BlockSpec(memory_space=pltpu.SMEM)
    bf, f4 = jnp.bfloat16, jnp.float32
    return pl.pallas_call(
        attend_kernel,
        name="attend",
        grid=(1,),
        out_shape=(
            jax.ShapeDtypeStruct((heads, length, LANES), bf),
            jax.ShapeDtypeStruct((heads, LANES, length), bf),
            jax.ShapeDtypeStruct((heads, HEAD, length), bf),
            jax.ShapeDtypeStruct((heads, length, LANES), bf),
            jax.ShapeDtypeStruct((blocks, heads * HEAD, rows), bf),
            jax.ShapeDtypeStruct((blocks, heads * HEAD, rows), f4),
            jax.ShapeDtypeStruct((2, length // QB), jnp.int32),
        ),
        in_specs=[sm, vm, quarter_spec(w, 0), whole_spec(small)],
        out_specs=[vm] * 6 + [sm],
        scratch_shapes=[
            pltpu.VMEM((2, width, heads * LANES), bf),
            pltpu.VMEM((3, heads * HEAD, width), bf),
            pltpu.VMEM((heads, 48, length), bf),
            pltpu.VMEM((heads, 48, QB), f4),
            pltpu.VMEM((heads, 1, QB), f4),
            pltpu.VMEM((8, rows), jnp.int32),
            pltpu.SMEM((16,), jnp.int32),
        ],
        compiler_params=pltpu.CompilerParams(vmem_limit_bytes=BIG),
    )(place, x.reshape(length, width), w, small)


def context_kernel(src, dst, lsem, send, recv):
    r, g, z, c = where_am_i()
    greet(r, g, 1, 8)
    own = pltpu.make_async_copy(src.at[g], dst.at[c, z], lsem)
    own.start()
    copies = []
    for d in range(1, 8):
        to = lax.rem(g + d, 8)
        copy = remote(src.at[to], dst.at[c, z], send.at[d - 1], recv.at[g], r, to)
        copy.start()
        copies.append(copy)
    for d in range(1, 8):
        b = lax.rem(g + d, 8)
        remote(src.at[g], dst.at[lax.rem(b, 2), lax.div(b, 2)], send.at[0], recv.at[b], r, b).wait_recv()
    for copy in copies:
        copy.wait_send()
    own.wait()


def exchange_context(ctx):
    dma = pltpu.SemaphoreType.DMA
    anywhere = pl.BlockSpec(memory_space=pl.ANY)
    return pl.pallas_call(
        context_kernel,
        name="exchange_context",
        out_shape=jax.ShapeDtypeStruct((2, 4) + ctx.shape[1:], ctx.dtype),
        in_specs=[anywhere],
        out_specs=anywhere,
        scratch_shapes=[dma, dma((7,)), dma((8,))],
        compiler_params=pltpu.CompilerParams(collective_id=2, has_side_effects=True),
    )(ctx)


def cotangent_kernel(src, pg, dst, pg_out, lsem, send, recv, psend, precv):
    r, g, z, c = where_am_i()
    greet(r, g, 1, 8)
    pair = remote(pg.at[1 - c], pg_out, psend, precv, r, 2 * z + 1 - c)
    pair.start()
    own = pltpu.make_async_copy(src.at[c, z], dst.at[g], lsem)
    own.start()
    copies = []
    for d in range(1, 8):
        to = lax.rem(g + d, 8)
        copy = remote(
            src.at[lax.rem(to, 2), lax.div(to, 2)], dst.at[g], send.at[d - 1], recv.at[g], r, to
        )
        copy.start()
        copies.append(copy)
    for d in range(1, 8):
        b = lax.rem(g + d, 8)
        remote(src.at[c, z], dst.at[b], send.at[0], recv.at[b], r, b).wait_recv()
    for copy in copies:
        copy.wait_send()
    pair.wait()
    own.wait()


def exchange_cotangent(src, pg):
    dma = pltpu.SemaphoreType.DMA
    anywhere = pl.BlockSpec(memory_space=pl.ANY)
    return pl.pallas_call(
        cotangent_kernel,
        name="exchange_cotangent",
        out_shape=(
            jax.ShapeDtypeStruct((8,) + src.shape[2:], src.dtype),
            jax.ShapeDtypeStruct(pg.shape[1:], pg.dtype),
        ),
        in_specs=[anywhere] * 2,
        out_specs=[anywhere] * 2,
        scratch_shapes=[dma, dma((7,)), dma((8,)), dma, dma],
        compiler_params=pltpu.CompilerParams(collective_id=3, has_side_effects=True),
    )(src, pg)


def dense_kernel(
    tok, og, ctx, w, small,
    layer_out, grad_one_out, gctx, pg, wo, wi, wu, gwo, gwi, gwu, sums, inner_sum,
):
    seqs, rows, width = tok.shape
    slabs = wi.shape[0]
    block = 256
    per = rows // block
    for g in range(8):
        c, z = g % 2, g // 2
        wo[48 * g : 48 * g + 48, :] = w[1, c, z, 0:48, :]
        wi[0, 48 * g : 48 * g + 48, :] = w[1, c, z, 48:96, :]
        wi[1, 48 * g : 48 * g + 48, :] = w[1, c, z, 96:144, :]
        wi[2, 48 * g : 48 * g + 48, :] = w[2, c, z, 0:48, :]
        wi[3, 48 * g : 48 * g + 48, :] = w[2, c, z, 48:96, :]
        wu[g // 2, 192 * c : 192 * c + 48, :] = w[2, c, z, 96:144, :]
        wu[g // 2, 192 * c + 48 : 192 * c + 192, :] = w[3, c, z, :, :]
    for ref in (gwo, gwi, gwu, sums, inner_sum):
        ref[...] = jnp.zeros_like(ref)

    vec = vectors_of(small)
    inner_bias = jnp.concatenate(
        [small[g, 8:16, 0:192].astype(jnp.float32)[0:1] for g in range(8)], axis=1
    )
    out_bias, outer_bias = vec[2:3, :], vec[3:4, :]
    gain_one, shift_one = vec[4:5, :], vec[5:6, :]
    gain_two, shift_two = vec[6:7, :], vec[7:8, :]

    def normal(value):
        centre = value - jnp.mean(value, axis=-1, keepdims=True)
        rate = lax.rsqrt(jnp.mean(centre * centre, axis=-1, keepdims=True) + norm_epsilon)
        return centre * rate, rate

    def normal_back(grad, gain, n, rate):
        u = grad * gain
        return rate * (
            u - jnp.mean(u, axis=-1, keepdims=True) - n * jnp.mean(u * n, axis=-1, keepdims=True)
        )

    def total(value):
        return jnp.sum(value, axis=0, keepdims=True)

    def turn_dot(left, right):
        return lax.dot_general(
            left, right, (((0,), (0,)), ((), ())), preferred_element_type=jnp.float32
        )

    def dot_turn(left, right):
        return lax.dot_general(
            left, right, (((1,), (1,)), ((), ())), preferred_element_type=jnp.float32
        )

    def one(b, carry):
        s = lax.div(b, per)
        r0 = pl.multiple_of(lax.rem(b, per) * block, block)
        here = pl.ds(r0, block)
        ctx_t = ctx[s, :, here]
        context = ctx_t.astype(jnp.float32).T.astype(jnp.bfloat16)
        x = tok[s, here, :].astype(jnp.float32)
        n_one, rate_one = normal(x + (dot(context, wo[...]) + out_bias))
        hidden = n_one * gain_one + shift_one
        low = hidden.astype(jnp.bfloat16)
        low_t = hidden.T.astype(jnp.bfloat16)
        feed = jnp.zeros((block, width), jnp.float32)
        slopes, actives = [], []
        for j in range(slabs):
            inner = dot(low, wi[j]) + inner_bias[:, j * width : (j + 1) * width]
            cdf = 0.5 + 0.5 * lax.erf(inner * (0.5 ** 0.5))
            pdf = jnp.exp(inner * inner * -0.5) * 0.3989422804014327
            slopes.append(cdf + inner * pdf)
            active = inner * cdf
            actives.append(active)
            feed = feed + dot(active.astype(jnp.bfloat16), wu[j])
        n_two, rate_two = normal(hidden + (feed + outer_bias))
        layer_out[s, here, :] = (n_two * gain_two + shift_two).astype(jnp.bfloat16)
        grad = og[s, here, :].astype(jnp.float32)
        grad_two = normal_back(grad, gain_two, n_two, rate_two)
        grad_feed = grad_two.astype(jnp.bfloat16)
        grad_hidden = grad_two
        for j in range(slabs):
            grad_inner = (dot_turn(grad_feed, wu[j]) * slopes[j]).astype(jnp.bfloat16)
            inner_sum[:, j * width : (j + 1) * width] += total(grad_inner.astype(jnp.float32))
            grad_hidden = grad_hidden + dot_turn(grad_inner, wi[j])
            gwi[j] += dot(low_t, grad_inner)
            gwu[j] += dot(actives[j].T.astype(jnp.bfloat16), grad_feed)
        grad_one = normal_back(grad_hidden, gain_one, n_one, rate_one)
        grad_one_out[s, here, :] = grad_one
        grad_att = grad_one.astype(jnp.bfloat16)
        gctx[s, :, here] = dot_turn(wo[...], grad_att).astype(jnp.bfloat16)
        gwo[...] += dot(ctx_t, grad_att)
        sums[0:1, :] += total(grad_att.astype(jnp.float32))
        sums[1:2, :] += total(grad_feed.astype(jnp.float32))
        sums[2:3, :] += total(grad_hidden * n_one)
        sums[3:4, :] += total(grad_hidden)
        sums[4:5, :] += total(grad * n_two)
        sums[5:6, :] += total(grad)
        return carry

    lax.fori_loop(0, seqs * per, one, 0)
    for g in range(8):
        c, z = g % 2, g // 2
        mine = slice(48 * g, 48 * g + 48)
        pg[c, 0, z, 0:48, :] = gwo[mine, :].astype(jnp.bfloat16)
        pg[c, 0, z, 48:96, :] = gwi[0, mine, :].astype(jnp.bfloat16)
        pg[c, 1, z, 0:48, :] = gwi[1, mine, :].astype(jnp.bfloat16)
        pg[c, 1, z, 48:96, :] = gwi[2, mine, :].astype(jnp.bfloat16)
        pg[c, 2, z, 0:48, :] = gwi[3, mine, :].astype(jnp.bfloat16)
        base = 192 * c
        pg[c, 0, z, 96:112, :] = gwu[z, base : base + 16, :].astype(jnp.bfloat16)
        pg[c, 1, z, 96:112, :] = gwu[z, base + 16 : base + 32, :].astype(jnp.bfloat16)
        pg[c, 2, z, 48:112, :] = gwu[z, base + 32 : base + 96, :].astype(jnp.bfloat16)
        pg[c, 3, z, 0:96, :] = gwu[z, base + 96 : base + 192, :].astype(jnp.bfloat16)
        pg[c, 3, z, 96:112, :] = jnp.concatenate(
            [sums[...]]
            + [inner_sum[:, j * width : (j + 1) * width] for j in range(slabs)]
            + [jnp.zeros((6, width), jnp.float32)],
            axis=0,
        ).astype(jnp.bfloat16)


def dense(tok, og, ctx, w, small):
    seqs, rows, width = tok.shape
    vm = pl.BlockSpec(memory_space=pltpu.VMEM)
    bf, f4 = jnp.bfloat16, jnp.float32
    return pl.pallas_call(
        dense_kernel,
        name="dense",
        out_shape=(
            jax.ShapeDtypeStruct((seqs, rows, width), bf),
            jax.ShapeDtypeStruct((seqs, rows, width), f4),
            jax.ShapeDtypeStruct((seqs, width, rows), bf),
            jax.ShapeDtypeStruct((2, 4, 4, 112, width), bf),
        ),
        in_specs=[vm] * 5,
        out_specs=[vm] * 4,
        scratch_shapes=[
            pltpu.VMEM((width, width), bf),
            pltpu.VMEM((4, width, width), bf),
            pltpu.VMEM((4, width, width), bf),
            pltpu.VMEM((width, width), f4),
            pltpu.VMEM((4, width, width), f4),
            pltpu.VMEM((4, width, width), f4),
            pltpu.VMEM((6, width), f4),
            pltpu.VMEM((1, 4 * width), f4),
        ],
        compiler_params=pltpu.CompilerParams(vmem_limit_bytes=BIG),
    )(tok, og, ctx, w, small)


def attend_back_kernel(
    place, spans, x, kv, qt, kt, qr, gctx, ctx32, pg, pg_in, out, gq, pr, dt, do, acc, dq,
):
    heads = kv.shape[0]
    length, width = x.shape
    blocks, _, rows = gctx.shape
    z = place[0]
    c = place[1]
    scale = HEAD ** -0.5

    def prepare(g, carry):
        r0 = pl.multiple_of(g * rows, rows)
        cols = pl.ds(r0, rows)
        for h in range(heads):
            part = slice(h * HEAD, (h + 1) * HEAD)
            grad = gctx[g, part, :]
            wide = grad.astype(jnp.float32)
            delta = -jnp.sum(wide * ctx32[g, part, :], axis=0, keepdims=True)
            dt[h, 0:64, cols] = jnp.zeros((64, rows), jnp.bfloat16)
            dt[h, 64:96, cols] = grad
            tail = jnp.concatenate(
                [jnp.zeros((8, rows), jnp.float32), *halves(delta), jnp.zeros((21, rows), jnp.float32)],
                axis=0,
            )
            dt[h, 96:128, cols] = tail.astype(jnp.bfloat16)
            turned = jnp.concatenate(
                [wide, jnp.zeros((96, rows), jnp.float32)], axis=0
            ).T.astype(jnp.bfloat16)
            for j in range(rows // QB):
                r1 = pl.multiple_of(2 * r0 + 2 * j * QB, QB)
                do[h, pl.ds(r1, QB), :] = turned[j * QB : (j + 1) * QB]
                do[h, pl.ds(r1 + QB, QB), :] = qr[h, pl.ds(r0 + j * QB, QB), :]
        return carry

    lax.fori_loop(0, blocks, prepare, 0)
    for s in range(4):
        pr[s] = (pg[c, s].astype(jnp.float32) + pg_in[s].astype(jnp.float32)).astype(jnp.bfloat16)
    acc[...] = jnp.zeros_like(acc)
    per = rows // QB

    def query_block(b, carry):
        q0 = pl.multiple_of(b * QB, QB)
        first = spans[0, b]
        dq[...] = jnp.zeros_like(dq)

        def key_block(keys):
            s = [dot(kv[h, keys, :], qt[h, :, pl.ds(q0, QB)]) for h in range(heads)]
            d = [dot(kv[h, keys, :], dt[h, :, pl.ds(q0, QB)]) for h in range(heads)]
            p = [jnp.exp2(v) for v in s]
            both = [
                jnp.concatenate(
                    [p[h].astype(jnp.bfloat16), (p[h] * d[h]).astype(jnp.bfloat16)], axis=1
                )
                for h in range(heads)
            ]
            for h in range(heads):
                acc[h, keys, :] += dot(both[h], do[h, pl.ds(2 * q0, 2 * QB), :])
            for h in range(heads):
                dq[h] += dot(kt[h, :, keys], both[h][:, QB:])

        in_pairs(first, spans[1, b], key_block)
        g = lax.div(b, per)
        off = pl.multiple_of(lax.rem(b, per) * QB, QB)
        for h in range(heads):
            out[g, h * HEAD : (h + 1) * HEAD, pl.ds(off, QB)] = (dq[h] * scale).astype(jnp.bfloat16)
        return carry

    lax.fori_loop(0, length // QB, query_block, 0)

    gq[...] = jnp.zeros_like(gq)
    span = heads * HEAD

    def finish(g, totals):
        r0 = pl.multiple_of(g * rows, rows)
        cols = pl.ds(r0, rows)
        for h in range(heads):
            both = acc[h, cols, :].T
            out[g, 2 * span + h * HEAD : 2 * span + (h + 1) * HEAD, :] = both[0:32].astype(jnp.bfloat16)
            out[g, span + h * HEAD : span + (h + 1) * HEAD, :] = (both[32:64] * scale).astype(
                jnp.bfloat16
            )
        piece = out[g]
        grad = dot(piece, x[cols, :])
        summed = jnp.sum(piece.astype(jnp.float32), axis=1, keepdims=True)
        return totals[0] + grad, totals[1] + summed

    grads, summed = lax.fori_loop(
        0,
        blocks,
        finish,
        (jnp.zeros((3 * span, width), jnp.float32), jnp.zeros((3 * span, 1), jnp.float32)),
    )
    grads_t = grads.T
    for g in range(8):
        cc, zz = g % 2, g // 2
        gq[cc, zz, :, 0 : 3 * span] = grads_t[48 * g : 48 * g + 48, :].astype(jnp.bfloat16)
    for cc in range(2):
        mine = jnp.concatenate(
            [
                summed[48 * cc : 48 * cc + 48, :],
                summed[2 * span + 48 * cc : 2 * span + 48 * cc + 48, :],
                jnp.zeros((48, 94), jnp.float32),
            ],
            axis=1,
        )
        gq[cc, z, :, 3 * span :] = mine.astype(jnp.bfloat16)


def attend_back(place, spans, x, kv, qt, kt, qr, gctx, ctx32, pg, pg_in):
    blocks, rows, width = x.shape
    length = blocks * rows
    heads = kv.shape[0]
    vm = pl.BlockSpec(memory_space=pltpu.VMEM)
    sm = pl.BlockSpec(memory_space=pltpu.SMEM)
    bf, f4 = jnp.bfloat16, jnp.float32
    return pl.pallas_call(
        attend_back_kernel,
        name="attend_back",
        out_shape=(
            jax.ShapeDtypeStruct((blocks, 3 * heads * HEAD, rows), bf),
            jax.ShapeDtypeStruct((2, 4, 48, width), bf),
            jax.ShapeDtypeStruct(pg_in.shape, bf),
        ),
        in_specs=[sm, sm] + [vm] * 9,
        out_specs=[vm] * 3,
        scratch_shapes=[
            pltpu.VMEM((heads, LANES, length), bf),
            pltpu.VMEM((heads, 2 * length, LANES), bf),
            pltpu.VMEM((heads, length, LANES), f4),
            pltpu.VMEM((heads, HEAD, QB), f4),
        ],
        compiler_params=pltpu.CompilerParams(vmem_limit_bytes=BIG),
    )(place, spans, x.reshape(length, width), kv, qt, kt, qr, gctx, ctx32, pg, pg_in)


def reduce_kernel(
    src, gq, pr, dst, p_out, q_out,
    gq_in, gq_sum, qa_in, qa_sum, qb_in, pa_in, pa_sum, pb_in, p_own, gq_own, pr_own,
    lsem, send, recv, gsend, grecv, qasend, qarecv, qbsend, qbrecv, qcsend, qcrecv,
    pasend, parecv, pbsend, pbrecv, pcsend, pcrecv,
):
    r, g, z, c = where_am_i()
    greet(r, g, 4, 8)
    pair = remote(gq.at[1 - c], gq_in, gsend, grecv, r, 2 * z + 1 - c)
    pair.start()
    waits = []
    for d in range(1, 4):
        rr = lax.rem(r + d, 4)
        copy = remote(pr.at[rr], pa_in.at[r], pasend.at[d - 1], parecv.at[r], rr, g)
        copy.start()
        waits.append(copy)
    own = pltpu.make_async_copy(src.at[g], dst.at[c, z], lsem.at[0])
    own.start()
    load_g = pltpu.make_async_copy(gq.at[c], gq_own, lsem.at[1])
    load_g.start()
    load_p = pltpu.make_async_copy(pr.at[r], pr_own, lsem.at[2])
    load_p.start()
    for d in range(1, 8):
        to = lax.rem(g + d, 8)
        copy = remote(src.at[to], dst.at[c, z], send.at[d - 1], recv.at[g], r, to)
        copy.start()
        waits.append(copy)

    def f32(value):
        return value.astype(jnp.float32)

    load_g.wait()
    pair.wait_recv()
    gq_sum[...] = (f32(gq_own[...]) + f32(gq_in[...])).astype(jnp.bfloat16)
    for d in range(1, 4):
        rr = lax.rem(r + d, 4)
        copy = remote(gq_sum.at[rr], qa_in.at[r], qasend.at[d - 1], qarecv.at[r], rr, g)
        copy.start()
        waits.append(copy)
    load_p.wait()
    for d in range(1, 4):
        b = lax.rem(r + d, 4)
        remote(pr.at[r], pa_in.at[b], pasend.at[0], parecv.at[b], b, g).wait_recv()
    total = f32(pr_own[...])
    for d in range(1, 4):
        total = total + f32(pa_in[lax.rem(r + d, 4)])
    pa_sum[...] = total.astype(jnp.bfloat16)
    for d in range(1, 4):
        zz = lax.rem(z + d, 4)
        copy = remote(pa_sum.at[zz], pb_in.at[z], pbsend.at[d - 1], pbrecv.at[z], r, 2 * zz + c)
        copy.start()
        waits.append(copy)
    for d in range(1, 4):
        b = lax.rem(r + d, 4)
        remote(gq_sum.at[r], qa_in.at[b], qasend.at[0], qarecv.at[b], b, g).wait_recv()
    total = f32(gq_sum[r])
    for d in range(1, 4):
        total = total + f32(qa_in[lax.rem(r + d, 4)])
    qa_sum[...] = total.astype(jnp.bfloat16)

    @pl.when(z != r)
    def _():
        remote(qa_sum, qb_in.at[z], qbsend, qbrecv.at[z], r, 2 * r + c).start()

    for d in range(1, 4):
        b = lax.rem(z + d, 4)
        remote(pa_sum.at[z], pb_in.at[b], pbsend.at[0], pbrecv.at[b], r, g).wait_recv()
    total = f32(pa_sum[z])
    for d in range(1, 4):
        total = total + f32(pb_in[lax.rem(z + d, 4)])
    p_own[...] = total.astype(jnp.bfloat16)
    keep_p = pltpu.make_async_copy(p_own, p_out.at[r], lsem.at[3])
    keep_p.start()
    for d in range(1, 4):
        rr = lax.rem(r + d, 4)
        copy = remote(p_own, p_out.at[r], pcsend.at[d - 1], pcrecv.at[r], rr, g)
        copy.start()
        waits.append(copy)

    @pl.when(z == r)
    def _():
        for d in range(1, 4):
            b = lax.rem(z + d, 4)
            remote(qa_sum, qb_in.at[b], qbsend, qbrecv.at[b], r, g).wait_recv()
        qb_in[z] = qa_sum[...]
        keep = pltpu.make_async_copy(qb_in, q_out, lsem.at[4])
        keep.start()
        for d in range(1, 4):
            remote(qb_in, q_out, qcsend.at[d - 1], qcrecv, lax.rem(r + d, 4), g).start()
        keep.wait()
        for d in range(1, 4):
            remote(qb_in, q_out, qcsend.at[d - 1], qcrecv, lax.rem(r + d, 4), g).wait_send()

    @pl.when(z != r)
    def _():
        remote(qb_in, q_out, qcsend.at[0], qcrecv, r, g).wait_recv()
        remote(qa_sum, qb_in.at[z], qbsend, qbrecv.at[z], r, 2 * r + c).wait_send()

    for d in range(1, 4):
        b = lax.rem(r + d, 4)
        remote(p_own, p_out.at[b], pcsend.at[0], pcrecv.at[b], b, g).wait_recv()
    for d in range(1, 8):
        b = lax.rem(g + d, 8)
        remote(src.at[g], dst.at[lax.rem(b, 2), lax.div(b, 2)], send.at[0], recv.at[b], r, b).wait_recv()
    pair.wait_send()
    for copy in waits:
        copy.wait_send()
    keep_p.wait()
    own.wait()


def reduce_all(src, gq, pr):
    dma = pltpu.SemaphoreType.DMA
    anywhere = pl.BlockSpec(memory_space=pl.ANY)
    bf = jnp.bfloat16
    width = gq.shape[-1]
    return pl.pallas_call(
        reduce_kernel,
        name="reduce",
        out_shape=(
            jax.ShapeDtypeStruct((2, 4) + src.shape[1:], bf),
            jax.ShapeDtypeStruct((4, 112, width), bf),
            jax.ShapeDtypeStruct((4, 48, width), bf),
        ),
        in_specs=[anywhere] * 3,
        out_specs=[anywhere] * 3,
        scratch_shapes=[
            pltpu.VMEM((4, 48, width), bf),
            pltpu.VMEM((4, 48, width), bf),
            pltpu.VMEM((4, 48, width), bf),
            pltpu.VMEM((48, width), bf),
            pltpu.VMEM((4, 48, width), bf),
            pltpu.VMEM((4, 4, 112, width), bf),
            pltpu.VMEM((4, 112, width), bf),
            pltpu.VMEM((4, 112, width), bf),
            pltpu.VMEM((112, width), bf),
            pltpu.VMEM((4, 48, width), bf),
            pltpu.VMEM((4, 112, width), bf),
            dma((5,)), dma((7,)), dma((8,)), dma, dma, dma((3,)), dma((4,)), dma, dma((4,)),
            dma((3,)), dma, dma((3,)), dma((4,)), dma((3,)), dma((4,)), dma((3,)), dma((4,)),
        ],
        compiler_params=pltpu.CompilerParams(
            collective_id=4, has_side_effects=True, vmem_limit_bytes=BIG // 2
        ),
    )(src, gq, pr)


def finish_kernel(
    place, parts, grad_one, w, p_in, q_in,
    out, g_q, g_k, g_v, g_o, g_in, g_up, rows_out, inner_out, wq,
):
    seqs, rows, width = grad_one.shape
    span = 96
    z = place[0]
    c = place[1]
    for i in range(3):
        for g in range(8):
            wq[i, 48 * g : 48 * g + 48, :] = w[0, g % 2, g // 2, 48 * i : 48 * i + 48, :]
    for s in range(seqs):
        total = grad_one[s]
        for i in range(3):
            turned = jnp.concatenate(
                [parts[s, zz, i * span : (i + 1) * span, :] for zz in range(4)], axis=0
            )
            back = turned.astype(jnp.float32).T.astype(jnp.bfloat16)
            total = total + lax.dot_general(
                back, wq[i], (((1,), (1,)), ((), ())), preferred_element_type=jnp.float32
            )
        out[s] = total.astype(jnp.bfloat16)
    wide = [q_in[zz].astype(jnp.float32) for zz in range(4)]
    for i, ref in enumerate((g_q, g_k, g_v)):
        ref[...] = jnp.concatenate([v[:, i * span : (i + 1) * span] for v in wide], axis=1)
    sums = p_in[3, 96:112, :]
    pick = jnp.where(
        iota((width, 48), 0) == 48 * (2 * z + c) + iota((width, 48), 1), 1.0, 0.0
    ).astype(jnp.bfloat16)
    rows_out[8:24, :] = dot(sums, pick)
    both = q_in[z].astype(jnp.float32)[:, 3 * span :].T
    rows_out[0:8, :] = both[0:8, :]
    pick = jnp.where(
        iota((width, 192), 0) == 192 * c + iota((width, 192), 1), 1.0, 0.0
    ).astype(jnp.bfloat16)
    inner = dot(sums, pick)
    inner_out[...] = jnp.sum(
        jnp.where(iota((16, 192), 0) == 6 + z, inner, 0.0), axis=0, keepdims=True
    )
    g_o[...] = p_in[0, 0:48, :].astype(jnp.float32)
    g_in[:, 0:384] = p_in[0, 48:96, :].astype(jnp.float32)
    g_in[:, 384:768] = p_in[1, 0:48, :].astype(jnp.float32)
    g_in[:, 768:1152] = p_in[1, 48:96, :].astype(jnp.float32)
    g_in[:, 1152:1536] = p_in[2, 0:48, :].astype(jnp.float32)
    g_up[0:16, :] = p_in[0, 96:112, :].astype(jnp.float32)
    g_up[16:32, :] = p_in[1, 96:112, :].astype(jnp.float32)
    g_up[32:96, :] = p_in[2, 48:112, :].astype(jnp.float32)
    g_up[96:192, :] = p_in[3, 0:96, :].astype(jnp.float32)


def finish(place, parts, grad_one, w, p_in, q_in):
    seqs, rows, width = grad_one.shape
    vm = pl.BlockSpec(memory_space=pltpu.VMEM)
    sm = pl.BlockSpec(memory_space=pltpu.SMEM)
    bf, f4 = jnp.bfloat16, jnp.float32
    shapes = ((48, width),) * 4 + ((48, 4 * width), (192, width), (24, 48), (1, 192))
    return pl.pallas_call(
        finish_kernel,
        name="finish",
        grid=(1,),
        out_shape=(jax.ShapeDtypeStruct((seqs, rows, width), bf),)
        + tuple(jax.ShapeDtypeStruct(shape, f4) for shape in shapes),
        in_specs=[
            sm, whole_spec(parts), whole_spec(grad_one), quarter_spec(w, 0), whole_spec(p_in), whole_spec(q_in)
        ],
        out_specs=[whole_spec(grad_one)]
        + [pl.BlockSpec(shape, functools.partial(zeros_for, len(shape))) for shape in shapes],
        scratch_shapes=[pltpu.VMEM((3, width, width), bf)],
        compiler_params=pltpu.CompilerParams(vmem_limit_bytes=BIG),
    )(place, parts, grad_one, w, p_in, q_in)


def line_of_chips(
    tokens, segment_ids, out_grad, query_weight, key_weight, value_weight, output_weight,
    inner_weight, outer_weight, query_bias, value_bias, output_bias, inner_bias, outer_bias,
    first_gain, first_shift, second_gain, second_shift,
):
    bf = jnp.bfloat16
    width = tokens.shape[2]
    g = lax.axis_index("grp")
    z, c = lax.div(g, 2), lax.rem(g, 2)
    place = jnp.stack([z, c]).astype(jnp.int32)
    weights = (query_weight, key_weight, value_weight, output_weight, inner_weight, outer_weight)
    vectors = (
        query_bias, value_bias, output_bias, outer_bias, first_gain, first_shift, second_gain, second_shift,
        inner_bias, segment_ids[0].astype(bf), segment_ids[1].astype(bf),
    )
    row = lax.broadcasted_iota(jnp.int32, (16, 512), 0)
    small = jnp.zeros((16, 512), bf)
    for i, vector in enumerate(vectors):
        small = jnp.where(row == i, jnp.pad(vector, (0, 512 - vector.shape[0]))[None], small)
    x, w, small = gather(tokens, weights, small)
    kv, qt, kt, qr, ctx, ctx32, spans = attend(place, x, w, small)
    mine = exchange_context(ctx).reshape(2, width, -1)
    layer_out, grad_one, gctx, pg = dense(tokens, out_grad, mine, w, small)
    gctx_in, pg_in = exchange_cotangent(gctx.reshape(2, 4, 96, -1), pg)
    parts, gq, pr = attend_back(place, spans, x, kv, qt, kt, qr, gctx_in, ctx32, pg, pg_in)
    parts_in, p_in, q_in = reduce_all(parts, gq, pr)
    input_grad, g_q, g_k, g_v, g_o, g_in, g_up, rows, inner_row = finish(
        place, parts_in, grad_one, w, p_in, q_in
    )
    return (
        layer_out, input_grad, g_q, g_k, g_v, g_o, g_in, g_up,
        rows[0], rows[1], rows[8], inner_row[0], rows[9], rows[10], rows[11], rows[12], rows[13],
    )


def solution(mesh):
    in_specs = (
        P("rep", "grp", None),
        P("rep", "grp"),
        P("rep", "grp", None),
        P("grp", None),
        P("grp", None),
        P("grp", None),
        P("grp", None),
        P("grp", None),
        P("grp", None),
        P("grp"),
        P("grp"),
        P("grp"),
        P("grp"),
        P("grp"),
        P("grp"),
        P("grp"),
        P("grp"),
        P("grp"),
    )
    out_specs = (
        P("rep", "grp", None),
        P("rep", "grp", None),
        P("grp", None),
        P("grp", None),
        P("grp", None),
        P("grp", None),
        P("grp", None),
        P("grp", None),
        P("grp"),
        P("grp"),
        P("grp"),
        P("grp"),
        P("grp"),
        P("grp"),
        P("grp"),
        P("grp"),
        P("grp"),
    )
    whole_line = mesh.shape["grp"] == 8 and mesh.shape["rep"] == 4
    return jax.shard_map(
        line_of_chips if whole_line else on_device, mesh=mesh, in_specs=in_specs, out_specs=out_specs, check_vma=False
    )
```

```python
import functools
from functools import reduce

import jax
import jax.numpy as jnp
from jax import lax
from jax.experimental import pallas as pl
from jax.experimental.pallas import tpu as pltpu
from jax.sharding import PartitionSpec as P

H = 12
MICRO = 2
SEQ_MB = 1


norm_epsilon = 1e-05
masked_score = -1000000000.0


def layer_norm(inputs, norm_gain, norm_shift):
    center = inputs - jnp.mean(inputs, axis=-1, keepdims=True)
    spread = jnp.mean(center * center, axis=-1, keepdims=True)
    return center * lax.rsqrt(spread + norm_epsilon) * norm_gain + norm_shift


def exact_gelu(inputs):
    return jax.nn.gelu(inputs, approximate=False)


def times_transpose(left, right):
    return lax.dot_general(
        left, right, (((1,), (1,)), ((), ())), preferred_element_type=jnp.float32
    )


def transpose_times(left, right):
    return lax.dot_general(
        left, right, (((0,), (0,)), ((), ())), preferred_element_type=jnp.float32
    )


def column_total(inputs):
    return jnp.sum(inputs.astype(jnp.float32), axis=0)


def masked_scores(query_group, key_group, same_doc, score_scale):
    scores = (
        jnp.einsum("bqhd,bkhd->bhqk", query_group, key_group, preferred_element_type=jnp.float32)
        * score_scale
    )
    return jnp.where(same_doc[:, None], scores, masked_score)


def group_forward(query_group, key_group, value_group, same_doc, score_scale):
    scores = masked_scores(query_group, key_group, same_doc, score_scale)
    highest = jnp.max(scores, axis=-1, keepdims=True)
    log_total = highest + jnp.log(jnp.sum(jnp.exp(scores - highest), axis=-1, keepdims=True))
    weights_low = jnp.exp(scores - log_total).astype(jnp.bfloat16)
    context = jnp.einsum(
        "bhqk,bkhd->bqhd", weights_low, value_group, preferred_element_type=jnp.float32
    )
    return (context.astype(jnp.bfloat16), log_total)


def group_backward(
    query_group, key_group, value_group, same_doc, log_total, grad_context, score_scale
):
    attn_weights = jnp.exp(masked_scores(query_group, key_group, same_doc, score_scale) - log_total)
    weights_low = attn_weights.astype(jnp.bfloat16)
    grad_weights = jnp.einsum(
        "bqhd,bkhd->bhqk", grad_context, value_group, preferred_element_type=jnp.float32
    )
    centre = jnp.sum(attn_weights * grad_weights, axis=-1, keepdims=True)
    grad_scores = (attn_weights * (grad_weights - centre)).astype(jnp.bfloat16)
    grad_query = jnp.einsum(
        "bhqk,bkhd->bqhd", grad_scores, key_group, preferred_element_type=jnp.float32
    )
    grad_query = (grad_query * score_scale).astype(jnp.bfloat16)
    grad_key = (
        jnp.einsum("bhqk,bqhd->bkhd", grad_scores, query_group, preferred_element_type=jnp.float32)
        * score_scale
    )
    grad_value = jnp.einsum(
        "bhqk,bqhd->bkhd", weights_low, grad_context, preferred_element_type=jnp.float32
    )
    return (grad_query, grad_key, grad_value)


def merge_groups(stacked, row_total, model_width):
    return jnp.moveaxis(stacked, 0, 2).reshape(row_total, model_width)


def gradient_terms(
    token_rows,
    context_rows,
    hidden_rows,
    active_rows,
    grad_queries,
    grad_keys,
    grad_values,
    grad_attention,
    grad_inner,
    grad_feed,
    norm_grads,
):
    return (
        transpose_times(token_rows, grad_queries),
        transpose_times(token_rows, grad_keys),
        transpose_times(token_rows, grad_values),
        transpose_times(context_rows, grad_attention),
        transpose_times(hidden_rows, grad_inner),
        transpose_times(active_rows, grad_feed),
        column_total(grad_queries),
        column_total(grad_values),
        column_total(grad_attention),
        column_total(grad_inner),
        column_total(grad_feed),
        norm_grads[0],
        norm_grads[1],
        norm_grads[2],
        norm_grads[3],
    )


def on_device(
    tokens,
    segment_ids,
    out_grad,
    query_weight,
    key_weight,
    value_weight,
    output_weight,
    inner_weight,
    outer_weight,
    query_bias,
    value_bias,
    output_bias,
    inner_bias,
    outer_bias,
    first_gain,
    first_shift,
    second_gain,
    second_shift,
):
    row_count = tokens.shape[1]
    model_width = tokens.shape[2]
    head_count = H
    head_size = model_width // head_count
    per_group = max(1, min(head_count, 128 // head_size))
    group_width = per_group * head_size
    group_count = head_count // per_group
    score_scale = head_size ** (-0.5)
    seq_count = SEQ_MB
    flat_rows = seq_count * row_count
    all_segments = lax.all_gather(segment_ids, "grp", axis=1, tiled=True)
    outputs = []
    input_grads = []
    shares_list = []
    for batch_index in range(MICRO):
        offset = batch_index * seq_count
        local_tokens = tokens[offset : offset + seq_count]
        flat_tokens = local_tokens.reshape(flat_rows, model_width)
        gathered = (
            lax.all_gather(query_weight, "grp", axis=0, tiled=True),
            lax.all_gather(key_weight, "grp", axis=0, tiled=True),
            lax.all_gather(value_weight, "grp", axis=0, tiled=True),
            lax.all_gather(output_weight, "grp", axis=0, tiled=True),
            lax.all_gather(inner_weight, "grp", axis=0, tiled=True),
            lax.all_gather(outer_weight, "grp", axis=0, tiled=True),
            lax.all_gather(query_bias, "grp", axis=0, tiled=True),
            lax.all_gather(value_bias, "grp", axis=0, tiled=True),
            lax.all_gather(output_bias, "grp", axis=0, tiled=True),
            lax.all_gather(inner_bias, "grp", axis=0, tiled=True),
            lax.all_gather(outer_bias, "grp", axis=0, tiled=True),
            lax.all_gather(first_gain, "grp", axis=0, tiled=True),
            lax.all_gather(first_shift, "grp", axis=0, tiled=True),
            lax.all_gather(second_gain, "grp", axis=0, tiled=True),
            lax.all_gather(second_shift, "grp", axis=0, tiled=True),
        )
        full_query, full_key, full_value, full_output, full_inner, full_outer = gathered[:6]
        (
            bias_query,
            bias_value,
            bias_output,
            bias_inner,
            bias_outer,
            gain_first,
            shift_first,
            gain_second,
            shift_second,
        ) = [vector.astype(jnp.float32) for vector in gathered[6:]]
        queries = (
            jnp.dot(flat_tokens, full_query, preferred_element_type=jnp.float32) + bias_query
        ).astype(jnp.bfloat16)
        key_rows = jnp.dot(flat_tokens, full_key, preferred_element_type=jnp.float32).astype(
            jnp.bfloat16
        )
        value_rows = (
            jnp.dot(flat_tokens, full_value, preferred_element_type=jnp.float32) + bias_value
        ).astype(jnp.bfloat16)
        key_split = key_rows.reshape(seq_count, row_count, model_width)
        value_split = value_rows.reshape(seq_count, row_count, model_width)
        key_all, value_all = (
            lax.all_gather(key_split, "grp", axis=1, tiled=True),
            lax.all_gather(value_split, "grp", axis=1, tiled=True),
        )
        length = key_all.shape[1]
        local_segments = segment_ids[offset : offset + seq_count]
        far_segments = all_segments[offset : offset + seq_count]
        same_doc = local_segments[:, :, None] == far_segments[:, None, :]
        query_split = queries.reshape(seq_count, row_count, model_width)

        def slice_group(array, group_index):
            piece = lax.dynamic_slice_in_dim(array, group_index * group_width, group_width, 2)
            return piece.reshape(array.shape[0], array.shape[1], per_group, head_size)

        def forward_group(group_index):
            context, log_total = group_forward(
                slice_group(query_split, group_index),
                slice_group(key_all, group_index),
                slice_group(value_all, group_index),
                same_doc,
                score_scale,
            )
            return (context.reshape(seq_count, row_count, group_width), log_total)

        context_groups, log_totals = lax.map(forward_group, jnp.arange(group_count))
        context_rows = merge_groups(context_groups, flat_rows, model_width)
        attention = (
            jnp.dot(context_rows, full_output, preferred_element_type=jnp.float32) + bias_output
        )
        residual_one = flat_tokens.astype(jnp.float32) + attention
        hidden_one, norm_one_pullback = jax.vjp(layer_norm, residual_one, gain_first, shift_first)
        hidden_low = hidden_one.astype(jnp.bfloat16)
        inner_pre = jnp.dot(hidden_low, full_inner, preferred_element_type=jnp.float32) + bias_inner
        activation, gelu_pullback = jax.vjp(exact_gelu, inner_pre)
        active_low = activation.astype(jnp.bfloat16)
        feed = jnp.dot(active_low, full_outer, preferred_element_type=jnp.float32) + bias_outer
        output_rows, norm_two_pullback = jax.vjp(
            layer_norm, hidden_one + feed, gain_second, shift_second
        )
        outputs.append(output_rows.astype(jnp.bfloat16).reshape(seq_count, row_count, model_width))
        cotangent = (
            out_grad[offset : offset + seq_count]
            .reshape(flat_rows, model_width)
            .astype(jnp.float32)
        )
        grad_two, grad_gain_two, grad_shift_two = norm_two_pullback(cotangent)
        grad_feed = grad_two.astype(jnp.bfloat16)
        grad_active = times_transpose(grad_feed, full_outer)
        grad_inner = gelu_pullback(grad_active)[0].astype(jnp.bfloat16)
        grad_hidden = grad_two + times_transpose(grad_inner, full_inner)
        grad_one, grad_gain_one, grad_shift_one = norm_one_pullback(grad_hidden)
        grad_attention = grad_one.astype(jnp.bfloat16)
        grad_context = times_transpose(grad_attention, full_output).astype(jnp.bfloat16)
        grad_context = grad_context.reshape(seq_count, row_count, model_width)

        def backward_group(pieces):
            group_index, log_total = pieces
            grad_query, grad_key, grad_value = group_backward(
                slice_group(query_split, group_index),
                slice_group(key_all, group_index),
                slice_group(value_all, group_index),
                same_doc,
                log_total,
                slice_group(grad_context, group_index),
                score_scale,
            )
            return (
                grad_query.reshape(seq_count, row_count, group_width),
                grad_key.reshape(seq_count, length, group_width),
                grad_value.reshape(seq_count, length, group_width),
            )

        query_groups, key_groups, value_groups = lax.map(
            backward_group, (jnp.arange(group_count), log_totals)
        )
        key_owned, value_owned = (
            lax.psum_scatter(key_groups, "grp", scatter_dimension=2, tiled=True),
            lax.psum_scatter(value_groups, "grp", scatter_dimension=2, tiled=True),
        )
        grad_keys = merge_groups(key_owned, flat_rows, model_width).astype(jnp.bfloat16)
        grad_values = merge_groups(value_owned, flat_rows, model_width).astype(jnp.bfloat16)
        grad_queries = merge_groups(query_groups, flat_rows, model_width)
        grad_tokens = (
            grad_one
            + times_transpose(grad_queries, full_query)
            + times_transpose(grad_keys, full_key)
            + times_transpose(grad_values, full_value)
        )
        input_grads.append(
            grad_tokens.astype(jnp.bfloat16).reshape(seq_count, row_count, model_width)
        )
        norm_grads = (grad_gain_one, grad_shift_one, grad_gain_two, grad_shift_two)
        terms = gradient_terms(
            flat_tokens,
            context_rows,
            hidden_low,
            active_low,
            grad_queries,
            grad_keys,
            grad_values,
            grad_attention,
            grad_inner,
            grad_feed,
            norm_grads,
        )
        shares = (
            lax.psum_scatter(terms[0], "grp", scatter_dimension=0, tiled=True),
            lax.psum_scatter(terms[1], "grp", scatter_dimension=0, tiled=True),
            lax.psum_scatter(terms[2], "grp", scatter_dimension=0, tiled=True),
            lax.psum_scatter(terms[3], "grp", scatter_dimension=0, tiled=True),
            lax.psum_scatter(terms[4], "grp", scatter_dimension=0, tiled=True),
            lax.psum_scatter(terms[5], "grp", scatter_dimension=0, tiled=True),
            lax.psum_scatter(terms[6], "grp", scatter_dimension=0, tiled=True),
            lax.psum_scatter(terms[7], "grp", scatter_dimension=0, tiled=True),
            lax.psum_scatter(terms[8], "grp", scatter_dimension=0, tiled=True),
            lax.psum_scatter(terms[9], "grp", scatter_dimension=0, tiled=True),
            lax.psum_scatter(terms[10], "grp", scatter_dimension=0, tiled=True),
            lax.psum_scatter(terms[11], "grp", scatter_dimension=0, tiled=True),
            lax.psum_scatter(terms[12], "grp", scatter_dimension=0, tiled=True),
            lax.psum_scatter(terms[13], "grp", scatter_dimension=0, tiled=True),
            lax.psum_scatter(terms[14], "grp", scatter_dimension=0, tiled=True),
        )
        shares_list.append(shares)
    owned = reduce(
        lambda left_part, right_part: jax.tree.map(jnp.add, left_part, right_part), shares_list
    )
    summed = (
        lax.psum(owned[0].astype(jnp.bfloat16), "rep").astype(jnp.float32),
        lax.psum(owned[1].astype(jnp.bfloat16), "rep").astype(jnp.float32),
        lax.psum(owned[2].astype(jnp.bfloat16), "rep").astype(jnp.float32),
        lax.psum(owned[3].astype(jnp.bfloat16), "rep").astype(jnp.float32),
        lax.psum(owned[4].astype(jnp.bfloat16), "rep").astype(jnp.float32),
        lax.psum(owned[5].astype(jnp.bfloat16), "rep").astype(jnp.float32),
        lax.psum(owned[6].astype(jnp.bfloat16), "rep").astype(jnp.float32),
        lax.psum(owned[7].astype(jnp.bfloat16), "rep").astype(jnp.float32),
        lax.psum(owned[8].astype(jnp.bfloat16), "rep").astype(jnp.float32),
        lax.psum(owned[9].astype(jnp.bfloat16), "rep").astype(jnp.float32),
        lax.psum(owned[10].astype(jnp.bfloat16), "rep").astype(jnp.float32),
        lax.psum(owned[11].astype(jnp.bfloat16), "rep").astype(jnp.float32),
        lax.psum(owned[12].astype(jnp.bfloat16), "rep").astype(jnp.float32),
        lax.psum(owned[13].astype(jnp.bfloat16), "rep").astype(jnp.float32),
        lax.psum(owned[14].astype(jnp.bfloat16), "rep").astype(jnp.float32),
    )
    return (
        jnp.concatenate(outputs, axis=0),
        jnp.concatenate(input_grads, axis=0),
        summed[0],
        summed[1],
        summed[2],
        summed[3],
        summed[4],
        summed[5],
        summed[6],
        summed[7],
        summed[8],
        summed[9],
        summed[10],
        summed[11],
        summed[12],
        summed[13],
        summed[14],
    )


HEAD = 32
LANES = 128
QB = 256
KB = 256
AWAY = 2.0 ** 100
LIMIT = 100.0
MESH = pl.DeviceIdType.MESH
BIG = 100 * 1024 * 1024 // 2
LOG2E = 1.4426950408889634


def halves(value):
    first = value.astype(jnp.bfloat16).astype(jnp.float32)
    rest = value - first
    second = rest.astype(jnp.bfloat16).astype(jnp.float32)
    third = (rest - second).astype(jnp.bfloat16).astype(jnp.float32)
    return first, second, third


def dot(left, right):
    return jnp.dot(left, right, preferred_element_type=jnp.float32)


def zeros_for(rank, *grid):
    return (0,) * rank


def whole_spec(array):
    return pl.BlockSpec(array.shape, functools.partial(zeros_for, array.ndim), pipeline_mode=pl.Buffered(1))


def quarter_spec(w, i):
    return pl.BlockSpec((1,) + w.shape[1:], lambda *grid: (i, 0, 0, 0, 0), pipeline_mode=pl.Buffered(1))


def iota(shape, dim):
    return lax.broadcasted_iota(jnp.int32, shape, dim)


def where_am_i():
    r = lax.axis_index("rep")
    g = lax.axis_index("grp")
    return r, g, lax.div(g, 2), lax.rem(g, 2)


def remote(src, dst, send, recv, r, g):
    return pltpu.make_async_remote_copy(
        src_ref=src, dst_ref=dst, send_sem=send, recv_sem=recv, device_id=(r, g), device_id_type=MESH
    )


def greet(r, g, reps, group):
    barrier = pltpu.get_barrier_semaphore()
    for d in range(1, group):
        pl.semaphore_signal(barrier, inc=1, device_id=(r, lax.rem(g + d, group)), device_id_type=MESH)
    for d in range(1, reps):
        pl.semaphore_signal(barrier, inc=1, device_id=(lax.rem(r + d, reps), g), device_id_type=MESH)
    pl.semaphore_wait(barrier, group + reps - 2)


def gather_kernel(
    tok, wq, wk, wv, wo, wi, wu, small, x_out, w_out, s_out,
    lsem, tsend, trecv, psend, wsend1, wrecv1, wsend2, wrecv2, wsend3, wrecv3, ssend, srecv,
):
    r, g, z, c = where_am_i()
    reps, chips = 4, 4
    p = 2 * z + 1 - c
    greet(r, g, reps, 2 * chips)
    width = wq.shape[1]
    slab = [wi.at[:, pl.ds(j * width, width)] for j in range(4)]
    first_part = pl.ds(0, 48)
    quarters = (
        ((wq, 0, 48), (wk, 48, 48), (wv, 96, 48)),
        ((wo, 0, 48), (slab[0], 48, 48), (slab[1], 96, 48)),
        ((slab[2], 0, 48), (slab[3], 48, 48), (wu.at[first_part, :], 96, 48)),
        ((wu.at[pl.ds(48, 144), :], 0, 144),),
    )
    for i, pieces in enumerate(quarters):
        @pl.when(r == i)
        def _():
            copies = [
                pltpu.make_async_copy(
                    ref, w_out.at[i, c, z, pl.ds(row, count), :], lsem.at[3 + k]
                )
                for k, (ref, row, count) in enumerate(pieces)
            ]
            for copy in copies:
                copy.start()
            for copy in copies:
                copy.wait()

    mine = w_out.at[r, c, z]
    own_x = pltpu.make_async_copy(tok.at[c], x_out.at[g], lsem.at[0])
    own_x.start()
    own_s = pltpu.make_async_copy(small, s_out.at[g], lsem.at[2])
    own_s.start()
    swap = remote(tok.at[1 - c], x_out.at[g], psend, trecv.at[g], r, p)
    swap.start()

    first = []
    for d in range(1, chips):
        zz = lax.rem(z + d, chips)
        copy = remote(mine, mine, wsend1.at[d - 1], wrecv1.at[z], r, 2 * zz + c)
        copy.start()
        first.append(copy)
    smalls = []
    for d in range(1, 2 * chips):
        copy = remote(small, s_out.at[g], ssend.at[d - 1], srecv.at[g], r, lax.rem(g + d, 2 * chips))
        copy.start()
        smalls.append(copy)

    def pass_on(b, src, way):
        to = g + 2 if way == 0 else g - 2
        return remote(src, x_out.at[b], tsend.at[way, b], trecv.at[b], r, to)

    def forward(b, src, way):
        ok = z < chips - 1 if way == 0 else z > 0

        @pl.when(ok)
        def _():
            pass_on(b, src, way).start()

    def arrived(b):
        remote(x_out.at[b], x_out.at[b], tsend.at[0, b], trecv.at[b], r, p).wait_recv()

    forward(g, tok.at[c], 0)
    forward(g, tok.at[c], 1)
    arrived(p)
    forward(p, x_out.at[p], 0)
    forward(p, x_out.at[p], 1)

    def tokens_from(d):
        for k in range(2):
            @pl.when(z >= d)
            def _():
                b = 2 * (z - d) + (c if k == 0 else 1 - c)
                arrived(b)
                forward(b, x_out.at[b], 0)

            @pl.when(z + d < chips)
            def _():
                b = 2 * (z + d) + (c if k == 0 else 1 - c)
                arrived(b)
                forward(b, x_out.at[b], 1)

    tokens_from(1)
    for d in range(1, chips):
        zz = lax.rem(z + d, chips)
        remote(mine, w_out.at[r, c, zz], wsend1.at[0], wrecv1.at[zz], r, p).wait_recv()
    second = []
    for d in range(1, reps):
        copy = remote(
            w_out.at[r, c], w_out.at[r, c], wsend2.at[d - 1], wrecv2.at[r], lax.rem(r + d, reps), g
        )
        copy.start()
        second.append(copy)
    third = [remote(w_out.at[r, c], w_out.at[r, c], wsend3.at[r], wrecv3.at[r], r, p)]
    third[0].start()
    tokens_from(2)
    for d in range(1, reps):
        q = lax.rem(r + d, reps)
        remote(w_out.at[q, c], w_out.at[q, c], wsend2.at[0], wrecv2.at[q], r, p).wait_recv()
        copy = remote(w_out.at[q, c], w_out.at[q, c], wsend3.at[q], wrecv3.at[q], r, p)
        copy.start()
        third.append(copy)
    tokens_from(3)
    for q in range(reps):
        remote(w_out.at[q, 1 - c], w_out.at[q, 1 - c], wsend3.at[q], wrecv3.at[q], r, p).wait_recv()
    for d in range(1, 2 * chips):
        b = lax.rem(g + d, 2 * chips)
        remote(small, s_out.at[b], ssend.at[0], srecv.at[b], r, p).wait_recv()
    own_x.wait()
    own_s.wait()
    swap.wait_send()
    for copy in first + smalls + second + third:
        copy.wait_send()
    for b in range(2 * chips):
        @pl.when((z < chips - 1) & (b < 2 * z + 2))
        def _():
            pass_on(b, x_out.at[b], 0).wait_send()

        @pl.when((z > 0) & (b >= 2 * z))
        def _():
            pass_on(b, x_out.at[b], 1).wait_send()


def gather(tokens, weights, small):
    dma = pltpu.SemaphoreType.DMA
    anywhere = pl.BlockSpec(memory_space=pl.ANY)
    rows, width = tokens.shape[1:]
    return pl.pallas_call(
        gather_kernel,
        name="gather",
        out_shape=(
            jax.ShapeDtypeStruct((8, rows, width), jnp.bfloat16),
            jax.ShapeDtypeStruct((4, 2, 4, 144, width), jnp.bfloat16),
            jax.ShapeDtypeStruct((8,) + small.shape, jnp.bfloat16),
        ),
        in_specs=[anywhere] * 8,
        out_specs=[anywhere] * 3,
        scratch_shapes=[
            dma((6,)), dma((2, 8)), dma((8,)), dma, dma((3,)), dma((4,)), dma((3,)), dma((4,)),
            dma((4,)), dma((4,)), dma((7,)), dma((8,)),
        ],
        compiler_params=pltpu.CompilerParams(collective_id=1, has_side_effects=True),
    )(tokens, *weights, small)


def span_of(starts, q0, docs):
    low = jnp.int32(0)
    high = starts[docs]
    for d in range(docs):
        low = jnp.where(starts[d] <= q0, jnp.maximum(low, starts[d]), low)
        high = jnp.where(starts[d + 1] >= q0 + QB, jnp.minimum(high, starts[d + 1]), high)
    first = lax.div(low, LANES)
    last = lax.div(high + LANES - 1, LANES)
    steps = lax.div(last - first + KB // LANES - 1, KB // LANES)
    total = lax.div(starts[docs], LANES)
    first = jnp.minimum(first, total - steps * (KB // LANES))
    return first, steps


def vectors_of(small):
    return jnp.concatenate([small[g, 0:8, 0:48].astype(jnp.float32) for g in range(8)], axis=1)


def in_pairs(first, steps, body):
    double = lax.div(steps, 2)

    def two(i, none):
        body(pl.ds(pl.multiple_of((first + i * (2 * KB // LANES)) * LANES, LANES), 2 * KB))
        return none

    lax.fori_loop(0, double, two, 0)

    @pl.when(steps > 2 * double)
    def _():
        body(pl.ds(pl.multiple_of((first + double * (2 * KB // LANES)) * LANES, LANES), KB))


def in_groups(first, steps, body, most):
    unit = KB // LANES

    def at(i):
        return pl.multiple_of((first + i * unit) * LANES, LANES)

    many = lax.div(steps, most)

    def group(i, none):
        body([at(most * i + 2 * k) for k in range(most // 2)], 2 * KB)
        return none

    lax.fori_loop(0, many, group, 0)
    if most == 4:
        @pl.when(steps - most * many >= 2)
        def _():
            body([at(most * many), at(most * many + 1)], KB)

    @pl.when(lax.rem(steps, 2) == 1)
    def _():
        body([at(steps - 1)], KB)


def attend_kernel(
    place, x, w, small, kv, qt, kt, qr, ctx, ctx32, spans, wrow, wtr, vt, acc, tall, seg, starts,
):
    heads = kv.shape[0]
    length, width = x.shape
    blocks, hw, rows = ctx.shape
    docs = 8
    z = place[0]
    c = place[1]
    span = heads * HEAD
    bias = vectors_of(small).astype(jnp.bfloat16)
    for g in range(8):
        two = small[g, 8:16, :].astype(jnp.float32)
        seg[g : g + 1, :] = jnp.where(c == 0, two[1:2], two[2:3]).astype(jnp.int32)

    full = [
        jnp.concatenate([w[0, g % 2, g // 2, 48 * i : 48 * i + 48, :] for g in range(8)], axis=0)
        for i in range(3)
    ]
    lane = iota((width, heads * LANES), 1)
    head, inner = lax.div(lane, LANES), lax.rem(lane, LANES)
    column = span * z + head * HEAD + lax.rem(inner, HEAD)
    hit = iota((width, heads * LANES), 0) == column
    pick_k = jnp.where(hit & (inner < 64), 1.0, 0.0).astype(jnp.bfloat16)
    pick_v = jnp.where(hit & (inner >= 64) & (inner < 96), 1.0, 0.0).astype(jnp.bfloat16)
    pick_q = jnp.where(hit & (inner >= 32) & (inner < 64), 1.0, 0.0).astype(jnp.bfloat16)
    wrow[0] = (dot(full[1], pick_k) + dot(full[2], pick_v)).astype(jnp.bfloat16)
    wrow[1] = dot(full[0], pick_q).astype(jnp.bfloat16)
    row_kv = dot(bias[1:2, :], pick_v)
    row_q = dot(bias[0:1, :], pick_q)
    pick_t = jnp.where(
        iota((span, width), 1) == span * z + iota((span, width), 0), 1.0, 0.0
    ).astype(jnp.bfloat16)
    for i in range(3):
        wtr[i] = lax.dot_general(
            pick_t, full[i], (((1,), (1,)), ((), ())), preferred_element_type=jnp.float32
        ).astype(jnp.bfloat16)
    column_bias = lax.dot_general(
        pick_t, bias, (((1,), (1,)), ((), ())), preferred_element_type=jnp.float32
    )
    col_q, col_v = column_bias[:, 0:1], column_bias[:, 1:2]

    ids = seg[...]
    starts[0] = jnp.int32(0)
    for d in range(1, docs):
        starts[d] = jnp.sum(jnp.where(ids < d, 1.0, 0.0)).astype(jnp.int32)
    starts[docs] = jnp.int32(length)

    scale = (HEAD ** -0.5) * LOG2E
    one_lane = lax.rem(iota((1, heads * LANES), 1), LANES)
    ones_row = jnp.where((one_lane >= 104) & (one_lane < 107), 1.0, 0.0)

    def project(b, carry):
        r0 = pl.multiple_of(b * rows, rows)
        xb = x[pl.ds(r0, rows), :]
        idrow = seg[pl.ds(b, 1), :]
        same = jnp.where(iota((8, rows), 0) == idrow, 1.0, 0.0)
        hot = jnp.concatenate(
            [jnp.zeros((96, rows), jnp.float32), same, jnp.zeros((24, rows), jnp.float32)], axis=0
        ).T
        flat = dot(xb, wrow[0]) + (row_kv + ones_row)
        for h in range(heads):
            kv[h, pl.ds(r0, rows), :] = (flat[:, h * LANES : (h + 1) * LANES] + hot).astype(
                jnp.bfloat16
            )
        flat = (dot(xb, wrow[1]) + row_q).astype(jnp.bfloat16)
        for h in range(heads):
            qr[h, pl.ds(r0, rows), :] = flat[:, h * LANES : (h + 1) * LANES]

        def turned(i):
            return lax.dot_general(
                wtr[i], xb, (((1,), (1,)), ((), ())), preferred_element_type=jnp.float32
            )

        q_t = (turned(0) + col_q).astype(jnp.bfloat16).astype(jnp.float32) * scale
        k_t = turned(1).astype(jnp.bfloat16)
        k_wide = k_t.astype(jnp.float32)
        norms = [
            jnp.maximum(
                carry[i],
                functools.reduce(
                    jnp.maximum,
                    [
                        jnp.sum(v[h * HEAD : (h + 1) * HEAD] ** 2, axis=0, keepdims=True)
                        for h in range(heads)
                    ],
                ),
            )
            for i, v in enumerate((q_t, k_wide))
        ]
        q_hi = q_t.astype(jnp.bfloat16)
        q_lo = (q_t - q_hi.astype(jnp.float32)).astype(jnp.bfloat16)
        v_t = (turned(2) + col_v).astype(jnp.bfloat16)
        far = jnp.concatenate([(same - 1.0) * AWAY, jnp.zeros((8, rows), jnp.float32)], axis=0)
        far = far.astype(jnp.bfloat16)
        one = jnp.where(iota((16, rows), 0) == 0, 1.0, 0.0).astype(jnp.bfloat16)
        cols = pl.ds(r0, rows)
        for h in range(heads):
            part = slice(h * HEAD, (h + 1) * HEAD)
            qt[h, 0:32, cols] = q_hi[part]
            qt[h, 32:64, cols] = q_lo[part]
            qt[h, 64:96, cols] = jnp.zeros((32, rows), jnp.bfloat16)
            qt[h, 96:112, cols] = far
            qt[h, 112:128, cols] = jnp.zeros((16, rows), jnp.bfloat16)
            kt[h, :, cols] = k_t[part]
            vt[h, 0:32, cols] = v_t[part]
            vt[h, 32:48, cols] = one
        return tuple(norms)

    zero = jnp.zeros((1, rows), jnp.float32)
    q_norm, k_norm = lax.fori_loop(0, blocks, project, (zero, zero))
    bounded = jnp.max(q_norm) * jnp.max(k_norm) < LIMIT * LIMIT

    per = rows // QB

    def query_block(b, carry):
        q0 = pl.multiple_of(b * QB, QB)
        first, steps = span_of(starts, q0, docs)
        spans[0, b] = first
        spans[1, b] = steps
        acc[...] = jnp.zeros_like(acc)

        def key_block(i, tops):
            k0 = pl.multiple_of((first + i * (KB // LANES)) * LANES, LANES)
            s = [dot(kv[h, pl.ds(k0, KB), :], qt[h, :, pl.ds(q0, QB)]) for h in range(heads)]
            new = [jnp.maximum(tops[h], jnp.max(s[h], axis=0, keepdims=True)) for h in range(heads)]
            p = [jnp.exp2(s[h] - new[h]).astype(jnp.bfloat16) for h in range(heads)]
            for h in range(heads):
                acc[h] = acc[h] * jnp.exp2(tops[h] - new[h]) + dot(vt[h, :, pl.ds(k0, KB)], p[h])
            return tuple(new)

        def plain_block(keys):
            s = [dot(kv[h, keys, :], qt[h, :, pl.ds(q0, QB)]) for h in range(heads)]
            p = [jnp.exp2(v).astype(jnp.bfloat16) for v in s]
            for h in range(heads):
                acc[h] += dot(vt[h, :, keys], p[h])

        @pl.when(bounded)
        def _():
            in_pairs(first, steps, plain_block)
            tall[...] = jnp.zeros_like(tall)

        @pl.when(jnp.logical_not(bounded))
        def _():
            lowest = jnp.full((1, QB), -3e38, jnp.float32)
            tops = lax.fori_loop(0, steps, key_block, (lowest,) * heads)
            for h in range(heads):
                tall[h] = tops[h]

        g = lax.div(b, per)
        off = pl.multiple_of(lax.rem(b, per) * QB, QB)
        same = jnp.where(iota((8, QB), 0) == seg[pl.ds(g, 1), pl.ds(off, QB)], 1.0, 0.0)
        for h in range(heads):
            total = acc[h, 32:33, :]
            out = acc[h, 0:32, :] / total
            ctx[g, h * HEAD : (h + 1) * HEAD, pl.ds(off, QB)] = out.astype(jnp.bfloat16)
            ctx32[g, h * HEAD : (h + 1) * HEAD, pl.ds(off, QB)] = out
            parts = halves(-(tall[h] + jnp.log2(total)))
            tail = jnp.concatenate(
                [(same - 1.0) * AWAY, *parts, jnp.zeros((5, QB), jnp.float32)], axis=0
            )
            qt[h, 96:112, pl.ds(q0, QB)] = tail.astype(jnp.bfloat16)
        return carry

    lax.fori_loop(0, length // QB, query_block, 0)


def attend(place, x, w, small):
    blocks, rows, width = x.shape
    length = blocks * rows
    heads = 3
    vm = pl.BlockSpec(memory_space=pltpu.VMEM)
    sm = pl.BlockSpec(memory_space=pltpu.SMEM)
    bf, f4 = jnp.bfloat16, jnp.float32
    return pl.pallas_call(
        attend_kernel,
        name="attend",
        grid=(1,),
        out_shape=(
            jax.ShapeDtypeStruct((heads, length, LANES), bf),
            jax.ShapeDtypeStruct((heads, LANES, length), bf),
            jax.ShapeDtypeStruct((heads, HEAD, length), bf),
            jax.ShapeDtypeStruct((heads, length, LANES), bf),
            jax.ShapeDtypeStruct((blocks, heads * HEAD, rows), bf),
            jax.ShapeDtypeStruct((blocks, heads * HEAD, rows), f4),
            jax.ShapeDtypeStruct((2, length // QB), jnp.int32),
        ),
        in_specs=[sm, vm, quarter_spec(w, 0), whole_spec(small)],
        out_specs=[vm] * 6 + [sm],
        scratch_shapes=[
            pltpu.VMEM((2, width, heads * LANES), bf),
            pltpu.VMEM((3, heads * HEAD, width), bf),
            pltpu.VMEM((heads, 48, length), bf),
            pltpu.VMEM((heads, 48, QB), f4),
            pltpu.VMEM((heads, 1, QB), f4),
            pltpu.VMEM((8, rows), jnp.int32),
            pltpu.SMEM((16,), jnp.int32),
        ],
        compiler_params=pltpu.CompilerParams(vmem_limit_bytes=BIG),
    )(place, x.reshape(length, width), w, small)


PIECE = 128


def middle_kernel(
    ctx, tok, og, w, small,
    layer_out, grad_one_out, gctx_out, pr,
    wo, wi, wu, gwo, gwi, gwu, sums, inner_sum, ctx_in, gctx, pg, pg_in,
    lsem, send, recv, gsend, grecv, glocal, psend, precv,
):
    seqs, rows, width = tok.shape
    slabs = wi.shape[0]
    pieces = rows // PIECE
    r, g, z, c = where_am_i()
    greet(r, g, 1, 8)

    def fetch(q):
        cols = pl.ds(pl.multiple_of(q * PIECE, PIECE), PIECE)
        for d in range(1, 8):
            to = lax.rem(g + d, 8)
            remote(
                ctx.at[to, :, cols], ctx_in.at[c, z, :, cols], send.at[q, d - 1], recv.at[q, g], r, to
            ).start()

    own = pltpu.make_async_copy(ctx.at[g], ctx_in.at[c, z], lsem)
    own.start()
    fetch(0)
    fetch(1)
    for i in range(8):
        cc, zz = i % 2, i // 2
        wo[48 * i : 48 * i + 48, :] = w[1, cc, zz, 0:48, :]
        wi[0, 48 * i : 48 * i + 48, :] = w[1, cc, zz, 48:96, :]
        wi[1, 48 * i : 48 * i + 48, :] = w[1, cc, zz, 96:144, :]
        wi[2, 48 * i : 48 * i + 48, :] = w[2, cc, zz, 0:48, :]
        wi[3, 48 * i : 48 * i + 48, :] = w[2, cc, zz, 48:96, :]
        wu[zz, 192 * cc : 192 * cc + 48, :] = w[2, cc, zz, 96:144, :]
        wu[zz, 192 * cc + 48 : 192 * cc + 192, :] = w[3, cc, zz, :, :]
    for ref in (gwo, gwi, gwu, sums, inner_sum):
        ref[...] = jnp.zeros_like(ref)
    fetch(2)
    fetch(3)

    vec = vectors_of(small)
    inner_bias = jnp.concatenate(
        [small[i, 8:16, 0:192].astype(jnp.float32)[0:1] for i in range(8)], axis=1
    )
    out_bias, outer_bias = vec[2:3, :], vec[3:4, :]
    gain_one, shift_one = vec[4:5, :], vec[5:6, :]
    gain_two, shift_two = vec[6:7, :], vec[7:8, :]

    def normal(value):
        centre = value - jnp.mean(value, axis=-1, keepdims=True)
        rate = lax.rsqrt(jnp.mean(centre * centre, axis=-1, keepdims=True) + norm_epsilon)
        return centre * rate, rate

    def normal_back(grad, gain, n, rate):
        u = grad * gain
        return rate * (
            u - jnp.mean(u, axis=-1, keepdims=True) - n * jnp.mean(u * n, axis=-1, keepdims=True)
        )

    def total(value):
        return jnp.sum(value, axis=0, keepdims=True)

    def dot_turn(left, right):
        return lax.dot_general(
            left, right, (((1,), (1,)), ((), ())), preferred_element_type=jnp.float32
        )

    def arrived(q, cols):
        for d in range(1, 8):
            b = lax.rem(g + d, 8)
            remote(
                ctx.at[g, :, cols], ctx_in.at[lax.rem(b, 2), lax.div(b, 2), :, cols],
                send.at[q, 0], recv.at[q, b], r, b,
            ).wait_recv()

    def return_piece(q, cols, d):
        to = lax.rem(g + d, 8)
        return remote(
            gctx.at[lax.rem(to, 2), lax.div(to, 2), :, cols], gctx_out.at[g, :, cols],
            gsend.at[q, d - 1], grecv.at[q, g], r, to,
        )

    def keep_piece(q, cols):
        return pltpu.make_async_copy(gctx.at[c, z, :, cols], gctx_out.at[g, :, cols], glocal.at[q])

    own.wait()

    def one(q, carry):
        r0 = pl.multiple_of(q * PIECE, PIECE)
        here = pl.ds(r0, PIECE)
        arrived(q, here)

        def both(ref):
            return jnp.concatenate([ref[s, here, :] for s in range(seqs)], axis=0)

        def split(ref, value):
            for s in range(seqs):
                ref[s, here, :] = value[s * PIECE : (s + 1) * PIECE].astype(ref.dtype)

        ctx_t = jnp.concatenate(
            [jnp.concatenate([ctx_in[s, zz, :, here] for zz in range(4)], axis=0) for s in range(seqs)],
            axis=1,
        )
        context = ctx_t.astype(jnp.float32).T.astype(jnp.bfloat16)
        x = both(tok).astype(jnp.float32)
        n_one, rate_one = normal(x + (dot(context, wo[...]) + out_bias))
        hidden = n_one * gain_one + shift_one
        low = hidden.astype(jnp.bfloat16)
        low_t = hidden.T.astype(jnp.bfloat16)
        feed = jnp.zeros(hidden.shape, jnp.float32)
        slopes, actives = [], []
        for j in range(slabs):
            inner = dot(low, wi[j]) + inner_bias[:, j * width : (j + 1) * width]
            cdf = 0.5 + 0.5 * lax.erf(inner * (0.5 ** 0.5))
            pdf = jnp.exp(inner * inner * -0.5) * 0.3989422804014327
            slopes.append(cdf + inner * pdf)
            active = inner * cdf
            actives.append(active)
            feed = feed + dot(active.astype(jnp.bfloat16), wu[j])
        n_two, rate_two = normal(hidden + (feed + outer_bias))
        split(layer_out, n_two * gain_two + shift_two)
        grad = both(og).astype(jnp.float32)
        grad_two = normal_back(grad, gain_two, n_two, rate_two)
        grad_feed = grad_two.astype(jnp.bfloat16)
        grad_hidden = grad_two
        for j in range(slabs):
            grad_inner = (dot_turn(grad_feed, wu[j]) * slopes[j]).astype(jnp.bfloat16)
            inner_sum[:, j * width : (j + 1) * width] += total(grad_inner.astype(jnp.float32))
            grad_hidden = grad_hidden + dot_turn(grad_inner, wi[j])
            gwi[j] += dot(low_t, grad_inner)
            gwu[j] += dot(actives[j].T.astype(jnp.bfloat16), grad_feed)
        grad_one = normal_back(grad_hidden, gain_one, n_one, rate_one)
        split(grad_one_out, grad_one)
        grad_att = grad_one.astype(jnp.bfloat16)
        back = dot_turn(wo[...], grad_att).astype(jnp.bfloat16)
        for s in range(seqs):
            for zz in range(4):
                gctx[s, zz, :, here] = back[96 * zz : 96 * zz + 96, s * PIECE : (s + 1) * PIECE]
        for d in range(1, 8):
            return_piece(q, here, d).start()
        keep_piece(q, here).start()
        gwo[...] += dot(ctx_t, grad_att)
        sums[0:1, :] += total(grad_att.astype(jnp.float32))
        sums[1:2, :] += total(grad_feed.astype(jnp.float32))
        sums[2:3, :] += total(grad_hidden * n_one)
        sums[3:4, :] += total(grad_hidden)
        sums[4:5, :] += total(grad * n_two)
        sums[5:6, :] += total(grad)
        return carry

    lax.fori_loop(0, pieces, one, 0)
    rows_of_sums = jnp.concatenate(
        [sums[...]]
        + [inner_sum[:, j * width : (j + 1) * width] for j in range(slabs)]
        + [jnp.zeros((6, width), jnp.float32)],
        axis=0,
    ).astype(jnp.bfloat16)
    for i in range(8):
        cc, zz = i % 2, i // 2
        mine = slice(48 * i, 48 * i + 48)
        pg[cc, 0, zz, 0:48, :] = gwo[mine, :].astype(jnp.bfloat16)
        pg[cc, 0, zz, 48:96, :] = gwi[0, mine, :].astype(jnp.bfloat16)
        pg[cc, 1, zz, 0:48, :] = gwi[1, mine, :].astype(jnp.bfloat16)
        pg[cc, 1, zz, 48:96, :] = gwi[2, mine, :].astype(jnp.bfloat16)
        pg[cc, 2, zz, 0:48, :] = gwi[3, mine, :].astype(jnp.bfloat16)
        base = 192 * cc
        pg[cc, 0, zz, 96:112, :] = gwu[zz, base : base + 16, :].astype(jnp.bfloat16)
        pg[cc, 1, zz, 96:112, :] = gwu[zz, base + 16 : base + 32, :].astype(jnp.bfloat16)
        pg[cc, 2, zz, 48:112, :] = gwu[zz, base + 32 : base + 96, :].astype(jnp.bfloat16)
        pg[cc, 3, zz, 0:96, :] = gwu[zz, base + 96 : base + 192, :].astype(jnp.bfloat16)
        pg[cc, 3, zz, 96:112, :] = rows_of_sums
    pair = remote(pg.at[1 - c], pg_in, psend, precv, r, 2 * z + 1 - c)
    pair.start()

    def settle(q, carry):
        cols = pl.ds(pl.multiple_of(q * PIECE, PIECE), PIECE)
        for d in range(1, 8):
            b = lax.rem(g + d, 8)
            remote(
                gctx.at[c, z, :, cols], gctx_out.at[b, :, cols], gsend.at[q, 0], grecv.at[q, b], r, b
            ).wait_recv()
            return_piece(q, cols, d).wait_send()
            to = lax.rem(g + d, 8)
            remote(
                ctx.at[to, :, cols], ctx_in.at[c, z, :, cols], send.at[q, d - 1], recv.at[q, g], r, to
            ).wait_send()
        keep_piece(q, cols).wait()
        return carry

    pair.wait_recv()
    for i in range(4):
        pr[i] = (pg[c, i].astype(jnp.float32) + pg_in[i].astype(jnp.float32)).astype(jnp.bfloat16)
    lax.fori_loop(0, pieces, settle, 0)
    pair.wait_send()


def middle(ctx, tok, og, w, small):
    seqs, rows, width = tok.shape
    vm = pl.BlockSpec(memory_space=pltpu.VMEM)
    anywhere = pl.BlockSpec(memory_space=pl.ANY)
    dma = pltpu.SemaphoreType.DMA
    bf, f4 = jnp.bfloat16, jnp.float32
    pieces = rows // PIECE
    return pl.pallas_call(
        middle_kernel,
        name="middle",
        out_shape=(
            jax.ShapeDtypeStruct((seqs, rows, width), bf),
            jax.ShapeDtypeStruct((seqs, rows, width), f4),
            jax.ShapeDtypeStruct(ctx.shape, bf),
            jax.ShapeDtypeStruct((4, 4, 112, width), bf),
        ),
        in_specs=[anywhere] + [vm] * 4,
        out_specs=[vm, vm, anywhere, vm],
        scratch_shapes=[
            pltpu.VMEM((width, width), bf),
            pltpu.VMEM((4, width, width), bf),
            pltpu.VMEM((4, width, width), bf),
            pltpu.VMEM((width, width), f4),
            pltpu.VMEM((4, width, width), f4),
            pltpu.VMEM((4, width, width), f4),
            pltpu.VMEM((6, width), f4),
            pltpu.VMEM((1, 4 * width), f4),
            pltpu.VMEM((2, 4) + ctx.shape[1:], bf),
            pltpu.VMEM((2, 4) + ctx.shape[1:], bf),
            pltpu.VMEM((2, 4, 4, 112, width), bf),
            pltpu.VMEM((4, 4, 112, width), bf),
            dma, dma((pieces, 7)), dma((pieces, 8)), dma((pieces, 7)), dma((pieces, 8)), dma((pieces,)), dma, dma,
        ],
        compiler_params=pltpu.CompilerParams(
            collective_id=2, has_side_effects=True, vmem_limit_bytes=BIG
        ),
    )(ctx, tok, og, w, small)


def attend_back_kernel(
    last, place, spans, x, kv, qt, kt, qr, gctx, ctx32, *refs,
):
    heads = kv.shape[0]
    span = heads * HEAD
    if last:
        grads_in, out, gq, dt, do, acc, dq = refs
    else:
        out, grads_out, dt, do, acc, dq = refs
    length, width = x.shape
    blocks, _, rows = gctx.shape
    z = place[0]
    c = place[1]
    scale = HEAD ** -0.5

    def prepare(g, carry):
        r0 = pl.multiple_of(g * rows, rows)
        cols = pl.ds(r0, rows)
        for h in range(heads):
            part = slice(h * HEAD, (h + 1) * HEAD)
            grad = gctx[g, part, :]
            wide = grad.astype(jnp.float32)
            delta = -jnp.sum(wide * ctx32[g, part, :], axis=0, keepdims=True)
            dt[h, 0:64, cols] = jnp.zeros((64, rows), jnp.bfloat16)
            dt[h, 64:96, cols] = grad
            tail = jnp.concatenate(
                [jnp.zeros((8, rows), jnp.float32), *halves(delta), jnp.zeros((21, rows), jnp.float32)],
                axis=0,
            )
            dt[h, 96:128, cols] = tail.astype(jnp.bfloat16)
            turned = jnp.concatenate(
                [wide, jnp.zeros((96, rows), jnp.float32)], axis=0
            ).T.astype(jnp.bfloat16)
            for j in range(rows // QB):
                r1 = pl.multiple_of(2 * r0 + 2 * j * QB, QB)
                do[h, pl.ds(r1, QB), :] = turned[j * QB : (j + 1) * QB]
                do[h, pl.ds(r1 + QB, QB), :] = qr[h, pl.ds(r0 + j * QB, QB), :]
        return carry

    lax.fori_loop(0, blocks, prepare, 0)
    acc[...] = jnp.zeros_like(acc)
    per = rows // QB

    def query_block(b, carry):
        q0 = pl.multiple_of(b * QB, QB)
        dq[...] = jnp.zeros_like(dq)

        def key_blocks(starts, size):
            jobs = [(h, pl.ds(start, size)) for start in starts for h in range(heads)]
            s = [dot(kv[h, k, :], qt[h, :, pl.ds(q0, QB)]) for h, k in jobs]
            d = [dot(kv[h, k, :], dt[h, :, pl.ds(q0, QB)]) for h, k in jobs]
            p = [jnp.exp2(v) for v in s]
            both = [
                jnp.concatenate([u.astype(jnp.bfloat16), (u * v).astype(jnp.bfloat16)], axis=1)
                for u, v in zip(p, d)
            ]
            for (h, k), v in zip(jobs, both):
                acc[h, k, :] += dot(v, do[h, pl.ds(2 * q0, 2 * QB), :])
            for (h, k), v in zip(jobs, both):
                dq[h] += dot(kt[h, :, k], v[:, QB:])

        in_groups(spans[0, b], spans[1, b], key_blocks, 4 if heads == 1 else 2)
        g = lax.div(b, per)
        off = pl.multiple_of(lax.rem(b, per) * QB, QB)
        for h in range(heads):
            out[g, h * HEAD : (h + 1) * HEAD, pl.ds(off, QB)] = (dq[h] * scale).astype(jnp.bfloat16)
        return carry

    lax.fori_loop(0, length // QB, query_block, 0)

    def finish_block(g, totals):
        r0 = pl.multiple_of(g * rows, rows)
        cols = pl.ds(r0, rows)
        for h in range(heads):
            both = acc[h, cols, :].T
            row = h * HEAD
            out[g, 2 * span + row : 2 * span + row + HEAD, :] = both[0:32].astype(jnp.bfloat16)
            out[g, span + row : span + row + HEAD, :] = (both[32:64] * scale).astype(jnp.bfloat16)
        piece = out[g]
        grad = dot(piece, x[cols, :])
        summed = jnp.sum(piece.astype(jnp.float32), axis=1, keepdims=True)
        return totals[0] + grad, totals[1] + summed

    grads, summed = lax.fori_loop(
        0,
        blocks,
        finish_block,
        (jnp.zeros((3 * span, width), jnp.float32), jnp.zeros((3 * span, 1), jnp.float32)),
    )
    if not last:
        grads_out[:, 0:width] = grads
        grads_out[:, width:] = jnp.broadcast_to(summed, (3 * span, LANES))
        return
    gq[...] = jnp.zeros_like(gq)
    before = grads_in.shape[0] // 3

    def joined(i, old, new):
        return [old[i * before : (i + 1) * before], new[i * span : (i + 1) * span]]

    old = grads_in[:, 0:width]
    whole = jnp.concatenate([v for i in range(3) for v in joined(i, old, grads)], axis=0).T
    total = 3 * (before + span)
    for g in range(8):
        gq[g % 2, g // 2, :, 0:total] = whole[48 * g : 48 * g + 48, :].astype(jnp.bfloat16)
    old = grads_in[:, width : width + 1]
    of_q = jnp.concatenate(joined(0, old, summed), axis=0)
    of_v = jnp.concatenate(joined(2, old, summed), axis=0)
    for cc in range(2):
        mine = jnp.concatenate(
            [
                of_q[48 * cc : 48 * cc + 48, :],
                of_v[48 * cc : 48 * cc + 48, :],
                jnp.zeros((48, 94), jnp.float32),
            ],
            axis=1,
        )
        gq[cc, z, :, total:] = mine.astype(jnp.bfloat16)


def attend_back(heads, index, place, spans, x, kv, qt, kt, qr, gctx, ctx32, grads=None):
    blocks, rows, width = x.shape
    length = blocks * rows
    last = grads is not None
    rest = (grads,) if last else ()
    sm = pl.BlockSpec(memory_space=pltpu.SMEM)
    bf, f4 = jnp.bfloat16, jnp.float32
    once = pl.Buffered(1)
    span = heads * HEAD

    def some_heads(array):
        return pl.BlockSpec((heads,) + array.shape[1:], lambda i: (index, 0, 0), pipeline_mode=once)

    def head_rows(array):
        return pl.BlockSpec((blocks, span, rows), lambda i: (0, index, 0), pipeline_mode=once)

    flat = x.reshape(length, width)
    shapes = (
        jax.ShapeDtypeStruct((blocks, 3 * span, rows), bf),
        jax.ShapeDtypeStruct((2, 4, 48, width), bf)
        if last
        else jax.ShapeDtypeStruct((3 * span, width + LANES), f4),
    )
    return pl.pallas_call(
        functools.partial(attend_back_kernel, last),
        name="attend_back",
        grid=(1,),
        out_shape=shapes,
        in_specs=[sm, sm, whole_spec(flat)]
        + [some_heads(v) for v in (kv, qt, kt, qr)]
        + [head_rows(v) for v in (gctx, ctx32)]
        + [whole_spec(v) for v in rest],
        out_specs=[whole_spec(v) for v in shapes],
        scratch_shapes=[
            pltpu.VMEM((heads, LANES, length), bf),
            pltpu.VMEM((heads, 2 * length, LANES), bf),
            pltpu.VMEM((heads, length, LANES), f4),
            pltpu.VMEM((heads, HEAD, QB), f4),
        ],
        compiler_params=pltpu.CompilerParams(vmem_limit_bytes=BIG),
        cost_estimate=pl.CostEstimate(
            flops=heads * 20 * 10 ** 9, bytes_accessed=heads * 8 * 10 ** 6, transcendentals=heads * 6 * 10 ** 6
        ),
    )(place, spans, flat, kv, qt, kt, qr, gctx, ctx32, *rest)


def reduce_kernel(
    src, gq, pr, dst, p_out, q_out,
    gq_in, gq_sum, qa_in, qa_sum, qb_in, pa_in, pa_sum, pb_in, p_own, gq_own, pr_own,
    lsem, send, recv, gsend, grecv, qasend, qarecv, qbsend, qbrecv, qcsend, qcrecv,
    pasend, parecv, pbsend, pbrecv, pcsend, pcrecv,
):
    r, g, z, c = where_am_i()
    greet(r, g, 4, 8)
    waits = []
    pair = remote(gq.at[1 - c], gq_in, gsend, grecv, r, 2 * z + 1 - c)
    pair.start()
    for d in range(1, 4):
        rr = lax.rem(r + d, 4)
        copy = remote(pr.at[rr], pa_in.at[r], pasend.at[d - 1], parecv.at[r], rr, g)
        copy.start()
        waits.append(copy)
    load_g = pltpu.make_async_copy(gq.at[c], gq_own, lsem.at[1])
    load_g.start()
    load_p = pltpu.make_async_copy(pr.at[r], pr_own, lsem.at[2])
    load_p.start()
    own = pltpu.make_async_copy(src.at[g], dst.at[g], lsem.at[0])
    own.start()

    def send_to(d):
        to = lax.rem(g + d, 8)
        copy = remote(src.at[to], dst.at[g], send.at[d - 1], recv.at[g], r, to)
        copy.start()
        waits.append(copy)

    def f32(value):
        return value.astype(jnp.float32)

    send_to(4)
    send_to(3)
    send_to(5)
    load_g.wait()
    pair.wait_recv()
    gq_sum[...] = (f32(gq_own[...]) + f32(gq_in[...])).astype(jnp.bfloat16)
    for d in range(1, 4):
        rr = lax.rem(r + d, 4)
        copy = remote(gq_sum.at[rr], qa_in.at[r], qasend.at[d - 1], qarecv.at[r], rr, g)
        copy.start()
        waits.append(copy)
    send_to(2)
    send_to(6)
    for d in range(1, 4):
        b = lax.rem(r + d, 4)
        remote(gq_sum.at[r], qa_in.at[b], qasend.at[0], qarecv.at[b], b, g).wait_recv()
    total = f32(gq_sum[r])
    for d in range(1, 4):
        total = total + f32(qa_in[lax.rem(r + d, 4)])
    qa_sum[...] = total.astype(jnp.bfloat16)

    @pl.when(z != r)
    def _():
        remote(qa_sum, qb_in.at[z], qbsend, qbrecv.at[z], r, 2 * r + c).start()

    load_p.wait()
    for d in range(1, 4):
        b = lax.rem(r + d, 4)
        remote(pr.at[r], pa_in.at[b], pasend.at[0], parecv.at[b], b, g).wait_recv()
    total = f32(pr_own[...])
    for d in range(1, 4):
        total = total + f32(pa_in[lax.rem(r + d, 4)])
    pa_sum[...] = total.astype(jnp.bfloat16)
    for d in range(1, 4):
        zz = lax.rem(z + d, 4)
        copy = remote(pa_sum.at[zz], pb_in.at[z], pbsend.at[d - 1], pbrecv.at[z], r, 2 * zz + c)
        copy.start()
        waits.append(copy)
    send_to(1)
    send_to(7)

    @pl.when(z == r)
    def _():
        for d in range(1, 4):
            b = lax.rem(z + d, 4)
            remote(qa_sum, qb_in.at[b], qbsend, qbrecv.at[b], r, g).wait_recv()
        qb_in[z] = qa_sum[...]
        pltpu.make_async_copy(qb_in, q_out, lsem.at[4]).start()
        for d in range(1, 4):
            remote(qb_in, q_out, qcsend.at[d - 1], qcrecv, lax.rem(r + d, 4), g).start()

    for d in range(1, 4):
        b = lax.rem(z + d, 4)
        remote(pa_sum.at[z], pb_in.at[b], pbsend.at[0], pbrecv.at[b], r, g).wait_recv()
    total = f32(pa_sum[z])
    for d in range(1, 4):
        total = total + f32(pb_in[lax.rem(z + d, 4)])
    p_own[...] = total.astype(jnp.bfloat16)
    keep_p = pltpu.make_async_copy(p_own, p_out.at[r], lsem.at[3])
    keep_p.start()
    for d in range(1, 4):
        rr = lax.rem(r + d, 4)
        copy = remote(p_own, p_out.at[r], pcsend.at[d - 1], pcrecv.at[r], rr, g)
        copy.start()
        waits.append(copy)

    @pl.when(z == r)
    def _():
        pltpu.make_async_copy(qb_in, q_out, lsem.at[4]).wait()
        for d in range(1, 4):
            remote(qb_in, q_out, qcsend.at[d - 1], qcrecv, lax.rem(r + d, 4), g).wait_send()

    @pl.when(z != r)
    def _():
        remote(qb_in, q_out, qcsend.at[0], qcrecv, r, g).wait_recv()
        remote(qa_sum, qb_in.at[z], qbsend, qbrecv.at[z], r, 2 * r + c).wait_send()

    for d in range(1, 4):
        b = lax.rem(r + d, 4)
        remote(p_own, p_out.at[b], pcsend.at[0], pcrecv.at[b], b, g).wait_recv()
    for d in range(1, 8):
        b = lax.rem(g + d, 8)
        remote(src.at[g], dst.at[b], send.at[0], recv.at[b], r, b).wait_recv()
    pair.wait_send()
    for copy in waits:
        copy.wait_send()
    keep_p.wait()
    own.wait()


def reduce_all(src, gq, pr):
    dma = pltpu.SemaphoreType.DMA
    anywhere = pl.BlockSpec(memory_space=pl.ANY)
    bf = jnp.bfloat16
    width = gq.shape[-1]
    return pl.pallas_call(
        reduce_kernel,
        name="reduce",
        out_shape=(
            jax.ShapeDtypeStruct(src.shape, bf),
            jax.ShapeDtypeStruct((4, 112, width), bf),
            jax.ShapeDtypeStruct((4, 48, width), bf),
        ),
        in_specs=[anywhere] * 3,
        out_specs=[anywhere] * 3,
        scratch_shapes=[
            pltpu.VMEM((4, 48, width), bf),
            pltpu.VMEM((4, 48, width), bf),
            pltpu.VMEM((4, 48, width), bf),
            pltpu.VMEM((48, width), bf),
            pltpu.VMEM((4, 48, width), bf),
            pltpu.VMEM((4, 4, 112, width), bf),
            pltpu.VMEM((4, 112, width), bf),
            pltpu.VMEM((4, 112, width), bf),
            pltpu.VMEM((112, width), bf),
            pltpu.VMEM((4, 48, width), bf),
            pltpu.VMEM((4, 112, width), bf),
            dma((5,)), dma((7,)), dma((8,)), dma, dma, dma((3,)), dma((4,)), dma, dma((4,)),
            dma((3,)), dma, dma((3,)), dma((4,)), dma((3,)), dma((4,)), dma((3,)), dma((4,)),
        ],
        compiler_params=pltpu.CompilerParams(
            collective_id=4, has_side_effects=True, vmem_limit_bytes=BIG // 2
        ),
    )(src, gq, pr)


def finish_kernel(
    place, in_0, in_1, grad_one, w, p_in, q_in,
    out, g_q, g_k, g_v, g_o, g_in, g_up, rows_out, inner_out, wq,
):
    seqs, rows, width = grad_one.shape
    span = 96
    z = place[0]
    c = place[1]
    for i in range(3):
        for g in range(8):
            wq[i, 48 * g : 48 * g + 48, :] = w[0, g % 2, g // 2, 48 * i : 48 * i + 48, :]
    for s in range(seqs):
        total = grad_one[s]
        for i in range(3):
            turned = jnp.concatenate(
                [
                    ref[2 * zz + s, i * count : (i + 1) * count, :]
                    for zz in range(4)
                    for ref, count in ((in_0, in_0.shape[1] // 3), (in_1, in_1.shape[1] // 3))
                ],
                axis=0,
            )
            back = turned.astype(jnp.float32).T.astype(jnp.bfloat16)
            total = total + lax.dot_general(
                back, wq[i], (((1,), (1,)), ((), ())), preferred_element_type=jnp.float32
            )
        out[s] = total.astype(jnp.bfloat16)
    wide = [q_in[zz].astype(jnp.float32) for zz in range(4)]
    for i, ref in enumerate((g_q, g_k, g_v)):
        ref[...] = jnp.concatenate([v[:, i * span : (i + 1) * span] for v in wide], axis=1)
    sums = p_in[3, 96:112, :]
    pick = jnp.where(
        iota((width, 48), 0) == 48 * (2 * z + c) + iota((width, 48), 1), 1.0, 0.0
    ).astype(jnp.bfloat16)
    rows_out[8:24, :] = dot(sums, pick)
    both = q_in[z].astype(jnp.float32)[:, 3 * span :].T
    rows_out[0:8, :] = both[0:8, :]
    pick = jnp.where(
        iota((width, 192), 0) == 192 * c + iota((width, 192), 1), 1.0, 0.0
    ).astype(jnp.bfloat16)
    inner = dot(sums, pick)
    inner_out[...] = jnp.sum(
        jnp.where(iota((16, 192), 0) == 6 + z, inner, 0.0), axis=0, keepdims=True
    )
    g_o[...] = p_in[0, 0:48, :].astype(jnp.float32)
    g_in[:, 0:384] = p_in[0, 48:96, :].astype(jnp.float32)
    g_in[:, 384:768] = p_in[1, 0:48, :].astype(jnp.float32)
    g_in[:, 768:1152] = p_in[1, 48:96, :].astype(jnp.float32)
    g_in[:, 1152:1536] = p_in[2, 0:48, :].astype(jnp.float32)
    g_up[0:16, :] = p_in[0, 96:112, :].astype(jnp.float32)
    g_up[16:32, :] = p_in[1, 96:112, :].astype(jnp.float32)
    g_up[32:96, :] = p_in[2, 48:112, :].astype(jnp.float32)
    g_up[96:192, :] = p_in[3, 0:96, :].astype(jnp.float32)


def finish(place, in_0, in_1, grad_one, w, p_in, q_in):
    seqs, rows, width = grad_one.shape
    vm = pl.BlockSpec(memory_space=pltpu.VMEM)
    sm = pl.BlockSpec(memory_space=pltpu.SMEM)
    bf, f4 = jnp.bfloat16, jnp.float32
    shapes = ((48, width),) * 4 + ((48, 4 * width), (192, width), (24, 48), (1, 192))
    return pl.pallas_call(
        finish_kernel,
        name="finish",
        grid=(1,),
        out_shape=(jax.ShapeDtypeStruct((seqs, rows, width), bf),)
        + tuple(jax.ShapeDtypeStruct(shape, f4) for shape in shapes),
        in_specs=[
            sm, whole_spec(in_0), whole_spec(in_1), whole_spec(grad_one), quarter_spec(w, 0), whole_spec(p_in), whole_spec(q_in)
        ],
        out_specs=[whole_spec(grad_one)]
        + [pl.BlockSpec(shape, functools.partial(zeros_for, len(shape))) for shape in shapes],
        scratch_shapes=[pltpu.VMEM((3, width, width), bf)],
        compiler_params=pltpu.CompilerParams(vmem_limit_bytes=BIG),
    )(place, in_0, in_1, grad_one, w, p_in, q_in)


def line_of_chips(
    tokens, segment_ids, out_grad, query_weight, key_weight, value_weight, output_weight,
    inner_weight, outer_weight, query_bias, value_bias, output_bias, inner_bias, outer_bias,
    first_gain, first_shift, second_gain, second_shift,
):
    bf = jnp.bfloat16
    width = tokens.shape[2]
    g = lax.axis_index("grp")
    z, c = lax.div(g, 2), lax.rem(g, 2)
    place = jnp.stack([z, c]).astype(jnp.int32)
    weights = (query_weight, key_weight, value_weight, output_weight, inner_weight, outer_weight)
    vectors = (
        query_bias, value_bias, output_bias, outer_bias, first_gain, first_shift, second_gain, second_shift,
        inner_bias, segment_ids[0].astype(bf), segment_ids[1].astype(bf),
    )
    row = lax.broadcasted_iota(jnp.int32, (16, 512), 0)
    small = jnp.zeros((16, 512), bf)
    for i, vector in enumerate(vectors):
        small = jnp.where(row == i, jnp.pad(vector, (0, 512 - vector.shape[0]))[None], small)
    x, w, small = gather(tokens, weights, small)
    kv, qt, kt, qr, ctx, ctx32, spans = attend(place, x, w, small)
    layer_out, grad_one, gctx_in, pr = middle(ctx, tokens, out_grad, w, small)
    back = functools.partial(
        attend_back, place=place, spans=spans, x=x, kv=kv, qt=qt, kt=kt, qr=qr, gctx=gctx_in, ctx32=ctx32
    )
    parts_0, grads_0 = back(2, 0)
    in_0 = lax.all_to_all(parts_0, "grp", 0, 0, tiled=True)
    parts_1, gq = back(1, 2, grads=grads_0)
    in_1, p_in, q_in = reduce_all(parts_1, gq, pr)
    input_grad, g_q, g_k, g_v, g_o, g_in, g_up, rows, inner_row = finish(
        place, in_0, in_1, grad_one, w, p_in, q_in
    )
    return (
        layer_out, input_grad, g_q, g_k, g_v, g_o, g_in, g_up,
        rows[0], rows[1], rows[8], inner_row[0], rows[9], rows[10], rows[11], rows[12], rows[13],
    )


def solution(mesh):
    in_specs = (
        P("rep", "grp", None),
        P("rep", "grp"),
        P("rep", "grp", None),
        P("grp", None),
        P("grp", None),
        P("grp", None),
        P("grp", None),
        P("grp", None),
        P("grp", None),
        P("grp"),
        P("grp"),
        P("grp"),
        P("grp"),
        P("grp"),
        P("grp"),
        P("grp"),
        P("grp"),
        P("grp"),
    )
    out_specs = (
        P("rep", "grp", None),
        P("rep", "grp", None),
        P("grp", None),
        P("grp", None),
        P("grp", None),
        P("grp", None),
        P("grp", None),
        P("grp", None),
        P("grp"),
        P("grp"),
        P("grp"),
        P("grp"),
        P("grp"),
        P("grp"),
        P("grp"),
        P("grp"),
        P("grp"),
    )
    whole_line = mesh.shape["grp"] == 8 and mesh.shape["rep"] == 4
    return jax.shard_map(
        line_of_chips if whole_line else on_device, mesh=mesh, in_specs=in_specs, out_specs=out_specs, check_vma=False
    )
```

```python
import functools
from functools import reduce

import jax
import jax.numpy as jnp
from jax import lax
from jax.experimental import pallas as pl
from jax.experimental.pallas import tpu as pltpu
from jax.sharding import PartitionSpec as P

H = 12
MICRO = 2
SEQ_MB = 1


norm_epsilon = 1e-05
masked_score = -1000000000.0


def layer_norm(inputs, norm_gain, norm_shift):
    center = inputs - jnp.mean(inputs, axis=-1, keepdims=True)
    spread = jnp.mean(center * center, axis=-1, keepdims=True)
    return center * lax.rsqrt(spread + norm_epsilon) * norm_gain + norm_shift


def exact_gelu(inputs):
    return jax.nn.gelu(inputs, approximate=False)


def times_transpose(left, right):
    return lax.dot_general(
        left, right, (((1,), (1,)), ((), ())), preferred_element_type=jnp.float32
    )


def transpose_times(left, right):
    return lax.dot_general(
        left, right, (((0,), (0,)), ((), ())), preferred_element_type=jnp.float32
    )


def column_total(inputs):
    return jnp.sum(inputs.astype(jnp.float32), axis=0)


def masked_scores(query_group, key_group, same_doc, score_scale):
    scores = (
        jnp.einsum("bqhd,bkhd->bhqk", query_group, key_group, preferred_element_type=jnp.float32)
        * score_scale
    )
    return jnp.where(same_doc[:, None], scores, masked_score)


def group_forward(query_group, key_group, value_group, same_doc, score_scale):
    scores = masked_scores(query_group, key_group, same_doc, score_scale)
    highest = jnp.max(scores, axis=-1, keepdims=True)
    log_total = highest + jnp.log(jnp.sum(jnp.exp(scores - highest), axis=-1, keepdims=True))
    weights_low = jnp.exp(scores - log_total).astype(jnp.bfloat16)
    context = jnp.einsum(
        "bhqk,bkhd->bqhd", weights_low, value_group, preferred_element_type=jnp.float32
    )
    return (context.astype(jnp.bfloat16), log_total)


def group_backward(
    query_group, key_group, value_group, same_doc, log_total, grad_context, score_scale
):
    attn_weights = jnp.exp(masked_scores(query_group, key_group, same_doc, score_scale) - log_total)
    weights_low = attn_weights.astype(jnp.bfloat16)
    grad_weights = jnp.einsum(
        "bqhd,bkhd->bhqk", grad_context, value_group, preferred_element_type=jnp.float32
    )
    centre = jnp.sum(attn_weights * grad_weights, axis=-1, keepdims=True)
    grad_scores = (attn_weights * (grad_weights - centre)).astype(jnp.bfloat16)
    grad_query = jnp.einsum(
        "bhqk,bkhd->bqhd", grad_scores, key_group, preferred_element_type=jnp.float32
    )
    grad_query = (grad_query * score_scale).astype(jnp.bfloat16)
    grad_key = (
        jnp.einsum("bhqk,bqhd->bkhd", grad_scores, query_group, preferred_element_type=jnp.float32)
        * score_scale
    )
    grad_value = jnp.einsum(
        "bhqk,bqhd->bkhd", weights_low, grad_context, preferred_element_type=jnp.float32
    )
    return (grad_query, grad_key, grad_value)


def merge_groups(stacked, row_total, model_width):
    return jnp.moveaxis(stacked, 0, 2).reshape(row_total, model_width)


def gradient_terms(
    token_rows,
    context_rows,
    hidden_rows,
    active_rows,
    grad_queries,
    grad_keys,
    grad_values,
    grad_attention,
    grad_inner,
    grad_feed,
    norm_grads,
):
    return (
        transpose_times(token_rows, grad_queries),
        transpose_times(token_rows, grad_keys),
        transpose_times(token_rows, grad_values),
        transpose_times(context_rows, grad_attention),
        transpose_times(hidden_rows, grad_inner),
        transpose_times(active_rows, grad_feed),
        column_total(grad_queries),
        column_total(grad_values),
        column_total(grad_attention),
        column_total(grad_inner),
        column_total(grad_feed),
        norm_grads[0],
        norm_grads[1],
        norm_grads[2],
        norm_grads[3],
    )


def on_device(
    tokens,
    segment_ids,
    out_grad,
    query_weight,
    key_weight,
    value_weight,
    output_weight,
    inner_weight,
    outer_weight,
    query_bias,
    value_bias,
    output_bias,
    inner_bias,
    outer_bias,
    first_gain,
    first_shift,
    second_gain,
    second_shift,
):
    row_count = tokens.shape[1]
    model_width = tokens.shape[2]
    head_count = H
    head_size = model_width // head_count
    per_group = max(1, min(head_count, 128 // head_size))
    group_width = per_group * head_size
    group_count = head_count // per_group
    score_scale = head_size ** (-0.5)
    seq_count = SEQ_MB
    flat_rows = seq_count * row_count
    all_segments = lax.all_gather(segment_ids, "grp", axis=1, tiled=True)
    outputs = []
    input_grads = []
    shares_list = []
    for batch_index in range(MICRO):
        offset = batch_index * seq_count
        local_tokens = tokens[offset : offset + seq_count]
        flat_tokens = local_tokens.reshape(flat_rows, model_width)
        gathered = (
            lax.all_gather(query_weight, "grp", axis=0, tiled=True),
            lax.all_gather(key_weight, "grp", axis=0, tiled=True),
            lax.all_gather(value_weight, "grp", axis=0, tiled=True),
            lax.all_gather(output_weight, "grp", axis=0, tiled=True),
            lax.all_gather(inner_weight, "grp", axis=0, tiled=True),
            lax.all_gather(outer_weight, "grp", axis=0, tiled=True),
            lax.all_gather(query_bias, "grp", axis=0, tiled=True),
            lax.all_gather(value_bias, "grp", axis=0, tiled=True),
            lax.all_gather(output_bias, "grp", axis=0, tiled=True),
            lax.all_gather(inner_bias, "grp", axis=0, tiled=True),
            lax.all_gather(outer_bias, "grp", axis=0, tiled=True),
            lax.all_gather(first_gain, "grp", axis=0, tiled=True),
            lax.all_gather(first_shift, "grp", axis=0, tiled=True),
            lax.all_gather(second_gain, "grp", axis=0, tiled=True),
            lax.all_gather(second_shift, "grp", axis=0, tiled=True),
        )
        full_query, full_key, full_value, full_output, full_inner, full_outer = gathered[:6]
        (
            bias_query,
            bias_value,
            bias_output,
            bias_inner,
            bias_outer,
            gain_first,
            shift_first,
            gain_second,
            shift_second,
        ) = [vector.astype(jnp.float32) for vector in gathered[6:]]
        queries = (
            jnp.dot(flat_tokens, full_query, preferred_element_type=jnp.float32) + bias_query
        ).astype(jnp.bfloat16)
        key_rows = jnp.dot(flat_tokens, full_key, preferred_element_type=jnp.float32).astype(
            jnp.bfloat16
        )
        value_rows = (
            jnp.dot(flat_tokens, full_value, preferred_element_type=jnp.float32) + bias_value
        ).astype(jnp.bfloat16)
        key_split = key_rows.reshape(seq_count, row_count, model_width)
        value_split = value_rows.reshape(seq_count, row_count, model_width)
        key_all, value_all = (
            lax.all_gather(key_split, "grp", axis=1, tiled=True),
            lax.all_gather(value_split, "grp", axis=1, tiled=True),
        )
        length = key_all.shape[1]
        local_segments = segment_ids[offset : offset + seq_count]
        far_segments = all_segments[offset : offset + seq_count]
        same_doc = local_segments[:, :, None] == far_segments[:, None, :]
        query_split = queries.reshape(seq_count, row_count, model_width)

        def slice_group(array, group_index):
            piece = lax.dynamic_slice_in_dim(array, group_index * group_width, group_width, 2)
            return piece.reshape(array.shape[0], array.shape[1], per_group, head_size)

        def forward_group(group_index):
            context, log_total = group_forward(
                slice_group(query_split, group_index),
                slice_group(key_all, group_index),
                slice_group(value_all, group_index),
                same_doc,
                score_scale,
            )
            return (context.reshape(seq_count, row_count, group_width), log_total)

        context_groups, log_totals = lax.map(forward_group, jnp.arange(group_count))
        context_rows = merge_groups(context_groups, flat_rows, model_width)
        attention = (
            jnp.dot(context_rows, full_output, preferred_element_type=jnp.float32) + bias_output
        )
        residual_one = flat_tokens.astype(jnp.float32) + attention
        hidden_one, norm_one_pullback = jax.vjp(layer_norm, residual_one, gain_first, shift_first)
        hidden_low = hidden_one.astype(jnp.bfloat16)
        inner_pre = jnp.dot(hidden_low, full_inner, preferred_element_type=jnp.float32) + bias_inner
        activation, gelu_pullback = jax.vjp(exact_gelu, inner_pre)
        active_low = activation.astype(jnp.bfloat16)
        feed = jnp.dot(active_low, full_outer, preferred_element_type=jnp.float32) + bias_outer
        output_rows, norm_two_pullback = jax.vjp(
            layer_norm, hidden_one + feed, gain_second, shift_second
        )
        outputs.append(output_rows.astype(jnp.bfloat16).reshape(seq_count, row_count, model_width))
        cotangent = (
            out_grad[offset : offset + seq_count]
            .reshape(flat_rows, model_width)
            .astype(jnp.float32)
        )
        grad_two, grad_gain_two, grad_shift_two = norm_two_pullback(cotangent)
        grad_feed = grad_two.astype(jnp.bfloat16)
        grad_active = times_transpose(grad_feed, full_outer)
        grad_inner = gelu_pullback(grad_active)[0].astype(jnp.bfloat16)
        grad_hidden = grad_two + times_transpose(grad_inner, full_inner)
        grad_one, grad_gain_one, grad_shift_one = norm_one_pullback(grad_hidden)
        grad_attention = grad_one.astype(jnp.bfloat16)
        grad_context = times_transpose(grad_attention, full_output).astype(jnp.bfloat16)
        grad_context = grad_context.reshape(seq_count, row_count, model_width)

        def backward_group(pieces):
            group_index, log_total = pieces
            grad_query, grad_key, grad_value = group_backward(
                slice_group(query_split, group_index),
                slice_group(key_all, group_index),
                slice_group(value_all, group_index),
                same_doc,
                log_total,
                slice_group(grad_context, group_index),
                score_scale,
            )
            return (
                grad_query.reshape(seq_count, row_count, group_width),
                grad_key.reshape(seq_count, length, group_width),
                grad_value.reshape(seq_count, length, group_width),
            )

        query_groups, key_groups, value_groups = lax.map(
            backward_group, (jnp.arange(group_count), log_totals)
        )
        key_owned, value_owned = (
            lax.psum_scatter(key_groups, "grp", scatter_dimension=2, tiled=True),
            lax.psum_scatter(value_groups, "grp", scatter_dimension=2, tiled=True),
        )
        grad_keys = merge_groups(key_owned, flat_rows, model_width).astype(jnp.bfloat16)
        grad_values = merge_groups(value_owned, flat_rows, model_width).astype(jnp.bfloat16)
        grad_queries = merge_groups(query_groups, flat_rows, model_width)
        grad_tokens = (
            grad_one
            + times_transpose(grad_queries, full_query)
            + times_transpose(grad_keys, full_key)
            + times_transpose(grad_values, full_value)
        )
        input_grads.append(
            grad_tokens.astype(jnp.bfloat16).reshape(seq_count, row_count, model_width)
        )
        norm_grads = (grad_gain_one, grad_shift_one, grad_gain_two, grad_shift_two)
        terms = gradient_terms(
            flat_tokens,
            context_rows,
            hidden_low,
            active_low,
            grad_queries,
            grad_keys,
            grad_values,
            grad_attention,
            grad_inner,
            grad_feed,
            norm_grads,
        )
        shares = (
            lax.psum_scatter(terms[0], "grp", scatter_dimension=0, tiled=True),
            lax.psum_scatter(terms[1], "grp", scatter_dimension=0, tiled=True),
            lax.psum_scatter(terms[2], "grp", scatter_dimension=0, tiled=True),
            lax.psum_scatter(terms[3], "grp", scatter_dimension=0, tiled=True),
            lax.psum_scatter(terms[4], "grp", scatter_dimension=0, tiled=True),
            lax.psum_scatter(terms[5], "grp", scatter_dimension=0, tiled=True),
            lax.psum_scatter(terms[6], "grp", scatter_dimension=0, tiled=True),
            lax.psum_scatter(terms[7], "grp", scatter_dimension=0, tiled=True),
            lax.psum_scatter(terms[8], "grp", scatter_dimension=0, tiled=True),
            lax.psum_scatter(terms[9], "grp", scatter_dimension=0, tiled=True),
            lax.psum_scatter(terms[10], "grp", scatter_dimension=0, tiled=True),
            lax.psum_scatter(terms[11], "grp", scatter_dimension=0, tiled=True),
            lax.psum_scatter(terms[12], "grp", scatter_dimension=0, tiled=True),
            lax.psum_scatter(terms[13], "grp", scatter_dimension=0, tiled=True),
            lax.psum_scatter(terms[14], "grp", scatter_dimension=0, tiled=True),
        )
        shares_list.append(shares)
    owned = reduce(
        lambda left_part, right_part: jax.tree.map(jnp.add, left_part, right_part), shares_list
    )
    summed = (
        lax.psum(owned[0].astype(jnp.bfloat16), "rep").astype(jnp.float32),
        lax.psum(owned[1].astype(jnp.bfloat16), "rep").astype(jnp.float32),
        lax.psum(owned[2].astype(jnp.bfloat16), "rep").astype(jnp.float32),
        lax.psum(owned[3].astype(jnp.bfloat16), "rep").astype(jnp.float32),
        lax.psum(owned[4].astype(jnp.bfloat16), "rep").astype(jnp.float32),
        lax.psum(owned[5].astype(jnp.bfloat16), "rep").astype(jnp.float32),
        lax.psum(owned[6].astype(jnp.bfloat16), "rep").astype(jnp.float32),
        lax.psum(owned[7].astype(jnp.bfloat16), "rep").astype(jnp.float32),
        lax.psum(owned[8].astype(jnp.bfloat16), "rep").astype(jnp.float32),
        lax.psum(owned[9].astype(jnp.bfloat16), "rep").astype(jnp.float32),
        lax.psum(owned[10].astype(jnp.bfloat16), "rep").astype(jnp.float32),
        lax.psum(owned[11].astype(jnp.bfloat16), "rep").astype(jnp.float32),
        lax.psum(owned[12].astype(jnp.bfloat16), "rep").astype(jnp.float32),
        lax.psum(owned[13].astype(jnp.bfloat16), "rep").astype(jnp.float32),
        lax.psum(owned[14].astype(jnp.bfloat16), "rep").astype(jnp.float32),
    )
    return (
        jnp.concatenate(outputs, axis=0),
        jnp.concatenate(input_grads, axis=0),
        summed[0],
        summed[1],
        summed[2],
        summed[3],
        summed[4],
        summed[5],
        summed[6],
        summed[7],
        summed[8],
        summed[9],
        summed[10],
        summed[11],
        summed[12],
        summed[13],
        summed[14],
    )


HEAD = 32
LANES = 128
QB = 256
KB = 256
AWAY = 2.0 ** 100
LIMIT = 100.0
MESH = pl.DeviceIdType.MESH
BIG = 62 * 1024 * 1024
LOG2E = 1.4426950408889634


def halves(value):
    first = value.astype(jnp.bfloat16).astype(jnp.float32)
    rest = value - first
    second = rest.astype(jnp.bfloat16).astype(jnp.float32)
    third = (rest - second).astype(jnp.bfloat16).astype(jnp.float32)
    return first, second, third


def dot(left, right):
    return jnp.dot(left, right, preferred_element_type=jnp.float32)


def zeros_for(rank, *grid):
    return (0,) * rank


def whole_spec(array):
    return pl.BlockSpec(array.shape, functools.partial(zeros_for, array.ndim), pipeline_mode=pl.Buffered(1))


def quarter_spec(w, i):
    return pl.BlockSpec((1,) + w.shape[1:], lambda *grid: (i, 0, 0, 0, 0), pipeline_mode=pl.Buffered(1))


def iota(shape, dim):
    return lax.broadcasted_iota(jnp.int32, shape, dim)


def where_am_i():
    r = lax.axis_index("rep")
    g = lax.axis_index("grp")
    return r, g, lax.div(g, 2), lax.rem(g, 2)


def remote(src, dst, send, recv, r, g):
    return pltpu.make_async_remote_copy(
        src_ref=src, dst_ref=dst, send_sem=send, recv_sem=recv, device_id=(r, g), device_id_type=MESH
    )


def greet(r, g, reps, group):
    barrier = pltpu.get_barrier_semaphore()
    for d in range(1, group):
        pl.semaphore_signal(barrier, inc=1, device_id=(r, lax.rem(g + d, group)), device_id_type=MESH)
    for d in range(1, reps):
        pl.semaphore_signal(barrier, inc=1, device_id=(lax.rem(r + d, reps), g), device_id_type=MESH)
    pl.semaphore_wait(barrier, group + reps - 2)


def vectors_of(small):
    return jnp.concatenate([small[g, 0:8, 0:48].astype(jnp.float32) for g in range(8)], axis=1)


def chip_at(z, i):
    order = ((0, 1, 2, 3), (1, 0, 2, 3), (2, 1, 3, 0), (3, 2, 1, 0))
    chip = jnp.int32(0)
    for a, row in enumerate(order):
        for k, value in enumerate(row):
            chip = jnp.where((z == a) & (i == k), value, chip)
    return chip


def gather_kernel(
    tok, wq, wk, wv, wo, wi, wu, vectors, inner, seg,
    x_out, w_out, s_out, kv_out, qh_out, kt_out, vt_out, q1_out, norms,
    small, x, kv, qh, kt, vt, q1, w0, smalls_in, wrow, wtr, mine,
    lsem, xsem, psems, tsend, trecv, psend, wsend1, wrecv1, wsend2, wrecv2, wsend3, wrecv3, ssend, srecv,
):
    r, g, z, c = where_am_i()
    reps, chips = 4, 4
    p = 2 * z + 1 - c
    heads = kv.shape[0]
    _, rows, width = x.shape
    small[0:8, :] = jnp.concatenate(
        [vectors[...].astype(jnp.float32), jnp.zeros((8, rows - 48), jnp.float32)], axis=1
    ).astype(jnp.bfloat16)
    small[8:16, :] = jnp.concatenate(
        [
            jnp.concatenate([inner[...].astype(jnp.float32), jnp.zeros((1, rows - 192), jnp.float32)], axis=1),
            seg[...].astype(jnp.float32),
            jnp.zeros((5, rows), jnp.float32),
        ],
        axis=0,
    ).astype(jnp.bfloat16)
    greet(r, g, reps, 2 * chips)
    slab = [wi.at[:, pl.ds(j * width, width)] for j in range(4)]
    quarters = (
        ((wq, 0, 48), (wk, 48, 48), (wv, 96, 48)),
        ((wo, 0, 48), (slab[0], 48, 48), (slab[1], 96, 48)),
        ((slab[2], 0, 48), (slab[3], 48, 48), (wu.at[pl.ds(0, 48), :], 96, 48)),
        ((wu.at[pl.ds(48, 144), :], 0, 144),),
    )
    swap = remote(tok.at[1 - c], x.at[g], psend, trecv.at[g], r, p)
    swap.start()
    own_x = pltpu.make_async_copy(tok.at[c], x.at[g], lsem.at[0])
    own_x.start()
    def pass_on(b, way, src=None):
        to = g + 2 if way == 0 else g - 2
        src = x.at[b] if src is None else src
        return remote(src, x.at[b], tsend.at[way, b], trecv.at[b], r, to)

    def forward(b, way, src=None):
        ok = z < chips - 1 if way == 0 else z > 0

        @pl.when(ok)
        def _():
            pass_on(b, way, src).start()

    def keep(b):
        return pltpu.make_async_copy(x.at[b], x_out.at[b], xsem.at[b])

    def arrived(b):
        remote(x.at[b], x.at[b], tsend.at[0, b], trecv.at[b], r, p).wait_recv()

    forward(g, 0, tok.at[c])
    forward(g, 1, tok.at[c])
    arrived(p)
    forward(p, 0)
    forward(p, 1)
    keep(p).start()
    for i, pieces in enumerate(quarters):
        @pl.when(r == i)
        def _():
            copies = [
                pltpu.make_async_copy(ref, mine.at[pl.ds(row, count), :], lsem.at[3 + k])
                for k, (ref, row, count) in enumerate(pieces)
            ]
            for copy in copies:
                copy.start()
            for copy in copies:
                copy.wait()

    own_w = pltpu.make_async_copy(mine, w_out.at[r, c, z], lsem.at[1])
    own_w.start()
    own_s = pltpu.make_async_copy(small, smalls_in.at[g], lsem.at[2])
    own_s.start()
    first = []
    for d in range(1, chips):
        zz = lax.rem(z + d, chips)
        copy = remote(mine, w_out.at[r, c, z], wsend1.at[d - 1], wrecv1.at[z], r, 2 * zz + c)
        copy.start()
        first.append(copy)
    smalls = []
    for d in range(1, 2 * chips):
        copy = remote(small, smalls_in.at[g], ssend.at[d - 1], srecv.at[g], r, lax.rem(g + d, 2 * chips))
        copy.start()
        smalls.append(copy)
    own_x.wait()
    keep(g).start()

    def tokens_from(d):
        for k in range(2):
            @pl.when(z >= d)
            def _():
                b = 2 * (z - d) + (c if k == 0 else 1 - c)
                arrived(b)
                forward(b, 0)
                keep(b).start()

            @pl.when(z + d < chips)
            def _():
                b = 2 * (z + d) + (c if k == 0 else 1 - c)
                arrived(b)
                forward(b, 1)
                keep(b).start()

    tokens_from(1)
    for d in range(1, chips):
        zz = lax.rem(z + d, chips)
        remote(mine, w_out.at[r, c, zz], wsend1.at[0], wrecv1.at[zz], r, p).wait_recv()
    own_w.wait()
    second = []
    for d in range(1, reps):
        copy = remote(
            w_out.at[r, c], w_out.at[r, c], wsend2.at[d - 1], wrecv2.at[r], lax.rem(r + d, reps), g
        )
        copy.start()
        second.append(copy)
    third = [remote(w_out.at[r, c], w_out.at[r, c], wsend3.at[r], wrecv3.at[r], r, p)]
    third[0].start()
    tokens_from(2)
    for d in range(1, reps):
        q = lax.rem(r + d, reps)
        remote(w_out.at[q, c], w_out.at[q, c], wsend2.at[0], wrecv2.at[q], r, p).wait_recv()
        copy = remote(w_out.at[q, c], w_out.at[q, c], wsend3.at[q], wrecv3.at[q], r, p)
        copy.start()
        third.append(copy)
    for q in range(reps):
        remote(w_out.at[q, 1 - c], w_out.at[q, 1 - c], wsend3.at[q], wrecv3.at[q], r, p).wait_recv()
    load_w = pltpu.make_async_copy(w_out.at[0], w0, lsem.at[1])
    load_w.start()
    for d in range(1, 2 * chips):
        b = lax.rem(g + d, 2 * chips)
        remote(small, smalls_in.at[b], ssend.at[0], srecv.at[b], r, p).wait_recv()
    own_s.wait()
    keep_s = pltpu.make_async_copy(smalls_in, s_out, lsem.at[2])
    keep_s.start()
    load_w.wait()

    span = heads * HEAD
    bias = vectors_of(smalls_in).astype(jnp.bfloat16)
    full = [
        jnp.concatenate([w0[i % 2, i // 2, 48 * k : 48 * k + 48, :] for i in range(8)], axis=0)
        for k in range(3)
    ]
    lane = iota((width, heads * LANES), 1)
    head, lane_in = lax.div(lane, LANES), lax.rem(lane, LANES)
    column = span * z + head * HEAD + lax.rem(lane_in, HEAD)
    hit = iota((width, heads * LANES), 0) == column
    pick_k = jnp.where(hit & (lane_in < 64), 1.0, 0.0).astype(jnp.bfloat16)
    pick_v = jnp.where(hit & (lane_in >= 64) & (lane_in < 96), 1.0, 0.0).astype(jnp.bfloat16)
    wrow[...] = (dot(full[1], pick_k) + dot(full[2], pick_v)).astype(jnp.bfloat16)
    row_kv = dot(bias[1:2, :], pick_v)
    pick_t = jnp.where(
        iota((span, width), 1) == span * z + iota((span, width), 0), 1.0, 0.0
    ).astype(jnp.bfloat16)

    def by_rows(left, right):
        return lax.dot_general(
            left, right, (((1,), (1,)), ((), ())), preferred_element_type=jnp.float32
        )

    for k in range(3):
        wtr[k] = by_rows(pick_t, full[k]).astype(jnp.bfloat16)
    column_bias = by_rows(pick_t, bias)
    col_q, col_v = column_bias[:, 0:1], column_bias[:, 1:2]
    scale = (HEAD ** -0.5) * LOG2E
    one_lane = lax.rem(iota((1, heads * LANES), 1), LANES)
    row_kv = row_kv + jnp.where((one_lane >= 104) & (one_lane < 107), 1.0, 0.0)
    one = jnp.where(iota((16, rows), 0) == 0, 1.0, 0.0).astype(jnp.bfloat16)

    def stores(b):
        cols = pl.ds(pl.multiple_of(b * rows, rows), rows)
        return [
            pltpu.make_async_copy(kv.at[:, cols, :], kv_out.at[:, cols, :], psems.at[0, b])
        ] + [
            pltpu.make_async_copy(ref.at[:, :, cols], out.at[:, :, cols], psems.at[1 + i, b])
            for i, (ref, out) in enumerate(((qh, qh_out), (kt, kt_out), (vt, vt_out), (q1, q1_out)))
        ]

    def project(i, most):
        half = lax.rem(i, 2)
        b = 2 * chip_at(z, lax.div(i, 2)) + c + half - 2 * c * half
        xb = x[b]
        two = smalls_in[b, 8:16, :].astype(jnp.float32)
        ids = jnp.where(c == 0, two[1:2], two[2:3])
        same = jnp.where(iota((8, rows), 0).astype(jnp.float32) == ids, 1.0, 0.0)
        hot = jnp.concatenate(
            [jnp.zeros((96, rows), jnp.float32), same, jnp.zeros((24, rows), jnp.float32)], axis=0
        ).T
        cols = pl.ds(pl.multiple_of(b * rows, rows), rows)
        flat = dot(xb, wrow[...]) + row_kv
        for h in range(heads):
            kv[h, cols, :] = (flat[:, h * LANES : (h + 1) * LANES] + hot).astype(jnp.bfloat16)
        q_t = (by_rows(wtr[0], xb) + col_q).astype(jnp.bfloat16)
        k_t = by_rows(wtr[1], xb).astype(jnp.bfloat16)
        v_t = (by_rows(wtr[2], xb) + col_v).astype(jnp.bfloat16)
        q_wide = q_t.astype(jnp.float32) * scale
        k_wide = k_t.astype(jnp.float32)
        q_hi = q_wide.astype(jnp.bfloat16)
        q_lo = (q_wide - q_hi.astype(jnp.float32)).astype(jnp.bfloat16)
        sizes = []
        for n, v in enumerate((q_wide, k_wide)):
            size = most[n]
            for h in range(heads):
                size = jnp.maximum(
                    size, jnp.sum(v[h * HEAD : (h + 1) * HEAD] ** 2, axis=0, keepdims=True)
                )
            sizes.append(size)
        for h in range(heads):
            part = slice(h * HEAD, (h + 1) * HEAD)
            qh[h, 0:32, cols] = q_hi[part]
            qh[h, 32:64, cols] = q_lo[part]
            kt[h, :, cols] = k_t[part]
            q1[h, :, cols] = q_t[part]
            vt[h, 0:32, cols] = v_t[part]
            vt[h, 32:48, cols] = one
        for copy in stores(b):
            copy.start()
        return tuple(sizes)

    zero = jnp.zeros((1, rows), jnp.float32)
    most = lax.fori_loop(0, 6, project, (zero, zero))
    tokens_from(3)
    most = lax.fori_loop(6, 8, project, most)
    norms[0:1, :] = most[0]
    norms[1:2, :] = most[1]

    def settle(b, none):
        keep(b).wait()
        for copy in stores(b):
            copy.wait()
        return none

    swap.wait_send()
    for copy in first + smalls + second + third:
        copy.wait_send()
    for b in range(2 * chips):
        @pl.when((z < chips - 1) & (b < 2 * z + 2))
        def _():
            pass_on(b, 0).wait_send()

        @pl.when((z > 0) & (b >= 2 * z))
        def _():
            pass_on(b, 1).wait_send()

    keep_s.wait()
    lax.fori_loop(0, 2 * chips, settle, 0)


def gather(tokens, weights, vectors, inner, seg):
    dma = pltpu.SemaphoreType.DMA
    anywhere = pl.BlockSpec(memory_space=pltpu.HBM)
    vm = pl.BlockSpec(memory_space=pltpu.VMEM)
    rows, width = tokens.shape[1:]
    bf, f4 = jnp.bfloat16, jnp.float32
    heads, length = 3, 8 * rows
    made = [
        (heads, length, LANES), (heads, 64, length), (heads, HEAD, length), (heads, 48, length), (heads, HEAD, length)
    ]
    return pl.pallas_call(
        gather_kernel,
        name="gather",
        out_shape=(
            jax.ShapeDtypeStruct((8, rows, width), bf),
            jax.ShapeDtypeStruct((4, 2, 4, 144, width), bf),
            jax.ShapeDtypeStruct((8, 16, rows), bf),
        )
        + tuple(jax.ShapeDtypeStruct(shape, bf) for shape in made)
        + (jax.ShapeDtypeStruct((2, rows), f4),),
        in_specs=[anywhere] * 7 + [vm] * 3,
        out_specs=[anywhere] * 8 + [vm],
        scratch_shapes=[
            pltpu.VMEM((16, rows), bf),
            pltpu.VMEM((8, rows, width), bf),
        ]
        + [pltpu.VMEM(shape, bf) for shape in made]
        + [
            pltpu.VMEM((2, 4, 144, width), bf),
            pltpu.VMEM((8, 16, rows), bf),
            pltpu.VMEM((width, heads * LANES), bf),
            pltpu.VMEM((3, heads * HEAD, width), bf),
            pltpu.VMEM((144, width), bf),
            dma((6,)), dma((8,)), dma((5, 8)), dma((2, 8)), dma((8,)), dma, dma((3,)), dma((4,)), dma((3,)), dma((4,)),
            dma((4,)), dma((4,)), dma((7,)), dma((8,)),
        ],
        compiler_params=pltpu.CompilerParams(
            collective_id=1, has_side_effects=True, vmem_limit_bytes=BIG
        ),
    )(tokens, *weights, vectors, inner, seg)


def span_of(starts, q0, docs):
    low = jnp.int32(0)
    high = starts[docs]
    for d in range(docs):
        low = jnp.where(starts[d] <= q0, jnp.maximum(low, starts[d]), low)
        high = jnp.where(starts[d + 1] >= q0 + QB, jnp.minimum(high, starts[d + 1]), high)
    first = lax.div(low, LANES)
    last = lax.div(high + LANES - 1, LANES)
    steps = lax.div(last - first + KB // LANES - 1, KB // LANES)
    total = lax.div(starts[docs], LANES)
    first = jnp.minimum(first, total - steps * (KB // LANES))
    return first, steps


def in_pairs(first, steps, body):
    double = lax.div(steps, 2)

    def two(i, none):
        body(pl.ds(pl.multiple_of((first + i * (2 * KB // LANES)) * LANES, LANES), 2 * KB))
        return none

    lax.fori_loop(0, double, two, 0)

    @pl.when(steps > 2 * double)
    def _():
        body(pl.ds(pl.multiple_of((first + double * (2 * KB // LANES)) * LANES, LANES), KB))


def in_groups(first, steps, body, most):
    unit = KB // LANES

    def at(i):
        return pl.multiple_of((first + i * unit) * LANES, LANES)

    many = lax.div(steps, most)

    def group(i, none):
        body([at(most * i + 2 * k) for k in range(most // 2)], 2 * KB)
        return none

    lax.fori_loop(0, many, group, 0)
    if most == 4:
        @pl.when(steps - most * many >= 2)
        def _():
            body([at(most * many), at(most * many + 1)], KB)

    @pl.when(lax.rem(steps, 2) == 1)
    def _():
        body([at(steps - 1)], KB)


def attend_kernel(
    place, kv, qh, vt, small, norms, ctx, ctx32, tail_out, spans, qt, acc, tall, seg, starts, sem,
):
    heads, length, _ = kv.shape
    blocks, hw, rows = ctx.shape
    docs = 8
    c = place[1]
    load = pltpu.make_async_copy(qh, qt.at[:, pl.ds(0, 64), :], sem)
    load.start()
    for g in range(8):
        two = small[g, 8:16, :].astype(jnp.float32)
        seg[g : g + 1, :] = jnp.where(c == 0, two[1:2], two[2:3]).astype(jnp.int32)
    ids = seg[...]
    starts[0] = jnp.int32(0)
    for d in range(1, docs):
        starts[d] = jnp.sum(jnp.where(ids < d, 1.0, 0.0)).astype(jnp.int32)
    starts[docs] = jnp.int32(length)

    def far(same):
        return (same - 1.0) * AWAY

    def fill(b, none):
        cols = pl.ds(pl.multiple_of(b * rows, rows), rows)
        same = jnp.where(iota((8, rows), 0) == seg[pl.ds(b, 1), :], 1.0, 0.0)
        low = jnp.concatenate([far(same), jnp.zeros((8, rows), jnp.float32)], axis=0)
        for h in range(heads):
            qt[h, 64:96, cols] = jnp.zeros((32, rows), jnp.bfloat16)
            qt[h, 96:112, cols] = low.astype(jnp.bfloat16)
            qt[h, 112:128, cols] = jnp.zeros((16, rows), jnp.bfloat16)
        return none

    lax.fori_loop(0, blocks, fill, 0)
    bounded = jnp.max(norms[0:1, :]) * jnp.max(norms[1:2, :]) < LIMIT * LIMIT
    load.wait()

    per = rows // QB

    def query_block(b, carry):
        q0 = pl.multiple_of(b * QB, QB)
        first, steps = span_of(starts, q0, docs)
        spans[0, b] = first
        spans[1, b] = steps
        acc[...] = jnp.zeros_like(acc)

        def key_block(i, tops):
            k0 = pl.multiple_of((first + i * (KB // LANES)) * LANES, LANES)
            s = [dot(kv[h, pl.ds(k0, KB), :], qt[h, :, pl.ds(q0, QB)]) for h in range(heads)]
            new = [jnp.maximum(tops[h], jnp.max(s[h], axis=0, keepdims=True)) for h in range(heads)]
            p = [jnp.exp2(s[h] - new[h]).astype(jnp.bfloat16) for h in range(heads)]
            for h in range(heads):
                acc[h] = acc[h] * jnp.exp2(tops[h] - new[h]) + dot(vt[h, :, pl.ds(k0, KB)], p[h])
            return tuple(new)

        def plain_block(keys):
            s = [dot(kv[h, keys, :], qt[h, :, pl.ds(q0, QB)]) for h in range(heads)]
            p = [jnp.exp2(v).astype(jnp.bfloat16) for v in s]
            for h in range(heads):
                acc[h] += dot(vt[h, :, keys], p[h])

        @pl.when(bounded)
        def _():
            in_pairs(first, steps, plain_block)
            tall[...] = jnp.zeros_like(tall)

        @pl.when(jnp.logical_not(bounded))
        def _():
            lowest = jnp.full((1, QB), -3e38, jnp.float32)
            tops = lax.fori_loop(0, steps, key_block, (lowest,) * heads)
            for h in range(heads):
                tall[h] = tops[h]

        g = lax.div(b, per)
        off = pl.multiple_of(lax.rem(b, per) * QB, QB)
        same = jnp.where(iota((8, QB), 0) == seg[pl.ds(g, 1), pl.ds(off, QB)], 1.0, 0.0)
        for h in range(heads):
            total = acc[h, 32:33, :]
            out = acc[h, 0:32, :] / total
            ctx[g, h * HEAD : (h + 1) * HEAD, pl.ds(off, QB)] = out.astype(jnp.bfloat16)
            ctx32[g, h * HEAD : (h + 1) * HEAD, pl.ds(off, QB)] = out
            parts = halves(-(tall[h] + jnp.log2(total)))
            tail = jnp.concatenate([far(same), *parts, jnp.zeros((5, QB), jnp.float32)], axis=0)
            tail_out[h, :, pl.ds(q0, QB)] = tail.astype(jnp.bfloat16)
        return carry

    lax.fori_loop(0, length // QB, query_block, 0)


def attend(place, kv, qh, vt, small, norms):
    heads, length, _ = kv.shape
    blocks, _, rows = small.shape
    sm = pl.BlockSpec(memory_space=pltpu.SMEM)
    anywhere = pl.BlockSpec(memory_space=pltpu.HBM)
    bf, f4 = jnp.bfloat16, jnp.float32
    shapes = (
        jax.ShapeDtypeStruct((blocks, heads * HEAD, rows), bf),
        jax.ShapeDtypeStruct((blocks, heads * HEAD, rows), f4),
        jax.ShapeDtypeStruct((heads, 16, length), bf),
    )
    return pl.pallas_call(
        attend_kernel,
        name="attend",
        grid=(1,),
        out_shape=shapes + (jax.ShapeDtypeStruct((2, length // QB), jnp.int32),),
        in_specs=[sm, whole_spec(kv), anywhere, whole_spec(vt), whole_spec(small), whole_spec(norms)],
        out_specs=[whole_spec(v) for v in shapes] + [sm],
        scratch_shapes=[
            pltpu.VMEM((heads, LANES, length), bf),
            pltpu.VMEM((heads, 48, QB), f4),
            pltpu.VMEM((heads, 1, QB), f4),
            pltpu.VMEM((8, rows), jnp.int32),
            pltpu.SMEM((16,), jnp.int32),
            pltpu.SemaphoreType.DMA,
        ],
        compiler_params=pltpu.CompilerParams(vmem_limit_bytes=BIG),
    )(place, kv, qh, vt, small, norms)


PIECE = 128


def middle_kernel(
    ctx, tok, og, w, small,
    layer_out, grad_one_out, gctx_out, pr,
    wo, wi, wu, gwo, gwi, gwu, sums, inner_sum, ctx_in, gctx, pg, pg_in,
    lsem, send, recv, gsend, grecv, glocal, psend, precv,
):
    seqs, rows, width = tok.shape
    slabs = wi.shape[0]
    pieces = rows // PIECE
    r, g, z, c = where_am_i()
    greet(r, g, 1, 8)

    def fetch(q):
        cols = pl.ds(pl.multiple_of(q * PIECE, PIECE), PIECE)
        for d in range(1, 8):
            to = lax.rem(g + d, 8)
            remote(
                ctx.at[to, :, cols], ctx_in.at[c, z, :, cols], send.at[q, d - 1], recv.at[q, g], r, to
            ).start()

    own = pltpu.make_async_copy(ctx.at[g], ctx_in.at[c, z], lsem)
    own.start()
    fetch(0)
    fetch(1)
    for i in range(8):
        cc, zz = i % 2, i // 2
        wo[48 * i : 48 * i + 48, :] = w[1, cc, zz, 0:48, :]
        wi[0, 48 * i : 48 * i + 48, :] = w[1, cc, zz, 48:96, :]
        wi[1, 48 * i : 48 * i + 48, :] = w[1, cc, zz, 96:144, :]
        wi[2, 48 * i : 48 * i + 48, :] = w[2, cc, zz, 0:48, :]
        wi[3, 48 * i : 48 * i + 48, :] = w[2, cc, zz, 48:96, :]
        wu[zz, 192 * cc : 192 * cc + 48, :] = w[2, cc, zz, 96:144, :]
        wu[zz, 192 * cc + 48 : 192 * cc + 192, :] = w[3, cc, zz, :, :]
    for ref in (gwo, gwi, gwu, sums, inner_sum):
        ref[...] = jnp.zeros_like(ref)
    fetch(2)
    fetch(3)

    vec = vectors_of(small)
    inner_bias = jnp.concatenate(
        [small[i, 8:16, 0:192].astype(jnp.float32)[0:1] for i in range(8)], axis=1
    )
    out_bias, outer_bias = vec[2:3, :], vec[3:4, :]
    gain_one, shift_one = vec[4:5, :], vec[5:6, :]
    gain_two, shift_two = vec[6:7, :], vec[7:8, :]

    def normal(value):
        centre = value - jnp.mean(value, axis=-1, keepdims=True)
        rate = lax.rsqrt(jnp.mean(centre * centre, axis=-1, keepdims=True) + norm_epsilon)
        return centre * rate, rate

    def normal_back(grad, gain, n, rate):
        u = grad * gain
        return rate * (
            u - jnp.mean(u, axis=-1, keepdims=True) - n * jnp.mean(u * n, axis=-1, keepdims=True)
        )

    def total(value):
        return jnp.sum(value, axis=0, keepdims=True)

    def dot_turn(left, right):
        return lax.dot_general(
            left, right, (((1,), (1,)), ((), ())), preferred_element_type=jnp.float32
        )

    def arrived(q, cols):
        for d in range(1, 8):
            b = lax.rem(g + d, 8)
            remote(
                ctx.at[g, :, cols], ctx_in.at[lax.rem(b, 2), lax.div(b, 2), :, cols],
                send.at[q, 0], recv.at[q, b], r, b,
            ).wait_recv()

    def return_piece(q, cols, d):
        to = lax.rem(g + d, 8)
        return remote(
            gctx.at[lax.rem(to, 2), lax.div(to, 2), :, cols], gctx_out.at[g, :, cols],
            gsend.at[q, d - 1], grecv.at[q, g], r, to,
        )

    def keep_piece(q, cols):
        return pltpu.make_async_copy(gctx.at[c, z, :, cols], gctx_out.at[g, :, cols], glocal.at[q])

    own.wait()

    def one(q, carry):
        r0 = pl.multiple_of(q * PIECE, PIECE)
        here = pl.ds(r0, PIECE)
        arrived(q, here)

        def both(ref):
            return jnp.concatenate([ref[s, here, :] for s in range(seqs)], axis=0)

        def split(ref, value):
            for s in range(seqs):
                ref[s, here, :] = value[s * PIECE : (s + 1) * PIECE].astype(ref.dtype)

        ctx_t = jnp.concatenate(
            [jnp.concatenate([ctx_in[s, zz, :, here] for zz in range(4)], axis=0) for s in range(seqs)],
            axis=1,
        )
        context = ctx_t.astype(jnp.float32).T.astype(jnp.bfloat16)
        x = both(tok).astype(jnp.float32)
        n_one, rate_one = normal(x + (dot(context, wo[...]) + out_bias))
        hidden = n_one * gain_one + shift_one
        low = hidden.astype(jnp.bfloat16)
        low_t = hidden.T.astype(jnp.bfloat16)
        feed = jnp.zeros(hidden.shape, jnp.float32)
        slopes, actives = [], []
        for j in range(slabs):
            inner = dot(low, wi[j]) + inner_bias[:, j * width : (j + 1) * width]
            cdf = 0.5 + 0.5 * lax.erf(inner * (0.5 ** 0.5))
            pdf = jnp.exp(inner * inner * -0.5) * 0.3989422804014327
            slopes.append(cdf + inner * pdf)
            active = inner * cdf
            actives.append(active)
            feed = feed + dot(active.astype(jnp.bfloat16), wu[j])
        n_two, rate_two = normal(hidden + (feed + outer_bias))
        split(layer_out, n_two * gain_two + shift_two)
        grad = both(og).astype(jnp.float32)
        grad_two = normal_back(grad, gain_two, n_two, rate_two)
        grad_feed = grad_two.astype(jnp.bfloat16)
        grad_hidden = grad_two
        for j in range(slabs):
            grad_inner = (dot_turn(grad_feed, wu[j]) * slopes[j]).astype(jnp.bfloat16)
            inner_sum[:, j * width : (j + 1) * width] += total(grad_inner.astype(jnp.float32))
            grad_hidden = grad_hidden + dot_turn(grad_inner, wi[j])
            gwi[j] += dot(low_t, grad_inner)
            gwu[j] += dot(actives[j].T.astype(jnp.bfloat16), grad_feed)
        grad_one = normal_back(grad_hidden, gain_one, n_one, rate_one)
        split(grad_one_out, grad_one)
        grad_att = grad_one.astype(jnp.bfloat16)
        back = dot_turn(wo[...], grad_att).astype(jnp.bfloat16)
        for s in range(seqs):
            for zz in range(4):
                gctx[s, zz, :, here] = back[96 * zz : 96 * zz + 96, s * PIECE : (s + 1) * PIECE]
        for d in range(1, 8):
            return_piece(q, here, d).start()
        keep_piece(q, here).start()
        gwo[...] += dot(ctx_t, grad_att)
        sums[0:1, :] += total(grad_att.astype(jnp.float32))
        sums[1:2, :] += total(grad_feed.astype(jnp.float32))
        sums[2:3, :] += total(grad_hidden * n_one)
        sums[3:4, :] += total(grad_hidden)
        sums[4:5, :] += total(grad * n_two)
        sums[5:6, :] += total(grad)
        return carry

    lax.fori_loop(0, pieces, one, 0)
    rows_of_sums = jnp.concatenate(
        [sums[...]]
        + [inner_sum[:, j * width : (j + 1) * width] for j in range(slabs)]
        + [jnp.zeros((6, width), jnp.float32)],
        axis=0,
    ).astype(jnp.bfloat16)
    for i in range(8):
        cc, zz = i % 2, i // 2
        mine = slice(48 * i, 48 * i + 48)
        pg[cc, 0, zz, 0:48, :] = gwo[mine, :].astype(jnp.bfloat16)
        pg[cc, 0, zz, 48:96, :] = gwi[0, mine, :].astype(jnp.bfloat16)
        pg[cc, 1, zz, 0:48, :] = gwi[1, mine, :].astype(jnp.bfloat16)
        pg[cc, 1, zz, 48:96, :] = gwi[2, mine, :].astype(jnp.bfloat16)
        pg[cc, 2, zz, 0:48, :] = gwi[3, mine, :].astype(jnp.bfloat16)
        base = 192 * cc
        pg[cc, 0, zz, 96:112, :] = gwu[zz, base : base + 16, :].astype(jnp.bfloat16)
        pg[cc, 1, zz, 96:112, :] = gwu[zz, base + 16 : base + 32, :].astype(jnp.bfloat16)
        pg[cc, 2, zz, 48:112, :] = gwu[zz, base + 32 : base + 96, :].astype(jnp.bfloat16)
        pg[cc, 3, zz, 0:96, :] = gwu[zz, base + 96 : base + 192, :].astype(jnp.bfloat16)
        pg[cc, 3, zz, 96:112, :] = rows_of_sums
    pair = remote(pg.at[1 - c], pg_in, psend, precv, r, 2 * z + 1 - c)
    pair.start()

    def settle(q, carry):
        cols = pl.ds(pl.multiple_of(q * PIECE, PIECE), PIECE)
        for d in range(1, 8):
            b = lax.rem(g + d, 8)
            remote(
                gctx.at[c, z, :, cols], gctx_out.at[b, :, cols], gsend.at[q, 0], grecv.at[q, b], r, b
            ).wait_recv()
            return_piece(q, cols, d).wait_send()
            to = lax.rem(g + d, 8)
            remote(
                ctx.at[to, :, cols], ctx_in.at[c, z, :, cols], send.at[q, d - 1], recv.at[q, g], r, to
            ).wait_send()
        keep_piece(q, cols).wait()
        return carry

    pair.wait_recv()
    for i in range(4):
        pr[i] = (pg[c, i].astype(jnp.float32) + pg_in[i].astype(jnp.float32)).astype(jnp.bfloat16)
    lax.fori_loop(0, pieces, settle, 0)
    pair.wait_send()


def middle(ctx, tok, og, w, small):
    seqs, rows, width = tok.shape
    vm = pl.BlockSpec(memory_space=pltpu.VMEM)
    anywhere = pl.BlockSpec(memory_space=pltpu.HBM)
    dma = pltpu.SemaphoreType.DMA
    bf, f4 = jnp.bfloat16, jnp.float32
    pieces = rows // PIECE
    return pl.pallas_call(
        middle_kernel,
        name="middle",
        out_shape=(
            jax.ShapeDtypeStruct((seqs, rows, width), bf),
            jax.ShapeDtypeStruct((seqs, rows, width), f4),
            jax.ShapeDtypeStruct(ctx.shape, bf),
            jax.ShapeDtypeStruct((4, 4, 112, width), bf),
        ),
        in_specs=[anywhere] + [vm] * 4,
        out_specs=[vm, vm, anywhere, vm],
        scratch_shapes=[
            pltpu.VMEM((width, width), bf),
            pltpu.VMEM((4, width, width), bf),
            pltpu.VMEM((4, width, width), bf),
            pltpu.VMEM((width, width), f4),
            pltpu.VMEM((4, width, width), f4),
            pltpu.VMEM((4, width, width), f4),
            pltpu.VMEM((6, width), f4),
            pltpu.VMEM((1, 4 * width), f4),
            pltpu.VMEM((2, 4) + ctx.shape[1:], bf),
            pltpu.VMEM((2, 4) + ctx.shape[1:], bf),
            pltpu.VMEM((2, 4, 4, 112, width), bf),
            pltpu.VMEM((4, 4, 112, width), bf),
            dma, dma((pieces, 7)), dma((pieces, 8)), dma((pieces, 7)), dma((pieces, 8)), dma((pieces,)), dma, dma,
        ],
        compiler_params=pltpu.CompilerParams(
            collective_id=2, has_side_effects=True, vmem_limit_bytes=BIG
        ),
    )(ctx, tok, og, w, small)


def attend_back_kernel(
    last, index, place, spans, x_hbm, qh, tail, kv, kt, q1, gctx, ctx32, *refs,
):
    heads = kv.shape[0]
    span = heads * HEAD
    if last:
        grads_in, out, gq, dt, do, acc, dq, qt, x, sems = refs
    else:
        out, grads_out, dt, do, acc, dq, qt, x, sems = refs
    length, width = x.shape
    mine = pl.ds(index * heads, heads)
    loads = [
        pltpu.make_async_copy(qh.at[mine], qt.at[:, pl.ds(0, 64), :], sems.at[0]),
        pltpu.make_async_copy(tail.at[mine], qt.at[:, pl.ds(96, 16), :], sems.at[1]),
        pltpu.make_async_copy(x_hbm, x, sems.at[2]),
    ]
    for load in loads:
        load.start()
    blocks, _, rows = gctx.shape
    z = place[0]
    c = place[1]
    scale = HEAD ** -0.5

    def prepare(g, carry):
        r0 = pl.multiple_of(g * rows, rows)
        cols = pl.ds(r0, rows)
        for h in range(heads):
            part = slice(h * HEAD, (h + 1) * HEAD)
            grad = gctx[g, part, :]
            wide = grad.astype(jnp.float32)
            delta = -jnp.sum(wide * ctx32[g, part, :], axis=0, keepdims=True)
            dt[h, 0:64, cols] = jnp.zeros((64, rows), jnp.bfloat16)
            dt[h, 64:96, cols] = grad
            qt[h, 64:96, cols] = jnp.zeros((32, rows), jnp.bfloat16)
            qt[h, 112:128, cols] = jnp.zeros((16, rows), jnp.bfloat16)
            tail = jnp.concatenate(
                [jnp.zeros((8, rows), jnp.float32), *halves(delta), jnp.zeros((21, rows), jnp.float32)],
                axis=0,
            )
            dt[h, 96:128, cols] = tail.astype(jnp.bfloat16)
            turned = jnp.concatenate(
                [wide, q1[h, :, cols].astype(jnp.float32), jnp.zeros((64, rows), jnp.float32)], axis=0
            ).T
            lane = iota((rows, LANES), 1)
            grad_rows = jnp.where(lane < HEAD, turned, 0.0).astype(jnp.bfloat16)
            query_rows = jnp.where(lane < HEAD, 0.0, turned).astype(jnp.bfloat16)
            for j in range(rows // QB):
                r1 = pl.multiple_of(2 * r0 + 2 * j * QB, QB)
                do[h, pl.ds(r1, QB), :] = grad_rows[j * QB : (j + 1) * QB]
                do[h, pl.ds(r1 + QB, QB), :] = query_rows[j * QB : (j + 1) * QB]
        return carry

    lax.fori_loop(0, blocks, prepare, 0)
    acc[...] = jnp.zeros_like(acc)
    per = rows // QB
    loads[0].wait()
    loads[1].wait()

    def query_block(b, carry):
        q0 = pl.multiple_of(b * QB, QB)
        dq[...] = jnp.zeros_like(dq)

        def key_blocks(starts, size):
            jobs = [(h, pl.ds(start, size)) for start in starts for h in range(heads)]
            s = [dot(kv[h, k, :], qt[h, :, pl.ds(q0, QB)]) for h, k in jobs]
            d = [dot(kv[h, k, :], dt[h, :, pl.ds(q0, QB)]) for h, k in jobs]
            p = [jnp.exp2(v) for v in s]
            both = [
                jnp.concatenate([u.astype(jnp.bfloat16), (u * v).astype(jnp.bfloat16)], axis=1)
                for u, v in zip(p, d)
            ]
            for (h, k), v in zip(jobs, both):
                acc[h, k, :] += dot(v, do[h, pl.ds(2 * q0, 2 * QB), :])
            for (h, k), v in zip(jobs, both):
                dq[h] += dot(kt[h, :, k], v[:, QB:])

        in_groups(spans[0, b], spans[1, b], key_blocks, 4 if heads == 1 else 2)
        g = lax.div(b, per)
        off = pl.multiple_of(lax.rem(b, per) * QB, QB)
        for h in range(heads):
            out[g, h * HEAD : (h + 1) * HEAD, pl.ds(off, QB)] = (dq[h] * scale).astype(jnp.bfloat16)
        return carry

    lax.fori_loop(0, length // QB, query_block, 0)

    loads[2].wait()

    def finish_block(g, totals):
        r0 = pl.multiple_of(g * rows, rows)
        cols = pl.ds(r0, rows)
        for h in range(heads):
            both = acc[h, cols, :].T
            row = h * HEAD
            out[g, 2 * span + row : 2 * span + row + HEAD, :] = both[0:32].astype(jnp.bfloat16)
            out[g, span + row : span + row + HEAD, :] = (both[32:64] * scale).astype(jnp.bfloat16)
        piece = out[g]
        grad = dot(piece, x[cols, :])
        summed = jnp.sum(piece.astype(jnp.float32), axis=1, keepdims=True)
        return totals[0] + grad, totals[1] + summed

    grads, summed = lax.fori_loop(
        0,
        blocks,
        finish_block,
        (jnp.zeros((3 * span, width), jnp.float32), jnp.zeros((3 * span, 1), jnp.float32)),
    )
    if not last:
        grads_out[:, 0:width] = grads
        grads_out[:, width:] = jnp.broadcast_to(summed, (3 * span, LANES))
        return
    gq[...] = jnp.zeros_like(gq)
    before = grads_in.shape[0] // 3

    def joined(i, old, new):
        return [old[i * before : (i + 1) * before], new[i * span : (i + 1) * span]]

    old = grads_in[:, 0:width]
    whole = jnp.concatenate([v for i in range(3) for v in joined(i, old, grads)], axis=0).T
    total = 3 * (before + span)
    for g in range(8):
        gq[g % 2, g // 2, :, 0:total] = whole[48 * g : 48 * g + 48, :].astype(jnp.bfloat16)
    old = grads_in[:, width : width + 1]
    of_q = jnp.concatenate(joined(0, old, summed), axis=0)
    of_v = jnp.concatenate(joined(2, old, summed), axis=0)
    for cc in range(2):
        mine = jnp.concatenate(
            [
                of_q[48 * cc : 48 * cc + 48, :],
                of_v[48 * cc : 48 * cc + 48, :],
                jnp.zeros((48, 94), jnp.float32),
            ],
            axis=1,
        )
        gq[cc, z, :, total:] = mine.astype(jnp.bfloat16)


def attend_back(heads, index, place, spans, x, qh, tail, kv, kt, q1, gctx, ctx32, grads=None):
    blocks, rows, width = x.shape
    length = blocks * rows
    last = grads is not None
    rest = (grads,) if last else ()
    sm = pl.BlockSpec(memory_space=pltpu.SMEM)
    bf, f4 = jnp.bfloat16, jnp.float32
    once = pl.Buffered(1)
    span = heads * HEAD

    def some_heads(array):
        return pl.BlockSpec((heads,) + array.shape[1:], lambda i: (index, 0, 0), pipeline_mode=once)

    def head_rows(array):
        return pl.BlockSpec((blocks, span, rows), lambda i: (0, index, 0), pipeline_mode=once)

    flat = x.reshape(length, width)
    shapes = (
        jax.ShapeDtypeStruct((blocks, 3 * span, rows), bf),
        jax.ShapeDtypeStruct((2, 4, 48, width), bf)
        if last
        else jax.ShapeDtypeStruct((3 * span, width + LANES), f4),
    )
    return pl.pallas_call(
        functools.partial(attend_back_kernel, last, index),
        name="attend_back",
        grid=(1,),
        out_shape=shapes,
        in_specs=[sm, sm] + [pl.BlockSpec(memory_space=pltpu.HBM)] * 3
        + [some_heads(v) for v in (kv, kt, q1)]
        + [head_rows(v) for v in (gctx, ctx32)]
        + [whole_spec(v) for v in rest],
        out_specs=[whole_spec(v) for v in shapes],
        scratch_shapes=[
            pltpu.VMEM((heads, LANES, length), bf),
            pltpu.VMEM((heads, 2 * length, LANES), bf),
            pltpu.VMEM((heads, length, LANES), f4),
            pltpu.VMEM((heads, HEAD, QB), f4),
            pltpu.VMEM((heads, LANES, length), bf),
            pltpu.VMEM((length, width), bf),
            pltpu.SemaphoreType.DMA((3,)),
        ],
        compiler_params=pltpu.CompilerParams(vmem_limit_bytes=BIG),
        cost_estimate=pl.CostEstimate(
            flops=heads * 20 * 10 ** 9, bytes_accessed=heads * 8 * 10 ** 6, transcendentals=heads * 6 * 10 ** 6
        ),
    )(place, spans, flat, qh, tail, kv, kt, q1, gctx, ctx32, *rest)


def reduce_kernel(
    src, gq, pr, dst, p_out, q_out,
    gq_in, gq_sum, qa_in, qa_sum, qb_in, pa_in, pa_sum, pb_in, p_own, gq_own, pr_own,
    lsem, send, recv, gsend, grecv, qasend, qarecv, qbsend, qbrecv, qcsend, qcrecv,
    pasend, parecv, pbsend, pbrecv, pcsend, pcrecv,
):
    r, g, z, c = where_am_i()
    greet(r, g, 4, 8)
    waits = []
    pair = remote(gq.at[1 - c], gq_in, gsend, grecv, r, 2 * z + 1 - c)
    pair.start()
    for d in range(1, 4):
        rr = lax.rem(r + d, 4)
        copy = remote(pr.at[rr], pa_in.at[r], pasend.at[d - 1], parecv.at[r], rr, g)
        copy.start()
        waits.append(copy)
    load_g = pltpu.make_async_copy(gq.at[c], gq_own, lsem.at[1])
    load_g.start()
    load_p = pltpu.make_async_copy(pr.at[r], pr_own, lsem.at[2])
    load_p.start()
    own = pltpu.make_async_copy(src.at[g], dst.at[g], lsem.at[0])
    own.start()

    def send_to(d):
        to = lax.rem(g + d, 8)
        copy = remote(src.at[to], dst.at[g], send.at[d - 1], recv.at[g], r, to)
        copy.start()
        waits.append(copy)

    def f32(value):
        return value.astype(jnp.float32)

    send_to(4)
    send_to(3)
    send_to(5)
    load_g.wait()
    pair.wait_recv()
    gq_sum[...] = (f32(gq_own[...]) + f32(gq_in[...])).astype(jnp.bfloat16)
    for d in range(1, 4):
        rr = lax.rem(r + d, 4)
        copy = remote(gq_sum.at[rr], qa_in.at[r], qasend.at[d - 1], qarecv.at[r], rr, g)
        copy.start()
        waits.append(copy)
    send_to(2)
    send_to(6)
    for d in range(1, 4):
        b = lax.rem(r + d, 4)
        remote(gq_sum.at[r], qa_in.at[b], qasend.at[0], qarecv.at[b], b, g).wait_recv()
    total = f32(gq_sum[r])
    for d in range(1, 4):
        total = total + f32(qa_in[lax.rem(r + d, 4)])
    qa_sum[...] = total.astype(jnp.bfloat16)

    @pl.when(z != r)
    def _():
        remote(qa_sum, qb_in.at[z], qbsend, qbrecv.at[z], r, 2 * r + c).start()

    load_p.wait()
    for d in range(1, 4):
        b = lax.rem(r + d, 4)
        remote(pr.at[r], pa_in.at[b], pasend.at[0], parecv.at[b], b, g).wait_recv()
    total = f32(pr_own[...])
    for d in range(1, 4):
        total = total + f32(pa_in[lax.rem(r + d, 4)])
    pa_sum[...] = total.astype(jnp.bfloat16)
    for d in range(1, 4):
        zz = lax.rem(z + d, 4)
        copy = remote(pa_sum.at[zz], pb_in.at[z], pbsend.at[d - 1], pbrecv.at[z], r, 2 * zz + c)
        copy.start()
        waits.append(copy)
    send_to(1)
    send_to(7)

    @pl.when(z == r)
    def _():
        for d in range(1, 4):
            b = lax.rem(z + d, 4)
            remote(qa_sum, qb_in.at[b], qbsend, qbrecv.at[b], r, g).wait_recv()
        qb_in[z] = qa_sum[...]
        pltpu.make_async_copy(qb_in, q_out, lsem.at[4]).start()
        for d in range(1, 4):
            remote(qb_in, q_out, qcsend.at[d - 1], qcrecv, lax.rem(r + d, 4), g).start()

    for d in range(1, 4):
        b = lax.rem(z + d, 4)
        remote(pa_sum.at[z], pb_in.at[b], pbsend.at[0], pbrecv.at[b], r, g).wait_recv()
    total = f32(pa_sum[z])
    for d in range(1, 4):
        total = total + f32(pb_in[lax.rem(z + d, 4)])
    p_own[...] = total.astype(jnp.bfloat16)
    keep_p = pltpu.make_async_copy(p_own, p_out.at[r], lsem.at[3])
    keep_p.start()
    for d in range(1, 4):
        rr = lax.rem(r + d, 4)
        copy = remote(p_own, p_out.at[r], pcsend.at[d - 1], pcrecv.at[r], rr, g)
        copy.start()
        waits.append(copy)

    @pl.when(z == r)
    def _():
        pltpu.make_async_copy(qb_in, q_out, lsem.at[4]).wait()
        for d in range(1, 4):
            remote(qb_in, q_out, qcsend.at[d - 1], qcrecv, lax.rem(r + d, 4), g).wait_send()

    @pl.when(z != r)
    def _():
        remote(qb_in, q_out, qcsend.at[0], qcrecv, r, g).wait_recv()
        remote(qa_sum, qb_in.at[z], qbsend, qbrecv.at[z], r, 2 * r + c).wait_send()

    for d in range(1, 4):
        b = lax.rem(r + d, 4)
        remote(p_own, p_out.at[b], pcsend.at[0], pcrecv.at[b], b, g).wait_recv()
    for d in range(1, 8):
        b = lax.rem(g + d, 8)
        remote(src.at[g], dst.at[b], send.at[0], recv.at[b], r, b).wait_recv()
    pair.wait_send()
    for copy in waits:
        copy.wait_send()
    keep_p.wait()
    own.wait()


def reduce_all(src, gq, pr):
    dma = pltpu.SemaphoreType.DMA
    anywhere = pl.BlockSpec(memory_space=pltpu.HBM)
    bf = jnp.bfloat16
    width = gq.shape[-1]
    return pl.pallas_call(
        reduce_kernel,
        name="reduce",
        out_shape=(
            jax.ShapeDtypeStruct(src.shape, bf),
            jax.ShapeDtypeStruct((4, 112, width), bf),
            jax.ShapeDtypeStruct((4, 48, width), bf),
        ),
        in_specs=[anywhere] * 3,
        out_specs=[anywhere] * 3,
        scratch_shapes=[
            pltpu.VMEM((4, 48, width), bf),
            pltpu.VMEM((4, 48, width), bf),
            pltpu.VMEM((4, 48, width), bf),
            pltpu.VMEM((48, width), bf),
            pltpu.VMEM((4, 48, width), bf),
            pltpu.VMEM((4, 4, 112, width), bf),
            pltpu.VMEM((4, 112, width), bf),
            pltpu.VMEM((4, 112, width), bf),
            pltpu.VMEM((112, width), bf),
            pltpu.VMEM((4, 48, width), bf),
            pltpu.VMEM((4, 112, width), bf),
            dma((5,)), dma((7,)), dma((8,)), dma, dma, dma((3,)), dma((4,)), dma, dma((4,)),
            dma((3,)), dma, dma((3,)), dma((4,)), dma((3,)), dma((4,)), dma((3,)), dma((4,)),
        ],
        compiler_params=pltpu.CompilerParams(
            collective_id=4, has_side_effects=True, vmem_limit_bytes=BIG
        ),
    )(src, gq, pr)


def finish_kernel(
    place, layer_in, in_0, in_1, grad_one, w, p_in, q_in,
    layer_out, out, g_q, g_k, g_v, g_o, g_in, g_up, rows_out, inner_out, wq, held, sems,
):
    seqs, rows, width = grad_one.shape
    span = 96
    z = place[0]
    c = place[1]
    load = pltpu.make_async_copy(layer_in, held, sems.at[0])
    load.start()
    for i in range(3):
        for g in range(8):
            wq[i, 48 * g : 48 * g + 48, :] = w[0, g % 2, g // 2, 48 * i : 48 * i + 48, :]
    for s in range(seqs):
        total = grad_one[s]
        for i in range(3):
            turned = jnp.concatenate(
                [
                    ref[2 * zz + s, i * count : (i + 1) * count, :]
                    for zz in range(4)
                    for ref, count in ((in_0, in_0.shape[1] // 3), (in_1, in_1.shape[1] // 3))
                ],
                axis=0,
            )
            back = turned.astype(jnp.float32).T.astype(jnp.bfloat16)
            total = total + lax.dot_general(
                back, wq[i], (((1,), (1,)), ((), ())), preferred_element_type=jnp.float32
            )
        out[s] = total.astype(jnp.bfloat16)
    load.wait()
    store = pltpu.make_async_copy(held, layer_out, sems.at[1])
    store.start()
    wide = [q_in[zz].astype(jnp.float32) for zz in range(4)]
    for i, ref in enumerate((g_q, g_k, g_v)):
        ref[...] = jnp.concatenate([v[:, i * span : (i + 1) * span] for v in wide], axis=1)
    sums = p_in[3, 96:112, :]
    pick = jnp.where(
        iota((width, 48), 0) == 48 * (2 * z + c) + iota((width, 48), 1), 1.0, 0.0
    ).astype(jnp.bfloat16)
    rows_out[8:24, :] = dot(sums, pick)
    both = q_in[z].astype(jnp.float32)[:, 3 * span :].T
    rows_out[0:8, :] = both[0:8, :]
    pick = jnp.where(
        iota((width, 192), 0) == 192 * c + iota((width, 192), 1), 1.0, 0.0
    ).astype(jnp.bfloat16)
    inner = dot(sums, pick)
    inner_out[...] = jnp.sum(
        jnp.where(iota((16, 192), 0) == 6 + z, inner, 0.0), axis=0, keepdims=True
    )
    g_o[...] = p_in[0, 0:48, :].astype(jnp.float32)
    g_in[:, 0:384] = p_in[0, 48:96, :].astype(jnp.float32)
    g_in[:, 384:768] = p_in[1, 0:48, :].astype(jnp.float32)
    g_in[:, 768:1152] = p_in[1, 48:96, :].astype(jnp.float32)
    g_in[:, 1152:1536] = p_in[2, 0:48, :].astype(jnp.float32)
    g_up[0:16, :] = p_in[0, 96:112, :].astype(jnp.float32)
    g_up[16:32, :] = p_in[1, 96:112, :].astype(jnp.float32)
    g_up[32:96, :] = p_in[2, 48:112, :].astype(jnp.float32)
    g_up[96:192, :] = p_in[3, 0:96, :].astype(jnp.float32)
    store.wait()


def finish(place, layer_in, in_0, in_1, grad_one, w, p_in, q_in):
    seqs, rows, width = grad_one.shape
    vm = pl.BlockSpec(memory_space=pltpu.VMEM)
    sm = pl.BlockSpec(memory_space=pltpu.SMEM)
    bf, f4 = jnp.bfloat16, jnp.float32
    shapes = ((48, width),) * 4 + ((48, 4 * width), (192, width), (24, 48), (1, 192))
    return pl.pallas_call(
        finish_kernel,
        name="finish",
        grid=(1,),
        out_shape=(jax.ShapeDtypeStruct((seqs, rows, width), bf),) * 2
        + tuple(jax.ShapeDtypeStruct(shape, f4) for shape in shapes),
        in_specs=[
            sm, pl.BlockSpec(memory_space=pltpu.HBM), whole_spec(in_0), whole_spec(in_1), whole_spec(grad_one), quarter_spec(w, 0), whole_spec(p_in), whole_spec(q_in)
        ],
        out_specs=[pl.BlockSpec(memory_space=pltpu.HBM), whole_spec(grad_one)]
        + [pl.BlockSpec(shape, functools.partial(zeros_for, len(shape))) for shape in shapes],
        scratch_shapes=[
            pltpu.VMEM((3, width, width), bf),
            pltpu.VMEM((seqs, rows, width), bf),
            pltpu.SemaphoreType.DMA((2,)),
        ],
        compiler_params=pltpu.CompilerParams(vmem_limit_bytes=BIG),
    )(place, layer_in, in_0, in_1, grad_one, w, p_in, q_in)


def line_of_chips(
    tokens, segment_ids, out_grad, query_weight, key_weight, value_weight, output_weight,
    inner_weight, outer_weight, query_bias, value_bias, output_bias, inner_bias, outer_bias,
    first_gain, first_shift, second_gain, second_shift,
):
    bf = jnp.bfloat16
    width = tokens.shape[2]
    g = lax.axis_index("grp")
    z, c = lax.div(g, 2), lax.rem(g, 2)
    place = jnp.stack([z, c]).astype(jnp.int32)
    weights = (query_weight, key_weight, value_weight, output_weight, inner_weight, outer_weight)
    vectors = jnp.concatenate(
        [
            v[None]
            for v in (
                query_bias, value_bias, output_bias, outer_bias,
                first_gain, first_shift, second_gain, second_shift,
            )
        ],
        axis=0,
    )
    x, w, small, kv, qh, kt, vt, q1, norms = gather(
        tokens, weights, vectors, inner_bias[None], segment_ids
    )
    ctx, ctx32, tail, spans = attend(place, kv, qh, vt, small, norms)
    layer_out, grad_one, gctx_in, pr = middle(ctx, tokens, out_grad, w, small)
    back = functools.partial(
        attend_back, place=place, spans=spans, x=x, qh=qh, tail=tail, kv=kv, kt=kt, q1=q1,
        gctx=gctx_in, ctx32=ctx32,
    )
    parts_0, grads_0 = back(2, 0)
    in_0 = lax.all_to_all(parts_0, "grp", 0, 0, tiled=True)
    parts_1, gq = back(1, 2, grads=grads_0)
    in_1, p_in, q_in = reduce_all(parts_1, gq, pr)
    layer_out, input_grad, g_q, g_k, g_v, g_o, g_in, g_up, rows, inner_row = finish(
        place, layer_out, in_0, in_1, grad_one, w, p_in, q_in
    )
    return (
        layer_out, input_grad, g_q, g_k, g_v, g_o, g_in, g_up,
        rows[0], rows[1], rows[8], inner_row[0], rows[9], rows[10], rows[11], rows[12], rows[13],
    )


def solution(mesh):
    in_specs = (
        P("rep", "grp", None),
        P("rep", "grp"),
        P("rep", "grp", None),
        P("grp", None),
        P("grp", None),
        P("grp", None),
        P("grp", None),
        P("grp", None),
        P("grp", None),
        P("grp"),
        P("grp"),
        P("grp"),
        P("grp"),
        P("grp"),
        P("grp"),
        P("grp"),
        P("grp"),
        P("grp"),
    )
    out_specs = (
        P("rep", "grp", None),
        P("rep", "grp", None),
        P("grp", None),
        P("grp", None),
        P("grp", None),
        P("grp", None),
        P("grp", None),
        P("grp", None),
        P("grp"),
        P("grp"),
        P("grp"),
        P("grp"),
        P("grp"),
        P("grp"),
        P("grp"),
        P("grp"),
        P("grp"),
    )
    whole_line = mesh.shape["grp"] == 8 and mesh.shape["rep"] == 4
    return jax.shard_map(
        line_of_chips if whole_line else on_device, mesh=mesh, in_specs=in_specs, out_specs=out_specs, check_vma=False
    )
```

```python
import functools
from functools import reduce

import jax
import jax.numpy as jnp
from jax import lax
from jax.experimental import pallas as pl
from jax.experimental.pallas import tpu as pltpu
from jax.sharding import PartitionSpec as P

H = 12
MICRO = 2
SEQ_MB = 1


norm_epsilon = 1e-05
masked_score = -1000000000.0


def layer_norm(inputs, norm_gain, norm_shift):
    center = inputs - jnp.mean(inputs, axis=-1, keepdims=True)
    spread = jnp.mean(center * center, axis=-1, keepdims=True)
    return center * lax.rsqrt(spread + norm_epsilon) * norm_gain + norm_shift


def exact_gelu(inputs):
    return jax.nn.gelu(inputs, approximate=False)


def times_transpose(left, right):
    return lax.dot_general(
        left, right, (((1,), (1,)), ((), ())), preferred_element_type=jnp.float32
    )


def transpose_times(left, right):
    return lax.dot_general(
        left, right, (((0,), (0,)), ((), ())), preferred_element_type=jnp.float32
    )


def column_total(inputs):
    return jnp.sum(inputs.astype(jnp.float32), axis=0)


def masked_scores(query_group, key_group, same_doc, score_scale):
    scores = (
        jnp.einsum("bqhd,bkhd->bhqk", query_group, key_group, preferred_element_type=jnp.float32)
        * score_scale
    )
    return jnp.where(same_doc[:, None], scores, masked_score)


def group_forward(query_group, key_group, value_group, same_doc, score_scale):
    scores = masked_scores(query_group, key_group, same_doc, score_scale)
    highest = jnp.max(scores, axis=-1, keepdims=True)
    log_total = highest + jnp.log(jnp.sum(jnp.exp(scores - highest), axis=-1, keepdims=True))
    weights_low = jnp.exp(scores - log_total).astype(jnp.bfloat16)
    context = jnp.einsum(
        "bhqk,bkhd->bqhd", weights_low, value_group, preferred_element_type=jnp.float32
    )
    return (context.astype(jnp.bfloat16), log_total)


def group_backward(
    query_group, key_group, value_group, same_doc, log_total, grad_context, score_scale
):
    attn_weights = jnp.exp(masked_scores(query_group, key_group, same_doc, score_scale) - log_total)
    weights_low = attn_weights.astype(jnp.bfloat16)
    grad_weights = jnp.einsum(
        "bqhd,bkhd->bhqk", grad_context, value_group, preferred_element_type=jnp.float32
    )
    centre = jnp.sum(attn_weights * grad_weights, axis=-1, keepdims=True)
    grad_scores = (attn_weights * (grad_weights - centre)).astype(jnp.bfloat16)
    grad_query = jnp.einsum(
        "bhqk,bkhd->bqhd", grad_scores, key_group, preferred_element_type=jnp.float32
    )
    grad_query = (grad_query * score_scale).astype(jnp.bfloat16)
    grad_key = (
        jnp.einsum("bhqk,bqhd->bkhd", grad_scores, query_group, preferred_element_type=jnp.float32)
        * score_scale
    )
    grad_value = jnp.einsum(
        "bhqk,bqhd->bkhd", weights_low, grad_context, preferred_element_type=jnp.float32
    )
    return (grad_query, grad_key, grad_value)


def merge_groups(stacked, row_total, model_width):
    return jnp.moveaxis(stacked, 0, 2).reshape(row_total, model_width)


def gradient_terms(
    token_rows,
    context_rows,
    hidden_rows,
    active_rows,
    grad_queries,
    grad_keys,
    grad_values,
    grad_attention,
    grad_inner,
    grad_feed,
    norm_grads,
):
    return (
        transpose_times(token_rows, grad_queries),
        transpose_times(token_rows, grad_keys),
        transpose_times(token_rows, grad_values),
        transpose_times(context_rows, grad_attention),
        transpose_times(hidden_rows, grad_inner),
        transpose_times(active_rows, grad_feed),
        column_total(grad_queries),
        column_total(grad_values),
        column_total(grad_attention),
        column_total(grad_inner),
        column_total(grad_feed),
        norm_grads[0],
        norm_grads[1],
        norm_grads[2],
        norm_grads[3],
    )


def on_device(
    tokens,
    segment_ids,
    out_grad,
    query_weight,
    key_weight,
    value_weight,
    output_weight,
    inner_weight,
    outer_weight,
    query_bias,
    value_bias,
    output_bias,
    inner_bias,
    outer_bias,
    first_gain,
    first_shift,
    second_gain,
    second_shift,
):
    row_count = tokens.shape[1]
    model_width = tokens.shape[2]
    head_count = H
    head_size = model_width // head_count
    per_group = max(1, min(head_count, 128 // head_size))
    group_width = per_group * head_size
    group_count = head_count // per_group
    score_scale = head_size ** (-0.5)
    seq_count = SEQ_MB
    flat_rows = seq_count * row_count
    all_segments = lax.all_gather(segment_ids, "grp", axis=1, tiled=True)
    outputs = []
    input_grads = []
    shares_list = []
    for batch_index in range(MICRO):
        offset = batch_index * seq_count
        local_tokens = tokens[offset : offset + seq_count]
        flat_tokens = local_tokens.reshape(flat_rows, model_width)
        gathered = (
            lax.all_gather(query_weight, "grp", axis=0, tiled=True),
            lax.all_gather(key_weight, "grp", axis=0, tiled=True),
            lax.all_gather(value_weight, "grp", axis=0, tiled=True),
            lax.all_gather(output_weight, "grp", axis=0, tiled=True),
            lax.all_gather(inner_weight, "grp", axis=0, tiled=True),
            lax.all_gather(outer_weight, "grp", axis=0, tiled=True),
            lax.all_gather(query_bias, "grp", axis=0, tiled=True),
            lax.all_gather(value_bias, "grp", axis=0, tiled=True),
            lax.all_gather(output_bias, "grp", axis=0, tiled=True),
            lax.all_gather(inner_bias, "grp", axis=0, tiled=True),
            lax.all_gather(outer_bias, "grp", axis=0, tiled=True),
            lax.all_gather(first_gain, "grp", axis=0, tiled=True),
            lax.all_gather(first_shift, "grp", axis=0, tiled=True),
            lax.all_gather(second_gain, "grp", axis=0, tiled=True),
            lax.all_gather(second_shift, "grp", axis=0, tiled=True),
        )
        full_query, full_key, full_value, full_output, full_inner, full_outer = gathered[:6]
        (
            bias_query,
            bias_value,
            bias_output,
            bias_inner,
            bias_outer,
            gain_first,
            shift_first,
            gain_second,
            shift_second,
        ) = [vector.astype(jnp.float32) for vector in gathered[6:]]
        queries = (
            jnp.dot(flat_tokens, full_query, preferred_element_type=jnp.float32) + bias_query
        ).astype(jnp.bfloat16)
        key_rows = jnp.dot(flat_tokens, full_key, preferred_element_type=jnp.float32).astype(
            jnp.bfloat16
        )
        value_rows = (
            jnp.dot(flat_tokens, full_value, preferred_element_type=jnp.float32) + bias_value
        ).astype(jnp.bfloat16)
        key_split = key_rows.reshape(seq_count, row_count, model_width)
        value_split = value_rows.reshape(seq_count, row_count, model_width)
        key_all, value_all = (
            lax.all_gather(key_split, "grp", axis=1, tiled=True),
            lax.all_gather(value_split, "grp", axis=1, tiled=True),
        )
        length = key_all.shape[1]
        local_segments = segment_ids[offset : offset + seq_count]
        far_segments = all_segments[offset : offset + seq_count]
        same_doc = local_segments[:, :, None] == far_segments[:, None, :]
        query_split = queries.reshape(seq_count, row_count, model_width)

        def slice_group(array, group_index):
            piece = lax.dynamic_slice_in_dim(array, group_index * group_width, group_width, 2)
            return piece.reshape(array.shape[0], array.shape[1], per_group, head_size)

        def forward_group(group_index):
            context, log_total = group_forward(
                slice_group(query_split, group_index),
                slice_group(key_all, group_index),
                slice_group(value_all, group_index),
                same_doc,
                score_scale,
            )
            return (context.reshape(seq_count, row_count, group_width), log_total)

        context_groups, log_totals = lax.map(forward_group, jnp.arange(group_count))
        context_rows = merge_groups(context_groups, flat_rows, model_width)
        attention = (
            jnp.dot(context_rows, full_output, preferred_element_type=jnp.float32) + bias_output
        )
        residual_one = flat_tokens.astype(jnp.float32) + attention
        hidden_one, norm_one_pullback = jax.vjp(layer_norm, residual_one, gain_first, shift_first)
        hidden_low = hidden_one.astype(jnp.bfloat16)
        inner_pre = jnp.dot(hidden_low, full_inner, preferred_element_type=jnp.float32) + bias_inner
        activation, gelu_pullback = jax.vjp(exact_gelu, inner_pre)
        active_low = activation.astype(jnp.bfloat16)
        feed = jnp.dot(active_low, full_outer, preferred_element_type=jnp.float32) + bias_outer
        output_rows, norm_two_pullback = jax.vjp(
            layer_norm, hidden_one + feed, gain_second, shift_second
        )
        outputs.append(output_rows.astype(jnp.bfloat16).reshape(seq_count, row_count, model_width))
        cotangent = (
            out_grad[offset : offset + seq_count]
            .reshape(flat_rows, model_width)
            .astype(jnp.float32)
        )
        grad_two, grad_gain_two, grad_shift_two = norm_two_pullback(cotangent)
        grad_feed = grad_two.astype(jnp.bfloat16)
        grad_active = times_transpose(grad_feed, full_outer)
        grad_inner = gelu_pullback(grad_active)[0].astype(jnp.bfloat16)
        grad_hidden = grad_two + times_transpose(grad_inner, full_inner)
        grad_one, grad_gain_one, grad_shift_one = norm_one_pullback(grad_hidden)
        grad_attention = grad_one.astype(jnp.bfloat16)
        grad_context = times_transpose(grad_attention, full_output).astype(jnp.bfloat16)
        grad_context = grad_context.reshape(seq_count, row_count, model_width)

        def backward_group(pieces):
            group_index, log_total = pieces
            grad_query, grad_key, grad_value = group_backward(
                slice_group(query_split, group_index),
                slice_group(key_all, group_index),
                slice_group(value_all, group_index),
                same_doc,
                log_total,
                slice_group(grad_context, group_index),
                score_scale,
            )
            return (
                grad_query.reshape(seq_count, row_count, group_width),
                grad_key.reshape(seq_count, length, group_width),
                grad_value.reshape(seq_count, length, group_width),
            )

        query_groups, key_groups, value_groups = lax.map(
            backward_group, (jnp.arange(group_count), log_totals)
        )
        key_owned, value_owned = (
            lax.psum_scatter(key_groups, "grp", scatter_dimension=2, tiled=True),
            lax.psum_scatter(value_groups, "grp", scatter_dimension=2, tiled=True),
        )
        grad_keys = merge_groups(key_owned, flat_rows, model_width).astype(jnp.bfloat16)
        grad_values = merge_groups(value_owned, flat_rows, model_width).astype(jnp.bfloat16)
        grad_queries = merge_groups(query_groups, flat_rows, model_width)
        grad_tokens = (
            grad_one
            + times_transpose(grad_queries, full_query)
            + times_transpose(grad_keys, full_key)
            + times_transpose(grad_values, full_value)
        )
        input_grads.append(
            grad_tokens.astype(jnp.bfloat16).reshape(seq_count, row_count, model_width)
        )
        norm_grads = (grad_gain_one, grad_shift_one, grad_gain_two, grad_shift_two)
        terms = gradient_terms(
            flat_tokens,
            context_rows,
            hidden_low,
            active_low,
            grad_queries,
            grad_keys,
            grad_values,
            grad_attention,
            grad_inner,
            grad_feed,
            norm_grads,
        )
        shares = (
            lax.psum_scatter(terms[0], "grp", scatter_dimension=0, tiled=True),
            lax.psum_scatter(terms[1], "grp", scatter_dimension=0, tiled=True),
            lax.psum_scatter(terms[2], "grp", scatter_dimension=0, tiled=True),
            lax.psum_scatter(terms[3], "grp", scatter_dimension=0, tiled=True),
            lax.psum_scatter(terms[4], "grp", scatter_dimension=0, tiled=True),
            lax.psum_scatter(terms[5], "grp", scatter_dimension=0, tiled=True),
            lax.psum_scatter(terms[6], "grp", scatter_dimension=0, tiled=True),
            lax.psum_scatter(terms[7], "grp", scatter_dimension=0, tiled=True),
            lax.psum_scatter(terms[8], "grp", scatter_dimension=0, tiled=True),
            lax.psum_scatter(terms[9], "grp", scatter_dimension=0, tiled=True),
            lax.psum_scatter(terms[10], "grp", scatter_dimension=0, tiled=True),
            lax.psum_scatter(terms[11], "grp", scatter_dimension=0, tiled=True),
            lax.psum_scatter(terms[12], "grp", scatter_dimension=0, tiled=True),
            lax.psum_scatter(terms[13], "grp", scatter_dimension=0, tiled=True),
            lax.psum_scatter(terms[14], "grp", scatter_dimension=0, tiled=True),
        )
        shares_list.append(shares)
    owned = reduce(
        lambda left_part, right_part: jax.tree.map(jnp.add, left_part, right_part), shares_list
    )
    summed = (
        lax.psum(owned[0].astype(jnp.bfloat16), "rep").astype(jnp.float32),
        lax.psum(owned[1].astype(jnp.bfloat16), "rep").astype(jnp.float32),
        lax.psum(owned[2].astype(jnp.bfloat16), "rep").astype(jnp.float32),
        lax.psum(owned[3].astype(jnp.bfloat16), "rep").astype(jnp.float32),
        lax.psum(owned[4].astype(jnp.bfloat16), "rep").astype(jnp.float32),
        lax.psum(owned[5].astype(jnp.bfloat16), "rep").astype(jnp.float32),
        lax.psum(owned[6].astype(jnp.bfloat16), "rep").astype(jnp.float32),
        lax.psum(owned[7].astype(jnp.bfloat16), "rep").astype(jnp.float32),
        lax.psum(owned[8].astype(jnp.bfloat16), "rep").astype(jnp.float32),
        lax.psum(owned[9].astype(jnp.bfloat16), "rep").astype(jnp.float32),
        lax.psum(owned[10].astype(jnp.bfloat16), "rep").astype(jnp.float32),
        lax.psum(owned[11].astype(jnp.bfloat16), "rep").astype(jnp.float32),
        lax.psum(owned[12].astype(jnp.bfloat16), "rep").astype(jnp.float32),
        lax.psum(owned[13].astype(jnp.bfloat16), "rep").astype(jnp.float32),
        lax.psum(owned[14].astype(jnp.bfloat16), "rep").astype(jnp.float32),
    )
    return (
        jnp.concatenate(outputs, axis=0),
        jnp.concatenate(input_grads, axis=0),
        summed[0],
        summed[1],
        summed[2],
        summed[3],
        summed[4],
        summed[5],
        summed[6],
        summed[7],
        summed[8],
        summed[9],
        summed[10],
        summed[11],
        summed[12],
        summed[13],
        summed[14],
    )


HEAD = 32
LANES = 128
QB = 256
AWAY = 2.0 ** 100
LIMIT = 100.0
LONG = 17
MESH = pl.DeviceIdType.MESH
BIG = 62 * 1024 * 1024
LOG2E = 1.4426950408889634


def halves(value):
    first = value.astype(jnp.bfloat16).astype(jnp.float32)
    rest = value - first
    second = rest.astype(jnp.bfloat16).astype(jnp.float32)
    third = (rest - second).astype(jnp.bfloat16).astype(jnp.float32)
    return first, second, third


def dot(left, right):
    return jnp.dot(left, right, preferred_element_type=jnp.float32)


def zeros_for(rank, *grid):
    return (0,) * rank


def whole_spec(array):
    return pl.BlockSpec(array.shape, functools.partial(zeros_for, array.ndim), pipeline_mode=pl.Buffered(1))


def quarter_spec(w, i):
    return pl.BlockSpec((1,) + w.shape[1:], lambda *grid: (i, 0, 0, 0, 0), pipeline_mode=pl.Buffered(1))


def iota(shape, dim):
    return lax.broadcasted_iota(jnp.int32, shape, dim)


def where_am_i():
    r = lax.axis_index("rep")
    g = lax.axis_index("grp")
    return r, g, lax.div(g, 2), lax.rem(g, 2)


def remote(src, dst, send, recv, r, g):
    return pltpu.make_async_remote_copy(
        src_ref=src, dst_ref=dst, send_sem=send, recv_sem=recv, device_id=(r, g), device_id_type=MESH
    )


def greet(r, g, reps, group):
    barrier = pltpu.get_barrier_semaphore()
    for d in range(1, group):
        pl.semaphore_signal(barrier, inc=1, device_id=(r, lax.rem(g + d, group)), device_id_type=MESH)
    for d in range(1, reps):
        pl.semaphore_signal(barrier, inc=1, device_id=(lax.rem(r + d, reps), g), device_id_type=MESH)
    pl.semaphore_wait(barrier, group + reps - 2)


def vectors_of(small):
    return jnp.concatenate([small[g, 0:8, 0:48].astype(jnp.float32) for g in range(8)], axis=1)


def chip_at(z, i):
    order = ((0, 1, 2, 3), (1, 0, 2, 3), (2, 1, 3, 0), (3, 2, 1, 0))
    chip = jnp.int32(0)
    for a, row in enumerate(order):
        for k, value in enumerate(row):
            chip = jnp.where((z == a) & (i == k), value, chip)
    return chip


def gather_kernel(
    tok, wq, wk, wv, wo, wi, wu, vectors, inner, seg,
    x_out, w_out, s_out, kv_out, qh_out, kt_out, vt_out, q1_out, norms,
    small, x, kv, qh, kt, vt, q1, w0, smalls_in, wrow, wtr, mine,
    lsem, xsem, psems, tsend, trecv, psend, wsend1, wrecv1, wsend2, wrecv2, wsend3, wrecv3, ssend, srecv,
):
    r, g, z, c = where_am_i()
    reps, chips = 4, 4
    p = 2 * z + 1 - c
    heads = kv.shape[0]
    _, rows, width = x.shape
    small[0:8, :] = jnp.concatenate(
        [vectors[...].astype(jnp.float32), jnp.zeros((8, rows - 48), jnp.float32)], axis=1
    ).astype(jnp.bfloat16)
    small[8:16, :] = jnp.concatenate(
        [
            jnp.concatenate([inner[...].astype(jnp.float32), jnp.zeros((1, rows - 192), jnp.float32)], axis=1),
            seg[...].astype(jnp.float32),
            jnp.zeros((5, rows), jnp.float32),
        ],
        axis=0,
    ).astype(jnp.bfloat16)
    greet(r, g, reps, 2 * chips)
    slab = [wi.at[:, pl.ds(j * width, width)] for j in range(4)]
    quarters = (
        ((wq, 0, 48), (wk, 48, 48), (wv, 96, 48)),
        ((wo, 0, 48), (slab[0], 48, 48), (slab[1], 96, 48)),
        ((slab[2], 0, 48), (slab[3], 48, 48), (wu.at[pl.ds(0, 48), :], 96, 48)),
        ((wu.at[pl.ds(48, 144), :], 0, 144),),
    )
    swap = remote(tok.at[1 - c], x.at[g], psend, trecv.at[g], r, p)
    swap.start()
    own_x = pltpu.make_async_copy(tok.at[c], x.at[g], lsem.at[0])
    own_x.start()
    def pass_on(b, way, src=None):
        to = g + 2 if way == 0 else g - 2
        src = x.at[b] if src is None else src
        return remote(src, x.at[b], tsend.at[way, b], trecv.at[b], r, to)

    def forward(b, way, src=None):
        ok = z < chips - 1 if way == 0 else z > 0

        @pl.when(ok)
        def _():
            pass_on(b, way, src).start()

    def keep(b):
        return pltpu.make_async_copy(x.at[b], x_out.at[b], xsem.at[b])

    def arrived(b):
        remote(x.at[b], x.at[b], tsend.at[0, b], trecv.at[b], r, p).wait_recv()

    forward(g, 0, tok.at[c])
    forward(g, 1, tok.at[c])
    arrived(p)
    forward(p, 0)
    forward(p, 1)
    keep(p).start()
    for i, pieces in enumerate(quarters):
        @pl.when(r == i)
        def _():
            copies = [
                pltpu.make_async_copy(ref, mine.at[pl.ds(row, count), :], lsem.at[3 + k])
                for k, (ref, row, count) in enumerate(pieces)
            ]
            for copy in copies:
                copy.start()
            for copy in copies:
                copy.wait()

    own_w = pltpu.make_async_copy(mine, w_out.at[r, c, z], lsem.at[1])
    own_w.start()
    own_s = pltpu.make_async_copy(small, smalls_in.at[g], lsem.at[2])
    own_s.start()
    first = []
    for d in range(1, chips):
        zz = lax.rem(z + d, chips)
        copy = remote(mine, w_out.at[r, c, z], wsend1.at[d - 1], wrecv1.at[z], r, 2 * zz + c)
        copy.start()
        first.append(copy)
    smalls = []
    for d in range(1, 2 * chips):
        copy = remote(small, smalls_in.at[g], ssend.at[d - 1], srecv.at[g], r, lax.rem(g + d, 2 * chips))
        copy.start()
        smalls.append(copy)
    own_x.wait()
    keep(g).start()

    def tokens_from(d):
        for k in range(2):
            @pl.when(z >= d)
            def _():
                b = 2 * (z - d) + (c if k == 0 else 1 - c)
                arrived(b)
                forward(b, 0)
                keep(b).start()

            @pl.when(z + d < chips)
            def _():
                b = 2 * (z + d) + (c if k == 0 else 1 - c)
                arrived(b)
                forward(b, 1)
                keep(b).start()

    tokens_from(1)
    for d in range(1, chips):
        zz = lax.rem(z + d, chips)
        remote(mine, w_out.at[r, c, zz], wsend1.at[0], wrecv1.at[zz], r, p).wait_recv()
    own_w.wait()
    second = []
    for d in range(1, reps):
        copy = remote(
            w_out.at[r, c], w_out.at[r, c], wsend2.at[d - 1], wrecv2.at[r], lax.rem(r + d, reps), g
        )
        copy.start()
        second.append(copy)
    third = [remote(w_out.at[r, c], w_out.at[r, c], wsend3.at[r], wrecv3.at[r], r, p)]
    third[0].start()
    tokens_from(2)
    for d in range(1, reps):
        q = lax.rem(r + d, reps)
        remote(w_out.at[q, c], w_out.at[q, c], wsend2.at[0], wrecv2.at[q], r, p).wait_recv()
        copy = remote(w_out.at[q, c], w_out.at[q, c], wsend3.at[q], wrecv3.at[q], r, p)
        copy.start()
        third.append(copy)
    for q in range(reps):
        remote(w_out.at[q, 1 - c], w_out.at[q, 1 - c], wsend3.at[q], wrecv3.at[q], r, p).wait_recv()
    load_w = pltpu.make_async_copy(w_out.at[0], w0, lsem.at[1])
    load_w.start()
    for d in range(1, 2 * chips):
        b = lax.rem(g + d, 2 * chips)
        remote(small, smalls_in.at[b], ssend.at[0], srecv.at[b], r, p).wait_recv()
    own_s.wait()
    keep_s = pltpu.make_async_copy(smalls_in, s_out, lsem.at[2])
    keep_s.start()
    load_w.wait()

    span = heads * HEAD
    bias = vectors_of(smalls_in).astype(jnp.bfloat16)
    full = [
        jnp.concatenate([w0[i % 2, i // 2, 48 * k : 48 * k + 48, :] for i in range(8)], axis=0)
        for k in range(3)
    ]
    lane = iota((width, heads * LANES), 1)
    head, lane_in = lax.div(lane, LANES), lax.rem(lane, LANES)
    column = span * z + head * HEAD + lax.rem(lane_in, HEAD)
    hit = iota((width, heads * LANES), 0) == column
    pick_k = jnp.where(hit & (lane_in < 64), 1.0, 0.0).astype(jnp.bfloat16)
    pick_v = jnp.where(hit & (lane_in >= 64) & (lane_in < 96), 1.0, 0.0).astype(jnp.bfloat16)
    wrow[...] = (dot(full[1], pick_k) + dot(full[2], pick_v)).astype(jnp.bfloat16)
    row_kv = dot(bias[1:2, :], pick_v)
    pick_t = jnp.where(
        iota((span, width), 1) == span * z + iota((span, width), 0), 1.0, 0.0
    ).astype(jnp.bfloat16)

    def by_rows(left, right):
        return lax.dot_general(
            left, right, (((1,), (1,)), ((), ())), preferred_element_type=jnp.float32
        )

    for k in range(3):
        wtr[k] = by_rows(pick_t, full[k]).astype(jnp.bfloat16)
    column_bias = by_rows(pick_t, bias)
    col_q, col_v = column_bias[:, 0:1], column_bias[:, 1:2]
    scale = (HEAD ** -0.5) * LOG2E
    one_lane = lax.rem(iota((1, heads * LANES), 1), LANES)
    row_kv = row_kv + jnp.where((one_lane >= 104) & (one_lane < 107), 1.0, 0.0)
    one = jnp.where(iota((16, rows), 0) == 0, 1.0, 0.0).astype(jnp.bfloat16)

    def stores(b):
        cols = pl.ds(pl.multiple_of(b * rows, rows), rows)
        return [
            pltpu.make_async_copy(kv.at[:, cols, :], kv_out.at[:, cols, :], psems.at[0, b])
        ] + [
            pltpu.make_async_copy(ref.at[:, :, cols], out.at[:, :, cols], psems.at[1 + i, b])
            for i, (ref, out) in enumerate(((qh, qh_out), (kt, kt_out), (vt, vt_out), (q1, q1_out)))
        ]

    def project(i, most):
        half = lax.rem(i, 2)
        b = 2 * chip_at(z, lax.div(i, 2)) + c + half - 2 * c * half
        xb = x[b]
        two = smalls_in[b, 8:16, :].astype(jnp.float32)
        ids = jnp.where(c == 0, two[1:2], two[2:3])
        same = jnp.where(iota((8, rows), 0).astype(jnp.float32) == ids, 1.0, 0.0)
        hot = jnp.concatenate(
            [jnp.zeros((96, rows), jnp.float32), same, jnp.zeros((24, rows), jnp.float32)], axis=0
        ).T
        cols = pl.ds(pl.multiple_of(b * rows, rows), rows)
        flat = dot(xb, wrow[...]) + row_kv
        for h in range(heads):
            kv[h, cols, :] = (flat[:, h * LANES : (h + 1) * LANES] + hot).astype(jnp.bfloat16)
        q_t = (by_rows(wtr[0], xb) + col_q).astype(jnp.bfloat16)
        k_t = by_rows(wtr[1], xb).astype(jnp.bfloat16)
        v_t = (by_rows(wtr[2], xb) + col_v).astype(jnp.bfloat16)
        q_wide = q_t.astype(jnp.float32) * scale
        k_wide = k_t.astype(jnp.float32)
        q_hi = q_wide.astype(jnp.bfloat16)
        q_lo = (q_wide - q_hi.astype(jnp.float32)).astype(jnp.bfloat16)
        sizes = []
        for n, v in enumerate((q_wide, k_wide)):
            size = most[n]
            for h in range(heads):
                size = jnp.maximum(
                    size, jnp.sum(v[h * HEAD : (h + 1) * HEAD] ** 2, axis=0, keepdims=True)
                )
            sizes.append(size)
        for h in range(heads):
            part = slice(h * HEAD, (h + 1) * HEAD)
            qh[h, 0:32, cols] = q_hi[part]
            qh[h, 32:64, cols] = q_lo[part]
            kt[h, :, cols] = k_t[part]
            q1[h, :, cols] = q_t[part]
            vt[h, 0:32, cols] = v_t[part]
            vt[h, 32:48, cols] = one
        for copy in stores(b):
            copy.start()
        return tuple(sizes)

    zero = jnp.zeros((1, rows), jnp.float32)
    most = lax.fori_loop(0, 6, project, (zero, zero))
    tokens_from(3)
    most = lax.fori_loop(6, 8, project, most)
    norms[0:1, :] = most[0]
    norms[1:2, :] = most[1]

    def settle(b, none):
        keep(b).wait()
        for copy in stores(b):
            copy.wait()
        return none

    swap.wait_send()
    for copy in first + smalls + second + third:
        copy.wait_send()
    for b in range(2 * chips):
        @pl.when((z < chips - 1) & (b < 2 * z + 2))
        def _():
            pass_on(b, 0).wait_send()

        @pl.when((z > 0) & (b >= 2 * z))
        def _():
            pass_on(b, 1).wait_send()

    keep_s.wait()
    lax.fori_loop(0, 2 * chips, settle, 0)


def gather(tokens, weights, vectors, inner, seg):
    dma = pltpu.SemaphoreType.DMA
    anywhere = pl.BlockSpec(memory_space=pltpu.HBM)
    vm = pl.BlockSpec(memory_space=pltpu.VMEM)
    rows, width = tokens.shape[1:]
    bf, f4 = jnp.bfloat16, jnp.float32
    heads, length = 3, 8 * rows
    made = [
        (heads, length, LANES), (heads, 64, length), (heads, HEAD, length), (heads, 48, length), (heads, HEAD, length)
    ]
    return pl.pallas_call(
        gather_kernel,
        name="gather",
        out_shape=(
            jax.ShapeDtypeStruct((8, rows, width), bf),
            jax.ShapeDtypeStruct((4, 2, 4, 144, width), bf),
            jax.ShapeDtypeStruct((8, 16, rows), bf),
        )
        + tuple(jax.ShapeDtypeStruct(shape, bf) for shape in made)
        + (jax.ShapeDtypeStruct((2, rows), f4),),
        in_specs=[anywhere] * 7 + [vm] * 3,
        out_specs=[anywhere] * 8 + [vm],
        scratch_shapes=[
            pltpu.VMEM((16, rows), bf),
            pltpu.VMEM((8, rows, width), bf),
        ]
        + [pltpu.VMEM(shape, bf) for shape in made]
        + [
            pltpu.VMEM((2, 4, 144, width), bf),
            pltpu.VMEM((8, 16, rows), bf),
            pltpu.VMEM((width, heads * LANES), bf),
            pltpu.VMEM((3, heads * HEAD, width), bf),
            pltpu.VMEM((144, width), bf),
            dma((6,)), dma((8,)), dma((5, 8)), dma((2, 8)), dma((8,)), dma, dma((3,)), dma((4,)), dma((3,)), dma((4,)),
            dma((4,)), dma((4,)), dma((7,)), dma((8,)),
        ],
        compiler_params=pltpu.CompilerParams(
            collective_id=1, has_side_effects=True, vmem_limit_bytes=BIG
        ),
    )(tokens, *weights, vectors, inner, seg)


def span_of(starts, q0, docs):
    low = jnp.int32(0)
    high = starts[docs]
    for d in range(docs):
        low = jnp.where(starts[d] <= q0, jnp.maximum(low, starts[d]), low)
        high = jnp.where(starts[d + 1] >= q0 + QB, jnp.minimum(high, starts[d + 1]), high)
    first = lax.div(low, LANES)
    return first, lax.div(high + LANES - 1, LANES) - first


def in_groups(first, count, total, body):
    def at(i):
        return pl.multiple_of(i * LANES, LANES)

    big = count >= LONG - 1

    @pl.when(big)
    def _():
        body(pl.ds(at(jnp.minimum(first, total - LONG)), LONG * LANES))

    first = jnp.where(big, first + LONG, first)
    count = jnp.where(big, jnp.maximum(count - LONG, 0), count)
    many = jnp.maximum(lax.div(count, 4) - 1, 0)

    def group(i, none):
        body(pl.ds(at(first + 4 * i), 4 * LANES))
        return none

    lax.fori_loop(0, many, group, 0)
    left = count - 4 * many
    for k in range(1, 8):
        @pl.when(left == k)
        def _():
            body(pl.ds(at(first + 4 * many), k * LANES))


def attend_kernel(
    place, kv, qh, vt, small, norms, ctx, ctx32, tail_out, spans, qt, acc, tall, seg, starts, sem,
):
    heads, length, _ = kv.shape
    blocks, hw, rows = ctx.shape
    docs = 8
    c = place[1]
    load = pltpu.make_async_copy(qh, qt.at[:, pl.ds(0, 64), :], sem)
    load.start()
    for g in range(8):
        two = small[g, 8:16, :].astype(jnp.float32)
        seg[g : g + 1, :] = jnp.where(c == 0, two[1:2], two[2:3]).astype(jnp.int32)
    ids = seg[...]
    starts[0] = jnp.int32(0)
    for d in range(1, docs):
        starts[d] = jnp.sum(jnp.where(ids < d, 1.0, 0.0)).astype(jnp.int32)
    starts[docs] = jnp.int32(length)

    def far(same):
        return (same - 1.0) * AWAY

    def fill(b, none):
        cols = pl.ds(pl.multiple_of(b * rows, rows), rows)
        same = jnp.where(iota((8, rows), 0) == seg[pl.ds(b, 1), :], 1.0, 0.0)
        low = jnp.concatenate([far(same), jnp.zeros((8, rows), jnp.float32)], axis=0)
        for h in range(heads):
            qt[h, 64:96, cols] = jnp.zeros((32, rows), jnp.bfloat16)
            qt[h, 96:112, cols] = low.astype(jnp.bfloat16)
            qt[h, 112:128, cols] = jnp.zeros((16, rows), jnp.bfloat16)
        return none

    lax.fori_loop(0, blocks, fill, 0)
    bounded = jnp.max(norms[0:1, :]) * jnp.max(norms[1:2, :]) < LIMIT * LIMIT
    load.wait()

    per = rows // QB

    def query_block(b, carry):
        q0 = pl.multiple_of(b * QB, QB)
        first, count = span_of(starts, q0, docs)
        spans[0, b] = first
        spans[1, b] = count
        acc[...] = jnp.zeros_like(acc)

        def key_block(i, tops):
            keys = pl.ds(pl.multiple_of((first + i) * LANES, LANES), LANES)
            s = [dot(kv[h, keys, :], qt[h, :, pl.ds(q0, QB)]) for h in range(heads)]
            new = [jnp.maximum(tops[h], jnp.max(s[h], axis=0, keepdims=True)) for h in range(heads)]
            p = [jnp.exp2(s[h] - new[h]).astype(jnp.bfloat16) for h in range(heads)]
            for h in range(heads):
                acc[h] = acc[h] * jnp.exp2(tops[h] - new[h]) + dot(vt[h, :, keys], p[h])
            return tuple(new)

        def plain_block(keys):
            s = [dot(kv[h, keys, :], qt[h, :, pl.ds(q0, QB)]) for h in range(heads)]
            p = [jnp.exp2(v).astype(jnp.bfloat16) for v in s]
            for h in range(heads):
                acc[h] += dot(vt[h, :, keys], p[h])

        @pl.when(bounded)
        def _():
            in_groups(first, count, length // LANES, plain_block)
            tall[...] = jnp.zeros_like(tall)

        @pl.when(jnp.logical_not(bounded))
        def _():
            lowest = jnp.full((1, QB), -3e38, jnp.float32)
            tops = lax.fori_loop(0, count, key_block, (lowest,) * heads)
            for h in range(heads):
                tall[h] = tops[h]

        g = lax.div(b, per)
        off = pl.multiple_of(lax.rem(b, per) * QB, QB)
        same = jnp.where(iota((8, QB), 0) == seg[pl.ds(g, 1), pl.ds(off, QB)], 1.0, 0.0)
        for h in range(heads):
            total = acc[h, 32:33, :]
            out = acc[h, 0:32, :] / total
            ctx[g, h * HEAD : (h + 1) * HEAD, pl.ds(off, QB)] = out.astype(jnp.bfloat16)
            ctx32[g, h * HEAD : (h + 1) * HEAD, pl.ds(off, QB)] = out
            parts = halves(-(tall[h] + jnp.log2(total)))
            tail = jnp.concatenate([far(same), *parts, jnp.zeros((5, QB), jnp.float32)], axis=0)
            tail_out[h, :, pl.ds(q0, QB)] = tail.astype(jnp.bfloat16)
        return carry

    lax.fori_loop(0, length // QB, query_block, 0)


def attend(place, kv, qh, vt, small, norms):
    heads, length, _ = kv.shape
    blocks, _, rows = small.shape
    sm = pl.BlockSpec(memory_space=pltpu.SMEM)
    anywhere = pl.BlockSpec(memory_space=pltpu.HBM)
    bf, f4 = jnp.bfloat16, jnp.float32
    shapes = (
        jax.ShapeDtypeStruct((blocks, heads * HEAD, rows), bf),
        jax.ShapeDtypeStruct((blocks, heads * HEAD, rows), f4),
        jax.ShapeDtypeStruct((heads, 16, length), bf),
    )
    return pl.pallas_call(
        attend_kernel,
        name="attend",
        grid=(1,),
        out_shape=shapes + (jax.ShapeDtypeStruct((2, length // QB), jnp.int32),),
        in_specs=[sm, whole_spec(kv), anywhere, whole_spec(vt), whole_spec(small), whole_spec(norms)],
        out_specs=[whole_spec(v) for v in shapes] + [sm],
        scratch_shapes=[
            pltpu.VMEM((heads, LANES, length), bf),
            pltpu.VMEM((heads, 48, QB), f4),
            pltpu.VMEM((heads, 1, QB), f4),
            pltpu.VMEM((8, rows), jnp.int32),
            pltpu.SMEM((16,), jnp.int32),
            pltpu.SemaphoreType.DMA,
        ],
        compiler_params=pltpu.CompilerParams(vmem_limit_bytes=BIG),
    )(place, kv, qh, vt, small, norms)


PIECE = 128


def middle_kernel(
    ctx, tok, og, w, small,
    layer_out, grad_one_out, gctx_out, pr,
    wo, wi, wu, gwo, gwi, gwu, sums, inner_sum, ctx_in, gctx, pg, pg_in,
    lsem, send, recv, gsend, grecv, glocal, psend, precv,
):
    seqs, rows, width = tok.shape
    slabs = wi.shape[0]
    pieces = rows // PIECE
    r, g, z, c = where_am_i()
    greet(r, g, 1, 8)

    def fetch(q):
        cols = pl.ds(pl.multiple_of(q * PIECE, PIECE), PIECE)
        for d in range(1, 8):
            to = lax.rem(g + d, 8)
            remote(
                ctx.at[to, :, cols], ctx_in.at[c, z, :, cols], send.at[q, d - 1], recv.at[q, g], r, to
            ).start()

    own = pltpu.make_async_copy(ctx.at[g], ctx_in.at[c, z], lsem)
    own.start()
    fetch(0)
    fetch(1)
    for i in range(8):
        cc, zz = i % 2, i // 2
        wo[48 * i : 48 * i + 48, :] = w[1, cc, zz, 0:48, :]
        wi[0, 48 * i : 48 * i + 48, :] = w[1, cc, zz, 48:96, :]
        wi[1, 48 * i : 48 * i + 48, :] = w[1, cc, zz, 96:144, :]
        wi[2, 48 * i : 48 * i + 48, :] = w[2, cc, zz, 0:48, :]
        wi[3, 48 * i : 48 * i + 48, :] = w[2, cc, zz, 48:96, :]
        wu[zz, 192 * cc : 192 * cc + 48, :] = w[2, cc, zz, 96:144, :]
        wu[zz, 192 * cc + 48 : 192 * cc + 192, :] = w[3, cc, zz, :, :]
    for ref in (gwo, gwi, gwu, sums, inner_sum):
        ref[...] = jnp.zeros_like(ref)
    fetch(2)
    fetch(3)

    vec = vectors_of(small)
    inner_bias = jnp.concatenate(
        [small[i, 8:16, 0:192].astype(jnp.float32)[0:1] for i in range(8)], axis=1
    )
    out_bias, outer_bias = vec[2:3, :], vec[3:4, :]
    gain_one, shift_one = vec[4:5, :], vec[5:6, :]
    gain_two, shift_two = vec[6:7, :], vec[7:8, :]

    def normal(value):
        centre = value - jnp.mean(value, axis=-1, keepdims=True)
        rate = lax.rsqrt(jnp.mean(centre * centre, axis=-1, keepdims=True) + norm_epsilon)
        return centre * rate, rate

    def normal_back(grad, gain, n, rate):
        u = grad * gain
        return rate * (
            u - jnp.mean(u, axis=-1, keepdims=True) - n * jnp.mean(u * n, axis=-1, keepdims=True)
        )

    def total(value):
        return jnp.sum(value, axis=0, keepdims=True)

    def dot_turn(left, right):
        return lax.dot_general(
            left, right, (((1,), (1,)), ((), ())), preferred_element_type=jnp.float32
        )

    def arrived(q, cols):
        for d in range(1, 8):
            b = lax.rem(g + d, 8)
            remote(
                ctx.at[g, :, cols], ctx_in.at[lax.rem(b, 2), lax.div(b, 2), :, cols],
                send.at[q, 0], recv.at[q, b], r, b,
            ).wait_recv()

    def return_piece(q, cols, d):
        to = lax.rem(g + d, 8)
        return remote(
            gctx.at[lax.rem(to, 2), lax.div(to, 2), :, cols], gctx_out.at[g, :, cols],
            gsend.at[q, d - 1], grecv.at[q, g], r, to,
        )

    def keep_piece(q, cols):
        return pltpu.make_async_copy(gctx.at[c, z, :, cols], gctx_out.at[g, :, cols], glocal.at[q])

    own.wait()

    def one(q, carry):
        r0 = pl.multiple_of(q * PIECE, PIECE)
        here = pl.ds(r0, PIECE)
        arrived(q, here)

        def both(ref):
            return jnp.concatenate([ref[s, here, :] for s in range(seqs)], axis=0)

        def split(ref, value):
            for s in range(seqs):
                ref[s, here, :] = value[s * PIECE : (s + 1) * PIECE].astype(ref.dtype)

        ctx_t = jnp.concatenate(
            [jnp.concatenate([ctx_in[s, zz, :, here] for zz in range(4)], axis=0) for s in range(seqs)],
            axis=1,
        )
        context = ctx_t.astype(jnp.float32).T.astype(jnp.bfloat16)
        x = both(tok).astype(jnp.float32)
        n_one, rate_one = normal(x + (dot(context, wo[...]) + out_bias))
        hidden = n_one * gain_one + shift_one
        low = hidden.astype(jnp.bfloat16)
        low_t = hidden.T.astype(jnp.bfloat16)
        feed = jnp.zeros(hidden.shape, jnp.float32)
        slopes, actives = [], []
        for j in range(slabs):
            inner = dot(low, wi[j]) + inner_bias[:, j * width : (j + 1) * width]
            cdf = 0.5 + 0.5 * lax.erf(inner * (0.5 ** 0.5))
            pdf = jnp.exp(inner * inner * -0.5) * 0.3989422804014327
            slopes.append(cdf + inner * pdf)
            active = inner * cdf
            actives.append(active)
            feed = feed + dot(active.astype(jnp.bfloat16), wu[j])
        n_two, rate_two = normal(hidden + (feed + outer_bias))
        split(layer_out, n_two * gain_two + shift_two)
        grad = both(og).astype(jnp.float32)
        grad_two = normal_back(grad, gain_two, n_two, rate_two)
        grad_feed = grad_two.astype(jnp.bfloat16)
        grad_hidden = grad_two
        for j in range(slabs):
            grad_inner = (dot_turn(grad_feed, wu[j]) * slopes[j]).astype(jnp.bfloat16)
            inner_sum[:, j * width : (j + 1) * width] += total(grad_inner.astype(jnp.float32))
            grad_hidden = grad_hidden + dot_turn(grad_inner, wi[j])
            gwi[j] += dot(low_t, grad_inner)
            gwu[j] += dot(actives[j].T.astype(jnp.bfloat16), grad_feed)
        grad_one = normal_back(grad_hidden, gain_one, n_one, rate_one)
        split(grad_one_out, grad_one)
        grad_att = grad_one.astype(jnp.bfloat16)
        back = dot_turn(wo[...], grad_att).astype(jnp.bfloat16)
        for s in range(seqs):
            for zz in range(4):
                gctx[s, zz, :, here] = back[96 * zz : 96 * zz + 96, s * PIECE : (s + 1) * PIECE]
        for d in range(1, 8):
            return_piece(q, here, d).start()
        keep_piece(q, here).start()
        gwo[...] += dot(ctx_t, grad_att)
        sums[0:1, :] += total(grad_att.astype(jnp.float32))
        sums[1:2, :] += total(grad_feed.astype(jnp.float32))
        sums[2:3, :] += total(grad_hidden * n_one)
        sums[3:4, :] += total(grad_hidden)
        sums[4:5, :] += total(grad * n_two)
        sums[5:6, :] += total(grad)
        return carry

    lax.fori_loop(0, pieces, one, 0)
    rows_of_sums = jnp.concatenate(
        [sums[...]]
        + [inner_sum[:, j * width : (j + 1) * width] for j in range(slabs)]
        + [jnp.zeros((6, width), jnp.float32)],
        axis=0,
    ).astype(jnp.bfloat16)
    for i in range(8):
        cc, zz = i % 2, i // 2
        mine = slice(48 * i, 48 * i + 48)
        pg[cc, 0, zz, 0:48, :] = gwo[mine, :].astype(jnp.bfloat16)
        pg[cc, 0, zz, 48:96, :] = gwi[0, mine, :].astype(jnp.bfloat16)
        pg[cc, 1, zz, 0:48, :] = gwi[1, mine, :].astype(jnp.bfloat16)
        pg[cc, 1, zz, 48:96, :] = gwi[2, mine, :].astype(jnp.bfloat16)
        pg[cc, 2, zz, 0:48, :] = gwi[3, mine, :].astype(jnp.bfloat16)
        base = 192 * cc
        pg[cc, 0, zz, 96:112, :] = gwu[zz, base : base + 16, :].astype(jnp.bfloat16)
        pg[cc, 1, zz, 96:112, :] = gwu[zz, base + 16 : base + 32, :].astype(jnp.bfloat16)
        pg[cc, 2, zz, 48:112, :] = gwu[zz, base + 32 : base + 96, :].astype(jnp.bfloat16)
        pg[cc, 3, zz, 0:96, :] = gwu[zz, base + 96 : base + 192, :].astype(jnp.bfloat16)
        pg[cc, 3, zz, 96:112, :] = rows_of_sums
    pair = remote(pg.at[1 - c], pg_in, psend, precv, r, 2 * z + 1 - c)
    pair.start()

    def settle(q, carry):
        cols = pl.ds(pl.multiple_of(q * PIECE, PIECE), PIECE)
        for d in range(1, 8):
            b = lax.rem(g + d, 8)
            remote(
                gctx.at[c, z, :, cols], gctx_out.at[b, :, cols], gsend.at[q, 0], grecv.at[q, b], r, b
            ).wait_recv()
            return_piece(q, cols, d).wait_send()
            to = lax.rem(g + d, 8)
            remote(
                ctx.at[to, :, cols], ctx_in.at[c, z, :, cols], send.at[q, d - 1], recv.at[q, g], r, to
            ).wait_send()
        keep_piece(q, cols).wait()
        return carry

    pair.wait_recv()
    for i in range(4):
        pr[i] = (pg[c, i].astype(jnp.float32) + pg_in[i].astype(jnp.float32)).astype(jnp.bfloat16)
    lax.fori_loop(0, pieces, settle, 0)
    pair.wait_send()


def middle(ctx, tok, og, w, small):
    seqs, rows, width = tok.shape
    vm = pl.BlockSpec(memory_space=pltpu.VMEM)
    anywhere = pl.BlockSpec(memory_space=pltpu.HBM)
    dma = pltpu.SemaphoreType.DMA
    bf, f4 = jnp.bfloat16, jnp.float32
    pieces = rows // PIECE
    return pl.pallas_call(
        middle_kernel,
        name="middle",
        out_shape=(
            jax.ShapeDtypeStruct((seqs, rows, width), bf),
            jax.ShapeDtypeStruct((seqs, rows, width), f4),
            jax.ShapeDtypeStruct(ctx.shape, bf),
            jax.ShapeDtypeStruct((4, 4, 112, width), bf),
        ),
        in_specs=[anywhere] + [vm] * 4,
        out_specs=[vm, vm, anywhere, vm],
        scratch_shapes=[
            pltpu.VMEM((width, width), bf),
            pltpu.VMEM((4, width, width), bf),
            pltpu.VMEM((4, width, width), bf),
            pltpu.VMEM((width, width), f4),
            pltpu.VMEM((4, width, width), f4),
            pltpu.VMEM((4, width, width), f4),
            pltpu.VMEM((6, width), f4),
            pltpu.VMEM((1, 4 * width), f4),
            pltpu.VMEM((2, 4) + ctx.shape[1:], bf),
            pltpu.VMEM((2, 4) + ctx.shape[1:], bf),
            pltpu.VMEM((2, 4, 4, 112, width), bf),
            pltpu.VMEM((4, 4, 112, width), bf),
            dma, dma((pieces, 7)), dma((pieces, 8)), dma((pieces, 7)), dma((pieces, 8)), dma((pieces,)), dma, dma,
        ],
        compiler_params=pltpu.CompilerParams(
            collective_id=2, has_side_effects=True, vmem_limit_bytes=BIG
        ),
    )(ctx, tok, og, w, small)


def attend_back_kernel(
    last, index, place, spans, x_hbm, qh, tail, kv, kt, q1, gctx, ctx32, *refs,
):
    heads = kv.shape[0]
    span = heads * HEAD
    if last:
        grads_in, out, gq, dt, do, acc, dq, qt, x, sems = refs
    else:
        out, grads_out, dt, do, acc, dq, qt, x, sems = refs
    length, width = x.shape
    mine = pl.ds(index * heads, heads)
    loads = [
        pltpu.make_async_copy(qh.at[mine], qt.at[:, pl.ds(0, 64), :], sems.at[0]),
        pltpu.make_async_copy(tail.at[mine], qt.at[:, pl.ds(96, 16), :], sems.at[1]),
        pltpu.make_async_copy(x_hbm, x, sems.at[2]),
    ]
    for load in loads:
        load.start()
    blocks, _, rows = gctx.shape
    z = place[0]
    c = place[1]
    scale = HEAD ** -0.5

    def prepare(g, carry):
        r0 = pl.multiple_of(g * rows, rows)
        cols = pl.ds(r0, rows)
        for h in range(heads):
            part = slice(h * HEAD, (h + 1) * HEAD)
            grad = gctx[g, part, :]
            wide = grad.astype(jnp.float32)
            delta = -jnp.sum(wide * ctx32[g, part, :], axis=0, keepdims=True)
            dt[h, 0:64, cols] = jnp.zeros((64, rows), jnp.bfloat16)
            dt[h, 64:96, cols] = grad
            qt[h, 64:96, cols] = jnp.zeros((32, rows), jnp.bfloat16)
            qt[h, 112:128, cols] = jnp.zeros((16, rows), jnp.bfloat16)
            tail = jnp.concatenate(
                [jnp.zeros((8, rows), jnp.float32), *halves(delta), jnp.zeros((21, rows), jnp.float32)],
                axis=0,
            )
            dt[h, 96:128, cols] = tail.astype(jnp.bfloat16)
            turned = jnp.concatenate(
                [wide, q1[h, :, cols].astype(jnp.float32), jnp.zeros((64, rows), jnp.float32)], axis=0
            ).T
            lane = iota((rows, LANES), 1)
            grad_rows = jnp.where(lane < HEAD, turned, 0.0).astype(jnp.bfloat16)
            query_rows = jnp.where(lane < HEAD, 0.0, turned).astype(jnp.bfloat16)
            for j in range(rows // QB):
                r1 = pl.multiple_of(2 * r0 + 2 * j * QB, QB)
                do[h, pl.ds(r1, QB), :] = grad_rows[j * QB : (j + 1) * QB]
                do[h, pl.ds(r1 + QB, QB), :] = query_rows[j * QB : (j + 1) * QB]
        return carry

    lax.fori_loop(0, blocks, prepare, 0)
    acc[...] = jnp.zeros_like(acc)
    per = rows // QB
    loads[0].wait()
    loads[1].wait()

    def query_block(b, carry):
        q0 = pl.multiple_of(b * QB, QB)
        dq[...] = jnp.zeros_like(dq)

        def key_block(keys):
            s = [dot(kv[h, keys, :], qt[h, :, pl.ds(q0, QB)]) for h in range(heads)]
            d = [dot(kv[h, keys, :], dt[h, :, pl.ds(q0, QB)]) for h in range(heads)]
            p = [jnp.exp2(v) for v in s]
            both = [
                jnp.concatenate([u.astype(jnp.bfloat16), (u * v).astype(jnp.bfloat16)], axis=1)
                for u, v in zip(p, d)
            ]
            for h in range(heads):
                acc[h, keys, :] += dot(both[h], do[h, pl.ds(2 * q0, 2 * QB), :])
            for h in range(heads):
                dq[h] += dot(kt[h, :, keys], both[h][:, QB:])

        in_groups(spans[0, b], spans[1, b], length // LANES, key_block)
        g = lax.div(b, per)
        off = pl.multiple_of(lax.rem(b, per) * QB, QB)
        for h in range(heads):
            out[g, h * HEAD : (h + 1) * HEAD, pl.ds(off, QB)] = (dq[h] * scale).astype(jnp.bfloat16)
        return carry

    lax.fori_loop(0, length // QB, query_block, 0)

    loads[2].wait()

    def finish_block(g, totals):
        r0 = pl.multiple_of(g * rows, rows)
        cols = pl.ds(r0, rows)
        for h in range(heads):
            both = acc[h, cols, :].T
            row = h * HEAD
            out[g, 2 * span + row : 2 * span + row + HEAD, :] = both[0:32].astype(jnp.bfloat16)
            out[g, span + row : span + row + HEAD, :] = (both[32:64] * scale).astype(jnp.bfloat16)
        piece = out[g]
        grad = dot(piece, x[cols, :])
        summed = jnp.sum(piece.astype(jnp.float32), axis=1, keepdims=True)
        return totals[0] + grad, totals[1] + summed

    grads, summed = lax.fori_loop(
        0,
        blocks,
        finish_block,
        (jnp.zeros((3 * span, width), jnp.float32), jnp.zeros((3 * span, 1), jnp.float32)),
    )
    if not last:
        grads_out[:, 0:width] = grads
        grads_out[:, width:] = jnp.broadcast_to(summed, (3 * span, LANES))
        return
    gq[...] = jnp.zeros_like(gq)
    before = grads_in.shape[0] // 3

    def joined(i, old, new):
        return [old[i * before : (i + 1) * before], new[i * span : (i + 1) * span]]

    old = grads_in[:, 0:width]
    whole = jnp.concatenate([v for i in range(3) for v in joined(i, old, grads)], axis=0).T
    total = 3 * (before + span)
    for g in range(8):
        gq[g % 2, g // 2, :, 0:total] = whole[48 * g : 48 * g + 48, :].astype(jnp.bfloat16)
    old = grads_in[:, width : width + 1]
    of_q = jnp.concatenate(joined(0, old, summed), axis=0)
    of_v = jnp.concatenate(joined(2, old, summed), axis=0)
    for cc in range(2):
        mine = jnp.concatenate(
            [
                of_q[48 * cc : 48 * cc + 48, :],
                of_v[48 * cc : 48 * cc + 48, :],
                jnp.zeros((48, 94), jnp.float32),
            ],
            axis=1,
        )
        gq[cc, z, :, total:] = mine.astype(jnp.bfloat16)


def attend_back(heads, index, place, spans, x, qh, tail, kv, kt, q1, gctx, ctx32, grads=None):
    blocks, rows, width = x.shape
    length = blocks * rows
    last = grads is not None
    rest = (grads,) if last else ()
    sm = pl.BlockSpec(memory_space=pltpu.SMEM)
    bf, f4 = jnp.bfloat16, jnp.float32
    once = pl.Buffered(1)
    span = heads * HEAD

    def some_heads(array):
        return pl.BlockSpec((heads,) + array.shape[1:], lambda i: (index, 0, 0), pipeline_mode=once)

    def head_rows(array):
        return pl.BlockSpec((blocks, span, rows), lambda i: (0, index, 0), pipeline_mode=once)

    flat = x.reshape(length, width)
    shapes = (
        jax.ShapeDtypeStruct((blocks, 3 * span, rows), bf),
        jax.ShapeDtypeStruct((2, 4, 48, width), bf)
        if last
        else jax.ShapeDtypeStruct((3 * span, width + LANES), f4),
    )
    return pl.pallas_call(
        functools.partial(attend_back_kernel, last, index),
        name="attend_back",
        grid=(1,),
        out_shape=shapes,
        in_specs=[sm, sm] + [pl.BlockSpec(memory_space=pltpu.HBM)] * 3
        + [some_heads(v) for v in (kv, kt, q1)]
        + [head_rows(v) for v in (gctx, ctx32)]
        + [whole_spec(v) for v in rest],
        out_specs=[whole_spec(v) for v in shapes],
        scratch_shapes=[
            pltpu.VMEM((heads, LANES, length), bf),
            pltpu.VMEM((heads, 2 * length, LANES), bf),
            pltpu.VMEM((heads, length, LANES), f4),
            pltpu.VMEM((heads, HEAD, QB), f4),
            pltpu.VMEM((heads, LANES, length), bf),
            pltpu.VMEM((length, width), bf),
            pltpu.SemaphoreType.DMA((3,)),
        ],
        compiler_params=pltpu.CompilerParams(vmem_limit_bytes=BIG),
        cost_estimate=pl.CostEstimate(
            flops=heads * 20 * 10 ** 9, bytes_accessed=heads * 8 * 10 ** 6, transcendentals=heads * 6 * 10 ** 6
        ),
    )(place, spans, flat, qh, tail, kv, kt, q1, gctx, ctx32, *rest)


def reduce_kernel(
    src, gq, pr, dst, p_out, q_out,
    gq_in, gq_sum, qa_in, qa_sum, qb_in, pa_in, pa_sum, pb_in, p_own, gq_own, pr_own,
    lsem, send, recv, gsend, grecv, qasend, qarecv, qbsend, qbrecv, qcsend, qcrecv,
    pasend, parecv, pbsend, pbrecv, pcsend, pcrecv,
):
    r, g, z, c = where_am_i()
    greet(r, g, 4, 8)
    waits = []
    pair = remote(gq.at[1 - c], gq_in, gsend, grecv, r, 2 * z + 1 - c)
    pair.start()
    for d in range(1, 4):
        rr = lax.rem(r + d, 4)
        copy = remote(pr.at[rr], pa_in.at[r], pasend.at[d - 1], parecv.at[r], rr, g)
        copy.start()
        waits.append(copy)
    load_g = pltpu.make_async_copy(gq.at[c], gq_own, lsem.at[1])
    load_g.start()
    load_p = pltpu.make_async_copy(pr.at[r], pr_own, lsem.at[2])
    load_p.start()
    own = pltpu.make_async_copy(src.at[g], dst.at[g], lsem.at[0])
    own.start()

    def send_to(d):
        to = lax.rem(g + d, 8)
        copy = remote(src.at[to], dst.at[g], send.at[d - 1], recv.at[g], r, to)
        copy.start()
        waits.append(copy)

    def f32(value):
        return value.astype(jnp.float32)

    send_to(4)
    send_to(3)
    send_to(5)
    load_g.wait()
    pair.wait_recv()
    gq_sum[...] = (f32(gq_own[...]) + f32(gq_in[...])).astype(jnp.bfloat16)
    for d in range(1, 4):
        rr = lax.rem(r + d, 4)
        copy = remote(gq_sum.at[rr], qa_in.at[r], qasend.at[d - 1], qarecv.at[r], rr, g)
        copy.start()
        waits.append(copy)
    send_to(2)
    send_to(6)
    for d in range(1, 4):
        b = lax.rem(r + d, 4)
        remote(gq_sum.at[r], qa_in.at[b], qasend.at[0], qarecv.at[b], b, g).wait_recv()
    total = f32(gq_sum[r])
    for d in range(1, 4):
        total = total + f32(qa_in[lax.rem(r + d, 4)])
    qa_sum[...] = total.astype(jnp.bfloat16)

    @pl.when(z != r)
    def _():
        remote(qa_sum, qb_in.at[z], qbsend, qbrecv.at[z], r, 2 * r + c).start()

    load_p.wait()
    for d in range(1, 4):
        b = lax.rem(r + d, 4)
        remote(pr.at[r], pa_in.at[b], pasend.at[0], parecv.at[b], b, g).wait_recv()
    total = f32(pr_own[...])
    for d in range(1, 4):
        total = total + f32(pa_in[lax.rem(r + d, 4)])
    pa_sum[...] = total.astype(jnp.bfloat16)
    for d in range(1, 4):
        zz = lax.rem(z + d, 4)
        copy = remote(pa_sum.at[zz], pb_in.at[z], pbsend.at[d - 1], pbrecv.at[z], r, 2 * zz + c)
        copy.start()
        waits.append(copy)
    send_to(1)
    send_to(7)

    @pl.when(z == r)
    def _():
        for d in range(1, 4):
            b = lax.rem(z + d, 4)
            remote(qa_sum, qb_in.at[b], qbsend, qbrecv.at[b], r, g).wait_recv()
        qb_in[z] = qa_sum[...]
        pltpu.make_async_copy(qb_in, q_out, lsem.at[4]).start()
        for d in range(1, 4):
            remote(qb_in, q_out, qcsend.at[d - 1], qcrecv, lax.rem(r + d, 4), g).start()

    for d in range(1, 4):
        b = lax.rem(z + d, 4)
        remote(pa_sum.at[z], pb_in.at[b], pbsend.at[0], pbrecv.at[b], r, g).wait_recv()
    total = f32(pa_sum[z])
    for d in range(1, 4):
        total = total + f32(pb_in[lax.rem(z + d, 4)])
    p_own[...] = total.astype(jnp.bfloat16)
    keep_p = pltpu.make_async_copy(p_own, p_out.at[r], lsem.at[3])
    keep_p.start()
    for d in range(1, 4):
        rr = lax.rem(r + d, 4)
        copy = remote(p_own, p_out.at[r], pcsend.at[d - 1], pcrecv.at[r], rr, g)
        copy.start()
        waits.append(copy)

    @pl.when(z == r)
    def _():
        pltpu.make_async_copy(qb_in, q_out, lsem.at[4]).wait()
        for d in range(1, 4):
            remote(qb_in, q_out, qcsend.at[d - 1], qcrecv, lax.rem(r + d, 4), g).wait_send()

    @pl.when(z != r)
    def _():
        remote(qb_in, q_out, qcsend.at[0], qcrecv, r, g).wait_recv()
        remote(qa_sum, qb_in.at[z], qbsend, qbrecv.at[z], r, 2 * r + c).wait_send()

    for d in range(1, 4):
        b = lax.rem(r + d, 4)
        remote(p_own, p_out.at[b], pcsend.at[0], pcrecv.at[b], b, g).wait_recv()
    for d in range(1, 8):
        b = lax.rem(g + d, 8)
        remote(src.at[g], dst.at[b], send.at[0], recv.at[b], r, b).wait_recv()
    pair.wait_send()
    for copy in waits:
        copy.wait_send()
    keep_p.wait()
    own.wait()


def reduce_all(src, gq, pr):
    dma = pltpu.SemaphoreType.DMA
    anywhere = pl.BlockSpec(memory_space=pltpu.HBM)
    bf = jnp.bfloat16
    width = gq.shape[-1]
    return pl.pallas_call(
        reduce_kernel,
        name="reduce",
        out_shape=(
            jax.ShapeDtypeStruct(src.shape, bf),
            jax.ShapeDtypeStruct((4, 112, width), bf),
            jax.ShapeDtypeStruct((4, 48, width), bf),
        ),
        in_specs=[anywhere] * 3,
        out_specs=[anywhere] * 3,
        scratch_shapes=[
            pltpu.VMEM((4, 48, width), bf),
            pltpu.VMEM((4, 48, width), bf),
            pltpu.VMEM((4, 48, width), bf),
            pltpu.VMEM((48, width), bf),
            pltpu.VMEM((4, 48, width), bf),
            pltpu.VMEM((4, 4, 112, width), bf),
            pltpu.VMEM((4, 112, width), bf),
            pltpu.VMEM((4, 112, width), bf),
            pltpu.VMEM((112, width), bf),
            pltpu.VMEM((4, 48, width), bf),
            pltpu.VMEM((4, 112, width), bf),
            dma((5,)), dma((7,)), dma((8,)), dma, dma, dma((3,)), dma((4,)), dma, dma((4,)),
            dma((3,)), dma, dma((3,)), dma((4,)), dma((3,)), dma((4,)), dma((3,)), dma((4,)),
        ],
        compiler_params=pltpu.CompilerParams(
            collective_id=4, has_side_effects=True, vmem_limit_bytes=BIG
        ),
    )(src, gq, pr)


def finish_kernel(
    place, layer_in, in_0, in_1, grad_one, w, p_in, q_in,
    layer_out, out, g_q, g_k, g_v, g_o, g_in, g_up, rows_out, inner_out, wq, held, sems,
):
    seqs, rows, width = grad_one.shape
    span = 96
    z = place[0]
    c = place[1]
    load = pltpu.make_async_copy(layer_in, held, sems.at[0])
    load.start()
    for i in range(3):
        for g in range(8):
            wq[i, 48 * g : 48 * g + 48, :] = w[0, g % 2, g // 2, 48 * i : 48 * i + 48, :]
    for s in range(seqs):
        total = grad_one[s]
        for i in range(3):
            turned = jnp.concatenate(
                [
                    ref[2 * zz + s, i * count : (i + 1) * count, :]
                    for zz in range(4)
                    for ref, count in ((in_0, in_0.shape[1] // 3), (in_1, in_1.shape[1] // 3))
                ],
                axis=0,
            )
            back = turned.astype(jnp.float32).T.astype(jnp.bfloat16)
            total = total + lax.dot_general(
                back, wq[i], (((1,), (1,)), ((), ())), preferred_element_type=jnp.float32
            )
        out[s] = total.astype(jnp.bfloat16)
    load.wait()
    store = pltpu.make_async_copy(held, layer_out, sems.at[1])
    store.start()
    wide = [q_in[zz].astype(jnp.float32) for zz in range(4)]
    for i, ref in enumerate((g_q, g_k, g_v)):
        ref[...] = jnp.concatenate([v[:, i * span : (i + 1) * span] for v in wide], axis=1)
    sums = p_in[3, 96:112, :]
    pick = jnp.where(
        iota((width, 48), 0) == 48 * (2 * z + c) + iota((width, 48), 1), 1.0, 0.0
    ).astype(jnp.bfloat16)
    rows_out[8:24, :] = dot(sums, pick)
    both = q_in[z].astype(jnp.float32)[:, 3 * span :].T
    rows_out[0:8, :] = both[0:8, :]
    pick = jnp.where(
        iota((width, 192), 0) == 192 * c + iota((width, 192), 1), 1.0, 0.0
    ).astype(jnp.bfloat16)
    inner = dot(sums, pick)
    inner_out[...] = jnp.sum(
        jnp.where(iota((16, 192), 0) == 6 + z, inner, 0.0), axis=0, keepdims=True
    )
    g_o[...] = p_in[0, 0:48, :].astype(jnp.float32)
    g_in[:, 0:384] = p_in[0, 48:96, :].astype(jnp.float32)
    g_in[:, 384:768] = p_in[1, 0:48, :].astype(jnp.float32)
    g_in[:, 768:1152] = p_in[1, 48:96, :].astype(jnp.float32)
    g_in[:, 1152:1536] = p_in[2, 0:48, :].astype(jnp.float32)
    g_up[0:16, :] = p_in[0, 96:112, :].astype(jnp.float32)
    g_up[16:32, :] = p_in[1, 96:112, :].astype(jnp.float32)
    g_up[32:96, :] = p_in[2, 48:112, :].astype(jnp.float32)
    g_up[96:192, :] = p_in[3, 0:96, :].astype(jnp.float32)
    store.wait()


def finish(place, layer_in, in_0, in_1, grad_one, w, p_in, q_in):
    seqs, rows, width = grad_one.shape
    vm = pl.BlockSpec(memory_space=pltpu.VMEM)
    sm = pl.BlockSpec(memory_space=pltpu.SMEM)
    bf, f4 = jnp.bfloat16, jnp.float32
    shapes = ((48, width),) * 4 + ((48, 4 * width), (192, width), (24, 48), (1, 192))
    return pl.pallas_call(
        finish_kernel,
        name="finish",
        grid=(1,),
        out_shape=(jax.ShapeDtypeStruct((seqs, rows, width), bf),) * 2
        + tuple(jax.ShapeDtypeStruct(shape, f4) for shape in shapes),
        in_specs=[
            sm, pl.BlockSpec(memory_space=pltpu.HBM), whole_spec(in_0), whole_spec(in_1), whole_spec(grad_one), quarter_spec(w, 0), whole_spec(p_in), whole_spec(q_in)
        ],
        out_specs=[pl.BlockSpec(memory_space=pltpu.HBM), whole_spec(grad_one)]
        + [pl.BlockSpec(shape, functools.partial(zeros_for, len(shape))) for shape in shapes],
        scratch_shapes=[
            pltpu.VMEM((3, width, width), bf),
            pltpu.VMEM((seqs, rows, width), bf),
            pltpu.SemaphoreType.DMA((2,)),
        ],
        compiler_params=pltpu.CompilerParams(vmem_limit_bytes=BIG),
    )(place, layer_in, in_0, in_1, grad_one, w, p_in, q_in)


def line_of_chips(
    tokens, segment_ids, out_grad, query_weight, key_weight, value_weight, output_weight,
    inner_weight, outer_weight, query_bias, value_bias, output_bias, inner_bias, outer_bias,
    first_gain, first_shift, second_gain, second_shift,
):
    bf = jnp.bfloat16
    width = tokens.shape[2]
    g = lax.axis_index("grp")
    z, c = lax.div(g, 2), lax.rem(g, 2)
    place = jnp.stack([z, c]).astype(jnp.int32)
    weights = (query_weight, key_weight, value_weight, output_weight, inner_weight, outer_weight)
    vectors = jnp.concatenate(
        [
            v[None]
            for v in (
                query_bias, value_bias, output_bias, outer_bias,
                first_gain, first_shift, second_gain, second_shift,
            )
        ],
        axis=0,
    )
    x, w, small, kv, qh, kt, vt, q1, norms = gather(
        tokens, weights, vectors, inner_bias[None], segment_ids
    )
    ctx, ctx32, tail, spans = attend(place, kv, qh, vt, small, norms)
    layer_out, grad_one, gctx_in, pr = middle(ctx, tokens, out_grad, w, small)
    back = functools.partial(
        attend_back, place=place, spans=spans, x=x, qh=qh, tail=tail, kv=kv, kt=kt, q1=q1,
        gctx=gctx_in, ctx32=ctx32,
    )
    parts_0, grads_0 = back(2, 0)
    in_0 = lax.all_to_all(parts_0, "grp", 0, 0, tiled=True)
    parts_1, gq = back(1, 2, grads=grads_0)
    in_1, p_in, q_in = reduce_all(parts_1, gq, pr)
    layer_out, input_grad, g_q, g_k, g_v, g_o, g_in, g_up, rows, inner_row = finish(
        place, layer_out, in_0, in_1, grad_one, w, p_in, q_in
    )
    return (
        layer_out, input_grad, g_q, g_k, g_v, g_o, g_in, g_up,
        rows[0], rows[1], rows[8], inner_row[0], rows[9], rows[10], rows[11], rows[12], rows[13],
    )


def solution(mesh):
    in_specs = (
        P("rep", "grp", None),
        P("rep", "grp"),
        P("rep", "grp", None),
        P("grp", None),
        P("grp", None),
        P("grp", None),
        P("grp", None),
        P("grp", None),
        P("grp", None),
        P("grp"),
        P("grp"),
        P("grp"),
        P("grp"),
        P("grp"),
        P("grp"),
        P("grp"),
        P("grp"),
        P("grp"),
    )
    out_specs = (
        P("rep", "grp", None),
        P("rep", "grp", None),
        P("grp", None),
        P("grp", None),
        P("grp", None),
        P("grp", None),
        P("grp", None),
        P("grp", None),
        P("grp"),
        P("grp"),
        P("grp"),
        P("grp"),
        P("grp"),
        P("grp"),
        P("grp"),
        P("grp"),
        P("grp"),
    )
    whole_line = mesh.shape["grp"] == 8 and mesh.shape["rep"] == 4
    return jax.shard_map(
        line_of_chips if whole_line else on_device, mesh=mesh, in_specs=in_specs, out_specs=out_specs, check_vma=False
    )
```

```python
import functools
from functools import reduce

import jax
import jax.numpy as jnp
from jax import lax
from jax.experimental import pallas as pl
from jax.experimental.pallas import tpu as pltpu
from jax.sharding import PartitionSpec as P

H = 12
MICRO = 2
SEQ_MB = 1


norm_epsilon = 1e-05
masked_score = -1000000000.0


def layer_norm(inputs, norm_gain, norm_shift):
    center = inputs - jnp.mean(inputs, axis=-1, keepdims=True)
    spread = jnp.mean(center * center, axis=-1, keepdims=True)
    return center * lax.rsqrt(spread + norm_epsilon) * norm_gain + norm_shift


def exact_gelu(inputs):
    return jax.nn.gelu(inputs, approximate=False)


def times_transpose(left, right):
    return lax.dot_general(
        left, right, (((1,), (1,)), ((), ())), preferred_element_type=jnp.float32
    )


def transpose_times(left, right):
    return lax.dot_general(
        left, right, (((0,), (0,)), ((), ())), preferred_element_type=jnp.float32
    )


def column_total(inputs):
    return jnp.sum(inputs.astype(jnp.float32), axis=0)


def masked_scores(query_group, key_group, same_doc, score_scale):
    scores = (
        jnp.einsum("bqhd,bkhd->bhqk", query_group, key_group, preferred_element_type=jnp.float32)
        * score_scale
    )
    return jnp.where(same_doc[:, None], scores, masked_score)


def group_forward(query_group, key_group, value_group, same_doc, score_scale):
    scores = masked_scores(query_group, key_group, same_doc, score_scale)
    highest = jnp.max(scores, axis=-1, keepdims=True)
    log_total = highest + jnp.log(jnp.sum(jnp.exp(scores - highest), axis=-1, keepdims=True))
    weights_low = jnp.exp(scores - log_total).astype(jnp.bfloat16)
    context = jnp.einsum(
        "bhqk,bkhd->bqhd", weights_low, value_group, preferred_element_type=jnp.float32
    )
    return (context.astype(jnp.bfloat16), log_total)


def group_backward(
    query_group, key_group, value_group, same_doc, log_total, grad_context, score_scale
):
    attn_weights = jnp.exp(masked_scores(query_group, key_group, same_doc, score_scale) - log_total)
    weights_low = attn_weights.astype(jnp.bfloat16)
    grad_weights = jnp.einsum(
        "bqhd,bkhd->bhqk", grad_context, value_group, preferred_element_type=jnp.float32
    )
    centre = jnp.sum(attn_weights * grad_weights, axis=-1, keepdims=True)
    grad_scores = (attn_weights * (grad_weights - centre)).astype(jnp.bfloat16)
    grad_query = jnp.einsum(
        "bhqk,bkhd->bqhd", grad_scores, key_group, preferred_element_type=jnp.float32
    )
    grad_query = (grad_query * score_scale).astype(jnp.bfloat16)
    grad_key = (
        jnp.einsum("bhqk,bqhd->bkhd", grad_scores, query_group, preferred_element_type=jnp.float32)
        * score_scale
    )
    grad_value = jnp.einsum(
        "bhqk,bqhd->bkhd", weights_low, grad_context, preferred_element_type=jnp.float32
    )
    return (grad_query, grad_key, grad_value)


def merge_groups(stacked, row_total, model_width):
    return jnp.moveaxis(stacked, 0, 2).reshape(row_total, model_width)


def gradient_terms(
    token_rows,
    context_rows,
    hidden_rows,
    active_rows,
    grad_queries,
    grad_keys,
    grad_values,
    grad_attention,
    grad_inner,
    grad_feed,
    norm_grads,
):
    return (
        transpose_times(token_rows, grad_queries),
        transpose_times(token_rows, grad_keys),
        transpose_times(token_rows, grad_values),
        transpose_times(context_rows, grad_attention),
        transpose_times(hidden_rows, grad_inner),
        transpose_times(active_rows, grad_feed),
        column_total(grad_queries),
        column_total(grad_values),
        column_total(grad_attention),
        column_total(grad_inner),
        column_total(grad_feed),
        norm_grads[0],
        norm_grads[1],
        norm_grads[2],
        norm_grads[3],
    )


def on_device(
    tokens,
    segment_ids,
    out_grad,
    query_weight,
    key_weight,
    value_weight,
    output_weight,
    inner_weight,
    outer_weight,
    query_bias,
    value_bias,
    output_bias,
    inner_bias,
    outer_bias,
    first_gain,
    first_shift,
    second_gain,
    second_shift,
):
    row_count = tokens.shape[1]
    model_width = tokens.shape[2]
    head_count = H
    head_size = model_width // head_count
    per_group = max(1, min(head_count, 128 // head_size))
    group_width = per_group * head_size
    group_count = head_count // per_group
    score_scale = head_size ** (-0.5)
    seq_count = SEQ_MB
    flat_rows = seq_count * row_count
    all_segments = lax.all_gather(segment_ids, "grp", axis=1, tiled=True)
    outputs = []
    input_grads = []
    shares_list = []
    for batch_index in range(MICRO):
        offset = batch_index * seq_count
        local_tokens = tokens[offset : offset + seq_count]
        flat_tokens = local_tokens.reshape(flat_rows, model_width)
        gathered = (
            lax.all_gather(query_weight, "grp", axis=0, tiled=True),
            lax.all_gather(key_weight, "grp", axis=0, tiled=True),
            lax.all_gather(value_weight, "grp", axis=0, tiled=True),
            lax.all_gather(output_weight, "grp", axis=0, tiled=True),
            lax.all_gather(inner_weight, "grp", axis=0, tiled=True),
            lax.all_gather(outer_weight, "grp", axis=0, tiled=True),
            lax.all_gather(query_bias, "grp", axis=0, tiled=True),
            lax.all_gather(value_bias, "grp", axis=0, tiled=True),
            lax.all_gather(output_bias, "grp", axis=0, tiled=True),
            lax.all_gather(inner_bias, "grp", axis=0, tiled=True),
            lax.all_gather(outer_bias, "grp", axis=0, tiled=True),
            lax.all_gather(first_gain, "grp", axis=0, tiled=True),
            lax.all_gather(first_shift, "grp", axis=0, tiled=True),
            lax.all_gather(second_gain, "grp", axis=0, tiled=True),
            lax.all_gather(second_shift, "grp", axis=0, tiled=True),
        )
        full_query, full_key, full_value, full_output, full_inner, full_outer = gathered[:6]
        (
            bias_query,
            bias_value,
            bias_output,
            bias_inner,
            bias_outer,
            gain_first,
            shift_first,
            gain_second,
            shift_second,
        ) = [vector.astype(jnp.float32) for vector in gathered[6:]]
        queries = (
            jnp.dot(flat_tokens, full_query, preferred_element_type=jnp.float32) + bias_query
        ).astype(jnp.bfloat16)
        key_rows = jnp.dot(flat_tokens, full_key, preferred_element_type=jnp.float32).astype(
            jnp.bfloat16
        )
        value_rows = (
            jnp.dot(flat_tokens, full_value, preferred_element_type=jnp.float32) + bias_value
        ).astype(jnp.bfloat16)
        key_split = key_rows.reshape(seq_count, row_count, model_width)
        value_split = value_rows.reshape(seq_count, row_count, model_width)
        key_all, value_all = (
            lax.all_gather(key_split, "grp", axis=1, tiled=True),
            lax.all_gather(value_split, "grp", axis=1, tiled=True),
        )
        length = key_all.shape[1]
        local_segments = segment_ids[offset : offset + seq_count]
        far_segments = all_segments[offset : offset + seq_count]
        same_doc = local_segments[:, :, None] == far_segments[:, None, :]
        query_split = queries.reshape(seq_count, row_count, model_width)

        def slice_group(array, group_index):
            piece = lax.dynamic_slice_in_dim(array, group_index * group_width, group_width, 2)
            return piece.reshape(array.shape[0], array.shape[1], per_group, head_size)

        def forward_group(group_index):
            context, log_total = group_forward(
                slice_group(query_split, group_index),
                slice_group(key_all, group_index),
                slice_group(value_all, group_index),
                same_doc,
                score_scale,
            )
            return (context.reshape(seq_count, row_count, group_width), log_total)

        context_groups, log_totals = lax.map(forward_group, jnp.arange(group_count))
        context_rows = merge_groups(context_groups, flat_rows, model_width)
        attention = (
            jnp.dot(context_rows, full_output, preferred_element_type=jnp.float32) + bias_output
        )
        residual_one = flat_tokens.astype(jnp.float32) + attention
        hidden_one, norm_one_pullback = jax.vjp(layer_norm, residual_one, gain_first, shift_first)
        hidden_low = hidden_one.astype(jnp.bfloat16)
        inner_pre = jnp.dot(hidden_low, full_inner, preferred_element_type=jnp.float32) + bias_inner
        activation, gelu_pullback = jax.vjp(exact_gelu, inner_pre)
        active_low = activation.astype(jnp.bfloat16)
        feed = jnp.dot(active_low, full_outer, preferred_element_type=jnp.float32) + bias_outer
        output_rows, norm_two_pullback = jax.vjp(
            layer_norm, hidden_one + feed, gain_second, shift_second
        )
        outputs.append(output_rows.astype(jnp.bfloat16).reshape(seq_count, row_count, model_width))
        cotangent = (
            out_grad[offset : offset + seq_count]
            .reshape(flat_rows, model_width)
            .astype(jnp.float32)
        )
        grad_two, grad_gain_two, grad_shift_two = norm_two_pullback(cotangent)
        grad_feed = grad_two.astype(jnp.bfloat16)
        grad_active = times_transpose(grad_feed, full_outer)
        grad_inner = gelu_pullback(grad_active)[0].astype(jnp.bfloat16)
        grad_hidden = grad_two + times_transpose(grad_inner, full_inner)
        grad_one, grad_gain_one, grad_shift_one = norm_one_pullback(grad_hidden)
        grad_attention = grad_one.astype(jnp.bfloat16)
        grad_context = times_transpose(grad_attention, full_output).astype(jnp.bfloat16)
        grad_context = grad_context.reshape(seq_count, row_count, model_width)

        def backward_group(pieces):
            group_index, log_total = pieces
            grad_query, grad_key, grad_value = group_backward(
                slice_group(query_split, group_index),
                slice_group(key_all, group_index),
                slice_group(value_all, group_index),
                same_doc,
                log_total,
                slice_group(grad_context, group_index),
                score_scale,
            )
            return (
                grad_query.reshape(seq_count, row_count, group_width),
                grad_key.reshape(seq_count, length, group_width),
                grad_value.reshape(seq_count, length, group_width),
            )

        query_groups, key_groups, value_groups = lax.map(
            backward_group, (jnp.arange(group_count), log_totals)
        )
        key_owned, value_owned = (
            lax.psum_scatter(key_groups, "grp", scatter_dimension=2, tiled=True),
            lax.psum_scatter(value_groups, "grp", scatter_dimension=2, tiled=True),
        )
        grad_keys = merge_groups(key_owned, flat_rows, model_width).astype(jnp.bfloat16)
        grad_values = merge_groups(value_owned, flat_rows, model_width).astype(jnp.bfloat16)
        grad_queries = merge_groups(query_groups, flat_rows, model_width)
        grad_tokens = (
            grad_one
            + times_transpose(grad_queries, full_query)
            + times_transpose(grad_keys, full_key)
            + times_transpose(grad_values, full_value)
        )
        input_grads.append(
            grad_tokens.astype(jnp.bfloat16).reshape(seq_count, row_count, model_width)
        )
        norm_grads = (grad_gain_one, grad_shift_one, grad_gain_two, grad_shift_two)
        terms = gradient_terms(
            flat_tokens,
            context_rows,
            hidden_low,
            active_low,
            grad_queries,
            grad_keys,
            grad_values,
            grad_attention,
            grad_inner,
            grad_feed,
            norm_grads,
        )
        shares = (
            lax.psum_scatter(terms[0], "grp", scatter_dimension=0, tiled=True),
            lax.psum_scatter(terms[1], "grp", scatter_dimension=0, tiled=True),
            lax.psum_scatter(terms[2], "grp", scatter_dimension=0, tiled=True),
            lax.psum_scatter(terms[3], "grp", scatter_dimension=0, tiled=True),
            lax.psum_scatter(terms[4], "grp", scatter_dimension=0, tiled=True),
            lax.psum_scatter(terms[5], "grp", scatter_dimension=0, tiled=True),
            lax.psum_scatter(terms[6], "grp", scatter_dimension=0, tiled=True),
            lax.psum_scatter(terms[7], "grp", scatter_dimension=0, tiled=True),
            lax.psum_scatter(terms[8], "grp", scatter_dimension=0, tiled=True),
            lax.psum_scatter(terms[9], "grp", scatter_dimension=0, tiled=True),
            lax.psum_scatter(terms[10], "grp", scatter_dimension=0, tiled=True),
            lax.psum_scatter(terms[11], "grp", scatter_dimension=0, tiled=True),
            lax.psum_scatter(terms[12], "grp", scatter_dimension=0, tiled=True),
            lax.psum_scatter(terms[13], "grp", scatter_dimension=0, tiled=True),
            lax.psum_scatter(terms[14], "grp", scatter_dimension=0, tiled=True),
        )
        shares_list.append(shares)
    owned = reduce(
        lambda left_part, right_part: jax.tree.map(jnp.add, left_part, right_part), shares_list
    )
    summed = (
        lax.psum(owned[0].astype(jnp.bfloat16), "rep").astype(jnp.float32),
        lax.psum(owned[1].astype(jnp.bfloat16), "rep").astype(jnp.float32),
        lax.psum(owned[2].astype(jnp.bfloat16), "rep").astype(jnp.float32),
        lax.psum(owned[3].astype(jnp.bfloat16), "rep").astype(jnp.float32),
        lax.psum(owned[4].astype(jnp.bfloat16), "rep").astype(jnp.float32),
        lax.psum(owned[5].astype(jnp.bfloat16), "rep").astype(jnp.float32),
        lax.psum(owned[6].astype(jnp.bfloat16), "rep").astype(jnp.float32),
        lax.psum(owned[7].astype(jnp.bfloat16), "rep").astype(jnp.float32),
        lax.psum(owned[8].astype(jnp.bfloat16), "rep").astype(jnp.float32),
        lax.psum(owned[9].astype(jnp.bfloat16), "rep").astype(jnp.float32),
        lax.psum(owned[10].astype(jnp.bfloat16), "rep").astype(jnp.float32),
        lax.psum(owned[11].astype(jnp.bfloat16), "rep").astype(jnp.float32),
        lax.psum(owned[12].astype(jnp.bfloat16), "rep").astype(jnp.float32),
        lax.psum(owned[13].astype(jnp.bfloat16), "rep").astype(jnp.float32),
        lax.psum(owned[14].astype(jnp.bfloat16), "rep").astype(jnp.float32),
    )
    return (
        jnp.concatenate(outputs, axis=0),
        jnp.concatenate(input_grads, axis=0),
        summed[0],
        summed[1],
        summed[2],
        summed[3],
        summed[4],
        summed[5],
        summed[6],
        summed[7],
        summed[8],
        summed[9],
        summed[10],
        summed[11],
        summed[12],
        summed[13],
        summed[14],
    )


HEAD = 32
LANES = 128
QB = 256
AWAY = 2.0 ** 100
LIMIT = 100.0
LONG = 17
MESH = pl.DeviceIdType.MESH
BIG = 62 * 1024 * 1024
LOG2E = 1.4426950408889634


def halves(value):
    first = value.astype(jnp.bfloat16).astype(jnp.float32)
    rest = value - first
    second = rest.astype(jnp.bfloat16).astype(jnp.float32)
    third = (rest - second).astype(jnp.bfloat16).astype(jnp.float32)
    return first, second, third


def dot(left, right):
    return jnp.dot(left, right, preferred_element_type=jnp.float32)


def zeros_for(rank, *grid):
    return (0,) * rank


def whole_spec(array):
    return pl.BlockSpec(array.shape, functools.partial(zeros_for, array.ndim), pipeline_mode=pl.Buffered(1))


def quarter_spec(w, i):
    return pl.BlockSpec((1,) + w.shape[1:], lambda *grid: (i, 0, 0, 0, 0), pipeline_mode=pl.Buffered(1))


def iota(shape, dim):
    return lax.broadcasted_iota(jnp.int32, shape, dim)


def where_am_i():
    r = lax.axis_index("rep")
    g = lax.axis_index("grp")
    return r, g, lax.div(g, 2), lax.rem(g, 2)


def remote(src, dst, send, recv, r, g):
    return pltpu.make_async_remote_copy(
        src_ref=src, dst_ref=dst, send_sem=send, recv_sem=recv, device_id=(r, g), device_id_type=MESH
    )


def greet(r, g, reps, group):
    barrier = pltpu.get_barrier_semaphore()
    for d in range(1, group):
        pl.semaphore_signal(barrier, inc=1, device_id=(r, lax.rem(g + d, group)), device_id_type=MESH)
    for d in range(1, reps):
        pl.semaphore_signal(barrier, inc=1, device_id=(lax.rem(r + d, reps), g), device_id_type=MESH)
    pl.semaphore_wait(barrier, group + reps - 2)


def vectors_of(small):
    return jnp.concatenate([small[g, 0:8, 0:48].astype(jnp.float32) for g in range(8)], axis=1)


def chip_at(z, i):
    order = ((0, 1, 2, 3), (1, 0, 2, 3), (2, 1, 3, 0), (3, 2, 1, 0))
    chip = jnp.int32(0)
    for a, row in enumerate(order):
        for k, value in enumerate(row):
            chip = jnp.where((z == a) & (i == k), value, chip)
    return chip


def gather_kernel(
    tok, wq, wk, wv, wo, wi, wu, vectors, inner, seg,
    x_out, w_out, s_out, kv_out, qh_out, kt_out, vt_out, q1_out, norms,
    small, x, kv, qh, kt, vt, q1, w0, smalls_in, wrow, wtr, mine,
    lsem, xsem, psems, tsend, trecv, psend, wsend1, wrecv1, wsend2, wrecv2, wsend3, wrecv3, ssend, srecv,
):
    r, g, z, c = where_am_i()
    reps, chips = 4, 4
    p = 2 * z + 1 - c
    heads = kv.shape[0]
    _, rows, width = x.shape
    small[0:8, :] = jnp.concatenate(
        [vectors[...].astype(jnp.float32), jnp.zeros((8, rows - 48), jnp.float32)], axis=1
    ).astype(jnp.bfloat16)
    small[8:16, :] = jnp.concatenate(
        [
            jnp.concatenate([inner[...].astype(jnp.float32), jnp.zeros((1, rows - 192), jnp.float32)], axis=1),
            seg[...].astype(jnp.float32),
            jnp.zeros((5, rows), jnp.float32),
        ],
        axis=0,
    ).astype(jnp.bfloat16)
    greet(r, g, reps, 2 * chips)
    slab = [wi.at[:, pl.ds(j * width, width)] for j in range(4)]
    quarters = (
        ((wq, 0, 48), (wk, 48, 48), (wv, 96, 48)),
        ((wo, 0, 48), (slab[0], 48, 48), (slab[1], 96, 48)),
        ((slab[2], 0, 48), (slab[3], 48, 48), (wu.at[pl.ds(0, 48), :], 96, 48)),
        ((wu.at[pl.ds(48, 144), :], 0, 144),),
    )
    swap = remote(tok.at[1 - c], x.at[g], psend, trecv.at[g], r, p)
    swap.start()
    own_x = pltpu.make_async_copy(tok.at[c], x.at[g], lsem.at[0])
    own_x.start()
    def pass_on(b, way, src=None):
        to = g + 2 if way == 0 else g - 2
        src = x.at[b] if src is None else src
        return remote(src, x.at[b], tsend.at[way, b], trecv.at[b], r, to)

    def forward(b, way, src=None):
        ok = z < chips - 1 if way == 0 else z > 0

        @pl.when(ok)
        def _():
            pass_on(b, way, src).start()

    def keep(b):
        return pltpu.make_async_copy(x.at[b], x_out.at[b], xsem.at[b])

    def arrived(b):
        remote(x.at[b], x.at[b], tsend.at[0, b], trecv.at[b], r, p).wait_recv()

    forward(g, 0, tok.at[c])
    forward(g, 1, tok.at[c])
    arrived(p)
    forward(p, 0)
    forward(p, 1)
    keep(p).start()
    for i, pieces in enumerate(quarters):
        @pl.when(r == i)
        def _():
            copies = [
                pltpu.make_async_copy(ref, mine.at[pl.ds(row, count), :], lsem.at[3 + k])
                for k, (ref, row, count) in enumerate(pieces)
            ]
            for copy in copies:
                copy.start()
            for copy in copies:
                copy.wait()

    own_w = pltpu.make_async_copy(mine, w_out.at[r, c, z], lsem.at[1])
    own_w.start()
    own_s = pltpu.make_async_copy(small, smalls_in.at[g], lsem.at[2])
    own_s.start()
    first = []
    for d in range(1, chips):
        zz = lax.rem(z + d, chips)
        copy = remote(mine, w_out.at[r, c, z], wsend1.at[d - 1], wrecv1.at[z], r, 2 * zz + c)
        copy.start()
        first.append(copy)
    smalls = []
    for d in range(1, 2 * chips):
        copy = remote(small, smalls_in.at[g], ssend.at[d - 1], srecv.at[g], r, lax.rem(g + d, 2 * chips))
        copy.start()
        smalls.append(copy)
    own_x.wait()
    keep(g).start()

    def tokens_from(d):
        for k in range(2):
            @pl.when(z >= d)
            def _():
                b = 2 * (z - d) + (c if k == 0 else 1 - c)
                arrived(b)
                forward(b, 0)
                keep(b).start()

            @pl.when(z + d < chips)
            def _():
                b = 2 * (z + d) + (c if k == 0 else 1 - c)
                arrived(b)
                forward(b, 1)
                keep(b).start()

    tokens_from(1)
    for d in range(1, chips):
        zz = lax.rem(z + d, chips)
        remote(mine, w_out.at[r, c, zz], wsend1.at[0], wrecv1.at[zz], r, p).wait_recv()
    own_w.wait()
    second = []
    for d in range(1, reps):
        copy = remote(
            w_out.at[r, c], w_out.at[r, c], wsend2.at[d - 1], wrecv2.at[r], lax.rem(r + d, reps), g
        )
        copy.start()
        second.append(copy)
    third = [remote(w_out.at[r, c], w_out.at[r, c], wsend3.at[r], wrecv3.at[r], r, p)]
    third[0].start()
    tokens_from(2)
    for d in range(1, reps):
        q = lax.rem(r + d, reps)
        remote(w_out.at[q, c], w_out.at[q, c], wsend2.at[0], wrecv2.at[q], r, p).wait_recv()
        copy = remote(w_out.at[q, c], w_out.at[q, c], wsend3.at[q], wrecv3.at[q], r, p)
        copy.start()
        third.append(copy)
    for q in range(reps):
        remote(w_out.at[q, 1 - c], w_out.at[q, 1 - c], wsend3.at[q], wrecv3.at[q], r, p).wait_recv()
    load_w = pltpu.make_async_copy(w_out.at[0], w0, lsem.at[1])
    load_w.start()
    for d in range(1, 2 * chips):
        b = lax.rem(g + d, 2 * chips)
        remote(small, smalls_in.at[b], ssend.at[0], srecv.at[b], r, p).wait_recv()
    own_s.wait()
    keep_s = pltpu.make_async_copy(smalls_in, s_out, lsem.at[2])
    keep_s.start()
    load_w.wait()

    span = heads * HEAD
    bias = vectors_of(smalls_in).astype(jnp.bfloat16)
    full = [
        jnp.concatenate([w0[i % 2, i // 2, 48 * k : 48 * k + 48, :] for i in range(8)], axis=0)
        for k in range(3)
    ]
    lane = iota((width, heads * LANES), 1)
    head, lane_in = lax.div(lane, LANES), lax.rem(lane, LANES)
    column = span * z + head * HEAD + lax.rem(lane_in, HEAD)
    hit = iota((width, heads * LANES), 0) == column
    pick_k = jnp.where(hit & (lane_in < 64), 1.0, 0.0).astype(jnp.bfloat16)
    pick_v = jnp.where(hit & (lane_in >= 64) & (lane_in < 96), 1.0, 0.0).astype(jnp.bfloat16)
    wrow[...] = (dot(full[1], pick_k) + dot(full[2], pick_v)).astype(jnp.bfloat16)
    row_kv = dot(bias[1:2, :], pick_v)
    pick_t = jnp.where(
        iota((span, width), 1) == span * z + iota((span, width), 0), 1.0, 0.0
    ).astype(jnp.bfloat16)

    def by_rows(left, right):
        return lax.dot_general(
            left, right, (((1,), (1,)), ((), ())), preferred_element_type=jnp.float32
        )

    for k in range(3):
        wtr[k] = by_rows(pick_t, full[k]).astype(jnp.bfloat16)
    column_bias = by_rows(pick_t, bias)
    col_q, col_v = column_bias[:, 0:1], column_bias[:, 1:2]
    scale = (HEAD ** -0.5) * LOG2E
    one_lane = lax.rem(iota((1, heads * LANES), 1), LANES)
    row_kv = row_kv + jnp.where((one_lane >= 104) & (one_lane < 107), 1.0, 0.0)
    one = jnp.where(iota((16, rows), 0) == 0, 1.0, 0.0).astype(jnp.bfloat16)

    def stores(b):
        cols = pl.ds(pl.multiple_of(b * rows, rows), rows)
        return [
            pltpu.make_async_copy(kv.at[:, cols, :], kv_out.at[:, cols, :], psems.at[0, b])
        ] + [
            pltpu.make_async_copy(ref.at[:, :, cols], out.at[:, :, cols], psems.at[1 + i, b])
            for i, (ref, out) in enumerate(((qh, qh_out), (kt, kt_out), (vt, vt_out), (q1, q1_out)))
        ]

    def project(i, most):
        half = lax.rem(i, 2)
        b = 2 * chip_at(z, lax.div(i, 2)) + c + half - 2 * c * half
        xb = x[b]
        two = smalls_in[b, 8:16, :].astype(jnp.float32)
        ids = jnp.where(c == 0, two[1:2], two[2:3])
        same = jnp.where(iota((8, rows), 0).astype(jnp.float32) == ids, 1.0, 0.0)
        hot = jnp.concatenate(
            [jnp.zeros((96, rows), jnp.float32), same, jnp.zeros((24, rows), jnp.float32)], axis=0
        ).T
        cols = pl.ds(pl.multiple_of(b * rows, rows), rows)
        flat = dot(xb, wrow[...]) + row_kv
        for h in range(heads):
            kv[h, cols, :] = (flat[:, h * LANES : (h + 1) * LANES] + hot).astype(jnp.bfloat16)
        q_t = (by_rows(wtr[0], xb) + col_q).astype(jnp.bfloat16)
        k_t = by_rows(wtr[1], xb).astype(jnp.bfloat16)
        v_t = (by_rows(wtr[2], xb) + col_v).astype(jnp.bfloat16)
        q_wide = q_t.astype(jnp.float32) * scale
        k_wide = k_t.astype(jnp.float32)
        q_hi = q_wide.astype(jnp.bfloat16)
        q_lo = (q_wide - q_hi.astype(jnp.float32)).astype(jnp.bfloat16)
        sizes = []
        for n, v in enumerate((q_wide, k_wide)):
            size = most[n]
            for h in range(heads):
                size = jnp.maximum(
                    size, jnp.sum(v[h * HEAD : (h + 1) * HEAD] ** 2, axis=0, keepdims=True)
                )
            sizes.append(size)
        for h in range(heads):
            part = slice(h * HEAD, (h + 1) * HEAD)
            qh[h, 0:32, cols] = q_hi[part]
            qh[h, 32:64, cols] = q_lo[part]
            kt[h, :, cols] = k_t[part]
            q1[h, :, cols] = q_t[part]
            vt[h, 0:32, cols] = v_t[part]
            vt[h, 32:48, cols] = one
        for copy in stores(b):
            copy.start()
        return tuple(sizes)

    zero = jnp.zeros((1, rows), jnp.float32)
    most = lax.fori_loop(0, 6, project, (zero, zero))
    tokens_from(3)
    most = lax.fori_loop(6, 8, project, most)
    norms[0:1, :] = most[0]
    norms[1:2, :] = most[1]

    def settle(b, none):
        keep(b).wait()
        for copy in stores(b):
            copy.wait()
        return none

    swap.wait_send()
    for copy in first + smalls + second + third:
        copy.wait_send()
    for b in range(2 * chips):
        @pl.when((z < chips - 1) & (b < 2 * z + 2))
        def _():
            pass_on(b, 0).wait_send()

        @pl.when((z > 0) & (b >= 2 * z))
        def _():
            pass_on(b, 1).wait_send()

    keep_s.wait()
    lax.fori_loop(0, 2 * chips, settle, 0)


def gather(tokens, weights, vectors, inner, seg):
    dma = pltpu.SemaphoreType.DMA
    anywhere = pl.BlockSpec(memory_space=pltpu.HBM)
    vm = pl.BlockSpec(memory_space=pltpu.VMEM)
    rows, width = tokens.shape[1:]
    bf, f4 = jnp.bfloat16, jnp.float32
    heads, length = 3, 8 * rows
    made = [
        (heads, length, LANES), (heads, 64, length), (heads, HEAD, length), (heads, 48, length), (heads, HEAD, length)
    ]
    return pl.pallas_call(
        gather_kernel,
        name="gather",
        out_shape=(
            jax.ShapeDtypeStruct((8, rows, width), bf),
            jax.ShapeDtypeStruct((4, 2, 4, 144, width), bf),
            jax.ShapeDtypeStruct((8, 16, rows), bf),
        )
        + tuple(jax.ShapeDtypeStruct(shape, bf) for shape in made)
        + (jax.ShapeDtypeStruct((2, rows), f4),),
        in_specs=[anywhere] * 7 + [vm] * 3,
        out_specs=[anywhere] * 8 + [vm],
        scratch_shapes=[
            pltpu.VMEM((16, rows), bf),
            pltpu.VMEM((8, rows, width), bf),
        ]
        + [pltpu.VMEM(shape, bf) for shape in made]
        + [
            pltpu.VMEM((2, 4, 144, width), bf),
            pltpu.VMEM((8, 16, rows), bf),
            pltpu.VMEM((width, heads * LANES), bf),
            pltpu.VMEM((3, heads * HEAD, width), bf),
            pltpu.VMEM((144, width), bf),
            dma((6,)), dma((8,)), dma((5, 8)), dma((2, 8)), dma((8,)), dma, dma((3,)), dma((4,)), dma((3,)), dma((4,)),
            dma((4,)), dma((4,)), dma((7,)), dma((8,)),
        ],
        compiler_params=pltpu.CompilerParams(
            collective_id=1, has_side_effects=True, vmem_limit_bytes=BIG
        ),
    )(tokens, *weights, vectors, inner, seg)


def span_of(starts, q0, docs):
    low = jnp.int32(0)
    high = starts[docs]
    for d in range(docs):
        low = jnp.where(starts[d] <= q0, jnp.maximum(low, starts[d]), low)
        high = jnp.where(starts[d + 1] >= q0 + QB, jnp.minimum(high, starts[d + 1]), high)
    first = lax.div(low, LANES)
    return first, lax.div(high + LANES - 1, LANES) - first


def in_groups(first, count, total, body):
    def at(i):
        return pl.multiple_of(i * LANES, LANES)

    big = count >= LONG - 1

    @pl.when(big)
    def _():
        body(pl.ds(at(jnp.minimum(first, total - LONG)), LONG * LANES))

    first = jnp.where(big, first + LONG, first)
    count = jnp.where(big, jnp.maximum(count - LONG, 0), count)
    many = jnp.maximum(lax.div(count, 4) - 1, 0)

    def group(i, none):
        body(pl.ds(at(first + 4 * i), 4 * LANES))
        return none

    lax.fori_loop(0, many, group, 0)
    left = count - 4 * many
    for k in range(1, 8):
        @pl.when(left == k)
        def _():
            body(pl.ds(at(first + 4 * many), k * LANES))


def attend_kernel(
    place, kv, qh, vt, small, norms, ctx, ctx32, tail_out, spans, qt, acc, tall, seg, starts, sem,
):
    heads, length, _ = kv.shape
    blocks, hw, rows = ctx.shape
    docs = 8
    c = place[1]
    load = pltpu.make_async_copy(qh, qt.at[:, pl.ds(0, 64), :], sem)
    load.start()
    for g in range(8):
        two = small[g, 8:16, :].astype(jnp.float32)
        seg[g : g + 1, :] = jnp.where(c == 0, two[1:2], two[2:3]).astype(jnp.int32)
    ids = seg[...]
    starts[0] = jnp.int32(0)
    for d in range(1, docs):
        starts[d] = jnp.sum(jnp.where(ids < d, 1.0, 0.0)).astype(jnp.int32)
    starts[docs] = jnp.int32(length)

    def far(same):
        return (same - 1.0) * AWAY

    def fill(b, none):
        cols = pl.ds(pl.multiple_of(b * rows, rows), rows)
        same = jnp.where(iota((8, rows), 0) == seg[pl.ds(b, 1), :], 1.0, 0.0)
        low = jnp.concatenate([far(same), jnp.zeros((8, rows), jnp.float32)], axis=0)
        for h in range(heads):
            qt[h, 64:96, cols] = jnp.zeros((32, rows), jnp.bfloat16)
            qt[h, 96:112, cols] = low.astype(jnp.bfloat16)
            qt[h, 112:128, cols] = jnp.zeros((16, rows), jnp.bfloat16)
        return none

    lax.fori_loop(0, blocks, fill, 0)
    bounded = jnp.max(norms[0:1, :]) * jnp.max(norms[1:2, :]) < LIMIT * LIMIT
    load.wait()

    per = rows // QB

    def query_block(b, carry):
        q0 = pl.multiple_of(b * QB, QB)
        first, count = span_of(starts, q0, docs)
        spans[0, b] = first
        spans[1, b] = count
        acc[...] = jnp.zeros_like(acc)

        def key_block(i, tops):
            keys = pl.ds(pl.multiple_of((first + i) * LANES, LANES), LANES)
            s = [dot(kv[h, keys, :], qt[h, :, pl.ds(q0, QB)]) for h in range(heads)]
            new = [jnp.maximum(tops[h], jnp.max(s[h], axis=0, keepdims=True)) for h in range(heads)]
            p = [jnp.exp2(s[h] - new[h]).astype(jnp.bfloat16) for h in range(heads)]
            for h in range(heads):
                acc[h] = acc[h] * jnp.exp2(tops[h] - new[h]) + dot(vt[h, :, keys], p[h])
            return tuple(new)

        def plain_block(keys):
            s = [dot(kv[h, keys, :], qt[h, :, pl.ds(q0, QB)]) for h in range(heads)]
            p = [jnp.exp2(v).astype(jnp.bfloat16) for v in s]
            for h in range(heads):
                acc[h] += dot(vt[h, :, keys], p[h])

        @pl.when(bounded)
        def _():
            in_groups(first, count, length // LANES, plain_block)
            tall[...] = jnp.zeros_like(tall)

        @pl.when(jnp.logical_not(bounded))
        def _():
            lowest = jnp.full((1, QB), -3e38, jnp.float32)
            tops = lax.fori_loop(0, count, key_block, (lowest,) * heads)
            for h in range(heads):
                tall[h] = tops[h]

        g = lax.div(b, per)
        off = pl.multiple_of(lax.rem(b, per) * QB, QB)
        same = jnp.where(iota((8, QB), 0) == seg[pl.ds(g, 1), pl.ds(off, QB)], 1.0, 0.0)
        for h in range(heads):
            total = acc[h, 32:33, :]
            out = acc[h, 0:32, :] / total
            ctx[g, h * HEAD : (h + 1) * HEAD, pl.ds(off, QB)] = out.astype(jnp.bfloat16)
            ctx32[g, h * HEAD : (h + 1) * HEAD, pl.ds(off, QB)] = out
            parts = halves(-(tall[h] + jnp.log2(total)))
            tail = jnp.concatenate([far(same), *parts, jnp.zeros((5, QB), jnp.float32)], axis=0)
            tail_out[h, :, pl.ds(q0, QB)] = tail.astype(jnp.bfloat16)
        return carry

    lax.fori_loop(0, length // QB, query_block, 0)


def attend(place, kv, qh, vt, small, norms):
    heads, length, _ = kv.shape
    blocks, _, rows = small.shape
    sm = pl.BlockSpec(memory_space=pltpu.SMEM)
    anywhere = pl.BlockSpec(memory_space=pltpu.HBM)
    bf, f4 = jnp.bfloat16, jnp.float32
    shapes = (
        jax.ShapeDtypeStruct((blocks, heads * HEAD, rows), bf),
        jax.ShapeDtypeStruct((blocks, heads * HEAD, rows), f4),
        jax.ShapeDtypeStruct((heads, 16, length), bf),
    )
    return pl.pallas_call(
        attend_kernel,
        name="attend",
        grid=(1,),
        out_shape=shapes + (jax.ShapeDtypeStruct((2, length // QB), jnp.int32),),
        in_specs=[sm, whole_spec(kv), anywhere, whole_spec(vt), whole_spec(small), whole_spec(norms)],
        out_specs=[whole_spec(v) for v in shapes] + [sm],
        scratch_shapes=[
            pltpu.VMEM((heads, LANES, length), bf),
            pltpu.VMEM((heads, 48, QB), f4),
            pltpu.VMEM((heads, 1, QB), f4),
            pltpu.VMEM((8, rows), jnp.int32),
            pltpu.SMEM((16,), jnp.int32),
            pltpu.SemaphoreType.DMA,
        ],
        compiler_params=pltpu.CompilerParams(vmem_limit_bytes=BIG),
    )(place, kv, qh, vt, small, norms)


PIECE = 128


def middle_kernel(
    ctx, tok, og, w, small,
    layer_out, grad_one_out, gctx_out, pr,
    wo, wi, wu, gwo, gwi, gwu, sums, inner_sum, ctx_in, gctx, pg, pg_in,
    lsem, send, recv, gsend, grecv, glocal, psend, precv,
):
    seqs, rows, width = tok.shape
    slabs = wi.shape[0]
    pieces = rows // PIECE
    r, g, z, c = where_am_i()
    greet(r, g, 1, 8)

    def fetch(q):
        cols = pl.ds(pl.multiple_of(q * PIECE, PIECE), PIECE)
        for d in range(1, 8):
            to = lax.rem(g + d, 8)
            remote(
                ctx.at[to, :, cols], ctx_in.at[c, z, :, cols], send.at[q, d - 1], recv.at[q, g], r, to
            ).start()

    own = pltpu.make_async_copy(ctx.at[g], ctx_in.at[c, z], lsem)
    own.start()
    fetch(0)
    fetch(1)
    for i in range(8):
        cc, zz = i % 2, i // 2
        wo[48 * i : 48 * i + 48, :] = w[1, cc, zz, 0:48, :]
        wi[0, 48 * i : 48 * i + 48, :] = w[1, cc, zz, 48:96, :]
        wi[1, 48 * i : 48 * i + 48, :] = w[1, cc, zz, 96:144, :]
        wi[2, 48 * i : 48 * i + 48, :] = w[2, cc, zz, 0:48, :]
        wi[3, 48 * i : 48 * i + 48, :] = w[2, cc, zz, 48:96, :]
        wu[zz, 192 * cc : 192 * cc + 48, :] = w[2, cc, zz, 96:144, :]
        wu[zz, 192 * cc + 48 : 192 * cc + 192, :] = w[3, cc, zz, :, :]
    for ref in (gwo, gwi, gwu, sums, inner_sum):
        ref[...] = jnp.zeros_like(ref)
    fetch(2)
    fetch(3)

    vec = vectors_of(small)
    inner_bias = jnp.concatenate(
        [small[i, 8:16, 0:192].astype(jnp.float32)[0:1] for i in range(8)], axis=1
    )
    out_bias, outer_bias = vec[2:3, :], vec[3:4, :]
    gain_one, shift_one = vec[4:5, :], vec[5:6, :]
    gain_two, shift_two = vec[6:7, :], vec[7:8, :]

    def normal(value):
        centre = value - jnp.mean(value, axis=-1, keepdims=True)
        rate = lax.rsqrt(jnp.mean(centre * centre, axis=-1, keepdims=True) + norm_epsilon)
        return centre * rate, rate

    def normal_back(grad, gain, n, rate):
        u = grad * gain
        return rate * (
            u - jnp.mean(u, axis=-1, keepdims=True) - n * jnp.mean(u * n, axis=-1, keepdims=True)
        )

    def total(value):
        return jnp.sum(value, axis=0, keepdims=True)

    def dot_turn(left, right):
        return lax.dot_general(
            left, right, (((1,), (1,)), ((), ())), preferred_element_type=jnp.float32
        )

    def arrived(q, cols):
        for d in range(1, 8):
            b = lax.rem(g + d, 8)
            remote(
                ctx.at[g, :, cols], ctx_in.at[lax.rem(b, 2), lax.div(b, 2), :, cols],
                send.at[q, 0], recv.at[q, b], r, b,
            ).wait_recv()

    def return_piece(q, cols, d):
        to = lax.rem(g + d, 8)
        return remote(
            gctx.at[lax.rem(to, 2), lax.div(to, 2), :, cols], gctx_out.at[g, :, cols],
            gsend.at[q, d - 1], grecv.at[q, g], r, to,
        )

    def keep_piece(q, cols):
        return pltpu.make_async_copy(gctx.at[c, z, :, cols], gctx_out.at[g, :, cols], glocal.at[q])

    own.wait()

    def one(q, carry):
        r0 = pl.multiple_of(q * PIECE, PIECE)
        here = pl.ds(r0, PIECE)
        arrived(q, here)

        def both(ref):
            return jnp.concatenate([ref[s, here, :] for s in range(seqs)], axis=0)

        def split(ref, value):
            for s in range(seqs):
                ref[s, here, :] = value[s * PIECE : (s + 1) * PIECE].astype(ref.dtype)

        ctx_t = jnp.concatenate(
            [jnp.concatenate([ctx_in[s, zz, :, here] for zz in range(4)], axis=0) for s in range(seqs)],
            axis=1,
        )
        context = ctx_t.astype(jnp.float32).T.astype(jnp.bfloat16)
        x = both(tok).astype(jnp.float32)
        n_one, rate_one = normal(x + (dot(context, wo[...]) + out_bias))
        hidden = n_one * gain_one + shift_one
        low = hidden.astype(jnp.bfloat16)
        low_t = hidden.T.astype(jnp.bfloat16)
        feed = jnp.zeros(hidden.shape, jnp.float32)
        slopes, actives = [], []
        for j in range(slabs):
            inner = dot(low, wi[j]) + inner_bias[:, j * width : (j + 1) * width]
            cdf = 0.5 + 0.5 * lax.erf(inner * (0.5 ** 0.5))
            pdf = jnp.exp(inner * inner * -0.5) * 0.3989422804014327
            slopes.append(cdf + inner * pdf)
            active = inner * cdf
            actives.append(active)
            feed = feed + dot(active.astype(jnp.bfloat16), wu[j])
        n_two, rate_two = normal(hidden + (feed + outer_bias))
        split(layer_out, n_two * gain_two + shift_two)
        grad = both(og).astype(jnp.float32)
        grad_two = normal_back(grad, gain_two, n_two, rate_two)
        grad_feed = grad_two.astype(jnp.bfloat16)
        grad_hidden = grad_two
        for j in range(slabs):
            grad_inner = (dot_turn(grad_feed, wu[j]) * slopes[j]).astype(jnp.bfloat16)
            inner_sum[:, j * width : (j + 1) * width] += total(grad_inner.astype(jnp.float32))
            grad_hidden = grad_hidden + dot_turn(grad_inner, wi[j])
            gwi[j] += dot(low_t, grad_inner)
            gwu[j] += dot(actives[j].T.astype(jnp.bfloat16), grad_feed)
        grad_one = normal_back(grad_hidden, gain_one, n_one, rate_one)
        split(grad_one_out, grad_one)
        grad_att = grad_one.astype(jnp.bfloat16)
        back = dot_turn(wo[...], grad_att).astype(jnp.bfloat16)
        for s in range(seqs):
            for zz in range(4):
                gctx[s, zz, :, here] = back[96 * zz : 96 * zz + 96, s * PIECE : (s + 1) * PIECE]
        for d in range(1, 8):
            return_piece(q, here, d).start()
        keep_piece(q, here).start()
        gwo[...] += dot(ctx_t, grad_att)
        sums[0:1, :] += total(grad_att.astype(jnp.float32))
        sums[1:2, :] += total(grad_feed.astype(jnp.float32))
        sums[2:3, :] += total(grad_hidden * n_one)
        sums[3:4, :] += total(grad_hidden)
        sums[4:5, :] += total(grad * n_two)
        sums[5:6, :] += total(grad)
        return carry

    lax.fori_loop(0, pieces, one, 0)
    rows_of_sums = jnp.concatenate(
        [sums[...]]
        + [inner_sum[:, j * width : (j + 1) * width] for j in range(slabs)]
        + [jnp.zeros((6, width), jnp.float32)],
        axis=0,
    ).astype(jnp.bfloat16)
    for i in range(8):
        cc, zz = i % 2, i // 2
        mine = slice(48 * i, 48 * i + 48)
        pg[cc, zz, 0, 0:48, :] = gwo[mine, :].astype(jnp.bfloat16)
        pg[cc, zz, 0, 48:96, :] = gwi[0, mine, :].astype(jnp.bfloat16)
        pg[cc, zz, 1, 0:48, :] = gwi[1, mine, :].astype(jnp.bfloat16)
        pg[cc, zz, 1, 48:96, :] = gwi[2, mine, :].astype(jnp.bfloat16)
        pg[cc, zz, 2, 0:48, :] = gwi[3, mine, :].astype(jnp.bfloat16)
        base = 192 * cc
        pg[cc, zz, 0, 96:112, :] = gwu[zz, base : base + 16, :].astype(jnp.bfloat16)
        pg[cc, zz, 1, 96:112, :] = gwu[zz, base + 16 : base + 32, :].astype(jnp.bfloat16)
        pg[cc, zz, 2, 48:112, :] = gwu[zz, base + 32 : base + 96, :].astype(jnp.bfloat16)
        pg[cc, zz, 3, 0:96, :] = gwu[zz, base + 96 : base + 192, :].astype(jnp.bfloat16)
        pg[cc, zz, 3, 96:112, :] = rows_of_sums
    pair = remote(pg.at[1 - c], pg_in, psend, precv, r, 2 * z + 1 - c)
    pair.start()

    def settle(q, carry):
        cols = pl.ds(pl.multiple_of(q * PIECE, PIECE), PIECE)
        for d in range(1, 8):
            b = lax.rem(g + d, 8)
            remote(
                gctx.at[c, z, :, cols], gctx_out.at[b, :, cols], gsend.at[q, 0], grecv.at[q, b], r, b
            ).wait_recv()
            return_piece(q, cols, d).wait_send()
            to = lax.rem(g + d, 8)
            remote(
                ctx.at[to, :, cols], ctx_in.at[c, z, :, cols], send.at[q, d - 1], recv.at[q, g], r, to
            ).wait_send()
        keep_piece(q, cols).wait()
        return carry

    pair.wait_recv()
    for i in range(4):
        pr[i] = (pg[c, i].astype(jnp.float32) + pg_in[i].astype(jnp.float32)).astype(jnp.bfloat16)
    lax.fori_loop(0, pieces, settle, 0)
    pair.wait_send()


def middle(ctx, tok, og, w, small):
    seqs, rows, width = tok.shape
    vm = pl.BlockSpec(memory_space=pltpu.VMEM)
    anywhere = pl.BlockSpec(memory_space=pltpu.HBM)
    dma = pltpu.SemaphoreType.DMA
    bf, f4 = jnp.bfloat16, jnp.float32
    pieces = rows // PIECE
    return pl.pallas_call(
        middle_kernel,
        name="middle",
        out_shape=(
            jax.ShapeDtypeStruct((seqs, rows, width), bf),
            jax.ShapeDtypeStruct((seqs, rows, width), f4),
            jax.ShapeDtypeStruct(ctx.shape, bf),
            jax.ShapeDtypeStruct((4, 4, 112, width), bf),
        ),
        in_specs=[anywhere] + [vm] * 4,
        out_specs=[vm, vm, anywhere, vm],
        scratch_shapes=[
            pltpu.VMEM((width, width), bf),
            pltpu.VMEM((4, width, width), bf),
            pltpu.VMEM((4, width, width), bf),
            pltpu.VMEM((width, width), f4),
            pltpu.VMEM((4, width, width), f4),
            pltpu.VMEM((4, width, width), f4),
            pltpu.VMEM((6, width), f4),
            pltpu.VMEM((1, 4 * width), f4),
            pltpu.VMEM((2, 4) + ctx.shape[1:], bf),
            pltpu.VMEM((2, 4) + ctx.shape[1:], bf),
            pltpu.VMEM((2, 4, 4, 112, width), bf),
            pltpu.VMEM((4, 4, 112, width), bf),
            dma, dma((pieces, 7)), dma((pieces, 8)), dma((pieces, 7)), dma((pieces, 8)), dma((pieces,)), dma, dma,
        ],
        compiler_params=pltpu.CompilerParams(
            collective_id=2, has_side_effects=True, vmem_limit_bytes=BIG
        ),
    )(ctx, tok, og, w, small)


def attend_back_kernel(
    last, index, place, spans, x_hbm, qh, tail, kv, kt, q1, gctx, ctx32, *refs,
):
    heads = kv.shape[0]
    span = heads * HEAD
    if last:
        grads_in, out, gq, dt, do, acc, dq, qt, x, sems = refs
    else:
        out, grads_out, dt, do, acc, dq, qt, x, sems = refs
    length, width = x.shape
    mine = pl.ds(index * heads, heads)
    loads = [
        pltpu.make_async_copy(qh.at[mine], qt.at[:, pl.ds(0, 64), :], sems.at[0]),
        pltpu.make_async_copy(tail.at[mine], qt.at[:, pl.ds(96, 16), :], sems.at[1]),
        pltpu.make_async_copy(x_hbm, x, sems.at[2]),
    ]
    for load in loads:
        load.start()
    blocks, _, rows = gctx.shape
    z = place[0]
    c = place[1]
    scale = HEAD ** -0.5

    def prepare(g, carry):
        r0 = pl.multiple_of(g * rows, rows)
        cols = pl.ds(r0, rows)
        for h in range(heads):
            part = slice(h * HEAD, (h + 1) * HEAD)
            grad = gctx[g, part, :]
            wide = grad.astype(jnp.float32)
            delta = -jnp.sum(wide * ctx32[g, part, :], axis=0, keepdims=True)
            dt[h, 0:64, cols] = jnp.zeros((64, rows), jnp.bfloat16)
            dt[h, 64:96, cols] = grad
            qt[h, 64:96, cols] = jnp.zeros((32, rows), jnp.bfloat16)
            qt[h, 112:128, cols] = jnp.zeros((16, rows), jnp.bfloat16)
            tail = jnp.concatenate(
                [jnp.zeros((8, rows), jnp.float32), *halves(delta), jnp.zeros((21, rows), jnp.float32)],
                axis=0,
            )
            dt[h, 96:128, cols] = tail.astype(jnp.bfloat16)
            turned = jnp.concatenate(
                [wide, q1[h, :, cols].astype(jnp.float32), jnp.zeros((64, rows), jnp.float32)], axis=0
            ).T
            lane = iota((rows, LANES), 1)
            grad_rows = jnp.where(lane < HEAD, turned, 0.0).astype(jnp.bfloat16)
            query_rows = jnp.where(lane < HEAD, 0.0, turned).astype(jnp.bfloat16)
            for j in range(rows // QB):
                r1 = pl.multiple_of(2 * r0 + 2 * j * QB, QB)
                do[h, pl.ds(r1, QB), :] = grad_rows[j * QB : (j + 1) * QB]
                do[h, pl.ds(r1 + QB, QB), :] = query_rows[j * QB : (j + 1) * QB]
        return carry

    lax.fori_loop(0, blocks, prepare, 0)
    acc[...] = jnp.zeros_like(acc)
    per = rows // QB
    loads[0].wait()
    loads[1].wait()

    def query_block(b, carry):
        q0 = pl.multiple_of(b * QB, QB)
        dq[...] = jnp.zeros_like(dq)

        def key_block(keys):
            s = [dot(kv[h, keys, :], qt[h, :, pl.ds(q0, QB)]) for h in range(heads)]
            d = [dot(kv[h, keys, :], dt[h, :, pl.ds(q0, QB)]) for h in range(heads)]
            p = [jnp.exp2(v) for v in s]
            both = [
                jnp.concatenate([u.astype(jnp.bfloat16), (u * v).astype(jnp.bfloat16)], axis=1)
                for u, v in zip(p, d)
            ]
            for h in range(heads):
                acc[h, keys, :] += dot(both[h], do[h, pl.ds(2 * q0, 2 * QB), :])
            for h in range(heads):
                dq[h] += dot(kt[h, :, keys], both[h][:, QB:])

        in_groups(spans[0, b], spans[1, b], length // LANES, key_block)
        g = lax.div(b, per)
        off = pl.multiple_of(lax.rem(b, per) * QB, QB)
        for h in range(heads):
            out[g, h * HEAD : (h + 1) * HEAD, pl.ds(off, QB)] = (dq[h] * scale).astype(jnp.bfloat16)
        return carry

    lax.fori_loop(0, length // QB, query_block, 0)

    loads[2].wait()

    def finish_block(g, totals):
        r0 = pl.multiple_of(g * rows, rows)
        cols = pl.ds(r0, rows)
        for h in range(heads):
            both = acc[h, cols, :].T
            row = h * HEAD
            out[g, 2 * span + row : 2 * span + row + HEAD, :] = both[0:32].astype(jnp.bfloat16)
            out[g, span + row : span + row + HEAD, :] = (both[32:64] * scale).astype(jnp.bfloat16)
        piece = out[g]
        grad = dot(piece, x[cols, :])
        summed = jnp.sum(piece.astype(jnp.float32), axis=1, keepdims=True)
        return totals[0] + grad, totals[1] + summed

    grads, summed = lax.fori_loop(
        0,
        blocks,
        finish_block,
        (jnp.zeros((3 * span, width), jnp.float32), jnp.zeros((3 * span, 1), jnp.float32)),
    )
    if not last:
        grads_out[:, 0:width] = grads
        grads_out[:, width:] = jnp.broadcast_to(summed, (3 * span, LANES))
        return
    gq[...] = jnp.zeros_like(gq)
    before = grads_in.shape[0] // 3

    def joined(i, old, new):
        return [old[i * before : (i + 1) * before], new[i * span : (i + 1) * span]]

    old = grads_in[:, 0:width]
    whole = jnp.concatenate([v for i in range(3) for v in joined(i, old, grads)], axis=0).T
    total = 3 * (before + span)
    for g in range(8):
        gq[g % 2, g // 2, :, 0:total] = whole[48 * g : 48 * g + 48, :].astype(jnp.bfloat16)
    old = grads_in[:, width : width + 1]
    of_q = jnp.concatenate(joined(0, old, summed), axis=0)
    of_v = jnp.concatenate(joined(2, old, summed), axis=0)
    for cc in range(2):
        mine = jnp.concatenate(
            [
                of_q[48 * cc : 48 * cc + 48, :],
                of_v[48 * cc : 48 * cc + 48, :],
                jnp.zeros((48, 94), jnp.float32),
            ],
            axis=1,
        )
        gq[cc, z, :, total:] = mine.astype(jnp.bfloat16)


def attend_back(heads, index, place, spans, x, qh, tail, kv, kt, q1, gctx, ctx32, grads=None):
    blocks, rows, width = x.shape
    length = blocks * rows
    last = grads is not None
    rest = (grads,) if last else ()
    sm = pl.BlockSpec(memory_space=pltpu.SMEM)
    bf, f4 = jnp.bfloat16, jnp.float32
    once = pl.Buffered(1)
    span = heads * HEAD

    def some_heads(array):
        return pl.BlockSpec((heads,) + array.shape[1:], lambda i: (index, 0, 0), pipeline_mode=once)

    def head_rows(array):
        return pl.BlockSpec((blocks, span, rows), lambda i: (0, index, 0), pipeline_mode=once)

    flat = x.reshape(length, width)
    shapes = (
        jax.ShapeDtypeStruct((blocks, 3 * span, rows), bf),
        jax.ShapeDtypeStruct((2, 4, 48, width), bf)
        if last
        else jax.ShapeDtypeStruct((3 * span, width + LANES), f4),
    )
    return pl.pallas_call(
        functools.partial(attend_back_kernel, last, index),
        name="attend_back",
        grid=(1,),
        out_shape=shapes,
        in_specs=[sm, sm] + [pl.BlockSpec(memory_space=pltpu.HBM)] * 3
        + [some_heads(v) for v in (kv, kt, q1)]
        + [head_rows(v) for v in (gctx, ctx32)]
        + [whole_spec(v) for v in rest],
        out_specs=[whole_spec(v) for v in shapes],
        scratch_shapes=[
            pltpu.VMEM((heads, LANES, length), bf),
            pltpu.VMEM((heads, 2 * length, LANES), bf),
            pltpu.VMEM((heads, length, LANES), f4),
            pltpu.VMEM((heads, HEAD, QB), f4),
            pltpu.VMEM((heads, LANES, length), bf),
            pltpu.VMEM((length, width), bf),
            pltpu.SemaphoreType.DMA((3,)),
        ],
        compiler_params=pltpu.CompilerParams(vmem_limit_bytes=BIG),
        cost_estimate=pl.CostEstimate(
            flops=heads * 20 * 10 ** 9, bytes_accessed=heads * 8 * 10 ** 6, transcendentals=heads * 6 * 10 ** 6
        ),
    )(place, spans, flat, qh, tail, kv, kt, q1, gctx, ctx32, *rest)


def reduce_kernel(
    src, gq, pz, dst, p_out, q_out,
    gq_in, gq_sum, qa_in, qa_sum, qb_in, pz_in, p_line, pa_in, p_own, gq_own,
    lsem, send, recv, gsend, grecv, qasend, qarecv, qbsend, qbrecv, qcsend, qcrecv,
    pasend, parecv, pcsend, pcrecv,
):
    r, g, z, c = where_am_i()
    greet(r, g, 4, 8)
    waits = []
    pair = remote(gq.at[1 - c], gq_in, gsend, grecv, r, 2 * z + 1 - c)
    pair.start()
    load_g = pltpu.make_async_copy(gq.at[c], gq_own, lsem.at[1])
    load_g.start()
    load_p = pltpu.make_async_copy(pz, pz_in, lsem.at[2])
    load_p.start()
    own = pltpu.make_async_copy(src.at[g], dst.at[g], lsem.at[0])
    own.start()

    def send_to(d):
        to = lax.rem(g + d, 8)
        copy = remote(src.at[to], dst.at[g], send.at[d - 1], recv.at[g], r, to)
        copy.start()
        waits.append(copy)

    def f32(value):
        return value.astype(jnp.float32)

    load_g.wait()
    pair.wait_recv()
    gq_sum[...] = (f32(gq_own[...]) + f32(gq_in[...])).astype(jnp.bfloat16)
    for d in range(1, 4):
        rr = lax.rem(r + d, 4)
        copy = remote(gq_sum.at[rr], qa_in.at[r], qasend.at[d - 1], qarecv.at[r], rr, g)
        copy.start()
        waits.append(copy)
    load_p.wait()
    total = f32(pz_in[0])
    for i in range(1, 4):
        total = total + f32(pz_in[i])
    p_line[...] = total.astype(jnp.bfloat16)
    for d in range(1, 4):
        rr = lax.rem(r + d, 4)
        copy = remote(p_line.at[rr], pa_in.at[r], pasend.at[d - 1], parecv.at[r], rr, g)
        copy.start()
        waits.append(copy)
    for d in range(1, 4):
        b = lax.rem(r + d, 4)
        remote(gq_sum.at[r], qa_in.at[b], qasend.at[0], qarecv.at[b], b, g).wait_recv()
    total = f32(gq_sum[r])
    for d in range(1, 4):
        total = total + f32(qa_in[lax.rem(r + d, 4)])
    qa_sum[...] = total.astype(jnp.bfloat16)

    @pl.when(z != r)
    def _():
        remote(qa_sum, qb_in.at[z], qbsend, qbrecv.at[z], r, 2 * r + c).start()

    for d in (4, 3, 5, 2, 6, 1, 7):
        send_to(d)
    for d in range(1, 4):
        b = lax.rem(r + d, 4)
        remote(p_line.at[r], pa_in.at[b], pasend.at[0], parecv.at[b], b, g).wait_recv()
    total = f32(p_line[r])
    for d in range(1, 4):
        total = total + f32(pa_in[lax.rem(r + d, 4)])
    p_own[...] = total.astype(jnp.bfloat16)
    keep_p = pltpu.make_async_copy(p_own, p_out.at[r], lsem.at[3])
    keep_p.start()
    for d in range(1, 4):
        rr = lax.rem(r + d, 4)
        copy = remote(p_own, p_out.at[r], pcsend.at[d - 1], pcrecv.at[r], rr, g)
        copy.start()
        waits.append(copy)

    @pl.when(z == r)
    def _():
        for d in range(1, 4):
            b = lax.rem(z + d, 4)
            remote(qa_sum, qb_in.at[b], qbsend, qbrecv.at[b], r, g).wait_recv()
        qb_in[z] = qa_sum[...]
        keep = pltpu.make_async_copy(qb_in, q_out, lsem.at[4])
        keep.start()
        for d in range(1, 4):
            remote(qb_in, q_out, qcsend.at[d - 1], qcrecv, lax.rem(r + d, 4), g).start()
        keep.wait()
        for d in range(1, 4):
            remote(qb_in, q_out, qcsend.at[d - 1], qcrecv, lax.rem(r + d, 4), g).wait_send()

    @pl.when(z != r)
    def _():
        remote(qb_in, q_out, qcsend.at[0], qcrecv, r, g).wait_recv()
        remote(qa_sum, qb_in.at[z], qbsend, qbrecv.at[z], r, 2 * r + c).wait_send()

    for d in range(1, 4):
        b = lax.rem(r + d, 4)
        remote(p_own, p_out.at[b], pcsend.at[0], pcrecv.at[b], b, g).wait_recv()
    for d in range(1, 8):
        b = lax.rem(g + d, 8)
        remote(src.at[g], dst.at[b], send.at[0], recv.at[b], r, b).wait_recv()
    pair.wait_send()
    for copy in waits:
        copy.wait_send()
    keep_p.wait()
    own.wait()


def reduce_all(src, gq, pz):
    dma = pltpu.SemaphoreType.DMA
    anywhere = pl.BlockSpec(memory_space=pltpu.HBM)
    bf = jnp.bfloat16
    width = gq.shape[-1]
    part = (4, 48, width)
    return pl.pallas_call(
        reduce_kernel,
        name="reduce",
        out_shape=(
            jax.ShapeDtypeStruct(src.shape, bf),
            jax.ShapeDtypeStruct((4, 112, width), bf),
            jax.ShapeDtypeStruct(part, bf),
        ),
        in_specs=[anywhere] * 3,
        out_specs=[anywhere] * 3,
        scratch_shapes=[
            pltpu.VMEM(part, bf),
            pltpu.VMEM(part, bf),
            pltpu.VMEM(part, bf),
            pltpu.VMEM((48, width), bf),
            pltpu.VMEM(part, bf),
            pltpu.VMEM((4, 4, 112, width), bf),
            pltpu.VMEM((4, 112, width), bf),
            pltpu.VMEM((4, 112, width), bf),
            pltpu.VMEM((112, width), bf),
            pltpu.VMEM(part, bf),
            dma((5,)), dma((7,)), dma((8,)), dma, dma, dma((3,)), dma((4,)), dma, dma((4,)), dma((3,)), dma,
            dma((3,)), dma((4,)), dma((3,)), dma((4,)),
        ],
        compiler_params=pltpu.CompilerParams(
            collective_id=4, has_side_effects=True, vmem_limit_bytes=BIG
        ),
    )(src, gq, pz)


def finish_kernel(
    place, layer_in, in_0, in_1, grad_one, w, p_in, q_in,
    layer_out, out, g_q, g_k, g_v, g_o, g_in, g_up, rows_out, inner_out, wq, held, sems,
):
    width = w.shape[-1]
    span = 96
    step = pl.program_id(0)
    z = place[0]
    c = place[1]
    load = pltpu.make_async_copy(layer_in, held, sems.at[0])
    store = pltpu.make_async_copy(held, layer_out, sems.at[1])

    @pl.when(step == 0)
    def _():
        load.start()
        for i in range(3):
            for g in range(8):
                wq[i, 48 * g : 48 * g + 48, :] = w[0, g % 2, g // 2, 48 * i : 48 * i + 48, :]

    total = grad_one[0]
    for i in range(3):
        turned = jnp.concatenate(
            [
                ref[zz, 0, i * count : (i + 1) * count, :]
                for zz in range(4)
                for ref, count in ((in_0, in_0.shape[2] // 3), (in_1, in_1.shape[2] // 3))
            ],
            axis=0,
        )
        back = turned.astype(jnp.float32).T.astype(jnp.bfloat16)
        total = total + lax.dot_general(
            back, wq[i], (((1,), (1,)), ((), ())), preferred_element_type=jnp.float32
        )
    out[0] = total.astype(jnp.bfloat16)

    @pl.when(step == 0)
    def _():
        load.wait()
        store.start()
        wide = [q_in[zz].astype(jnp.float32) for zz in range(4)]
        for i, ref in enumerate((g_q, g_k, g_v)):
            ref[...] = jnp.concatenate([v[:, i * span : (i + 1) * span] for v in wide], axis=1)
        sums = p_in[3, 96:112, :]
        pick = jnp.where(
            iota((width, 48), 0) == 48 * (2 * z + c) + iota((width, 48), 1), 1.0, 0.0
        ).astype(jnp.bfloat16)
        rows_out[8:24, :] = dot(sums, pick)
        both = q_in[z].astype(jnp.float32)[:, 3 * span :].T
        rows_out[0:8, :] = both[0:8, :]
        pick = jnp.where(
            iota((width, 192), 0) == 192 * c + iota((width, 192), 1), 1.0, 0.0
        ).astype(jnp.bfloat16)
        inner = dot(sums, pick)
        inner_out[...] = jnp.sum(
            jnp.where(iota((16, 192), 0) == 6 + z, inner, 0.0), axis=0, keepdims=True
        )
        g_o[...] = p_in[0, 0:48, :].astype(jnp.float32)
        g_in[:, 0:384] = p_in[0, 48:96, :].astype(jnp.float32)
        g_in[:, 384:768] = p_in[1, 0:48, :].astype(jnp.float32)
        g_in[:, 768:1152] = p_in[1, 48:96, :].astype(jnp.float32)
        g_in[:, 1152:1536] = p_in[2, 0:48, :].astype(jnp.float32)
        g_up[0:16, :] = p_in[0, 96:112, :].astype(jnp.float32)
        g_up[16:32, :] = p_in[1, 96:112, :].astype(jnp.float32)
        g_up[32:96, :] = p_in[2, 48:112, :].astype(jnp.float32)
        g_up[96:192, :] = p_in[3, 0:96, :].astype(jnp.float32)

    @pl.when(step == 1)
    def _():
        store.wait()


def finish(place, layer_in, in_0, in_1, grad_one, w, p_in, q_in):
    seqs, rows, width = grad_one.shape
    sm = pl.BlockSpec(memory_space=pltpu.SMEM)
    hbm = pl.BlockSpec(memory_space=pltpu.HBM)
    bf, f4 = jnp.bfloat16, jnp.float32
    shapes = ((48, width),) * 4 + ((48, 4 * width), (192, width), (24, 48), (1, 192))
    in_0, in_1 = (v.reshape((4, 2) + v.shape[1:]) for v in (in_0, in_1))

    def of_sequence(v):
        return pl.BlockSpec((4, 1) + v.shape[2:], lambda i: (0, i, 0, 0))

    one = pl.BlockSpec((1, rows, width), lambda i: (i, 0, 0))
    return pl.pallas_call(
        finish_kernel,
        name="finish",
        grid=(seqs,),
        out_shape=(jax.ShapeDtypeStruct((seqs, rows, width), bf),) * 2
        + tuple(jax.ShapeDtypeStruct(shape, f4) for shape in shapes),
        in_specs=[
            sm, hbm, of_sequence(in_0), of_sequence(in_1), one,
            quarter_spec(w, 0), whole_spec(p_in), whole_spec(q_in),
        ],
        out_specs=[hbm, one]
        + [pl.BlockSpec(shape, functools.partial(zeros_for, len(shape))) for shape in shapes],
        scratch_shapes=[
            pltpu.VMEM((3, width, width), bf),
            pltpu.VMEM((seqs, rows, width), bf),
            pltpu.SemaphoreType.DMA((2,)),
        ],
        compiler_params=pltpu.CompilerParams(vmem_limit_bytes=BIG - 1600 * 1024),
    )(place, layer_in, in_0, in_1, grad_one, w, p_in, q_in)


def line_of_chips(
    tokens, segment_ids, out_grad, query_weight, key_weight, value_weight, output_weight,
    inner_weight, outer_weight, query_bias, value_bias, output_bias, inner_bias, outer_bias,
    first_gain, first_shift, second_gain, second_shift,
):
    bf = jnp.bfloat16
    width = tokens.shape[2]
    g = lax.axis_index("grp")
    z, c = lax.div(g, 2), lax.rem(g, 2)
    place = jnp.stack([z, c]).astype(jnp.int32)
    weights = (query_weight, key_weight, value_weight, output_weight, inner_weight, outer_weight)
    vectors = jnp.concatenate(
        [
            v[None]
            for v in (
                query_bias, value_bias, output_bias, outer_bias,
                first_gain, first_shift, second_gain, second_shift,
            )
        ],
        axis=0,
    )
    x, w, small, kv, qh, kt, vt, q1, norms = gather(
        tokens, weights, vectors, inner_bias[None], segment_ids
    )
    ctx, ctx32, tail, spans = attend(place, kv, qh, vt, small, norms)
    layer_out, grad_one, gctx_in, pr = middle(ctx, tokens, out_grad, w, small)
    same_core = [[i + j for i in range(0, 8, 2)] for j in range(2)]
    pz = lax.all_to_all(pr, "grp", 0, 0, axis_index_groups=same_core, tiled=True)
    back = functools.partial(
        attend_back, place=place, spans=spans, x=x, qh=qh, tail=tail, kv=kv, kt=kt, q1=q1,
        gctx=gctx_in, ctx32=ctx32,
    )
    parts_0, grads_0 = back(2, 0)
    in_0 = lax.all_to_all(parts_0, "grp", 0, 0, tiled=True)
    parts_1, gq = back(1, 2, grads=grads_0)
    in_1, p_in, q_in = reduce_all(parts_1, gq, pz)
    layer_out, input_grad, g_q, g_k, g_v, g_o, g_in, g_up, rows, inner_row = finish(
        place, layer_out, in_0, in_1, grad_one, w, p_in, q_in
    )
    return (
        layer_out, input_grad, g_q, g_k, g_v, g_o, g_in, g_up,
        rows[0], rows[1], rows[8], inner_row[0], rows[9], rows[10], rows[11], rows[12], rows[13],
    )


def solution(mesh):
    in_specs = (
        P("rep", "grp", None),
        P("rep", "grp"),
        P("rep", "grp", None),
        P("grp", None),
        P("grp", None),
        P("grp", None),
        P("grp", None),
        P("grp", None),
        P("grp", None),
        P("grp"),
        P("grp"),
        P("grp"),
        P("grp"),
        P("grp"),
        P("grp"),
        P("grp"),
        P("grp"),
        P("grp"),
    )
    out_specs = (
        P("rep", "grp", None),
        P("rep", "grp", None),
        P("grp", None),
        P("grp", None),
        P("grp", None),
        P("grp", None),
        P("grp", None),
        P("grp", None),
        P("grp"),
        P("grp"),
        P("grp"),
        P("grp"),
        P("grp"),
        P("grp"),
        P("grp"),
        P("grp"),
        P("grp"),
    )
    whole_line = mesh.shape["grp"] == 8 and mesh.shape["rep"] == 4
    return jax.shard_map(
        line_of_chips if whole_line else on_device, mesh=mesh, in_specs=in_specs, out_specs=out_specs, check_vma=False
    )
```

```python
import functools
from functools import reduce

import jax
import jax.numpy as jnp
from jax import lax
from jax.experimental import pallas as pl
from jax.experimental.pallas import tpu as pltpu
from jax.sharding import PartitionSpec as P

H = 12
MICRO = 2
SEQ_MB = 1


norm_epsilon = 1e-05
masked_score = -1000000000.0


def layer_norm(inputs, norm_gain, norm_shift):
    center = inputs - jnp.mean(inputs, axis=-1, keepdims=True)
    spread = jnp.mean(center * center, axis=-1, keepdims=True)
    return center * lax.rsqrt(spread + norm_epsilon) * norm_gain + norm_shift


def exact_gelu(inputs):
    return jax.nn.gelu(inputs, approximate=False)


def times_transpose(left, right):
    return lax.dot_general(
        left, right, (((1,), (1,)), ((), ())), preferred_element_type=jnp.float32
    )


def transpose_times(left, right):
    return lax.dot_general(
        left, right, (((0,), (0,)), ((), ())), preferred_element_type=jnp.float32
    )


def column_total(inputs):
    return jnp.sum(inputs.astype(jnp.float32), axis=0)


def masked_scores(query_group, key_group, same_doc, score_scale):
    scores = (
        jnp.einsum("bqhd,bkhd->bhqk", query_group, key_group, preferred_element_type=jnp.float32)
        * score_scale
    )
    return jnp.where(same_doc[:, None], scores, masked_score)


def group_forward(query_group, key_group, value_group, same_doc, score_scale):
    scores = masked_scores(query_group, key_group, same_doc, score_scale)
    highest = jnp.max(scores, axis=-1, keepdims=True)
    log_total = highest + jnp.log(jnp.sum(jnp.exp(scores - highest), axis=-1, keepdims=True))
    weights_low = jnp.exp(scores - log_total).astype(jnp.bfloat16)
    context = jnp.einsum(
        "bhqk,bkhd->bqhd", weights_low, value_group, preferred_element_type=jnp.float32
    )
    return (context.astype(jnp.bfloat16), log_total)


def group_backward(
    query_group, key_group, value_group, same_doc, log_total, grad_context, score_scale
):
    attn_weights = jnp.exp(masked_scores(query_group, key_group, same_doc, score_scale) - log_total)
    weights_low = attn_weights.astype(jnp.bfloat16)
    grad_weights = jnp.einsum(
        "bqhd,bkhd->bhqk", grad_context, value_group, preferred_element_type=jnp.float32
    )
    centre = jnp.sum(attn_weights * grad_weights, axis=-1, keepdims=True)
    grad_scores = (attn_weights * (grad_weights - centre)).astype(jnp.bfloat16)
    grad_query = jnp.einsum(
        "bhqk,bkhd->bqhd", grad_scores, key_group, preferred_element_type=jnp.float32
    )
    grad_query = (grad_query * score_scale).astype(jnp.bfloat16)
    grad_key = (
        jnp.einsum("bhqk,bqhd->bkhd", grad_scores, query_group, preferred_element_type=jnp.float32)
        * score_scale
    )
    grad_value = jnp.einsum(
        "bhqk,bqhd->bkhd", weights_low, grad_context, preferred_element_type=jnp.float32
    )
    return (grad_query, grad_key, grad_value)


def merge_groups(stacked, row_total, model_width):
    return jnp.moveaxis(stacked, 0, 2).reshape(row_total, model_width)


def gradient_terms(
    token_rows,
    context_rows,
    hidden_rows,
    active_rows,
    grad_queries,
    grad_keys,
    grad_values,
    grad_attention,
    grad_inner,
    grad_feed,
    norm_grads,
):
    return (
        transpose_times(token_rows, grad_queries),
        transpose_times(token_rows, grad_keys),
        transpose_times(token_rows, grad_values),
        transpose_times(context_rows, grad_attention),
        transpose_times(hidden_rows, grad_inner),
        transpose_times(active_rows, grad_feed),
        column_total(grad_queries),
        column_total(grad_values),
        column_total(grad_attention),
        column_total(grad_inner),
        column_total(grad_feed),
        norm_grads[0],
        norm_grads[1],
        norm_grads[2],
        norm_grads[3],
    )


def on_device(
    tokens,
    segment_ids,
    out_grad,
    query_weight,
    key_weight,
    value_weight,
    output_weight,
    inner_weight,
    outer_weight,
    query_bias,
    value_bias,
    output_bias,
    inner_bias,
    outer_bias,
    first_gain,
    first_shift,
    second_gain,
    second_shift,
):
    row_count = tokens.shape[1]
    model_width = tokens.shape[2]
    head_count = H
    head_size = model_width // head_count
    per_group = max(1, min(head_count, 128 // head_size))
    group_width = per_group * head_size
    group_count = head_count // per_group
    score_scale = head_size ** (-0.5)
    seq_count = SEQ_MB
    flat_rows = seq_count * row_count
    all_segments = lax.all_gather(segment_ids, "grp", axis=1, tiled=True)
    outputs = []
    input_grads = []
    shares_list = []
    for batch_index in range(MICRO):
        offset = batch_index * seq_count
        local_tokens = tokens[offset : offset + seq_count]
        flat_tokens = local_tokens.reshape(flat_rows, model_width)
        gathered = (
            lax.all_gather(query_weight, "grp", axis=0, tiled=True),
            lax.all_gather(key_weight, "grp", axis=0, tiled=True),
            lax.all_gather(value_weight, "grp", axis=0, tiled=True),
            lax.all_gather(output_weight, "grp", axis=0, tiled=True),
            lax.all_gather(inner_weight, "grp", axis=0, tiled=True),
            lax.all_gather(outer_weight, "grp", axis=0, tiled=True),
            lax.all_gather(query_bias, "grp", axis=0, tiled=True),
            lax.all_gather(value_bias, "grp", axis=0, tiled=True),
            lax.all_gather(output_bias, "grp", axis=0, tiled=True),
            lax.all_gather(inner_bias, "grp", axis=0, tiled=True),
            lax.all_gather(outer_bias, "grp", axis=0, tiled=True),
            lax.all_gather(first_gain, "grp", axis=0, tiled=True),
            lax.all_gather(first_shift, "grp", axis=0, tiled=True),
            lax.all_gather(second_gain, "grp", axis=0, tiled=True),
            lax.all_gather(second_shift, "grp", axis=0, tiled=True),
        )
        full_query, full_key, full_value, full_output, full_inner, full_outer = gathered[:6]
        (
            bias_query,
            bias_value,
            bias_output,
            bias_inner,
            bias_outer,
            gain_first,
            shift_first,
            gain_second,
            shift_second,
        ) = [vector.astype(jnp.float32) for vector in gathered[6:]]
        queries = (
            jnp.dot(flat_tokens, full_query, preferred_element_type=jnp.float32) + bias_query
        ).astype(jnp.bfloat16)
        key_rows = jnp.dot(flat_tokens, full_key, preferred_element_type=jnp.float32).astype(
            jnp.bfloat16
        )
        value_rows = (
            jnp.dot(flat_tokens, full_value, preferred_element_type=jnp.float32) + bias_value
        ).astype(jnp.bfloat16)
        key_split = key_rows.reshape(seq_count, row_count, model_width)
        value_split = value_rows.reshape(seq_count, row_count, model_width)
        key_all, value_all = (
            lax.all_gather(key_split, "grp", axis=1, tiled=True),
            lax.all_gather(value_split, "grp", axis=1, tiled=True),
        )
        length = key_all.shape[1]
        local_segments = segment_ids[offset : offset + seq_count]
        far_segments = all_segments[offset : offset + seq_count]
        same_doc = local_segments[:, :, None] == far_segments[:, None, :]
        query_split = queries.reshape(seq_count, row_count, model_width)

        def slice_group(array, group_index):
            piece = lax.dynamic_slice_in_dim(array, group_index * group_width, group_width, 2)
            return piece.reshape(array.shape[0], array.shape[1], per_group, head_size)

        def forward_group(group_index):
            context, log_total = group_forward(
                slice_group(query_split, group_index),
                slice_group(key_all, group_index),
                slice_group(value_all, group_index),
                same_doc,
                score_scale,
            )
            return (context.reshape(seq_count, row_count, group_width), log_total)

        context_groups, log_totals = lax.map(forward_group, jnp.arange(group_count))
        context_rows = merge_groups(context_groups, flat_rows, model_width)
        attention = (
            jnp.dot(context_rows, full_output, preferred_element_type=jnp.float32) + bias_output
        )
        residual_one = flat_tokens.astype(jnp.float32) + attention
        hidden_one, norm_one_pullback = jax.vjp(layer_norm, residual_one, gain_first, shift_first)
        hidden_low = hidden_one.astype(jnp.bfloat16)
        inner_pre = jnp.dot(hidden_low, full_inner, preferred_element_type=jnp.float32) + bias_inner
        activation, gelu_pullback = jax.vjp(exact_gelu, inner_pre)
        active_low = activation.astype(jnp.bfloat16)
        feed = jnp.dot(active_low, full_outer, preferred_element_type=jnp.float32) + bias_outer
        output_rows, norm_two_pullback = jax.vjp(
            layer_norm, hidden_one + feed, gain_second, shift_second
        )
        outputs.append(output_rows.astype(jnp.bfloat16).reshape(seq_count, row_count, model_width))
        cotangent = (
            out_grad[offset : offset + seq_count]
            .reshape(flat_rows, model_width)
            .astype(jnp.float32)
        )
        grad_two, grad_gain_two, grad_shift_two = norm_two_pullback(cotangent)
        grad_feed = grad_two.astype(jnp.bfloat16)
        grad_active = times_transpose(grad_feed, full_outer)
        grad_inner = gelu_pullback(grad_active)[0].astype(jnp.bfloat16)
        grad_hidden = grad_two + times_transpose(grad_inner, full_inner)
        grad_one, grad_gain_one, grad_shift_one = norm_one_pullback(grad_hidden)
        grad_attention = grad_one.astype(jnp.bfloat16)
        grad_context = times_transpose(grad_attention, full_output).astype(jnp.bfloat16)
        grad_context = grad_context.reshape(seq_count, row_count, model_width)

        def backward_group(pieces):
            group_index, log_total = pieces
            grad_query, grad_key, grad_value = group_backward(
                slice_group(query_split, group_index),
                slice_group(key_all, group_index),
                slice_group(value_all, group_index),
                same_doc,
                log_total,
                slice_group(grad_context, group_index),
                score_scale,
            )
            return (
                grad_query.reshape(seq_count, row_count, group_width),
                grad_key.reshape(seq_count, length, group_width),
                grad_value.reshape(seq_count, length, group_width),
            )

        query_groups, key_groups, value_groups = lax.map(
            backward_group, (jnp.arange(group_count), log_totals)
        )
        key_owned, value_owned = (
            lax.psum_scatter(key_groups, "grp", scatter_dimension=2, tiled=True),
            lax.psum_scatter(value_groups, "grp", scatter_dimension=2, tiled=True),
        )
        grad_keys = merge_groups(key_owned, flat_rows, model_width).astype(jnp.bfloat16)
        grad_values = merge_groups(value_owned, flat_rows, model_width).astype(jnp.bfloat16)
        grad_queries = merge_groups(query_groups, flat_rows, model_width)
        grad_tokens = (
            grad_one
            + times_transpose(grad_queries, full_query)
            + times_transpose(grad_keys, full_key)
            + times_transpose(grad_values, full_value)
        )
        input_grads.append(
            grad_tokens.astype(jnp.bfloat16).reshape(seq_count, row_count, model_width)
        )
        norm_grads = (grad_gain_one, grad_shift_one, grad_gain_two, grad_shift_two)
        terms = gradient_terms(
            flat_tokens,
            context_rows,
            hidden_low,
            active_low,
            grad_queries,
            grad_keys,
            grad_values,
            grad_attention,
            grad_inner,
            grad_feed,
            norm_grads,
        )
        shares = (
            lax.psum_scatter(terms[0], "grp", scatter_dimension=0, tiled=True),
            lax.psum_scatter(terms[1], "grp", scatter_dimension=0, tiled=True),
            lax.psum_scatter(terms[2], "grp", scatter_dimension=0, tiled=True),
            lax.psum_scatter(terms[3], "grp", scatter_dimension=0, tiled=True),
            lax.psum_scatter(terms[4], "grp", scatter_dimension=0, tiled=True),
            lax.psum_scatter(terms[5], "grp", scatter_dimension=0, tiled=True),
            lax.psum_scatter(terms[6], "grp", scatter_dimension=0, tiled=True),
            lax.psum_scatter(terms[7], "grp", scatter_dimension=0, tiled=True),
            lax.psum_scatter(terms[8], "grp", scatter_dimension=0, tiled=True),
            lax.psum_scatter(terms[9], "grp", scatter_dimension=0, tiled=True),
            lax.psum_scatter(terms[10], "grp", scatter_dimension=0, tiled=True),
            lax.psum_scatter(terms[11], "grp", scatter_dimension=0, tiled=True),
            lax.psum_scatter(terms[12], "grp", scatter_dimension=0, tiled=True),
            lax.psum_scatter(terms[13], "grp", scatter_dimension=0, tiled=True),
            lax.psum_scatter(terms[14], "grp", scatter_dimension=0, tiled=True),
        )
        shares_list.append(shares)
    owned = reduce(
        lambda left_part, right_part: jax.tree.map(jnp.add, left_part, right_part), shares_list
    )
    summed = (
        lax.psum(owned[0].astype(jnp.bfloat16), "rep").astype(jnp.float32),
        lax.psum(owned[1].astype(jnp.bfloat16), "rep").astype(jnp.float32),
        lax.psum(owned[2].astype(jnp.bfloat16), "rep").astype(jnp.float32),
        lax.psum(owned[3].astype(jnp.bfloat16), "rep").astype(jnp.float32),
        lax.psum(owned[4].astype(jnp.bfloat16), "rep").astype(jnp.float32),
        lax.psum(owned[5].astype(jnp.bfloat16), "rep").astype(jnp.float32),
        lax.psum(owned[6].astype(jnp.bfloat16), "rep").astype(jnp.float32),
        lax.psum(owned[7].astype(jnp.bfloat16), "rep").astype(jnp.float32),
        lax.psum(owned[8].astype(jnp.bfloat16), "rep").astype(jnp.float32),
        lax.psum(owned[9].astype(jnp.bfloat16), "rep").astype(jnp.float32),
        lax.psum(owned[10].astype(jnp.bfloat16), "rep").astype(jnp.float32),
        lax.psum(owned[11].astype(jnp.bfloat16), "rep").astype(jnp.float32),
        lax.psum(owned[12].astype(jnp.bfloat16), "rep").astype(jnp.float32),
        lax.psum(owned[13].astype(jnp.bfloat16), "rep").astype(jnp.float32),
        lax.psum(owned[14].astype(jnp.bfloat16), "rep").astype(jnp.float32),
    )
    return (
        jnp.concatenate(outputs, axis=0),
        jnp.concatenate(input_grads, axis=0),
        summed[0],
        summed[1],
        summed[2],
        summed[3],
        summed[4],
        summed[5],
        summed[6],
        summed[7],
        summed[8],
        summed[9],
        summed[10],
        summed[11],
        summed[12],
        summed[13],
        summed[14],
    )


HEAD = 32
LANES = 128
QB = 256
AWAY = 2.0 ** 100
LIMIT = 100.0
LONG = 17
MESH = pl.DeviceIdType.MESH
BIG = 62 * 1024 * 1024
LOG2E = 1.4426950408889634


def halves(value):
    first = value.astype(jnp.bfloat16).astype(jnp.float32)
    rest = value - first
    second = rest.astype(jnp.bfloat16).astype(jnp.float32)
    third = (rest - second).astype(jnp.bfloat16).astype(jnp.float32)
    return first, second, third


def dot(left, right):
    return jnp.dot(left, right, preferred_element_type=jnp.float32)


def zeros_for(rank, *grid):
    return (0,) * rank


def whole_spec(array):
    return pl.BlockSpec(array.shape, functools.partial(zeros_for, array.ndim), pipeline_mode=pl.Buffered(1))


def quarter_spec(w, i):
    return pl.BlockSpec((1,) + w.shape[1:], lambda *grid: (i, 0, 0, 0, 0), pipeline_mode=pl.Buffered(1))


def iota(shape, dim):
    return lax.broadcasted_iota(jnp.int32, shape, dim)


def where_am_i():
    r = lax.axis_index("rep")
    g = lax.axis_index("grp")
    return r, g, lax.div(g, 2), lax.rem(g, 2)


def remote(src, dst, send, recv, r, g):
    return pltpu.make_async_remote_copy(
        src_ref=src, dst_ref=dst, send_sem=send, recv_sem=recv, device_id=(r, g), device_id_type=MESH
    )


def greet(r, g, reps, group):
    barrier = pltpu.get_barrier_semaphore()
    for d in range(1, group):
        pl.semaphore_signal(barrier, inc=1, device_id=(r, lax.rem(g + d, group)), device_id_type=MESH)
    for d in range(1, reps):
        pl.semaphore_signal(barrier, inc=1, device_id=(lax.rem(r + d, reps), g), device_id_type=MESH)
    pl.semaphore_wait(barrier, group + reps - 2)


def vectors_of(small):
    return jnp.concatenate([small[g, 0:8, 0:48].astype(jnp.float32) for g in range(8)], axis=1)


def chip_at(z, i):
    order = ((0, 1, 2, 3), (1, 0, 2, 3), (2, 1, 3, 0), (3, 2, 1, 0))
    chip = jnp.int32(0)
    for a, row in enumerate(order):
        for k, value in enumerate(row):
            chip = jnp.where((z == a) & (i == k), value, chip)
    return chip


def gather_kernel(
    tok, wq, wk, wv, wo, wi, wu, vectors, inner, seg,
    x_out, w_out, s_out, kv_out, qh_out, kt_out, vt_out, q1_out, norms,
    small, x, kv, qh, kt, vt, q1, w0, smalls_in, wrow, wtr, mine,
    lsem, xsem, psems, tsend, trecv, psend, wsend1, wrecv1, wsend2, wrecv2, wsend3, wrecv3, ssend, srecv,
):
    r, g, z, c = where_am_i()
    reps, chips = 4, 4
    p = 2 * z + 1 - c
    heads = kv.shape[0]
    _, rows, width = x.shape
    small[0:8, :] = jnp.concatenate(
        [vectors[...].astype(jnp.float32), jnp.zeros((8, rows - 48), jnp.float32)], axis=1
    ).astype(jnp.bfloat16)
    small[8:16, :] = jnp.concatenate(
        [
            jnp.concatenate([inner[...].astype(jnp.float32), jnp.zeros((1, rows - 192), jnp.float32)], axis=1),
            seg[...].astype(jnp.float32),
            jnp.zeros((5, rows), jnp.float32),
        ],
        axis=0,
    ).astype(jnp.bfloat16)
    greet(r, g, reps, 2 * chips)
    slab = [wi.at[:, pl.ds(j * width, width)] for j in range(4)]
    quarters = (
        ((wq, 0, 48), (wk, 48, 48), (wv, 96, 48)),
        ((wo, 0, 48), (slab[0], 48, 48), (slab[1], 96, 48)),
        ((slab[2], 0, 48), (slab[3], 48, 48), (wu.at[pl.ds(0, 48), :], 96, 48)),
        ((wu.at[pl.ds(48, 144), :], 0, 144),),
    )
    swap = remote(tok.at[1 - c], x.at[g], psend, trecv.at[g], r, p)
    swap.start()
    own_x = pltpu.make_async_copy(tok.at[c], x.at[g], lsem.at[0])
    own_x.start()
    def pass_on(b, way, src=None):
        to = g + 2 if way == 0 else g - 2
        src = x.at[b] if src is None else src
        return remote(src, x.at[b], tsend.at[way, b], trecv.at[b], r, to)

    def forward(b, way, src=None):
        ok = z < chips - 1 if way == 0 else z > 0

        @pl.when(ok)
        def _():
            pass_on(b, way, src).start()

    def keep(b):
        return pltpu.make_async_copy(x.at[b], x_out.at[b], xsem.at[b])

    def arrived(b):
        remote(x.at[b], x.at[b], tsend.at[0, b], trecv.at[b], r, p).wait_recv()

    forward(g, 0, tok.at[c])
    forward(g, 1, tok.at[c])
    arrived(p)
    forward(p, 0)
    forward(p, 1)
    keep(p).start()
    for i, pieces in enumerate(quarters):
        @pl.when(r == i)
        def _():
            copies = [
                pltpu.make_async_copy(ref, mine.at[pl.ds(row, count), :], lsem.at[3 + k])
                for k, (ref, row, count) in enumerate(pieces)
            ]
            for copy in copies:
                copy.start()
            for copy in copies:
                copy.wait()

    own_w = pltpu.make_async_copy(mine, w_out.at[r, c, z], lsem.at[1])
    own_w.start()
    own_s = pltpu.make_async_copy(small, smalls_in.at[g], lsem.at[2])
    own_s.start()
    first = []
    for d in range(1, chips):
        zz = lax.rem(z + d, chips)
        copy = remote(mine, w_out.at[r, c, z], wsend1.at[d - 1], wrecv1.at[z], r, 2 * zz + c)
        copy.start()
        first.append(copy)
    smalls = []
    for d in range(1, 2 * chips):
        copy = remote(small, smalls_in.at[g], ssend.at[d - 1], srecv.at[g], r, lax.rem(g + d, 2 * chips))
        copy.start()
        smalls.append(copy)
    own_x.wait()
    keep(g).start()

    def tokens_from(d):
        for k in range(2):
            @pl.when(z >= d)
            def _():
                b = 2 * (z - d) + (c if k == 0 else 1 - c)
                arrived(b)
                forward(b, 0)
                keep(b).start()

            @pl.when(z + d < chips)
            def _():
                b = 2 * (z + d) + (c if k == 0 else 1 - c)
                arrived(b)
                forward(b, 1)
                keep(b).start()

    tokens_from(1)
    for d in range(1, chips):
        zz = lax.rem(z + d, chips)
        remote(mine, w_out.at[r, c, zz], wsend1.at[0], wrecv1.at[zz], r, p).wait_recv()
    own_w.wait()
    second = []
    for d in range(1, reps):
        copy = remote(
            w_out.at[r, c], w_out.at[r, c], wsend2.at[d - 1], wrecv2.at[r], lax.rem(r + d, reps), g
        )
        copy.start()
        second.append(copy)
    third = [remote(w_out.at[r, c], w_out.at[r, c], wsend3.at[r], wrecv3.at[r], r, p)]
    third[0].start()
    tokens_from(2)
    for d in range(1, reps):
        q = lax.rem(r + d, reps)
        remote(w_out.at[q, c], w_out.at[q, c], wsend2.at[0], wrecv2.at[q], r, p).wait_recv()
        copy = remote(w_out.at[q, c], w_out.at[q, c], wsend3.at[q], wrecv3.at[q], r, p)
        copy.start()
        third.append(copy)
    for q in range(reps):
        remote(w_out.at[q, 1 - c], w_out.at[q, 1 - c], wsend3.at[q], wrecv3.at[q], r, p).wait_recv()
    load_w = pltpu.make_async_copy(w_out.at[0], w0, lsem.at[1])
    load_w.start()
    for d in range(1, 2 * chips):
        b = lax.rem(g + d, 2 * chips)
        remote(small, smalls_in.at[b], ssend.at[0], srecv.at[b], r, p).wait_recv()
    own_s.wait()
    keep_s = pltpu.make_async_copy(smalls_in, s_out, lsem.at[2])
    keep_s.start()
    load_w.wait()

    span = heads * HEAD
    bias = vectors_of(smalls_in).astype(jnp.bfloat16)
    full = [
        jnp.concatenate([w0[i % 2, i // 2, 48 * k : 48 * k + 48, :] for i in range(8)], axis=0)
        for k in range(3)
    ]
    lane = iota((width, heads * LANES), 1)
    head, lane_in = lax.div(lane, LANES), lax.rem(lane, LANES)
    column = span * z + head * HEAD + lax.rem(lane_in, HEAD)
    hit = iota((width, heads * LANES), 0) == column
    pick_k = jnp.where(hit & (lane_in < 64), 1.0, 0.0).astype(jnp.bfloat16)
    pick_v = jnp.where(hit & (lane_in >= 64) & (lane_in < 96), 1.0, 0.0).astype(jnp.bfloat16)
    wrow[...] = (dot(full[1], pick_k) + dot(full[2], pick_v)).astype(jnp.bfloat16)
    row_kv = dot(bias[1:2, :], pick_v)
    pick_t = jnp.where(
        iota((span, width), 1) == span * z + iota((span, width), 0), 1.0, 0.0
    ).astype(jnp.bfloat16)

    def by_rows(left, right):
        return lax.dot_general(
            left, right, (((1,), (1,)), ((), ())), preferred_element_type=jnp.float32
        )

    for k in range(3):
        wtr[k] = by_rows(pick_t, full[k]).astype(jnp.bfloat16)
    column_bias = by_rows(pick_t, bias)
    col_q, col_v = column_bias[:, 0:1], column_bias[:, 1:2]
    scale = (HEAD ** -0.5) * LOG2E
    one_lane = lax.rem(iota((1, heads * LANES), 1), LANES)
    row_kv = row_kv + jnp.where((one_lane >= 104) & (one_lane < 107), 1.0, 0.0)
    one = jnp.where(iota((16, rows), 0) == 0, 1.0, 0.0).astype(jnp.bfloat16)

    def stores(b):
        cols = pl.ds(pl.multiple_of(b * rows, rows), rows)
        return [
            pltpu.make_async_copy(kv.at[:, cols, :], kv_out.at[:, cols, :], psems.at[0, b])
        ] + [
            pltpu.make_async_copy(ref.at[:, :, cols], out.at[:, :, cols], psems.at[1 + i, b])
            for i, (ref, out) in enumerate(((qh, qh_out), (kt, kt_out), (vt, vt_out), (q1, q1_out)))
        ]

    def project(i, most):
        half = lax.rem(i, 2)
        b = 2 * chip_at(z, lax.div(i, 2)) + c + half - 2 * c * half
        xb = x[b]
        two = smalls_in[b, 8:16, :].astype(jnp.float32)
        ids = jnp.where(c == 0, two[1:2], two[2:3])
        same = jnp.where(iota((8, rows), 0).astype(jnp.float32) == ids, 1.0, 0.0)
        hot = jnp.concatenate(
            [jnp.zeros((96, rows), jnp.float32), same, jnp.zeros((24, rows), jnp.float32)], axis=0
        ).T
        cols = pl.ds(pl.multiple_of(b * rows, rows), rows)
        flat = dot(xb, wrow[...]) + row_kv
        for h in range(heads):
            kv[h, cols, :] = (flat[:, h * LANES : (h + 1) * LANES] + hot).astype(jnp.bfloat16)
        q_t = (by_rows(wtr[0], xb) + col_q).astype(jnp.bfloat16)
        k_t = by_rows(wtr[1], xb).astype(jnp.bfloat16)
        v_t = (by_rows(wtr[2], xb) + col_v).astype(jnp.bfloat16)
        q_wide = q_t.astype(jnp.float32) * scale
        k_wide = k_t.astype(jnp.float32)
        q_hi = q_wide.astype(jnp.bfloat16)
        q_lo = (q_wide - q_hi.astype(jnp.float32)).astype(jnp.bfloat16)
        sizes = []
        for n, v in enumerate((q_wide, k_wide)):
            size = most[n]
            for h in range(heads):
                size = jnp.maximum(
                    size, jnp.sum(v[h * HEAD : (h + 1) * HEAD] ** 2, axis=0, keepdims=True)
                )
            sizes.append(size)
        for h in range(heads):
            part = slice(h * HEAD, (h + 1) * HEAD)
            qh[h, 0:32, cols] = q_hi[part]
            qh[h, 32:64, cols] = q_lo[part]
            kt[h, :, cols] = k_t[part]
            q1[h, :, cols] = q_t[part]
            vt[h, 0:32, cols] = v_t[part]
            vt[h, 32:48, cols] = one
        for copy in stores(b):
            copy.start()
        return tuple(sizes)

    zero = jnp.zeros((1, rows), jnp.float32)
    most = lax.fori_loop(0, 6, project, (zero, zero))
    tokens_from(3)
    most = lax.fori_loop(6, 8, project, most)
    norms[0:1, :] = most[0]
    norms[1:2, :] = most[1]

    def settle(b, none):
        keep(b).wait()
        for copy in stores(b):
            copy.wait()
        return none

    swap.wait_send()
    for copy in first + smalls + second + third:
        copy.wait_send()
    for b in range(2 * chips):
        @pl.when((z < chips - 1) & (b < 2 * z + 2))
        def _():
            pass_on(b, 0).wait_send()

        @pl.when((z > 0) & (b >= 2 * z))
        def _():
            pass_on(b, 1).wait_send()

    keep_s.wait()
    lax.fori_loop(0, 2 * chips, settle, 0)


def gather(tokens, weights, vectors, inner, seg):
    dma = pltpu.SemaphoreType.DMA
    anywhere = pl.BlockSpec(memory_space=pltpu.HBM)
    vm = pl.BlockSpec(memory_space=pltpu.VMEM)
    rows, width = tokens.shape[1:]
    bf, f4 = jnp.bfloat16, jnp.float32
    heads, length = 3, 8 * rows
    made = [
        (heads, length, LANES), (heads, 64, length), (heads, HEAD, length), (heads, 48, length), (heads, HEAD, length)
    ]
    return pl.pallas_call(
        gather_kernel,
        name="gather",
        out_shape=(
            jax.ShapeDtypeStruct((8, rows, width), bf),
            jax.ShapeDtypeStruct((4, 2, 4, 144, width), bf),
            jax.ShapeDtypeStruct((8, 16, rows), bf),
        )
        + tuple(jax.ShapeDtypeStruct(shape, bf) for shape in made)
        + (jax.ShapeDtypeStruct((2, rows), f4),),
        in_specs=[anywhere] * 7 + [vm] * 3,
        out_specs=[anywhere] * 8 + [vm],
        scratch_shapes=[
            pltpu.VMEM((16, rows), bf),
            pltpu.VMEM((8, rows, width), bf),
        ]
        + [pltpu.VMEM(shape, bf) for shape in made]
        + [
            pltpu.VMEM((2, 4, 144, width), bf),
            pltpu.VMEM((8, 16, rows), bf),
            pltpu.VMEM((width, heads * LANES), bf),
            pltpu.VMEM((3, heads * HEAD, width), bf),
            pltpu.VMEM((144, width), bf),
            dma((6,)), dma((8,)), dma((5, 8)), dma((2, 8)), dma((8,)), dma, dma((3,)), dma((4,)), dma((3,)), dma((4,)),
            dma((4,)), dma((4,)), dma((7,)), dma((8,)),
        ],
        compiler_params=pltpu.CompilerParams(
            collective_id=1, has_side_effects=True, vmem_limit_bytes=BIG
        ),
    )(tokens, *weights, vectors, inner, seg)


def span_of(starts, q0, docs):
    low = jnp.int32(0)
    high = starts[docs]
    for d in range(docs):
        low = jnp.where(starts[d] <= q0, jnp.maximum(low, starts[d]), low)
        high = jnp.where(starts[d + 1] >= q0 + QB, jnp.minimum(high, starts[d + 1]), high)
    first = lax.div(low, LANES)
    return first, lax.div(high + LANES - 1, LANES) - first


def in_groups(first, count, total, body):
    def at(i):
        return pl.multiple_of(i * LANES, LANES)

    big = count >= LONG - 1

    @pl.when(big)
    def _():
        body(pl.ds(at(jnp.minimum(first, total - LONG)), LONG * LANES))

    first = jnp.where(big, first + LONG, first)
    count = jnp.where(big, jnp.maximum(count - LONG, 0), count)
    many = jnp.maximum(lax.div(count, 4) - 1, 0)

    def group(i, none):
        body(pl.ds(at(first + 4 * i), 4 * LANES))
        return none

    lax.fori_loop(0, many, group, 0)
    left = count - 4 * many
    for k in range(1, 8):
        @pl.when(left == k)
        def _():
            body(pl.ds(at(first + 4 * many), k * LANES))


def attend_kernel(
    place, kv_hbm, qh, vt_hbm, small, norms, ctx, tail_out, spans, qt, acc, tall, seg, starts, kv, vt, sems,
):
    heads, length, _ = kv.shape
    blocks, hw, rows = ctx.shape
    docs = 8
    c = place[1]
    loads = [
        pltpu.make_async_copy(kv_hbm, kv, sems.at[0]),
        pltpu.make_async_copy(qh, qt.at[:, pl.ds(0, 64), :], sems.at[1]),
        pltpu.make_async_copy(vt_hbm, vt, sems.at[2]),
    ]
    for load in loads:
        load.start()
    for g in range(8):
        two = small[g, 8:16, :].astype(jnp.float32)
        seg[g : g + 1, :] = jnp.where(c == 0, two[1:2], two[2:3]).astype(jnp.int32)
    ids = seg[...]
    starts[0] = jnp.int32(0)
    for d in range(1, docs):
        starts[d] = jnp.sum(jnp.where(ids < d, 1.0, 0.0)).astype(jnp.int32)
    starts[docs] = jnp.int32(length)

    def far(same):
        return (same - 1.0) * AWAY

    def fill(b, none):
        cols = pl.ds(pl.multiple_of(b * rows, rows), rows)
        same = jnp.where(iota((8, rows), 0) == seg[pl.ds(b, 1), :], 1.0, 0.0)
        low = jnp.concatenate([far(same), jnp.zeros((8, rows), jnp.float32)], axis=0)
        for h in range(heads):
            qt[h, 64:96, cols] = jnp.zeros((32, rows), jnp.bfloat16)
            qt[h, 96:112, cols] = low.astype(jnp.bfloat16)
            qt[h, 112:128, cols] = jnp.zeros((16, rows), jnp.bfloat16)
        return none

    lax.fori_loop(0, blocks, fill, 0)
    bounded = jnp.max(norms[0:1, :]) * jnp.max(norms[1:2, :]) < LIMIT * LIMIT
    for load in loads:
        load.wait()

    per = rows // QB

    def query_block(b, carry):
        q0 = pl.multiple_of(b * QB, QB)
        first, count = span_of(starts, q0, docs)
        spans[0, b] = first
        spans[1, b] = count
        acc[...] = jnp.zeros_like(acc)

        def key_block(i, tops):
            keys = pl.ds(pl.multiple_of((first + i) * LANES, LANES), LANES)
            s = [dot(kv[h, keys, :], qt[h, :, pl.ds(q0, QB)]) for h in range(heads)]
            new = [jnp.maximum(tops[h], jnp.max(s[h], axis=0, keepdims=True)) for h in range(heads)]
            p = [jnp.exp2(s[h] - new[h]).astype(jnp.bfloat16) for h in range(heads)]
            for h in range(heads):
                acc[h] = acc[h] * jnp.exp2(tops[h] - new[h]) + dot(vt[h, :, keys], p[h])
            return tuple(new)

        def plain_block(keys):
            s = [dot(kv[h, keys, :], qt[h, :, pl.ds(q0, QB)]) for h in range(heads)]
            p = [jnp.exp2(v).astype(jnp.bfloat16) for v in s]
            for h in range(heads):
                acc[h] += dot(vt[h, :, keys], p[h])

        @pl.when(bounded)
        def _():
            in_groups(first, count, length // LANES, plain_block)
            tall[...] = jnp.zeros_like(tall)

        @pl.when(jnp.logical_not(bounded))
        def _():
            lowest = jnp.full((1, QB), -3e38, jnp.float32)
            tops = lax.fori_loop(0, count, key_block, (lowest,) * heads)
            for h in range(heads):
                tall[h] = tops[h]

        g = lax.div(b, per)
        off = pl.multiple_of(lax.rem(b, per) * QB, QB)
        same = jnp.where(iota((8, QB), 0) == seg[pl.ds(g, 1), pl.ds(off, QB)], 1.0, 0.0)
        for h in range(heads):
            total = acc[h, 32:33, :]
            out = acc[h, 0:32, :] / total
            ctx[g, h * HEAD : (h + 1) * HEAD, pl.ds(off, QB)] = out.astype(jnp.bfloat16)
            parts = halves(-(tall[h] + jnp.log2(total)))
            tail = jnp.concatenate([far(same), *parts, jnp.zeros((5, QB), jnp.float32)], axis=0)
            tail_out[h, :, pl.ds(q0, QB)] = tail.astype(jnp.bfloat16)
        return carry

    lax.fori_loop(0, length // QB, query_block, 0)


def attend(place, kv, qh, vt, small, norms):
    heads, length, _ = kv.shape
    blocks, _, rows = small.shape
    sm = pl.BlockSpec(memory_space=pltpu.SMEM)
    anywhere = pl.BlockSpec(memory_space=pltpu.HBM)
    bf, f4 = jnp.bfloat16, jnp.float32
    shapes = (
        jax.ShapeDtypeStruct((blocks, heads * HEAD, rows), bf),
        jax.ShapeDtypeStruct((heads, 16, length), bf),
    )
    return pl.pallas_call(
        attend_kernel,
        name="attend",
        grid=(1,),
        out_shape=shapes + (jax.ShapeDtypeStruct((2, length // QB), jnp.int32),),
        in_specs=[sm, anywhere, anywhere, anywhere, whole_spec(small), whole_spec(norms)],
        out_specs=[whole_spec(v) for v in shapes] + [sm],
        scratch_shapes=[
            pltpu.VMEM((heads, LANES, length), bf),
            pltpu.VMEM((heads, 48, QB), f4),
            pltpu.VMEM((heads, 1, QB), f4),
            pltpu.VMEM((8, rows), jnp.int32),
            pltpu.SMEM((16,), jnp.int32),
            pltpu.VMEM(kv.shape, bf),
            pltpu.VMEM(vt.shape, bf),
            pltpu.SemaphoreType.DMA((3,)),
        ],
        compiler_params=pltpu.CompilerParams(vmem_limit_bytes=BIG),
    )(place, kv, qh, vt, small, norms)


PIECE = 128


def middle_kernel(
    ctx, tok_hbm, og_hbm, w_hbm, small,
    layer_hbm, grad_hbm, gctx_out, pr,
    wo, wi, wu, gwo, gwi, gwu, sums, inner_sum, ctx_in, gctx, pg, pg_in,
    tok, og, w, layer_out, grad_one_out, insems, outsems, lsem, send, recv, gsend, grecv, glocal, psend, precv,
):
    seqs, rows, width = tok.shape
    slabs = wi.shape[0]
    pieces = rows // PIECE
    r, g, z, c = where_am_i()
    loads = [
        pltpu.make_async_copy(w_hbm, w, insems.at[0]),
        pltpu.make_async_copy(tok_hbm, tok, insems.at[1]),
        pltpu.make_async_copy(og_hbm, og, insems.at[2]),
    ]
    for load in loads:
        load.start()
    greet(r, g, 1, 8)

    def fetch(q):
        cols = pl.ds(pl.multiple_of(q * PIECE, PIECE), PIECE)
        for d in range(1, 8):
            to = lax.rem(g + d, 8)
            remote(
                ctx.at[to, :, cols], ctx_in.at[c, z, :, cols], send.at[q, d - 1], recv.at[q, g], r, to
            ).start()

    own = pltpu.make_async_copy(ctx.at[g], ctx_in.at[c, z], lsem)
    own.start()
    fetch(0)
    fetch(1)
    loads[0].wait()
    for i in range(8):
        cc, zz = i % 2, i // 2
        wo[48 * i : 48 * i + 48, :] = w[1, cc, zz, 0:48, :]
        wi[0, 48 * i : 48 * i + 48, :] = w[1, cc, zz, 48:96, :]
        wi[1, 48 * i : 48 * i + 48, :] = w[1, cc, zz, 96:144, :]
        wi[2, 48 * i : 48 * i + 48, :] = w[2, cc, zz, 0:48, :]
        wi[3, 48 * i : 48 * i + 48, :] = w[2, cc, zz, 48:96, :]
        wu[zz, 192 * cc : 192 * cc + 48, :] = w[2, cc, zz, 96:144, :]
        wu[zz, 192 * cc + 48 : 192 * cc + 192, :] = w[3, cc, zz, :, :]
    for ref in (gwo, gwi, gwu, sums, inner_sum):
        ref[...] = jnp.zeros_like(ref)
    fetch(2)
    fetch(3)

    vec = vectors_of(small)
    inner_bias = jnp.concatenate(
        [small[i, 8:16, 0:192].astype(jnp.float32)[0:1] for i in range(8)], axis=1
    )
    out_bias, outer_bias = vec[2:3, :], vec[3:4, :]
    gain_one, shift_one = vec[4:5, :], vec[5:6, :]
    gain_two, shift_two = vec[6:7, :], vec[7:8, :]

    def normal(value):
        centre = value - jnp.mean(value, axis=-1, keepdims=True)
        rate = lax.rsqrt(jnp.mean(centre * centre, axis=-1, keepdims=True) + norm_epsilon)
        return centre * rate, rate

    def normal_back(grad, gain, n, rate):
        u = grad * gain
        return rate * (
            u - jnp.mean(u, axis=-1, keepdims=True) - n * jnp.mean(u * n, axis=-1, keepdims=True)
        )

    def total(value):
        return jnp.sum(value, axis=0, keepdims=True)

    def dot_turn(left, right):
        return lax.dot_general(
            left, right, (((1,), (1,)), ((), ())), preferred_element_type=jnp.float32
        )

    def arrived(q, cols):
        for d in range(1, 8):
            b = lax.rem(g + d, 8)
            remote(
                ctx.at[g, :, cols], ctx_in.at[lax.rem(b, 2), lax.div(b, 2), :, cols],
                send.at[q, 0], recv.at[q, b], r, b,
            ).wait_recv()

    def return_piece(q, cols, d):
        to = lax.rem(g + d, 8)
        return remote(
            gctx.at[lax.rem(to, 2), lax.div(to, 2), :, cols], gctx_out.at[g, :, cols],
            gsend.at[q, d - 1], grecv.at[q, g], r, to,
        )

    def keep_piece(q, cols):
        return pltpu.make_async_copy(gctx.at[c, z, :, cols], gctx_out.at[g, :, cols], glocal.at[q])

    own.wait()
    loads[1].wait()
    loads[2].wait()

    def results(q):
        here = pl.ds(pl.multiple_of(q * PIECE, PIECE), PIECE)
        return [
            pltpu.make_async_copy(ref.at[:, here, :], out.at[:, here, :], outsems.at[k, q])
            for k, (ref, out) in enumerate(((layer_out, layer_hbm), (grad_one_out, grad_hbm)))
        ]

    def one(q, carry):
        r0 = pl.multiple_of(q * PIECE, PIECE)
        here = pl.ds(r0, PIECE)
        arrived(q, here)

        def both(ref):
            return jnp.concatenate([ref[s, here, :] for s in range(seqs)], axis=0)

        def split(ref, value):
            for s in range(seqs):
                ref[s, here, :] = value[s * PIECE : (s + 1) * PIECE].astype(ref.dtype)

        ctx_t = jnp.concatenate(
            [jnp.concatenate([ctx_in[s, zz, :, here] for zz in range(4)], axis=0) for s in range(seqs)],
            axis=1,
        )
        context = ctx_t.astype(jnp.float32).T.astype(jnp.bfloat16)
        x = both(tok).astype(jnp.float32)
        n_one, rate_one = normal(x + (dot(context, wo[...]) + out_bias))
        hidden = n_one * gain_one + shift_one
        low = hidden.astype(jnp.bfloat16)
        low_t = hidden.T.astype(jnp.bfloat16)
        feed = jnp.zeros(hidden.shape, jnp.float32)
        slopes, actives = [], []
        for j in range(slabs):
            inner = dot(low, wi[j]) + inner_bias[:, j * width : (j + 1) * width]
            cdf = 0.5 + 0.5 * lax.erf(inner * (0.5 ** 0.5))
            pdf = jnp.exp(inner * inner * -0.5) * 0.3989422804014327
            slopes.append(cdf + inner * pdf)
            active = inner * cdf
            actives.append(active)
            feed = feed + dot(active.astype(jnp.bfloat16), wu[j])
        n_two, rate_two = normal(hidden + (feed + outer_bias))
        split(layer_out, n_two * gain_two + shift_two)
        grad = both(og).astype(jnp.float32)
        grad_two = normal_back(grad, gain_two, n_two, rate_two)
        grad_feed = grad_two.astype(jnp.bfloat16)
        grad_hidden = grad_two
        for j in range(slabs):
            grad_inner = (dot_turn(grad_feed, wu[j]) * slopes[j]).astype(jnp.bfloat16)
            inner_sum[:, j * width : (j + 1) * width] += total(grad_inner.astype(jnp.float32))
            grad_hidden = grad_hidden + dot_turn(grad_inner, wi[j])
            gwi[j] += dot(low_t, grad_inner)
            gwu[j] += dot(actives[j].T.astype(jnp.bfloat16), grad_feed)
        grad_one = normal_back(grad_hidden, gain_one, n_one, rate_one)
        split(grad_one_out, grad_one)
        grad_att = grad_one.astype(jnp.bfloat16)
        back = dot_turn(wo[...], grad_att).astype(jnp.bfloat16)
        for s in range(seqs):
            for zz in range(4):
                gctx[s, zz, :, here] = back[96 * zz : 96 * zz + 96, s * PIECE : (s + 1) * PIECE]
        for d in range(1, 8):
            return_piece(q, here, d).start()
        keep_piece(q, here).start()
        for copy in results(q):
            copy.start()
        gwo[...] += dot(ctx_t, grad_att)
        sums[0:1, :] += total(grad_att.astype(jnp.float32))
        sums[1:2, :] += total(grad_feed.astype(jnp.float32))
        sums[2:3, :] += total(grad_hidden * n_one)
        sums[3:4, :] += total(grad_hidden)
        sums[4:5, :] += total(grad * n_two)
        sums[5:6, :] += total(grad)
        return carry

    lax.fori_loop(0, pieces, one, 0)
    rows_of_sums = jnp.concatenate(
        [sums[...]]
        + [inner_sum[:, j * width : (j + 1) * width] for j in range(slabs)]
        + [jnp.zeros((6, width), jnp.float32)],
        axis=0,
    ).astype(jnp.bfloat16)
    for i in range(8):
        cc, zz = i % 2, i // 2
        mine = slice(48 * i, 48 * i + 48)
        pg[cc, zz, 0, 0:48, :] = gwo[mine, :].astype(jnp.bfloat16)
        pg[cc, zz, 0, 48:96, :] = gwi[0, mine, :].astype(jnp.bfloat16)
        pg[cc, zz, 1, 0:48, :] = gwi[1, mine, :].astype(jnp.bfloat16)
        pg[cc, zz, 1, 48:96, :] = gwi[2, mine, :].astype(jnp.bfloat16)
        pg[cc, zz, 2, 0:48, :] = gwi[3, mine, :].astype(jnp.bfloat16)
        base = 192 * cc
        pg[cc, zz, 0, 96:112, :] = gwu[zz, base : base + 16, :].astype(jnp.bfloat16)
        pg[cc, zz, 1, 96:112, :] = gwu[zz, base + 16 : base + 32, :].astype(jnp.bfloat16)
        pg[cc, zz, 2, 48:112, :] = gwu[zz, base + 32 : base + 96, :].astype(jnp.bfloat16)
        pg[cc, zz, 3, 0:96, :] = gwu[zz, base + 96 : base + 192, :].astype(jnp.bfloat16)
        pg[cc, zz, 3, 96:112, :] = rows_of_sums
    pair = remote(pg.at[1 - c], pg_in, psend, precv, r, 2 * z + 1 - c)
    pair.start()

    def settle(q, carry):
        cols = pl.ds(pl.multiple_of(q * PIECE, PIECE), PIECE)
        for d in range(1, 8):
            b = lax.rem(g + d, 8)
            remote(
                gctx.at[c, z, :, cols], gctx_out.at[b, :, cols], gsend.at[q, 0], grecv.at[q, b], r, b
            ).wait_recv()
            return_piece(q, cols, d).wait_send()
            to = lax.rem(g + d, 8)
            remote(
                ctx.at[to, :, cols], ctx_in.at[c, z, :, cols], send.at[q, d - 1], recv.at[q, g], r, to
            ).wait_send()
        keep_piece(q, cols).wait()
        for copy in results(q):
            copy.wait()
        return carry

    pair.wait_recv()
    for i in range(4):
        pr[i] = (pg[c, i].astype(jnp.float32) + pg_in[i].astype(jnp.float32)).astype(jnp.bfloat16)
    lax.fori_loop(0, pieces, settle, 0)
    pair.wait_send()


def middle(ctx, tok, og, w, small):
    seqs, rows, width = tok.shape
    vm = pl.BlockSpec(memory_space=pltpu.VMEM)
    anywhere = pl.BlockSpec(memory_space=pltpu.HBM)
    dma = pltpu.SemaphoreType.DMA
    bf, f4 = jnp.bfloat16, jnp.float32
    pieces = rows // PIECE
    return pl.pallas_call(
        middle_kernel,
        name="middle",
        out_shape=(
            jax.ShapeDtypeStruct((seqs, rows, width), bf),
            jax.ShapeDtypeStruct((seqs, rows, width), f4),
            jax.ShapeDtypeStruct(ctx.shape, bf),
            jax.ShapeDtypeStruct((4, 4, 112, width), bf),
        ),
        in_specs=[anywhere] * 4 + [vm],
        out_specs=[anywhere, anywhere, anywhere, vm],
        scratch_shapes=[
            pltpu.VMEM((width, width), bf),
            pltpu.VMEM((4, width, width), bf),
            pltpu.VMEM((4, width, width), bf),
            pltpu.VMEM((width, width), f4),
            pltpu.VMEM((4, width, width), f4),
            pltpu.VMEM((4, width, width), f4),
            pltpu.VMEM((6, width), f4),
            pltpu.VMEM((1, 4 * width), f4),
            pltpu.VMEM((2, 4) + ctx.shape[1:], bf),
            pltpu.VMEM((2, 4) + ctx.shape[1:], bf),
            pltpu.VMEM((2, 4, 4, 112, width), bf),
            pltpu.VMEM((4, 4, 112, width), bf),
            pltpu.VMEM((seqs, rows, width), bf),
            pltpu.VMEM((seqs, rows, width), bf),
            pltpu.VMEM(w.shape, bf),
            pltpu.VMEM((seqs, rows, width), bf),
            pltpu.VMEM((seqs, rows, width), f4),
            dma((3,)), dma((2, pieces)), dma, dma((pieces, 7)), dma((pieces, 8)), dma((pieces, 7)), dma((pieces, 8)), dma((pieces,)), dma, dma,
        ],
        compiler_params=pltpu.CompilerParams(
            collective_id=2, has_side_effects=True, vmem_limit_bytes=BIG
        ),
    )(ctx, tok, og, w, small)


def attend_back_kernel(
    last, index, place, spans, x_hbm, qh, tail, kv_hbm, kt_hbm, q1, gctx, ctx, *refs,
):
    heads = q1.shape[0]
    span = heads * HEAD
    if last:
        grads_in, out, gq, dt, do, acc, dq, qt, x, kv, kt, sems = refs
    else:
        out, grads_out, dt, do, acc, dq, qt, x, kv, kt, sems = refs
    length, width = x.shape
    mine = pl.ds(index * heads, heads)
    loads = [
        pltpu.make_async_copy(qh.at[mine], qt.at[:, pl.ds(0, 64), :], sems.at[0]),
        pltpu.make_async_copy(tail.at[mine], qt.at[:, pl.ds(96, 16), :], sems.at[1]),
        pltpu.make_async_copy(kv_hbm.at[mine], kv, sems.at[3]),
        pltpu.make_async_copy(kt_hbm.at[mine], kt, sems.at[4]),
        pltpu.make_async_copy(x_hbm, x, sems.at[2]),
    ]
    for load in loads:
        load.start()
    blocks, _, rows = gctx.shape
    z = place[0]
    c = place[1]
    scale = HEAD ** -0.5

    def prepare(g, carry):
        r0 = pl.multiple_of(g * rows, rows)
        cols = pl.ds(r0, rows)
        for h in range(heads):
            part = slice(h * HEAD, (h + 1) * HEAD)
            grad = gctx[g, part, :]
            wide = grad.astype(jnp.float32)
            delta = -jnp.sum(wide * ctx[g, part, :].astype(jnp.float32), axis=0, keepdims=True)
            dt[h, 0:64, cols] = jnp.zeros((64, rows), jnp.bfloat16)
            dt[h, 64:96, cols] = grad
            qt[h, 64:96, cols] = jnp.zeros((32, rows), jnp.bfloat16)
            qt[h, 112:128, cols] = jnp.zeros((16, rows), jnp.bfloat16)
            tail = jnp.concatenate(
                [jnp.zeros((8, rows), jnp.float32), *halves(delta), jnp.zeros((21, rows), jnp.float32)],
                axis=0,
            )
            dt[h, 96:128, cols] = tail.astype(jnp.bfloat16)
            turned = jnp.concatenate(
                [wide, q1[h, :, cols].astype(jnp.float32), jnp.zeros((64, rows), jnp.float32)], axis=0
            ).T
            lane = iota((rows, LANES), 1)
            grad_rows = jnp.where(lane < HEAD, turned, 0.0).astype(jnp.bfloat16)
            query_rows = jnp.where(lane < HEAD, 0.0, turned).astype(jnp.bfloat16)
            for j in range(rows // QB):
                r1 = pl.multiple_of(2 * r0 + 2 * j * QB, QB)
                do[h, pl.ds(r1, QB), :] = grad_rows[j * QB : (j + 1) * QB]
                do[h, pl.ds(r1 + QB, QB), :] = query_rows[j * QB : (j + 1) * QB]
        return carry

    lax.fori_loop(0, blocks, prepare, 0)
    acc[...] = jnp.zeros_like(acc)
    per = rows // QB
    for load in loads[:4]:
        load.wait()

    def query_block(b, carry):
        q0 = pl.multiple_of(b * QB, QB)
        dq[...] = jnp.zeros_like(dq)

        def key_block(keys):
            s = [dot(kv[h, keys, :], qt[h, :, pl.ds(q0, QB)]) for h in range(heads)]
            d = [dot(kv[h, keys, :], dt[h, :, pl.ds(q0, QB)]) for h in range(heads)]
            p = [jnp.exp2(v) for v in s]
            both = [
                jnp.concatenate([u.astype(jnp.bfloat16), (u * v).astype(jnp.bfloat16)], axis=1)
                for u, v in zip(p, d)
            ]
            for h in range(heads):
                acc[h, keys, :] += dot(both[h], do[h, pl.ds(2 * q0, 2 * QB), :])
            for h in range(heads):
                dq[h] += dot(kt[h, :, keys], both[h][:, QB:])

        in_groups(spans[0, b], spans[1, b], length // LANES, key_block)
        g = lax.div(b, per)
        off = pl.multiple_of(lax.rem(b, per) * QB, QB)
        for h in range(heads):
            out[g, h * HEAD : (h + 1) * HEAD, pl.ds(off, QB)] = (dq[h] * scale).astype(jnp.bfloat16)
        return carry

    lax.fori_loop(0, length // QB, query_block, 0)

    loads[4].wait()

    def finish_block(g, totals):
        r0 = pl.multiple_of(g * rows, rows)
        cols = pl.ds(r0, rows)
        for h in range(heads):
            both = acc[h, cols, :].T
            row = h * HEAD
            out[g, 2 * span + row : 2 * span + row + HEAD, :] = both[0:32].astype(jnp.bfloat16)
            out[g, span + row : span + row + HEAD, :] = (both[32:64] * scale).astype(jnp.bfloat16)
        piece = out[g]
        grad = dot(piece, x[cols, :])
        summed = jnp.sum(piece.astype(jnp.float32), axis=1, keepdims=True)
        return totals[0] + grad, totals[1] + summed

    grads, summed = lax.fori_loop(
        0,
        blocks,
        finish_block,
        (jnp.zeros((3 * span, width), jnp.float32), jnp.zeros((3 * span, 1), jnp.float32)),
    )
    if not last:
        grads_out[:, 0:width] = grads
        grads_out[:, width:] = jnp.broadcast_to(summed, (3 * span, LANES))
        return
    gq[...] = jnp.zeros_like(gq)
    before = grads_in.shape[0] // 3

    def joined(i, old, new):
        return [old[i * before : (i + 1) * before], new[i * span : (i + 1) * span]]

    old = grads_in[:, 0:width]
    whole = jnp.concatenate([v for i in range(3) for v in joined(i, old, grads)], axis=0).T
    total = 3 * (before + span)
    for g in range(8):
        gq[g % 2, g // 2, :, 0:total] = whole[48 * g : 48 * g + 48, :].astype(jnp.bfloat16)
    old = grads_in[:, width : width + 1]
    of_q = jnp.concatenate(joined(0, old, summed), axis=0)
    of_v = jnp.concatenate(joined(2, old, summed), axis=0)
    for cc in range(2):
        mine = jnp.concatenate(
            [
                of_q[48 * cc : 48 * cc + 48, :],
                of_v[48 * cc : 48 * cc + 48, :],
                jnp.zeros((48, 94), jnp.float32),
            ],
            axis=1,
        )
        gq[cc, z, :, total:] = mine.astype(jnp.bfloat16)


def attend_back(heads, index, place, spans, x, qh, tail, kv, kt, q1, gctx, ctx, grads=None):
    blocks, rows, width = x.shape
    length = blocks * rows
    last = grads is not None
    rest = (grads,) if last else ()
    sm = pl.BlockSpec(memory_space=pltpu.SMEM)
    bf, f4 = jnp.bfloat16, jnp.float32
    once = pl.Buffered(1)
    span = heads * HEAD

    def some_heads(array):
        return pl.BlockSpec((heads,) + array.shape[1:], lambda i: (index, 0, 0), pipeline_mode=once)

    def head_rows(array):
        return pl.BlockSpec((blocks, span, rows), lambda i: (0, index, 0), pipeline_mode=once)

    flat = x.reshape(length, width)
    shapes = (
        jax.ShapeDtypeStruct((blocks, 3 * span, rows), bf),
        jax.ShapeDtypeStruct((2, 4, 48, width), bf)
        if last
        else jax.ShapeDtypeStruct((3 * span, width + LANES), f4),
    )
    return pl.pallas_call(
        functools.partial(attend_back_kernel, last, index),
        name="attend_back",
        grid=(1,),
        out_shape=shapes,
        in_specs=[sm, sm] + [pl.BlockSpec(memory_space=pltpu.HBM)] * 5
        + [some_heads(q1)]
        + [head_rows(v) for v in (gctx, ctx)]
        + [whole_spec(v) for v in rest],
        out_specs=[whole_spec(v) for v in shapes],
        scratch_shapes=[
            pltpu.VMEM((heads, LANES, length), bf),
            pltpu.VMEM((heads, 2 * length, LANES), bf),
            pltpu.VMEM((heads, length, LANES), f4),
            pltpu.VMEM((heads, HEAD, QB), f4),
            pltpu.VMEM((heads, LANES, length), bf),
            pltpu.VMEM((length, width), bf),
            pltpu.VMEM((heads,) + kv.shape[1:], bf),
            pltpu.VMEM((heads,) + kt.shape[1:], bf),
            pltpu.SemaphoreType.DMA((5,)),
        ],
        compiler_params=pltpu.CompilerParams(vmem_limit_bytes=BIG),
        cost_estimate=pl.CostEstimate(
            flops=heads * 20 * 10 ** 9, bytes_accessed=heads * 8 * 10 ** 6, transcendentals=heads * 6 * 10 ** 6
        ),
    )(place, spans, flat, qh, tail, kv, kt, q1, gctx, ctx, *rest)


def reduce_kernel(
    src, gq, pz, dst, p_out, q_out,
    gq_in, gq_sum, qa_in, qa_sum, qb_in, pz_in, p_line, pa_in, p_own, gq_own,
    lsem, send, recv, gsend, grecv, qasend, qarecv, qbsend, qbrecv, qcsend, qcrecv,
    pasend, parecv, pcsend, pcrecv,
):
    r, g, z, c = where_am_i()
    greet(r, g, 4, 8)
    waits = []
    pair = remote(gq.at[1 - c], gq_in, gsend, grecv, r, 2 * z + 1 - c)
    pair.start()
    load_g = pltpu.make_async_copy(gq.at[c], gq_own, lsem.at[1])
    load_g.start()
    load_p = pltpu.make_async_copy(pz, pz_in, lsem.at[2])
    load_p.start()
    own = pltpu.make_async_copy(src.at[g], dst.at[g], lsem.at[0])
    own.start()

    def send_to(d):
        to = lax.rem(g + d, 8)
        copy = remote(src.at[to], dst.at[g], send.at[d - 1], recv.at[g], r, to)
        copy.start()
        waits.append(copy)

    def f32(value):
        return value.astype(jnp.float32)

    load_g.wait()
    pair.wait_recv()
    gq_sum[...] = (f32(gq_own[...]) + f32(gq_in[...])).astype(jnp.bfloat16)
    for d in range(1, 4):
        rr = lax.rem(r + d, 4)
        copy = remote(gq_sum.at[rr], qa_in.at[r], qasend.at[d - 1], qarecv.at[r], rr, g)
        copy.start()
        waits.append(copy)
    load_p.wait()
    total = f32(pz_in[0])
    for i in range(1, 4):
        total = total + f32(pz_in[i])
    p_line[...] = total.astype(jnp.bfloat16)
    for d in range(1, 4):
        rr = lax.rem(r + d, 4)
        copy = remote(p_line.at[rr], pa_in.at[r], pasend.at[d - 1], parecv.at[r], rr, g)
        copy.start()
        waits.append(copy)
    for d in range(1, 4):
        b = lax.rem(r + d, 4)
        remote(gq_sum.at[r], qa_in.at[b], qasend.at[0], qarecv.at[b], b, g).wait_recv()
    total = f32(gq_sum[r])
    for d in range(1, 4):
        total = total + f32(qa_in[lax.rem(r + d, 4)])
    qa_sum[...] = total.astype(jnp.bfloat16)

    @pl.when(z != r)
    def _():
        remote(qa_sum, qb_in.at[z], qbsend, qbrecv.at[z], r, 2 * r + c).start()

    for d in (4, 3, 5, 2, 6, 1, 7):
        send_to(d)
    for d in range(1, 4):
        b = lax.rem(r + d, 4)
        remote(p_line.at[r], pa_in.at[b], pasend.at[0], parecv.at[b], b, g).wait_recv()
    total = f32(p_line[r])
    for d in range(1, 4):
        total = total + f32(pa_in[lax.rem(r + d, 4)])
    p_own[...] = total.astype(jnp.bfloat16)
    keep_p = pltpu.make_async_copy(p_own, p_out.at[r], lsem.at[3])
    keep_p.start()
    for d in range(1, 4):
        rr = lax.rem(r + d, 4)
        copy = remote(p_own, p_out.at[r], pcsend.at[d - 1], pcrecv.at[r], rr, g)
        copy.start()
        waits.append(copy)

    @pl.when(z == r)
    def _():
        for d in range(1, 4):
            b = lax.rem(z + d, 4)
            remote(qa_sum, qb_in.at[b], qbsend, qbrecv.at[b], r, g).wait_recv()
        qb_in[z] = qa_sum[...]
        keep = pltpu.make_async_copy(qb_in, q_out, lsem.at[4])
        keep.start()
        for d in range(1, 4):
            remote(qb_in, q_out, qcsend.at[d - 1], qcrecv, lax.rem(r + d, 4), g).start()
        keep.wait()
        for d in range(1, 4):
            remote(qb_in, q_out, qcsend.at[d - 1], qcrecv, lax.rem(r + d, 4), g).wait_send()

    @pl.when(z != r)
    def _():
        remote(qb_in, q_out, qcsend.at[0], qcrecv, r, g).wait_recv()
        remote(qa_sum, qb_in.at[z], qbsend, qbrecv.at[z], r, 2 * r + c).wait_send()

    for d in range(1, 4):
        b = lax.rem(r + d, 4)
        remote(p_own, p_out.at[b], pcsend.at[0], pcrecv.at[b], b, g).wait_recv()
    for d in range(1, 8):
        b = lax.rem(g + d, 8)
        remote(src.at[g], dst.at[b], send.at[0], recv.at[b], r, b).wait_recv()
    pair.wait_send()
    for copy in waits:
        copy.wait_send()
    keep_p.wait()
    own.wait()


def reduce_all(src, gq, pz):
    dma = pltpu.SemaphoreType.DMA
    anywhere = pl.BlockSpec(memory_space=pltpu.HBM)
    bf = jnp.bfloat16
    width = gq.shape[-1]
    part = (4, 48, width)
    return pl.pallas_call(
        reduce_kernel,
        name="reduce",
        out_shape=(
            jax.ShapeDtypeStruct(src.shape, bf),
            jax.ShapeDtypeStruct((4, 112, width), bf),
            jax.ShapeDtypeStruct(part, bf),
        ),
        in_specs=[anywhere] * 3,
        out_specs=[anywhere] * 3,
        scratch_shapes=[
            pltpu.VMEM(part, bf),
            pltpu.VMEM(part, bf),
            pltpu.VMEM(part, bf),
            pltpu.VMEM((48, width), bf),
            pltpu.VMEM(part, bf),
            pltpu.VMEM((4, 4, 112, width), bf),
            pltpu.VMEM((4, 112, width), bf),
            pltpu.VMEM((4, 112, width), bf),
            pltpu.VMEM((112, width), bf),
            pltpu.VMEM(part, bf),
            dma((5,)), dma((7,)), dma((8,)), dma, dma, dma((3,)), dma((4,)), dma, dma((4,)), dma((3,)), dma,
            dma((3,)), dma((4,)), dma((3,)), dma((4,)),
        ],
        compiler_params=pltpu.CompilerParams(
            collective_id=4, has_side_effects=True, vmem_limit_bytes=BIG
        ),
    )(src, gq, pz)


def finish_kernel(
    place, layer_in, in_0, in_1, grad_one, w, p_in, q_in,
    layer_out, out, g_q, g_k, g_v, g_o, g_in, g_up, rows_out, inner_out, wq, held, sems,
):
    width = w.shape[-1]
    span = 96
    step = pl.program_id(0)
    z = place[0]
    c = place[1]
    load = pltpu.make_async_copy(layer_in, held, sems.at[0])
    store = pltpu.make_async_copy(held, layer_out, sems.at[1])

    @pl.when(step == 0)
    def _():
        load.start()
        for i in range(3):
            for g in range(8):
                wq[i, 48 * g : 48 * g + 48, :] = w[0, g % 2, g // 2, 48 * i : 48 * i + 48, :]

    total = grad_one[0]
    for i in range(3):
        turned = jnp.concatenate(
            [
                ref[zz, 0, i * count : (i + 1) * count, :]
                for zz in range(4)
                for ref, count in ((in_0, in_0.shape[2] // 3), (in_1, in_1.shape[2] // 3))
            ],
            axis=0,
        )
        back = turned.astype(jnp.float32).T.astype(jnp.bfloat16)
        total = total + lax.dot_general(
            back, wq[i], (((1,), (1,)), ((), ())), preferred_element_type=jnp.float32
        )
    out[0] = total.astype(jnp.bfloat16)

    @pl.when(step == 0)
    def _():
        load.wait()
        store.start()
        wide = [q_in[zz].astype(jnp.float32) for zz in range(4)]
        for i, ref in enumerate((g_q, g_k, g_v)):
            ref[...] = jnp.concatenate([v[:, i * span : (i + 1) * span] for v in wide], axis=1)
        sums = p_in[3, 96:112, :]
        pick = jnp.where(
            iota((width, 48), 0) == 48 * (2 * z + c) + iota((width, 48), 1), 1.0, 0.0
        ).astype(jnp.bfloat16)
        rows_out[8:24, :] = dot(sums, pick)
        both = q_in[z].astype(jnp.float32)[:, 3 * span :].T
        rows_out[0:8, :] = both[0:8, :]
        pick = jnp.where(
            iota((width, 192), 0) == 192 * c + iota((width, 192), 1), 1.0, 0.0
        ).astype(jnp.bfloat16)
        inner = dot(sums, pick)
        inner_out[...] = jnp.sum(
            jnp.where(iota((16, 192), 0) == 6 + z, inner, 0.0), axis=0, keepdims=True
        )
        g_o[...] = p_in[0, 0:48, :].astype(jnp.float32)
        g_in[:, 0:384] = p_in[0, 48:96, :].astype(jnp.float32)
        g_in[:, 384:768] = p_in[1, 0:48, :].astype(jnp.float32)
        g_in[:, 768:1152] = p_in[1, 48:96, :].astype(jnp.float32)
        g_in[:, 1152:1536] = p_in[2, 0:48, :].astype(jnp.float32)
        g_up[0:16, :] = p_in[0, 96:112, :].astype(jnp.float32)
        g_up[16:32, :] = p_in[1, 96:112, :].astype(jnp.float32)
        g_up[32:96, :] = p_in[2, 48:112, :].astype(jnp.float32)
        g_up[96:192, :] = p_in[3, 0:96, :].astype(jnp.float32)

    @pl.when(step == 1)
    def _():
        store.wait()


def finish(place, layer_in, in_0, in_1, grad_one, w, p_in, q_in):
    seqs, rows, width = grad_one.shape
    sm = pl.BlockSpec(memory_space=pltpu.SMEM)
    hbm = pl.BlockSpec(memory_space=pltpu.HBM)
    bf, f4 = jnp.bfloat16, jnp.float32
    shapes = ((48, width),) * 4 + ((48, 4 * width), (192, width), (24, 48), (1, 192))
    in_0, in_1 = (v.reshape((4, 2) + v.shape[1:]) for v in (in_0, in_1))

    def of_sequence(v):
        return pl.BlockSpec((4, 1) + v.shape[2:], lambda i: (0, i, 0, 0))

    one = pl.BlockSpec((1, rows, width), lambda i: (i, 0, 0))
    return pl.pallas_call(
        finish_kernel,
        name="finish",
        grid=(seqs,),
        out_shape=(jax.ShapeDtypeStruct((seqs, rows, width), bf),) * 2
        + tuple(jax.ShapeDtypeStruct(shape, f4) for shape in shapes),
        in_specs=[
            sm, hbm, of_sequence(in_0), of_sequence(in_1), one,
            quarter_spec(w, 0), whole_spec(p_in), whole_spec(q_in),
        ],
        out_specs=[hbm, one]
        + [pl.BlockSpec(shape, functools.partial(zeros_for, len(shape))) for shape in shapes],
        scratch_shapes=[
            pltpu.VMEM((3, width, width), bf),
            pltpu.VMEM((seqs, rows, width), bf),
            pltpu.SemaphoreType.DMA((2,)),
        ],
        compiler_params=pltpu.CompilerParams(vmem_limit_bytes=BIG - 1600 * 1024),
    )(place, layer_in, in_0, in_1, grad_one, w, p_in, q_in)


def line_of_chips(
    tokens, segment_ids, out_grad, query_weight, key_weight, value_weight, output_weight,
    inner_weight, outer_weight, query_bias, value_bias, output_bias, inner_bias, outer_bias,
    first_gain, first_shift, second_gain, second_shift,
):
    bf = jnp.bfloat16
    width = tokens.shape[2]
    g = lax.axis_index("grp")
    z, c = lax.div(g, 2), lax.rem(g, 2)
    place = jnp.stack([z, c]).astype(jnp.int32)
    weights = (query_weight, key_weight, value_weight, output_weight, inner_weight, outer_weight)
    vectors = jnp.concatenate(
        [
            v[None]
            for v in (
                query_bias, value_bias, output_bias, outer_bias,
                first_gain, first_shift, second_gain, second_shift,
            )
        ],
        axis=0,
    )
    x, w, small, kv, qh, kt, vt, q1, norms = gather(
        tokens, weights, vectors, inner_bias[None], segment_ids
    )
    ctx, tail, spans = attend(place, kv, qh, vt, small, norms)
    layer_out, grad_one, gctx_in, pr = middle(ctx, tokens, out_grad, w, small)
    same_core = [[i + j for i in range(0, 8, 2)] for j in range(2)]
    pz = lax.all_to_all(pr, "grp", 0, 0, axis_index_groups=same_core, tiled=True)
    back = functools.partial(
        attend_back, place=place, spans=spans, x=x, qh=qh, tail=tail, kv=kv, kt=kt, q1=q1,
        gctx=gctx_in, ctx=ctx,
    )
    parts_0, grads_0 = back(2, 0)
    in_0 = lax.all_to_all(parts_0, "grp", 0, 0, tiled=True)
    parts_1, gq = back(1, 2, grads=grads_0)
    in_1, p_in, q_in = reduce_all(parts_1, gq, pz)
    layer_out, input_grad, g_q, g_k, g_v, g_o, g_in, g_up, rows, inner_row = finish(
        place, layer_out, in_0, in_1, grad_one, w, p_in, q_in
    )
    return (
        layer_out, input_grad, g_q, g_k, g_v, g_o, g_in, g_up,
        rows[0], rows[1], rows[8], inner_row[0], rows[9], rows[10], rows[11], rows[12], rows[13],
    )


def solution(mesh):
    in_specs = (
        P("rep", "grp", None),
        P("rep", "grp"),
        P("rep", "grp", None),
        P("grp", None),
        P("grp", None),
        P("grp", None),
        P("grp", None),
        P("grp", None),
        P("grp", None),
        P("grp"),
        P("grp"),
        P("grp"),
        P("grp"),
        P("grp"),
        P("grp"),
        P("grp"),
        P("grp"),
        P("grp"),
    )
    out_specs = (
        P("rep", "grp", None),
        P("rep", "grp", None),
        P("grp", None),
        P("grp", None),
        P("grp", None),
        P("grp", None),
        P("grp", None),
        P("grp", None),
        P("grp"),
        P("grp"),
        P("grp"),
        P("grp"),
        P("grp"),
        P("grp"),
        P("grp"),
        P("grp"),
        P("grp"),
    )
    whole_line = mesh.shape["grp"] == 8 and mesh.shape["rep"] == 4
    return jax.shard_map(
        line_of_chips if whole_line else on_device, mesh=mesh, in_specs=in_specs, out_specs=out_specs, check_vma=False
    )
```

```python
import functools
from functools import reduce

import jax
import jax.numpy as jnp
from jax import lax
from jax.experimental import pallas as pl
from jax.experimental.pallas import tpu as pltpu
from jax.sharding import PartitionSpec as P

H = 12
MICRO = 2
SEQ_MB = 1


norm_epsilon = 1e-05
masked_score = -1000000000.0


def layer_norm(inputs, norm_gain, norm_shift):
    center = inputs - jnp.mean(inputs, axis=-1, keepdims=True)
    spread = jnp.mean(center * center, axis=-1, keepdims=True)
    return center * lax.rsqrt(spread + norm_epsilon) * norm_gain + norm_shift


def exact_gelu(inputs):
    return jax.nn.gelu(inputs, approximate=False)


def times_transpose(left, right):
    return lax.dot_general(
        left, right, (((1,), (1,)), ((), ())), preferred_element_type=jnp.float32
    )


def transpose_times(left, right):
    return lax.dot_general(
        left, right, (((0,), (0,)), ((), ())), preferred_element_type=jnp.float32
    )


def column_total(inputs):
    return jnp.sum(inputs.astype(jnp.float32), axis=0)


def masked_scores(query_group, key_group, same_doc, score_scale):
    scores = (
        jnp.einsum("bqhd,bkhd->bhqk", query_group, key_group, preferred_element_type=jnp.float32)
        * score_scale
    )
    return jnp.where(same_doc[:, None], scores, masked_score)


def group_forward(query_group, key_group, value_group, same_doc, score_scale):
    scores = masked_scores(query_group, key_group, same_doc, score_scale)
    highest = jnp.max(scores, axis=-1, keepdims=True)
    log_total = highest + jnp.log(jnp.sum(jnp.exp(scores - highest), axis=-1, keepdims=True))
    weights_low = jnp.exp(scores - log_total).astype(jnp.bfloat16)
    context = jnp.einsum(
        "bhqk,bkhd->bqhd", weights_low, value_group, preferred_element_type=jnp.float32
    )
    return (context.astype(jnp.bfloat16), log_total)


def group_backward(
    query_group, key_group, value_group, same_doc, log_total, grad_context, score_scale
):
    attn_weights = jnp.exp(masked_scores(query_group, key_group, same_doc, score_scale) - log_total)
    weights_low = attn_weights.astype(jnp.bfloat16)
    grad_weights = jnp.einsum(
        "bqhd,bkhd->bhqk", grad_context, value_group, preferred_element_type=jnp.float32
    )
    centre = jnp.sum(attn_weights * grad_weights, axis=-1, keepdims=True)
    grad_scores = (attn_weights * (grad_weights - centre)).astype(jnp.bfloat16)
    grad_query = jnp.einsum(
        "bhqk,bkhd->bqhd", grad_scores, key_group, preferred_element_type=jnp.float32
    )
    grad_query = (grad_query * score_scale).astype(jnp.bfloat16)
    grad_key = (
        jnp.einsum("bhqk,bqhd->bkhd", grad_scores, query_group, preferred_element_type=jnp.float32)
        * score_scale
    )
    grad_value = jnp.einsum(
        "bhqk,bqhd->bkhd", weights_low, grad_context, preferred_element_type=jnp.float32
    )
    return (grad_query, grad_key, grad_value)


def merge_groups(stacked, row_total, model_width):
    return jnp.moveaxis(stacked, 0, 2).reshape(row_total, model_width)


def gradient_terms(
    token_rows,
    context_rows,
    hidden_rows,
    active_rows,
    grad_queries,
    grad_keys,
    grad_values,
    grad_attention,
    grad_inner,
    grad_feed,
    norm_grads,
):
    return (
        transpose_times(token_rows, grad_queries),
        transpose_times(token_rows, grad_keys),
        transpose_times(token_rows, grad_values),
        transpose_times(context_rows, grad_attention),
        transpose_times(hidden_rows, grad_inner),
        transpose_times(active_rows, grad_feed),
        column_total(grad_queries),
        column_total(grad_values),
        column_total(grad_attention),
        column_total(grad_inner),
        column_total(grad_feed),
        norm_grads[0],
        norm_grads[1],
        norm_grads[2],
        norm_grads[3],
    )


def on_device(
    tokens,
    segment_ids,
    out_grad,
    query_weight,
    key_weight,
    value_weight,
    output_weight,
    inner_weight,
    outer_weight,
    query_bias,
    value_bias,
    output_bias,
    inner_bias,
    outer_bias,
    first_gain,
    first_shift,
    second_gain,
    second_shift,
):
    row_count = tokens.shape[1]
    model_width = tokens.shape[2]
    head_count = H
    head_size = model_width // head_count
    per_group = max(1, min(head_count, 128 // head_size))
    group_width = per_group * head_size
    group_count = head_count // per_group
    score_scale = head_size ** (-0.5)
    seq_count = SEQ_MB
    flat_rows = seq_count * row_count
    all_segments = lax.all_gather(segment_ids, "grp", axis=1, tiled=True)
    outputs = []
    input_grads = []
    shares_list = []
    for batch_index in range(MICRO):
        offset = batch_index * seq_count
        local_tokens = tokens[offset : offset + seq_count]
        flat_tokens = local_tokens.reshape(flat_rows, model_width)
        gathered = (
            lax.all_gather(query_weight, "grp", axis=0, tiled=True),
            lax.all_gather(key_weight, "grp", axis=0, tiled=True),
            lax.all_gather(value_weight, "grp", axis=0, tiled=True),
            lax.all_gather(output_weight, "grp", axis=0, tiled=True),
            lax.all_gather(inner_weight, "grp", axis=0, tiled=True),
            lax.all_gather(outer_weight, "grp", axis=0, tiled=True),
            lax.all_gather(query_bias, "grp", axis=0, tiled=True),
            lax.all_gather(value_bias, "grp", axis=0, tiled=True),
            lax.all_gather(output_bias, "grp", axis=0, tiled=True),
            lax.all_gather(inner_bias, "grp", axis=0, tiled=True),
            lax.all_gather(outer_bias, "grp", axis=0, tiled=True),
            lax.all_gather(first_gain, "grp", axis=0, tiled=True),
            lax.all_gather(first_shift, "grp", axis=0, tiled=True),
            lax.all_gather(second_gain, "grp", axis=0, tiled=True),
            lax.all_gather(second_shift, "grp", axis=0, tiled=True),
        )
        full_query, full_key, full_value, full_output, full_inner, full_outer = gathered[:6]
        (
            bias_query,
            bias_value,
            bias_output,
            bias_inner,
            bias_outer,
            gain_first,
            shift_first,
            gain_second,
            shift_second,
        ) = [vector.astype(jnp.float32) for vector in gathered[6:]]
        queries = (
            jnp.dot(flat_tokens, full_query, preferred_element_type=jnp.float32) + bias_query
        ).astype(jnp.bfloat16)
        key_rows = jnp.dot(flat_tokens, full_key, preferred_element_type=jnp.float32).astype(
            jnp.bfloat16
        )
        value_rows = (
            jnp.dot(flat_tokens, full_value, preferred_element_type=jnp.float32) + bias_value
        ).astype(jnp.bfloat16)
        key_split = key_rows.reshape(seq_count, row_count, model_width)
        value_split = value_rows.reshape(seq_count, row_count, model_width)
        key_all, value_all = (
            lax.all_gather(key_split, "grp", axis=1, tiled=True),
            lax.all_gather(value_split, "grp", axis=1, tiled=True),
        )
        length = key_all.shape[1]
        local_segments = segment_ids[offset : offset + seq_count]
        far_segments = all_segments[offset : offset + seq_count]
        same_doc = local_segments[:, :, None] == far_segments[:, None, :]
        query_split = queries.reshape(seq_count, row_count, model_width)

        def slice_group(array, group_index):
            piece = lax.dynamic_slice_in_dim(array, group_index * group_width, group_width, 2)
            return piece.reshape(array.shape[0], array.shape[1], per_group, head_size)

        def forward_group(group_index):
            context, log_total = group_forward(
                slice_group(query_split, group_index),
                slice_group(key_all, group_index),
                slice_group(value_all, group_index),
                same_doc,
                score_scale,
            )
            return (context.reshape(seq_count, row_count, group_width), log_total)

        context_groups, log_totals = lax.map(forward_group, jnp.arange(group_count))
        context_rows = merge_groups(context_groups, flat_rows, model_width)
        attention = (
            jnp.dot(context_rows, full_output, preferred_element_type=jnp.float32) + bias_output
        )
        residual_one = flat_tokens.astype(jnp.float32) + attention
        hidden_one, norm_one_pullback = jax.vjp(layer_norm, residual_one, gain_first, shift_first)
        hidden_low = hidden_one.astype(jnp.bfloat16)
        inner_pre = jnp.dot(hidden_low, full_inner, preferred_element_type=jnp.float32) + bias_inner
        activation, gelu_pullback = jax.vjp(exact_gelu, inner_pre)
        active_low = activation.astype(jnp.bfloat16)
        feed = jnp.dot(active_low, full_outer, preferred_element_type=jnp.float32) + bias_outer
        output_rows, norm_two_pullback = jax.vjp(
            layer_norm, hidden_one + feed, gain_second, shift_second
        )
        outputs.append(output_rows.astype(jnp.bfloat16).reshape(seq_count, row_count, model_width))
        cotangent = (
            out_grad[offset : offset + seq_count]
            .reshape(flat_rows, model_width)
            .astype(jnp.float32)
        )
        grad_two, grad_gain_two, grad_shift_two = norm_two_pullback(cotangent)
        grad_feed = grad_two.astype(jnp.bfloat16)
        grad_active = times_transpose(grad_feed, full_outer)
        grad_inner = gelu_pullback(grad_active)[0].astype(jnp.bfloat16)
        grad_hidden = grad_two + times_transpose(grad_inner, full_inner)
        grad_one, grad_gain_one, grad_shift_one = norm_one_pullback(grad_hidden)
        grad_attention = grad_one.astype(jnp.bfloat16)
        grad_context = times_transpose(grad_attention, full_output).astype(jnp.bfloat16)
        grad_context = grad_context.reshape(seq_count, row_count, model_width)

        def backward_group(pieces):
            group_index, log_total = pieces
            grad_query, grad_key, grad_value = group_backward(
                slice_group(query_split, group_index),
                slice_group(key_all, group_index),
                slice_group(value_all, group_index),
                same_doc,
                log_total,
                slice_group(grad_context, group_index),
                score_scale,
            )
            return (
                grad_query.reshape(seq_count, row_count, group_width),
                grad_key.reshape(seq_count, length, group_width),
                grad_value.reshape(seq_count, length, group_width),
            )

        query_groups, key_groups, value_groups = lax.map(
            backward_group, (jnp.arange(group_count), log_totals)
        )
        key_owned, value_owned = (
            lax.psum_scatter(key_groups, "grp", scatter_dimension=2, tiled=True),
            lax.psum_scatter(value_groups, "grp", scatter_dimension=2, tiled=True),
        )
        grad_keys = merge_groups(key_owned, flat_rows, model_width).astype(jnp.bfloat16)
        grad_values = merge_groups(value_owned, flat_rows, model_width).astype(jnp.bfloat16)
        grad_queries = merge_groups(query_groups, flat_rows, model_width)
        grad_tokens = (
            grad_one
            + times_transpose(grad_queries, full_query)
            + times_transpose(grad_keys, full_key)
            + times_transpose(grad_values, full_value)
        )
        input_grads.append(
            grad_tokens.astype(jnp.bfloat16).reshape(seq_count, row_count, model_width)
        )
        norm_grads = (grad_gain_one, grad_shift_one, grad_gain_two, grad_shift_two)
        terms = gradient_terms(
            flat_tokens,
            context_rows,
            hidden_low,
            active_low,
            grad_queries,
            grad_keys,
            grad_values,
            grad_attention,
            grad_inner,
            grad_feed,
            norm_grads,
        )
        shares = (
            lax.psum_scatter(terms[0], "grp", scatter_dimension=0, tiled=True),
            lax.psum_scatter(terms[1], "grp", scatter_dimension=0, tiled=True),
            lax.psum_scatter(terms[2], "grp", scatter_dimension=0, tiled=True),
            lax.psum_scatter(terms[3], "grp", scatter_dimension=0, tiled=True),
            lax.psum_scatter(terms[4], "grp", scatter_dimension=0, tiled=True),
            lax.psum_scatter(terms[5], "grp", scatter_dimension=0, tiled=True),
            lax.psum_scatter(terms[6], "grp", scatter_dimension=0, tiled=True),
            lax.psum_scatter(terms[7], "grp", scatter_dimension=0, tiled=True),
            lax.psum_scatter(terms[8], "grp", scatter_dimension=0, tiled=True),
            lax.psum_scatter(terms[9], "grp", scatter_dimension=0, tiled=True),
            lax.psum_scatter(terms[10], "grp", scatter_dimension=0, tiled=True),
            lax.psum_scatter(terms[11], "grp", scatter_dimension=0, tiled=True),
            lax.psum_scatter(terms[12], "grp", scatter_dimension=0, tiled=True),
            lax.psum_scatter(terms[13], "grp", scatter_dimension=0, tiled=True),
            lax.psum_scatter(terms[14], "grp", scatter_dimension=0, tiled=True),
        )
        shares_list.append(shares)
    owned = reduce(
        lambda left_part, right_part: jax.tree.map(jnp.add, left_part, right_part), shares_list
    )
    summed = (
        lax.psum(owned[0].astype(jnp.bfloat16), "rep").astype(jnp.float32),
        lax.psum(owned[1].astype(jnp.bfloat16), "rep").astype(jnp.float32),
        lax.psum(owned[2].astype(jnp.bfloat16), "rep").astype(jnp.float32),
        lax.psum(owned[3].astype(jnp.bfloat16), "rep").astype(jnp.float32),
        lax.psum(owned[4].astype(jnp.bfloat16), "rep").astype(jnp.float32),
        lax.psum(owned[5].astype(jnp.bfloat16), "rep").astype(jnp.float32),
        lax.psum(owned[6].astype(jnp.bfloat16), "rep").astype(jnp.float32),
        lax.psum(owned[7].astype(jnp.bfloat16), "rep").astype(jnp.float32),
        lax.psum(owned[8].astype(jnp.bfloat16), "rep").astype(jnp.float32),
        lax.psum(owned[9].astype(jnp.bfloat16), "rep").astype(jnp.float32),
        lax.psum(owned[10].astype(jnp.bfloat16), "rep").astype(jnp.float32),
        lax.psum(owned[11].astype(jnp.bfloat16), "rep").astype(jnp.float32),
        lax.psum(owned[12].astype(jnp.bfloat16), "rep").astype(jnp.float32),
        lax.psum(owned[13].astype(jnp.bfloat16), "rep").astype(jnp.float32),
        lax.psum(owned[14].astype(jnp.bfloat16), "rep").astype(jnp.float32),
    )
    return (
        jnp.concatenate(outputs, axis=0),
        jnp.concatenate(input_grads, axis=0),
        summed[0],
        summed[1],
        summed[2],
        summed[3],
        summed[4],
        summed[5],
        summed[6],
        summed[7],
        summed[8],
        summed[9],
        summed[10],
        summed[11],
        summed[12],
        summed[13],
        summed[14],
    )


HEAD = 32
LANES = 128
QB = 256
AWAY = 2.0 ** 100
LIMIT = 100.0
LONG = 17
MESH = pl.DeviceIdType.MESH
BIG = 62 * 1024 * 1024
SCALE = HEAD ** -0.5 * 1.4426950408889634


def halves(value):
    first = value.astype(jnp.bfloat16).astype(jnp.float32)
    rest = value - first
    second = rest.astype(jnp.bfloat16).astype(jnp.float32)
    third = (rest - second).astype(jnp.bfloat16).astype(jnp.float32)
    return first, second, third


def dot(left, right):
    return jnp.dot(left, right, preferred_element_type=jnp.float32)


def zeros_for(rank, *grid):
    return (0,) * rank


def whole_spec(array):
    return pl.BlockSpec(array.shape, functools.partial(zeros_for, array.ndim), pipeline_mode=pl.Buffered(1))


def quarter_spec(w, i):
    return pl.BlockSpec((1,) + w.shape[1:], lambda *grid: (i, 0, 0, 0, 0), pipeline_mode=pl.Buffered(1))


def iota(shape, dim):
    return lax.broadcasted_iota(jnp.int32, shape, dim)


def where_am_i():
    r = lax.axis_index("rep")
    g = lax.axis_index("grp")
    return r, g, lax.div(g, 2), lax.rem(g, 2)


def remote(src, dst, send, recv, r, g):
    return pltpu.make_async_remote_copy(
        src_ref=src, dst_ref=dst, send_sem=send, recv_sem=recv, device_id=(r, g), device_id_type=MESH
    )


def greet(r, g, reps, group):
    barrier = pltpu.get_barrier_semaphore()
    for d in range(1, group):
        pl.semaphore_signal(barrier, inc=1, device_id=(r, lax.rem(g + d, group)), device_id_type=MESH)
    for d in range(1, reps):
        pl.semaphore_signal(barrier, inc=1, device_id=(lax.rem(r + d, reps), g), device_id_type=MESH)
    pl.semaphore_wait(barrier, group + reps - 2)


def vectors_of(small):
    return jnp.concatenate([small[g, 0:8, 0:48].astype(jnp.float32) for g in range(8)], axis=1)


def chip_at(z, i):
    order = ((0, 1, 2, 3), (1, 0, 2, 3), (2, 1, 3, 0), (3, 2, 1, 0))
    chip = jnp.int32(0)
    for a, row in enumerate(order):
        for k, value in enumerate(row):
            chip = jnp.where((z == a) & (i == k), value, chip)
    return chip


def gather_kernel(
    tok, wq, wk, wv, wo, wi, wu, vectors, inner, seg,
    x_out, w_out, s_out, kv_out, kt_out, vt_out, q1_out, norms,
    small, x, kv, kt, vt, q1, w0, smalls_in, wrow, wtr, mine,
    lsem, xsem, psems, tsend, trecv, psend, wsend1, wrecv1, wsend2, wrecv2, wsend3, wrecv3, ssend, srecv,
):
    r, g, z, c = where_am_i()
    reps, chips = 4, 4
    p = 2 * z + 1 - c
    heads = kv.shape[0]
    _, rows, width = x.shape
    small[0:8, :] = jnp.concatenate(
        [vectors[...].astype(jnp.float32), jnp.zeros((8, rows - 48), jnp.float32)], axis=1
    ).astype(jnp.bfloat16)
    small[8:16, :] = jnp.concatenate(
        [
            jnp.concatenate([inner[...].astype(jnp.float32), jnp.zeros((1, rows - 192), jnp.float32)], axis=1),
            seg[...].astype(jnp.float32),
            jnp.zeros((5, rows), jnp.float32),
        ],
        axis=0,
    ).astype(jnp.bfloat16)
    greet(r, g, reps, 2 * chips)
    slab = [wi.at[:, pl.ds(j * width, width)] for j in range(4)]
    quarters = (
        ((wq, 0, 48), (wk, 48, 48), (wv, 96, 48)),
        ((wo, 0, 48), (slab[0], 48, 48), (slab[1], 96, 48)),
        ((slab[2], 0, 48), (slab[3], 48, 48), (wu.at[pl.ds(0, 48), :], 96, 48)),
        ((wu.at[pl.ds(48, 144), :], 0, 144),),
    )
    swap = remote(tok.at[1 - c], x.at[g], psend, trecv.at[g], r, p)
    swap.start()
    own_x = pltpu.make_async_copy(tok.at[c], x.at[g], lsem.at[0])
    own_x.start()
    def pass_on(b, way, src=None):
        to = g + 2 if way == 0 else g - 2
        src = x.at[b] if src is None else src
        return remote(src, x.at[b], tsend.at[way, b], trecv.at[b], r, to)

    def forward(b, way, src=None):
        ok = z < chips - 1 if way == 0 else z > 0

        @pl.when(ok)
        def _():
            pass_on(b, way, src).start()

    def keep(b):
        return pltpu.make_async_copy(x.at[b], x_out.at[b], xsem.at[b])

    def arrived(b):
        remote(x.at[b], x.at[b], tsend.at[0, b], trecv.at[b], r, p).wait_recv()

    forward(g, 0, tok.at[c])
    forward(g, 1, tok.at[c])
    arrived(p)
    forward(p, 0)
    forward(p, 1)
    keep(p).start()
    for i, pieces in enumerate(quarters):
        @pl.when(r == i)
        def _():
            copies = [
                pltpu.make_async_copy(ref, mine.at[pl.ds(row, count), :], lsem.at[3 + k])
                for k, (ref, row, count) in enumerate(pieces)
            ]
            for copy in copies:
                copy.start()
            for copy in copies:
                copy.wait()

    own_w = pltpu.make_async_copy(mine, w_out.at[r, c, z], lsem.at[1])
    own_w.start()
    own_s = pltpu.make_async_copy(small, smalls_in.at[g], lsem.at[2])
    own_s.start()
    first = []
    for d in range(1, chips):
        zz = lax.rem(z + d, chips)
        copy = remote(mine, w_out.at[r, c, z], wsend1.at[d - 1], wrecv1.at[z], r, 2 * zz + c)
        copy.start()
        first.append(copy)
    smalls = []
    for d in range(1, 2 * chips):
        copy = remote(small, smalls_in.at[g], ssend.at[d - 1], srecv.at[g], r, lax.rem(g + d, 2 * chips))
        copy.start()
        smalls.append(copy)
    own_x.wait()
    keep(g).start()

    def tokens_from(d):
        for k in range(2):
            @pl.when(z >= d)
            def _():
                b = 2 * (z - d) + (c if k == 0 else 1 - c)
                arrived(b)
                forward(b, 0)
                keep(b).start()

            @pl.when(z + d < chips)
            def _():
                b = 2 * (z + d) + (c if k == 0 else 1 - c)
                arrived(b)
                forward(b, 1)
                keep(b).start()

    tokens_from(1)
    for d in range(1, chips):
        zz = lax.rem(z + d, chips)
        remote(mine, w_out.at[r, c, zz], wsend1.at[0], wrecv1.at[zz], r, p).wait_recv()
    own_w.wait()
    second = []
    for d in range(1, reps):
        copy = remote(
            w_out.at[r, c], w_out.at[r, c], wsend2.at[d - 1], wrecv2.at[r], lax.rem(r + d, reps), g
        )
        copy.start()
        second.append(copy)
    third = [remote(w_out.at[r, c], w_out.at[r, c], wsend3.at[r], wrecv3.at[r], r, p)]
    third[0].start()
    tokens_from(2)
    for d in range(1, reps):
        q = lax.rem(r + d, reps)
        remote(w_out.at[q, c], w_out.at[q, c], wsend2.at[0], wrecv2.at[q], r, p).wait_recv()
        copy = remote(w_out.at[q, c], w_out.at[q, c], wsend3.at[q], wrecv3.at[q], r, p)
        copy.start()
        third.append(copy)
    for q in range(reps):
        remote(w_out.at[q, 1 - c], w_out.at[q, 1 - c], wsend3.at[q], wrecv3.at[q], r, p).wait_recv()
    load_w = pltpu.make_async_copy(w_out.at[0], w0, lsem.at[1])
    load_w.start()
    for d in range(1, 2 * chips):
        b = lax.rem(g + d, 2 * chips)
        remote(small, smalls_in.at[b], ssend.at[0], srecv.at[b], r, p).wait_recv()
    own_s.wait()
    keep_s = pltpu.make_async_copy(smalls_in, s_out, lsem.at[2])
    keep_s.start()
    load_w.wait()

    span = heads * HEAD
    bias = vectors_of(smalls_in).astype(jnp.bfloat16)
    full = [
        jnp.concatenate([w0[i % 2, i // 2, 48 * k : 48 * k + 48, :] for i in range(8)], axis=0)
        for k in range(3)
    ]
    lane = iota((width, heads * LANES), 1)
    head, lane_in = lax.div(lane, LANES), lax.rem(lane, LANES)
    column = span * z + head * HEAD + lax.rem(lane_in, HEAD)
    hit = iota((width, heads * LANES), 0) == column
    pick_k = jnp.where(hit & (lane_in < HEAD), 1.0, 0.0).astype(jnp.bfloat16)
    pick_v = jnp.where(hit & (lane_in >= 64) & (lane_in < 96), 1.0, 0.0).astype(jnp.bfloat16)
    wrow[...] = (dot(full[1], pick_k) + dot(full[2], pick_v)).astype(jnp.bfloat16)
    row_kv = dot(bias[1:2, :], pick_v)
    pick_t = jnp.where(
        iota((span, width), 1) == span * z + iota((span, width), 0), 1.0, 0.0
    ).astype(jnp.bfloat16)

    def by_rows(left, right):
        return lax.dot_general(
            left, right, (((1,), (1,)), ((), ())), preferred_element_type=jnp.float32
        )

    for k in range(3):
        wtr[k] = by_rows(pick_t, full[k]).astype(jnp.bfloat16)
    column_bias = by_rows(pick_t, bias)
    col_q, col_v = column_bias[:, 0:1], column_bias[:, 1:2]
    one_lane = lax.rem(iota((1, heads * LANES), 1), LANES)
    row_kv = row_kv + jnp.where((one_lane >= 104) & (one_lane < 107), 1.0, 0.0)
    one = jnp.where(iota((16, rows), 0) == 0, 1.0, 0.0).astype(jnp.bfloat16)

    def stores(b):
        cols = pl.ds(pl.multiple_of(b * rows, rows), rows)
        return [
            pltpu.make_async_copy(kv.at[:, cols, :], kv_out.at[:, cols, :], psems.at[0, b])
        ] + [
            pltpu.make_async_copy(ref.at[:, :, cols], out.at[:, :, cols], psems.at[1 + i, b])
            for i, (ref, out) in enumerate(((kt, kt_out), (vt, vt_out), (q1, q1_out)))
        ]

    def project(i, most):
        half = lax.rem(i, 2)
        b = 2 * chip_at(z, lax.div(i, 2)) + c + half - 2 * c * half
        xb = x[b]
        two = smalls_in[b, 8:16, :].astype(jnp.float32)
        ids = jnp.where(c == 0, two[1:2], two[2:3])
        same = jnp.where(iota((8, rows), 0).astype(jnp.float32) == ids, 1.0, 0.0)
        hot = jnp.concatenate(
            [jnp.zeros((96, rows), jnp.float32), same, jnp.zeros((24, rows), jnp.float32)], axis=0
        ).T
        cols = pl.ds(pl.multiple_of(b * rows, rows), rows)
        flat = dot(xb, wrow[...]) + row_kv
        for h in range(heads):
            kv[h, cols, :] = (flat[:, h * LANES : (h + 1) * LANES] + hot).astype(jnp.bfloat16)
        q_t = (by_rows(wtr[0], xb) + col_q).astype(jnp.bfloat16)
        k_t = by_rows(wtr[1], xb).astype(jnp.bfloat16)
        v_t = (by_rows(wtr[2], xb) + col_v).astype(jnp.bfloat16)
        q_wide = q_t.astype(jnp.float32) * SCALE
        k_wide = k_t.astype(jnp.float32)
        sizes = []
        for n, v in enumerate((q_wide, k_wide)):
            size = most[n]
            for h in range(heads):
                size = jnp.maximum(
                    size, jnp.sum(v[h * HEAD : (h + 1) * HEAD] ** 2, axis=0, keepdims=True)
                )
            sizes.append(size)
        for h in range(heads):
            part = slice(h * HEAD, (h + 1) * HEAD)
            kt[h, :, cols] = k_t[part]
            q1[h, :, cols] = q_t[part]
            vt[h, 0:32, cols] = v_t[part]
            vt[h, 32:48, cols] = one
        for copy in stores(b):
            copy.start()
        return tuple(sizes)

    zero = jnp.zeros((1, rows), jnp.float32)
    most = lax.fori_loop(0, 6, project, (zero, zero))
    tokens_from(3)
    most = lax.fori_loop(6, 8, project, most)
    norms[0:1, :] = most[0]
    norms[1:2, :] = most[1]

    def settle(b, none):
        keep(b).wait()
        for copy in stores(b):
            copy.wait()
        return none

    swap.wait_send()
    for copy in first + smalls + second + third:
        copy.wait_send()
    for b in range(2 * chips):
        @pl.when((z < chips - 1) & (b < 2 * z + 2))
        def _():
            pass_on(b, 0).wait_send()

        @pl.when((z > 0) & (b >= 2 * z))
        def _():
            pass_on(b, 1).wait_send()

    keep_s.wait()
    lax.fori_loop(0, 2 * chips, settle, 0)


def gather(tokens, weights, vectors, inner, seg):
    dma = pltpu.SemaphoreType.DMA
    anywhere = pl.BlockSpec(memory_space=pltpu.HBM)
    vm = pl.BlockSpec(memory_space=pltpu.VMEM)
    rows, width = tokens.shape[1:]
    bf, f4 = jnp.bfloat16, jnp.float32
    heads, length = 3, 8 * rows
    made = [
        (heads, length, LANES), (heads, HEAD, length), (heads, 48, length), (heads, HEAD, length)
    ]
    return pl.pallas_call(
        gather_kernel,
        name="gather",
        out_shape=(
            jax.ShapeDtypeStruct((8, rows, width), bf),
            jax.ShapeDtypeStruct((4, 2, 4, 144, width), bf),
            jax.ShapeDtypeStruct((8, 16, rows), bf),
        )
        + tuple(jax.ShapeDtypeStruct(shape, bf) for shape in made)
        + (jax.ShapeDtypeStruct((2, rows), f4),),
        in_specs=[anywhere] * 7 + [vm] * 3,
        out_specs=[anywhere] * 7 + [vm],
        scratch_shapes=[
            pltpu.VMEM((16, rows), bf),
            pltpu.VMEM((8, rows, width), bf),
        ]
        + [pltpu.VMEM(shape, bf) for shape in made]
        + [
            pltpu.VMEM((2, 4, 144, width), bf),
            pltpu.VMEM((8, 16, rows), bf),
            pltpu.VMEM((width, heads * LANES), bf),
            pltpu.VMEM((3, heads * HEAD, width), bf),
            pltpu.VMEM((144, width), bf),
            dma((6,)), dma((8,)), dma((4, 8)), dma((2, 8)), dma((8,)), dma, dma((3,)), dma((4,)), dma((3,)), dma((4,)),
            dma((4,)), dma((4,)), dma((7,)), dma((8,)),
        ],
        compiler_params=pltpu.CompilerParams(
            collective_id=1, has_side_effects=True, vmem_limit_bytes=BIG
        ),
    )(tokens, *weights, vectors, inner, seg)


def span_of(starts, q0, docs):
    low = jnp.int32(0)
    high = starts[docs]
    for d in range(docs):
        low = jnp.where(starts[d] <= q0, jnp.maximum(low, starts[d]), low)
        high = jnp.where(starts[d + 1] >= q0 + QB, jnp.minimum(high, starts[d + 1]), high)
    first = lax.div(low, LANES)
    return first, lax.div(high + LANES - 1, LANES) - first


def in_groups(first, count, total, body):
    def at(i):
        return pl.multiple_of(i * LANES, LANES)

    big = count >= LONG - 1

    @pl.when(big)
    def _():
        body(pl.ds(at(jnp.minimum(first, total - LONG)), LONG * LANES))

    first = jnp.where(big, first + LONG, first)
    count = jnp.where(big, jnp.maximum(count - LONG, 0), count)
    many = jnp.maximum(lax.div(count, 4) - 1, 0)

    def group(i, none):
        body(pl.ds(at(first + 4 * i), 4 * LANES))
        return none

    lax.fori_loop(0, many, group, 0)
    left = count - 4 * many
    for k in range(1, 8):
        @pl.when(left == k)
        def _():
            body(pl.ds(at(first + 4 * many), k * LANES))


def attend_kernel(
    place, kv_hbm, q1, vt_hbm, small, norms, ctx, tail_out, spans, qt, acc, tall, seg, starts, kv, vt, sems,
):
    heads, length, _ = kv.shape
    blocks, hw, rows = ctx.shape
    docs = 8
    c = place[1]
    loads = [
        pltpu.make_async_copy(kv_hbm, kv, sems.at[0]),
        pltpu.make_async_copy(q1, qt.at[:, pl.ds(0, HEAD), :], sems.at[1]),
        pltpu.make_async_copy(vt_hbm, vt, sems.at[2]),
    ]
    for load in loads:
        load.start()
    for g in range(8):
        two = small[g, 8:16, :].astype(jnp.float32)
        seg[g : g + 1, :] = jnp.where(c == 0, two[1:2], two[2:3]).astype(jnp.int32)
    ids = seg[...]
    starts[0] = jnp.int32(0)
    for d in range(1, docs):
        starts[d] = jnp.sum(jnp.where(ids < d, 1.0, 0.0)).astype(jnp.int32)
    starts[docs] = jnp.int32(length)

    def far(same):
        return (same - 1.0) * AWAY

    def fill(b, none):
        cols = pl.ds(pl.multiple_of(b * rows, rows), rows)
        same = jnp.where(iota((8, rows), 0) == seg[pl.ds(b, 1), :], 1.0, 0.0)
        low = jnp.concatenate([far(same), jnp.zeros((8, rows), jnp.float32)], axis=0)
        for h in range(heads):
            qt[h, HEAD:96, cols] = jnp.zeros((96 - HEAD, rows), jnp.bfloat16)
            qt[h, 96:112, cols] = low.astype(jnp.bfloat16)
            qt[h, 112:128, cols] = jnp.zeros((16, rows), jnp.bfloat16)
        return none

    lax.fori_loop(0, blocks, fill, 0)
    bounded = jnp.max(norms[0:1, :]) * jnp.max(norms[1:2, :]) < LIMIT * LIMIT
    for load in loads:
        load.wait()

    per = rows // QB

    def query_block(b, carry):
        q0 = pl.multiple_of(b * QB, QB)
        first, count = span_of(starts, q0, docs)
        spans[0, b] = first
        spans[1, b] = count
        acc[...] = jnp.zeros_like(acc)

        def key_block(i, tops):
            keys = pl.ds(pl.multiple_of((first + i) * LANES, LANES), LANES)
            s = [dot(kv[h, keys, :], qt[h, :, pl.ds(q0, QB)]) for h in range(heads)]
            new = [jnp.maximum(tops[h], jnp.max(s[h], axis=0, keepdims=True)) for h in range(heads)]
            p = [jnp.exp2((s[h] - new[h]) * SCALE).astype(jnp.bfloat16) for h in range(heads)]
            for h in range(heads):
                acc[h] = acc[h] * jnp.exp2((tops[h] - new[h]) * SCALE) + dot(vt[h, :, keys], p[h])
            return tuple(new)

        def plain_block(keys):
            s = [dot(kv[h, keys, :], qt[h, :, pl.ds(q0, QB)]) for h in range(heads)]
            p = [jnp.exp2(v * SCALE).astype(jnp.bfloat16) for v in s]
            for h in range(heads):
                acc[h] += dot(vt[h, :, keys], p[h])

        @pl.when(bounded)
        def _():
            in_groups(first, count, length // LANES, plain_block)
            tall[...] = jnp.zeros_like(tall)

        @pl.when(jnp.logical_not(bounded))
        def _():
            lowest = jnp.full((1, QB), -3e38, jnp.float32)
            tops = lax.fori_loop(0, count, key_block, (lowest,) * heads)
            for h in range(heads):
                tall[h] = tops[h]

        g = lax.div(b, per)
        off = pl.multiple_of(lax.rem(b, per) * QB, QB)
        same = jnp.where(iota((8, QB), 0) == seg[pl.ds(g, 1), pl.ds(off, QB)], 1.0, 0.0)
        for h in range(heads):
            total = acc[h, 32:33, :]
            out = acc[h, 0:32, :] / total
            ctx[g, h * HEAD : (h + 1) * HEAD, pl.ds(off, QB)] = out.astype(jnp.bfloat16)
            parts = halves(-(tall[h] + jnp.log2(total) / SCALE))
            tail = jnp.concatenate([far(same), *parts, jnp.zeros((5, QB), jnp.float32)], axis=0)
            tail_out[h, :, pl.ds(q0, QB)] = tail.astype(jnp.bfloat16)
        return carry

    lax.fori_loop(0, length // QB, query_block, 0)


def attend(place, kv, q1, vt, small, norms):
    heads, length, _ = kv.shape
    blocks, _, rows = small.shape
    sm = pl.BlockSpec(memory_space=pltpu.SMEM)
    anywhere = pl.BlockSpec(memory_space=pltpu.HBM)
    bf, f4 = jnp.bfloat16, jnp.float32
    shapes = (
        jax.ShapeDtypeStruct((blocks, heads * HEAD, rows), bf),
        jax.ShapeDtypeStruct((heads, 16, length), bf),
    )
    return pl.pallas_call(
        attend_kernel,
        name="attend",
        grid=(1,),
        out_shape=shapes + (jax.ShapeDtypeStruct((2, length // QB), jnp.int32),),
        in_specs=[sm, anywhere, anywhere, anywhere, whole_spec(small), whole_spec(norms)],
        out_specs=[whole_spec(v) for v in shapes] + [sm],
        scratch_shapes=[
            pltpu.VMEM((heads, LANES, length), bf),
            pltpu.VMEM((heads, 48, QB), f4),
            pltpu.VMEM((heads, 1, QB), f4),
            pltpu.VMEM((8, rows), jnp.int32),
            pltpu.SMEM((16,), jnp.int32),
            pltpu.VMEM(kv.shape, bf),
            pltpu.VMEM(vt.shape, bf),
            pltpu.SemaphoreType.DMA((3,)),
        ],
        compiler_params=pltpu.CompilerParams(vmem_limit_bytes=BIG),
    )(place, kv, q1, vt, small, norms)


PIECE = 128


def middle_kernel(
    ctx, tok_hbm, og_hbm, w_hbm, small,
    layer_hbm, grad_hbm, gctx_out, pr,
    wo, wi, wu, gwo, gwi, gwu, sums, inner_sum, ctx_in, gctx, pg, pg_in,
    tok, og, w, layer_out, grad_one_out, insems, outsems, lsem, send, recv, gsend, grecv, glocal, psend, precv,
):
    seqs, rows, width = tok.shape
    slabs = wi.shape[0]
    pieces = rows // PIECE
    r, g, z, c = where_am_i()
    loads = [
        pltpu.make_async_copy(w_hbm, w, insems.at[0]),
        pltpu.make_async_copy(tok_hbm, tok, insems.at[1]),
        pltpu.make_async_copy(og_hbm, og, insems.at[2]),
    ]
    for load in loads:
        load.start()
    greet(r, g, 1, 8)

    def fetch(q):
        cols = pl.ds(pl.multiple_of(q * PIECE, PIECE), PIECE)
        for d in range(1, 8):
            to = lax.rem(g + d, 8)
            remote(
                ctx.at[to, :, cols], ctx_in.at[c, z, :, cols], send.at[q, d - 1], recv.at[q, g], r, to
            ).start()

    own = pltpu.make_async_copy(ctx.at[g], ctx_in.at[c, z], lsem)
    own.start()
    fetch(0)
    fetch(1)
    loads[0].wait()
    for i in range(8):
        cc, zz = i % 2, i // 2
        wo[48 * i : 48 * i + 48, :] = w[1, cc, zz, 0:48, :]
        wi[0, 48 * i : 48 * i + 48, :] = w[1, cc, zz, 48:96, :]
        wi[1, 48 * i : 48 * i + 48, :] = w[1, cc, zz, 96:144, :]
        wi[2, 48 * i : 48 * i + 48, :] = w[2, cc, zz, 0:48, :]
        wi[3, 48 * i : 48 * i + 48, :] = w[2, cc, zz, 48:96, :]
        wu[zz, 192 * cc : 192 * cc + 48, :] = w[2, cc, zz, 96:144, :]
        wu[zz, 192 * cc + 48 : 192 * cc + 192, :] = w[3, cc, zz, :, :]
    for ref in (gwo, gwi, gwu, sums, inner_sum):
        ref[...] = jnp.zeros_like(ref)
    fetch(2)
    fetch(3)

    vec = vectors_of(small)
    inner_bias = jnp.concatenate(
        [small[i, 8:16, 0:192].astype(jnp.float32)[0:1] for i in range(8)], axis=1
    )
    out_bias, outer_bias = vec[2:3, :], vec[3:4, :]
    gain_one, shift_one = vec[4:5, :], vec[5:6, :]
    gain_two, shift_two = vec[6:7, :], vec[7:8, :]

    def normal(value):
        centre = value - jnp.mean(value, axis=-1, keepdims=True)
        rate = lax.rsqrt(jnp.mean(centre * centre, axis=-1, keepdims=True) + norm_epsilon)
        return centre * rate, rate

    def normal_back(grad, gain, n, rate):
        u = grad * gain
        return rate * (
            u - jnp.mean(u, axis=-1, keepdims=True) - n * jnp.mean(u * n, axis=-1, keepdims=True)
        )

    def total(value):
        return jnp.sum(value, axis=0, keepdims=True)

    def dot_turn(left, right):
        return lax.dot_general(
            left, right, (((1,), (1,)), ((), ())), preferred_element_type=jnp.float32
        )

    def arrived(q, cols):
        for d in range(1, 8):
            b = lax.rem(g + d, 8)
            remote(
                ctx.at[g, :, cols], ctx_in.at[lax.rem(b, 2), lax.div(b, 2), :, cols],
                send.at[q, 0], recv.at[q, b], r, b,
            ).wait_recv()

    def return_piece(q, cols, d):
        to = lax.rem(g + d, 8)
        return remote(
            gctx.at[lax.rem(to, 2), lax.div(to, 2), :, cols], gctx_out.at[g, :, cols],
            gsend.at[q, d - 1], grecv.at[q, g], r, to,
        )

    def keep_piece(q, cols):
        return pltpu.make_async_copy(gctx.at[c, z, :, cols], gctx_out.at[g, :, cols], glocal.at[q])

    own.wait()
    loads[1].wait()
    loads[2].wait()

    def results(q):
        here = pl.ds(pl.multiple_of(q * PIECE, PIECE), PIECE)
        return [
            pltpu.make_async_copy(ref.at[:, here, :], out.at[:, here, :], outsems.at[k, q])
            for k, (ref, out) in enumerate(((layer_out, layer_hbm), (grad_one_out, grad_hbm)))
        ]

    def one(q, carry):
        r0 = pl.multiple_of(q * PIECE, PIECE)
        here = pl.ds(r0, PIECE)
        arrived(q, here)

        def both(ref):
            return jnp.concatenate([ref[s, here, :] for s in range(seqs)], axis=0)

        def split(ref, value):
            for s in range(seqs):
                ref[s, here, :] = value[s * PIECE : (s + 1) * PIECE].astype(ref.dtype)

        ctx_t = jnp.concatenate(
            [jnp.concatenate([ctx_in[s, zz, :, here] for zz in range(4)], axis=0) for s in range(seqs)],
            axis=1,
        )
        context = ctx_t.astype(jnp.float32).T.astype(jnp.bfloat16)
        x = both(tok).astype(jnp.float32)
        n_one, rate_one = normal(x + (dot(context, wo[...]) + out_bias))
        hidden = n_one * gain_one + shift_one
        low = hidden.astype(jnp.bfloat16)
        low_t = hidden.T.astype(jnp.bfloat16)
        feed = jnp.zeros(hidden.shape, jnp.float32)
        slopes, actives = [], []
        for j in range(slabs):
            inner = dot(low, wi[j]) + inner_bias[:, j * width : (j + 1) * width]
            cdf = 0.5 + 0.5 * lax.erf(inner * (0.5 ** 0.5))
            pdf = jnp.exp(inner * inner * -0.5) * 0.3989422804014327
            slopes.append(cdf + inner * pdf)
            active = inner * cdf
            actives.append(active)
            feed = feed + dot(active.astype(jnp.bfloat16), wu[j])
        n_two, rate_two = normal(hidden + (feed + outer_bias))
        split(layer_out, n_two * gain_two + shift_two)
        grad = both(og).astype(jnp.float32)
        grad_two = normal_back(grad, gain_two, n_two, rate_two)
        grad_feed = grad_two.astype(jnp.bfloat16)
        grad_hidden = grad_two
        for j in range(slabs):
            grad_inner = (dot_turn(grad_feed, wu[j]) * slopes[j]).astype(jnp.bfloat16)
            inner_sum[:, j * width : (j + 1) * width] += total(grad_inner.astype(jnp.float32))
            grad_hidden = grad_hidden + dot_turn(grad_inner, wi[j])
            gwi[j] += dot(low_t, grad_inner)
            gwu[j] += dot(actives[j].T.astype(jnp.bfloat16), grad_feed)
        grad_one = normal_back(grad_hidden, gain_one, n_one, rate_one)
        split(grad_one_out, grad_one)
        grad_att = grad_one.astype(jnp.bfloat16)
        back = dot_turn(wo[...], grad_att).astype(jnp.bfloat16)
        for s in range(seqs):
            for zz in range(4):
                gctx[s, zz, :, here] = back[96 * zz : 96 * zz + 96, s * PIECE : (s + 1) * PIECE]
        for d in range(1, 8):
            return_piece(q, here, d).start()
        keep_piece(q, here).start()
        for copy in results(q):
            copy.start()
        gwo[...] += dot(ctx_t, grad_att)
        sums[0:1, :] += total(grad_att.astype(jnp.float32))
        sums[1:2, :] += total(grad_feed.astype(jnp.float32))
        sums[2:3, :] += total(grad_hidden * n_one)
        sums[3:4, :] += total(grad_hidden)
        sums[4:5, :] += total(grad * n_two)
        sums[5:6, :] += total(grad)
        return carry

    lax.fori_loop(0, pieces, one, 0)
    rows_of_sums = jnp.concatenate(
        [sums[...]]
        + [inner_sum[:, j * width : (j + 1) * width] for j in range(slabs)]
        + [jnp.zeros((6, width), jnp.float32)],
        axis=0,
    ).astype(jnp.bfloat16)
    for i in range(8):
        cc, zz = i % 2, i // 2
        mine = slice(48 * i, 48 * i + 48)
        pg[cc, zz, 0, 0:48, :] = gwo[mine, :].astype(jnp.bfloat16)
        pg[cc, zz, 0, 48:96, :] = gwi[0, mine, :].astype(jnp.bfloat16)
        pg[cc, zz, 1, 0:48, :] = gwi[1, mine, :].astype(jnp.bfloat16)
        pg[cc, zz, 1, 48:96, :] = gwi[2, mine, :].astype(jnp.bfloat16)
        pg[cc, zz, 2, 0:48, :] = gwi[3, mine, :].astype(jnp.bfloat16)
        base = 192 * cc
        pg[cc, zz, 0, 96:112, :] = gwu[zz, base : base + 16, :].astype(jnp.bfloat16)
        pg[cc, zz, 1, 96:112, :] = gwu[zz, base + 16 : base + 32, :].astype(jnp.bfloat16)
        pg[cc, zz, 2, 48:112, :] = gwu[zz, base + 32 : base + 96, :].astype(jnp.bfloat16)
        pg[cc, zz, 3, 0:96, :] = gwu[zz, base + 96 : base + 192, :].astype(jnp.bfloat16)
        pg[cc, zz, 3, 96:112, :] = rows_of_sums
    pair = remote(pg.at[1 - c], pg_in, psend, precv, r, 2 * z + 1 - c)
    pair.start()

    def settle(q, carry):
        cols = pl.ds(pl.multiple_of(q * PIECE, PIECE), PIECE)
        for d in range(1, 8):
            b = lax.rem(g + d, 8)
            remote(
                gctx.at[c, z, :, cols], gctx_out.at[b, :, cols], gsend.at[q, 0], grecv.at[q, b], r, b
            ).wait_recv()
            return_piece(q, cols, d).wait_send()
            to = lax.rem(g + d, 8)
            remote(
                ctx.at[to, :, cols], ctx_in.at[c, z, :, cols], send.at[q, d - 1], recv.at[q, g], r, to
            ).wait_send()
        keep_piece(q, cols).wait()
        for copy in results(q):
            copy.wait()
        return carry

    pair.wait_recv()
    for i in range(4):
        pr[i] = (pg[c, i].astype(jnp.float32) + pg_in[i].astype(jnp.float32)).astype(jnp.bfloat16)
    lax.fori_loop(0, pieces, settle, 0)
    pair.wait_send()


def middle(ctx, tok, og, w, small):
    seqs, rows, width = tok.shape
    vm = pl.BlockSpec(memory_space=pltpu.VMEM)
    anywhere = pl.BlockSpec(memory_space=pltpu.HBM)
    dma = pltpu.SemaphoreType.DMA
    bf, f4 = jnp.bfloat16, jnp.float32
    pieces = rows // PIECE
    return pl.pallas_call(
        middle_kernel,
        name="middle",
        out_shape=(
            jax.ShapeDtypeStruct((seqs, rows, width), bf),
            jax.ShapeDtypeStruct((seqs, rows, width), f4),
            jax.ShapeDtypeStruct(ctx.shape, bf),
            jax.ShapeDtypeStruct((4, 4, 112, width), bf),
        ),
        in_specs=[anywhere] * 4 + [vm],
        out_specs=[anywhere, anywhere, anywhere, vm],
        scratch_shapes=[
            pltpu.VMEM((width, width), bf),
            pltpu.VMEM((4, width, width), bf),
            pltpu.VMEM((4, width, width), bf),
            pltpu.VMEM((width, width), f4),
            pltpu.VMEM((4, width, width), f4),
            pltpu.VMEM((4, width, width), f4),
            pltpu.VMEM((6, width), f4),
            pltpu.VMEM((1, 4 * width), f4),
            pltpu.VMEM((2, 4) + ctx.shape[1:], bf),
            pltpu.VMEM((2, 4) + ctx.shape[1:], bf),
            pltpu.VMEM((2, 4, 4, 112, width), bf),
            pltpu.VMEM((4, 4, 112, width), bf),
            pltpu.VMEM((seqs, rows, width), bf),
            pltpu.VMEM((seqs, rows, width), bf),
            pltpu.VMEM(w.shape, bf),
            pltpu.VMEM((seqs, rows, width), bf),
            pltpu.VMEM((seqs, rows, width), f4),
            dma((3,)), dma((2, pieces)), dma, dma((pieces, 7)), dma((pieces, 8)), dma((pieces, 7)), dma((pieces, 8)), dma((pieces,)), dma, dma,
        ],
        compiler_params=pltpu.CompilerParams(
            collective_id=2, has_side_effects=True, vmem_limit_bytes=BIG
        ),
    )(ctx, tok, og, w, small)


def attend_back_kernel(
    last, index, place, spans, x_hbm, q_hbm, tail, kv_hbm, kt_hbm, q1, gctx, ctx, *refs,
):
    heads = q1.shape[0]
    span = heads * HEAD
    if last:
        grads_in, out, gq, dt, do, acc, dq, qt, x, kv, kt, sems = refs
    else:
        out, grads_out, dt, do, acc, dq, qt, x, kv, kt, sems = refs
    length, width = x.shape
    mine = pl.ds(index * heads, heads)
    loads = [
        pltpu.make_async_copy(q_hbm.at[mine], qt.at[:, pl.ds(0, HEAD), :], sems.at[0]),
        pltpu.make_async_copy(tail.at[mine], qt.at[:, pl.ds(96, 16), :], sems.at[1]),
        pltpu.make_async_copy(kv_hbm.at[mine], kv, sems.at[3]),
        pltpu.make_async_copy(kt_hbm.at[mine], kt, sems.at[4]),
        pltpu.make_async_copy(x_hbm, x, sems.at[2]),
    ]
    for load in loads:
        load.start()
    blocks, _, rows = gctx.shape
    z = place[0]
    c = place[1]
    scale = HEAD ** -0.5

    def prepare(g, carry):
        r0 = pl.multiple_of(g * rows, rows)
        cols = pl.ds(r0, rows)
        for h in range(heads):
            part = slice(h * HEAD, (h + 1) * HEAD)
            grad = gctx[g, part, :]
            wide = grad.astype(jnp.float32)
            delta = -jnp.sum(wide * ctx[g, part, :].astype(jnp.float32), axis=0, keepdims=True)
            dt[h, 0:64, cols] = jnp.zeros((64, rows), jnp.bfloat16)
            dt[h, 64:96, cols] = grad
            qt[h, HEAD:96, cols] = jnp.zeros((96 - HEAD, rows), jnp.bfloat16)
            qt[h, 112:128, cols] = jnp.zeros((16, rows), jnp.bfloat16)
            tail = jnp.concatenate(
                [jnp.zeros((8, rows), jnp.float32), *halves(delta), jnp.zeros((21, rows), jnp.float32)],
                axis=0,
            )
            dt[h, 96:128, cols] = tail.astype(jnp.bfloat16)
            turned = jnp.concatenate(
                [wide, q1[h, :, cols].astype(jnp.float32), jnp.zeros((64, rows), jnp.float32)], axis=0
            ).T
            lane = iota((rows, LANES), 1)
            grad_rows = jnp.where(lane < HEAD, turned, 0.0).astype(jnp.bfloat16)
            query_rows = jnp.where(lane < HEAD, 0.0, turned).astype(jnp.bfloat16)
            for j in range(rows // QB):
                r1 = pl.multiple_of(2 * r0 + 2 * j * QB, QB)
                do[h, pl.ds(r1, QB), :] = grad_rows[j * QB : (j + 1) * QB]
                do[h, pl.ds(r1 + QB, QB), :] = query_rows[j * QB : (j + 1) * QB]
        return carry

    lax.fori_loop(0, blocks, prepare, 0)
    acc[...] = jnp.zeros_like(acc)
    per = rows // QB
    for load in loads[:4]:
        load.wait()

    def query_block(b, carry):
        q0 = pl.multiple_of(b * QB, QB)
        dq[...] = jnp.zeros_like(dq)

        def key_block(keys):
            s = [dot(kv[h, keys, :], qt[h, :, pl.ds(q0, QB)]) for h in range(heads)]
            d = [dot(kv[h, keys, :], dt[h, :, pl.ds(q0, QB)]) for h in range(heads)]
            p = [jnp.exp2(v * SCALE) for v in s]
            both = [
                jnp.concatenate([u.astype(jnp.bfloat16), (u * v).astype(jnp.bfloat16)], axis=1)
                for u, v in zip(p, d)
            ]
            for h in range(heads):
                acc[h, keys, :] += dot(both[h], do[h, pl.ds(2 * q0, 2 * QB), :])
            for h in range(heads):
                dq[h] += dot(kt[h, :, keys], both[h][:, QB:])

        in_groups(spans[0, b], spans[1, b], length // LANES, key_block)
        g = lax.div(b, per)
        off = pl.multiple_of(lax.rem(b, per) * QB, QB)
        for h in range(heads):
            out[g, h * HEAD : (h + 1) * HEAD, pl.ds(off, QB)] = (dq[h] * scale).astype(jnp.bfloat16)
        return carry

    lax.fori_loop(0, length // QB, query_block, 0)

    loads[4].wait()

    def finish_block(g, totals):
        r0 = pl.multiple_of(g * rows, rows)
        cols = pl.ds(r0, rows)
        for h in range(heads):
            both = acc[h, cols, :].T
            row = h * HEAD
            out[g, 2 * span + row : 2 * span + row + HEAD, :] = both[0:32].astype(jnp.bfloat16)
            out[g, span + row : span + row + HEAD, :] = (both[32:64] * scale).astype(jnp.bfloat16)
        piece = out[g]
        grad = dot(piece, x[cols, :])
        summed = jnp.sum(piece.astype(jnp.float32), axis=1, keepdims=True)
        return totals[0] + grad, totals[1] + summed

    grads, summed = lax.fori_loop(
        0,
        blocks,
        finish_block,
        (jnp.zeros((3 * span, width), jnp.float32), jnp.zeros((3 * span, 1), jnp.float32)),
    )
    if not last:
        grads_out[:, 0:width] = grads
        grads_out[:, width:] = jnp.broadcast_to(summed, (3 * span, LANES))
        return
    gq[...] = jnp.zeros_like(gq)
    before = grads_in.shape[0] // 3

    def joined(i, old, new):
        return [old[i * before : (i + 1) * before], new[i * span : (i + 1) * span]]

    old = grads_in[:, 0:width]
    whole = jnp.concatenate([v for i in range(3) for v in joined(i, old, grads)], axis=0).T
    total = 3 * (before + span)
    for g in range(8):
        gq[g % 2, g // 2, :, 0:total] = whole[48 * g : 48 * g + 48, :].astype(jnp.bfloat16)
    old = grads_in[:, width : width + 1]
    of_q = jnp.concatenate(joined(0, old, summed), axis=0)
    of_v = jnp.concatenate(joined(2, old, summed), axis=0)
    for cc in range(2):
        mine = jnp.concatenate(
            [
                of_q[48 * cc : 48 * cc + 48, :],
                of_v[48 * cc : 48 * cc + 48, :],
                jnp.zeros((48, 94), jnp.float32),
            ],
            axis=1,
        )
        gq[cc, z, :, total:] = mine.astype(jnp.bfloat16)


def attend_back(heads, index, place, spans, x, tail, kv, kt, q1, gctx, ctx, grads=None):
    blocks, rows, width = x.shape
    length = blocks * rows
    last = grads is not None
    rest = (grads,) if last else ()
    sm = pl.BlockSpec(memory_space=pltpu.SMEM)
    bf, f4 = jnp.bfloat16, jnp.float32
    once = pl.Buffered(1)
    span = heads * HEAD

    def some_heads(array):
        return pl.BlockSpec((heads,) + array.shape[1:], lambda i: (index, 0, 0), pipeline_mode=once)

    def head_rows(array):
        return pl.BlockSpec((blocks, span, rows), lambda i: (0, index, 0), pipeline_mode=once)

    flat = x.reshape(length, width)
    shapes = (
        jax.ShapeDtypeStruct((blocks, 3 * span, rows), bf),
        jax.ShapeDtypeStruct((2, 4, 48, width), bf)
        if last
        else jax.ShapeDtypeStruct((3 * span, width + LANES), f4),
    )
    return pl.pallas_call(
        functools.partial(attend_back_kernel, last, index),
        name="attend_back",
        grid=(1,),
        out_shape=shapes,
        in_specs=[sm, sm] + [pl.BlockSpec(memory_space=pltpu.HBM)] * 5
        + [some_heads(q1)]
        + [head_rows(v) for v in (gctx, ctx)]
        + [whole_spec(v) for v in rest],
        out_specs=[whole_spec(v) for v in shapes],
        scratch_shapes=[
            pltpu.VMEM((heads, LANES, length), bf),
            pltpu.VMEM((heads, 2 * length, LANES), bf),
            pltpu.VMEM((heads, length, LANES), f4),
            pltpu.VMEM((heads, HEAD, QB), f4),
            pltpu.VMEM((heads, LANES, length), bf),
            pltpu.VMEM((length, width), bf),
            pltpu.VMEM((heads,) + kv.shape[1:], bf),
            pltpu.VMEM((heads,) + kt.shape[1:], bf),
            pltpu.SemaphoreType.DMA((5,)),
        ],
        compiler_params=pltpu.CompilerParams(vmem_limit_bytes=BIG),
        cost_estimate=pl.CostEstimate(
            flops=heads * 20 * 10 ** 9, bytes_accessed=heads * 8 * 10 ** 6, transcendentals=heads * 6 * 10 ** 6
        ),
    )(place, spans, flat, q1, tail, kv, kt, q1, gctx, ctx, *rest)


def reduce_kernel(
    src, gq, pz, dst, p_out, q_out,
    gq_in, gq_sum, qa_in, qa_sum, qb_in, pz_in, p_line, pa_in, p_own, gq_own,
    lsem, send, recv, gsend, grecv, qasend, qarecv, qbsend, qbrecv, qcsend, qcrecv,
    pasend, parecv, pcsend, pcrecv,
):
    r, g, z, c = where_am_i()
    greet(r, g, 4, 8)
    waits = []
    pair = remote(gq.at[1 - c], gq_in, gsend, grecv, r, 2 * z + 1 - c)
    pair.start()
    load_g = pltpu.make_async_copy(gq.at[c], gq_own, lsem.at[1])
    load_g.start()
    load_p = pltpu.make_async_copy(pz, pz_in, lsem.at[2])
    load_p.start()
    own = pltpu.make_async_copy(src.at[g], dst.at[g], lsem.at[0])
    own.start()

    def send_to(d):
        to = lax.rem(g + d, 8)
        copy = remote(src.at[to], dst.at[g], send.at[d - 1], recv.at[g], r, to)
        copy.start()
        waits.append(copy)

    def f32(value):
        return value.astype(jnp.float32)

    load_g.wait()
    pair.wait_recv()
    gq_sum[...] = (f32(gq_own[...]) + f32(gq_in[...])).astype(jnp.bfloat16)
    for d in range(1, 4):
        rr = lax.rem(r + d, 4)
        copy = remote(gq_sum.at[rr], qa_in.at[r], qasend.at[d - 1], qarecv.at[r], rr, g)
        copy.start()
        waits.append(copy)
    load_p.wait()
    total = f32(pz_in[0])
    for i in range(1, 4):
        total = total + f32(pz_in[i])
    p_line[...] = total.astype(jnp.bfloat16)
    for d in range(1, 4):
        rr = lax.rem(r + d, 4)
        copy = remote(p_line.at[rr], pa_in.at[r], pasend.at[d - 1], parecv.at[r], rr, g)
        copy.start()
        waits.append(copy)
    for d in range(1, 4):
        b = lax.rem(r + d, 4)
        remote(gq_sum.at[r], qa_in.at[b], qasend.at[0], qarecv.at[b], b, g).wait_recv()
    total = f32(gq_sum[r])
    for d in range(1, 4):
        total = total + f32(qa_in[lax.rem(r + d, 4)])
    qa_sum[...] = total.astype(jnp.bfloat16)

    @pl.when(z != r)
    def _():
        remote(qa_sum, qb_in.at[z], qbsend, qbrecv.at[z], r, 2 * r + c).start()

    for d in (4, 3, 5, 2, 6, 1, 7):
        send_to(d)
    for d in range(1, 4):
        b = lax.rem(r + d, 4)
        remote(p_line.at[r], pa_in.at[b], pasend.at[0], parecv.at[b], b, g).wait_recv()
    total = f32(p_line[r])
    for d in range(1, 4):
        total = total + f32(pa_in[lax.rem(r + d, 4)])
    p_own[...] = total.astype(jnp.bfloat16)
    keep_p = pltpu.make_async_copy(p_own, p_out.at[r], lsem.at[3])
    keep_p.start()
    for d in range(1, 4):
        rr = lax.rem(r + d, 4)
        copy = remote(p_own, p_out.at[r], pcsend.at[d - 1], pcrecv.at[r], rr, g)
        copy.start()
        waits.append(copy)

    @pl.when(z == r)
    def _():
        for d in range(1, 4):
            b = lax.rem(z + d, 4)
            remote(qa_sum, qb_in.at[b], qbsend, qbrecv.at[b], r, g).wait_recv()
        qb_in[z] = qa_sum[...]
        keep = pltpu.make_async_copy(qb_in, q_out, lsem.at[4])
        keep.start()
        for d in range(1, 4):
            remote(qb_in, q_out, qcsend.at[d - 1], qcrecv, lax.rem(r + d, 4), g).start()
        keep.wait()
        for d in range(1, 4):
            remote(qb_in, q_out, qcsend.at[d - 1], qcrecv, lax.rem(r + d, 4), g).wait_send()

    @pl.when(z != r)
    def _():
        remote(qb_in, q_out, qcsend.at[0], qcrecv, r, g).wait_recv()
        remote(qa_sum, qb_in.at[z], qbsend, qbrecv.at[z], r, 2 * r + c).wait_send()

    for d in range(1, 4):
        b = lax.rem(r + d, 4)
        remote(p_own, p_out.at[b], pcsend.at[0], pcrecv.at[b], b, g).wait_recv()
    for d in range(1, 8):
        b = lax.rem(g + d, 8)
        remote(src.at[g], dst.at[b], send.at[0], recv.at[b], r, b).wait_recv()
    pair.wait_send()
    for copy in waits:
        copy.wait_send()
    keep_p.wait()
    own.wait()


def reduce_all(src, gq, pz):
    dma = pltpu.SemaphoreType.DMA
    anywhere = pl.BlockSpec(memory_space=pltpu.HBM)
    bf = jnp.bfloat16
    width = gq.shape[-1]
    part = (4, 48, width)
    return pl.pallas_call(
        reduce_kernel,
        name="reduce",
        out_shape=(
            jax.ShapeDtypeStruct(src.shape, bf),
            jax.ShapeDtypeStruct((4, 112, width), bf),
            jax.ShapeDtypeStruct(part, bf),
        ),
        in_specs=[anywhere] * 3,
        out_specs=[anywhere] * 3,
        scratch_shapes=[
            pltpu.VMEM(part, bf),
            pltpu.VMEM(part, bf),
            pltpu.VMEM(part, bf),
            pltpu.VMEM((48, width), bf),
            pltpu.VMEM(part, bf),
            pltpu.VMEM((4, 4, 112, width), bf),
            pltpu.VMEM((4, 112, width), bf),
            pltpu.VMEM((4, 112, width), bf),
            pltpu.VMEM((112, width), bf),
            pltpu.VMEM(part, bf),
            dma((5,)), dma((7,)), dma((8,)), dma, dma, dma((3,)), dma((4,)), dma, dma((4,)), dma((3,)), dma,
            dma((3,)), dma((4,)), dma((3,)), dma((4,)),
        ],
        compiler_params=pltpu.CompilerParams(
            collective_id=4, has_side_effects=True, vmem_limit_bytes=BIG
        ),
    )(src, gq, pz)


def finish_kernel(
    place, layer_in, in_0, in_1, grad_one, w, p_in, q_in,
    layer_out, out, g_q, g_k, g_v, g_o, g_in, g_up, rows_out, inner_out, wq, held, sems,
):
    width = w.shape[-1]
    span = 96
    step = pl.program_id(0)
    z = place[0]
    c = place[1]
    load = pltpu.make_async_copy(layer_in, held, sems.at[0])
    store = pltpu.make_async_copy(held, layer_out, sems.at[1])

    @pl.when(step == 0)
    def _():
        load.start()
        for i in range(3):
            for g in range(8):
                wq[i, 48 * g : 48 * g + 48, :] = w[0, g % 2, g // 2, 48 * i : 48 * i + 48, :]

    total = grad_one[0]
    for i in range(3):
        turned = jnp.concatenate(
            [
                ref[zz, 0, i * count : (i + 1) * count, :]
                for zz in range(4)
                for ref, count in ((in_0, in_0.shape[2] // 3), (in_1, in_1.shape[2] // 3))
            ],
            axis=0,
        )
        back = turned.astype(jnp.float32).T.astype(jnp.bfloat16)
        total = total + lax.dot_general(
            back, wq[i], (((1,), (1,)), ((), ())), preferred_element_type=jnp.float32
        )
    out[0] = total.astype(jnp.bfloat16)

    @pl.when(step == 0)
    def _():
        load.wait()
        store.start()
        wide = [q_in[zz].astype(jnp.float32) for zz in range(4)]
        for i, ref in enumerate((g_q, g_k, g_v)):
            ref[...] = jnp.concatenate([v[:, i * span : (i + 1) * span] for v in wide], axis=1)
        sums = p_in[3, 96:112, :]
        pick = jnp.where(
            iota((width, 48), 0) == 48 * (2 * z + c) + iota((width, 48), 1), 1.0, 0.0
        ).astype(jnp.bfloat16)
        rows_out[8:24, :] = dot(sums, pick)
        both = q_in[z].astype(jnp.float32)[:, 3 * span :].T
        rows_out[0:8, :] = both[0:8, :]
        pick = jnp.where(
            iota((width, 192), 0) == 192 * c + iota((width, 192), 1), 1.0, 0.0
        ).astype(jnp.bfloat16)
        inner = dot(sums, pick)
        inner_out[...] = jnp.sum(
            jnp.where(iota((16, 192), 0) == 6 + z, inner, 0.0), axis=0, keepdims=True
        )
        g_o[...] = p_in[0, 0:48, :].astype(jnp.float32)
        g_in[:, 0:384] = p_in[0, 48:96, :].astype(jnp.float32)
        g_in[:, 384:768] = p_in[1, 0:48, :].astype(jnp.float32)
        g_in[:, 768:1152] = p_in[1, 48:96, :].astype(jnp.float32)
        g_in[:, 1152:1536] = p_in[2, 0:48, :].astype(jnp.float32)
        g_up[0:16, :] = p_in[0, 96:112, :].astype(jnp.float32)
        g_up[16:32, :] = p_in[1, 96:112, :].astype(jnp.float32)
        g_up[32:96, :] = p_in[2, 48:112, :].astype(jnp.float32)
        g_up[96:192, :] = p_in[3, 0:96, :].astype(jnp.float32)

    @pl.when(step == 1)
    def _():
        store.wait()


def finish(place, layer_in, in_0, in_1, grad_one, w, p_in, q_in):
    seqs, rows, width = grad_one.shape
    sm = pl.BlockSpec(memory_space=pltpu.SMEM)
    hbm = pl.BlockSpec(memory_space=pltpu.HBM)
    bf, f4 = jnp.bfloat16, jnp.float32
    shapes = ((48, width),) * 4 + ((48, 4 * width), (192, width), (24, 48), (1, 192))
    in_0, in_1 = (v.reshape((4, 2) + v.shape[1:]) for v in (in_0, in_1))

    def of_sequence(v):
        return pl.BlockSpec((4, 1) + v.shape[2:], lambda i: (0, i, 0, 0))

    one = pl.BlockSpec((1, rows, width), lambda i: (i, 0, 0))
    return pl.pallas_call(
        finish_kernel,
        name="finish",
        grid=(seqs,),
        out_shape=(jax.ShapeDtypeStruct((seqs, rows, width), bf),) * 2
        + tuple(jax.ShapeDtypeStruct(shape, f4) for shape in shapes),
        in_specs=[
            sm, hbm, of_sequence(in_0), of_sequence(in_1), one,
            quarter_spec(w, 0), whole_spec(p_in), whole_spec(q_in),
        ],
        out_specs=[hbm, one]
        + [pl.BlockSpec(shape, functools.partial(zeros_for, len(shape))) for shape in shapes],
        scratch_shapes=[
            pltpu.VMEM((3, width, width), bf),
            pltpu.VMEM((seqs, rows, width), bf),
            pltpu.SemaphoreType.DMA((2,)),
        ],
        compiler_params=pltpu.CompilerParams(vmem_limit_bytes=BIG - 1600 * 1024),
    )(place, layer_in, in_0, in_1, grad_one, w, p_in, q_in)


def line_of_chips(
    tokens, segment_ids, out_grad, query_weight, key_weight, value_weight, output_weight,
    inner_weight, outer_weight, query_bias, value_bias, output_bias, inner_bias, outer_bias,
    first_gain, first_shift, second_gain, second_shift,
):
    bf = jnp.bfloat16
    width = tokens.shape[2]
    g = lax.axis_index("grp")
    z, c = lax.div(g, 2), lax.rem(g, 2)
    place = jnp.stack([z, c]).astype(jnp.int32)
    weights = (query_weight, key_weight, value_weight, output_weight, inner_weight, outer_weight)
    vectors = jnp.concatenate(
        [
            v[None]
            for v in (
                query_bias, value_bias, output_bias, outer_bias,
                first_gain, first_shift, second_gain, second_shift,
            )
        ],
        axis=0,
    )
    x, w, small, kv, kt, vt, q1, norms = gather(
        tokens, weights, vectors, inner_bias[None], segment_ids
    )
    ctx, tail, spans = attend(place, kv, q1, vt, small, norms)
    layer_out, grad_one, gctx_in, pr = middle(ctx, tokens, out_grad, w, small)
    same_core = [[i + j for i in range(0, 8, 2)] for j in range(2)]
    pz = lax.all_to_all(pr, "grp", 0, 0, axis_index_groups=same_core, tiled=True)
    back = functools.partial(
        attend_back, place=place, spans=spans, x=x, tail=tail, kv=kv, kt=kt, q1=q1,
        gctx=gctx_in, ctx=ctx,
    )
    parts_0, grads_0 = back(2, 0)
    in_0 = lax.all_to_all(parts_0, "grp", 0, 0, tiled=True)
    parts_1, gq = back(1, 2, grads=grads_0)
    in_1, p_in, q_in = reduce_all(parts_1, gq, pz)
    layer_out, input_grad, g_q, g_k, g_v, g_o, g_in, g_up, rows, inner_row = finish(
        place, layer_out, in_0, in_1, grad_one, w, p_in, q_in
    )
    return (
        layer_out, input_grad, g_q, g_k, g_v, g_o, g_in, g_up,
        rows[0], rows[1], rows[8], inner_row[0], rows[9], rows[10], rows[11], rows[12], rows[13],
    )


def solution(mesh):
    in_specs = (
        P("rep", "grp", None),
        P("rep", "grp"),
        P("rep", "grp", None),
        P("grp", None),
        P("grp", None),
        P("grp", None),
        P("grp", None),
        P("grp", None),
        P("grp", None),
        P("grp"),
        P("grp"),
        P("grp"),
        P("grp"),
        P("grp"),
        P("grp"),
        P("grp"),
        P("grp"),
        P("grp"),
    )
    out_specs = (
        P("rep", "grp", None),
        P("rep", "grp", None),
        P("grp", None),
        P("grp", None),
        P("grp", None),
        P("grp", None),
        P("grp", None),
        P("grp", None),
        P("grp"),
        P("grp"),
        P("grp"),
        P("grp"),
        P("grp"),
        P("grp"),
        P("grp"),
        P("grp"),
        P("grp"),
    )
    whole_line = mesh.shape["grp"] == 8 and mesh.shape["rep"] == 4
    return jax.shard_map(
        line_of_chips if whole_line else on_device, mesh=mesh, in_specs=in_specs, out_specs=out_specs, check_vma=False
    )
```

```python
import functools
from functools import reduce

import jax
import jax.numpy as jnp
from jax import lax
from jax.experimental import pallas as pl
from jax.experimental.pallas import tpu as pltpu
from jax.sharding import PartitionSpec as P

H = 12
MICRO = 2
SEQ_MB = 1


norm_epsilon = 1e-05
masked_score = -1000000000.0


def layer_norm(inputs, norm_gain, norm_shift):
    center = inputs - jnp.mean(inputs, axis=-1, keepdims=True)
    spread = jnp.mean(center * center, axis=-1, keepdims=True)
    return center * lax.rsqrt(spread + norm_epsilon) * norm_gain + norm_shift


def exact_gelu(inputs):
    return jax.nn.gelu(inputs, approximate=False)


def times_transpose(left, right):
    return lax.dot_general(
        left, right, (((1,), (1,)), ((), ())), preferred_element_type=jnp.float32
    )


def transpose_times(left, right):
    return lax.dot_general(
        left, right, (((0,), (0,)), ((), ())), preferred_element_type=jnp.float32
    )


def column_total(inputs):
    return jnp.sum(inputs.astype(jnp.float32), axis=0)


def masked_scores(query_group, key_group, same_doc, score_scale):
    scores = (
        jnp.einsum("bqhd,bkhd->bhqk", query_group, key_group, preferred_element_type=jnp.float32)
        * score_scale
    )
    return jnp.where(same_doc[:, None], scores, masked_score)


def group_forward(query_group, key_group, value_group, same_doc, score_scale):
    scores = masked_scores(query_group, key_group, same_doc, score_scale)
    highest = jnp.max(scores, axis=-1, keepdims=True)
    log_total = highest + jnp.log(jnp.sum(jnp.exp(scores - highest), axis=-1, keepdims=True))
    weights_low = jnp.exp(scores - log_total).astype(jnp.bfloat16)
    context = jnp.einsum(
        "bhqk,bkhd->bqhd", weights_low, value_group, preferred_element_type=jnp.float32
    )
    return (context.astype(jnp.bfloat16), log_total)


def group_backward(
    query_group, key_group, value_group, same_doc, log_total, grad_context, score_scale
):
    attn_weights = jnp.exp(masked_scores(query_group, key_group, same_doc, score_scale) - log_total)
    weights_low = attn_weights.astype(jnp.bfloat16)
    grad_weights = jnp.einsum(
        "bqhd,bkhd->bhqk", grad_context, value_group, preferred_element_type=jnp.float32
    )
    centre = jnp.sum(attn_weights * grad_weights, axis=-1, keepdims=True)
    grad_scores = (attn_weights * (grad_weights - centre)).astype(jnp.bfloat16)
    grad_query = jnp.einsum(
        "bhqk,bkhd->bqhd", grad_scores, key_group, preferred_element_type=jnp.float32
    )
    grad_query = (grad_query * score_scale).astype(jnp.bfloat16)
    grad_key = (
        jnp.einsum("bhqk,bqhd->bkhd", grad_scores, query_group, preferred_element_type=jnp.float32)
        * score_scale
    )
    grad_value = jnp.einsum(
        "bhqk,bqhd->bkhd", weights_low, grad_context, preferred_element_type=jnp.float32
    )
    return (grad_query, grad_key, grad_value)


def merge_groups(stacked, row_total, model_width):
    return jnp.moveaxis(stacked, 0, 2).reshape(row_total, model_width)


def gradient_terms(
    token_rows,
    context_rows,
    hidden_rows,
    active_rows,
    grad_queries,
    grad_keys,
    grad_values,
    grad_attention,
    grad_inner,
    grad_feed,
    norm_grads,
):
    return (
        transpose_times(token_rows, grad_queries),
        transpose_times(token_rows, grad_keys),
        transpose_times(token_rows, grad_values),
        transpose_times(context_rows, grad_attention),
        transpose_times(hidden_rows, grad_inner),
        transpose_times(active_rows, grad_feed),
        column_total(grad_queries),
        column_total(grad_values),
        column_total(grad_attention),
        column_total(grad_inner),
        column_total(grad_feed),
        norm_grads[0],
        norm_grads[1],
        norm_grads[2],
        norm_grads[3],
    )


def on_device(
    tokens,
    segment_ids,
    out_grad,
    query_weight,
    key_weight,
    value_weight,
    output_weight,
    inner_weight,
    outer_weight,
    query_bias,
    value_bias,
    output_bias,
    inner_bias,
    outer_bias,
    first_gain,
    first_shift,
    second_gain,
    second_shift,
):
    row_count = tokens.shape[1]
    model_width = tokens.shape[2]
    head_count = H
    head_size = model_width // head_count
    per_group = max(1, min(head_count, 128 // head_size))
    group_width = per_group * head_size
    group_count = head_count // per_group
    score_scale = head_size ** (-0.5)
    seq_count = SEQ_MB
    flat_rows = seq_count * row_count
    all_segments = lax.all_gather(segment_ids, "grp", axis=1, tiled=True)
    outputs = []
    input_grads = []
    shares_list = []
    for batch_index in range(MICRO):
        offset = batch_index * seq_count
        local_tokens = tokens[offset : offset + seq_count]
        flat_tokens = local_tokens.reshape(flat_rows, model_width)
        gathered = (
            lax.all_gather(query_weight, "grp", axis=0, tiled=True),
            lax.all_gather(key_weight, "grp", axis=0, tiled=True),
            lax.all_gather(value_weight, "grp", axis=0, tiled=True),
            lax.all_gather(output_weight, "grp", axis=0, tiled=True),
            lax.all_gather(inner_weight, "grp", axis=0, tiled=True),
            lax.all_gather(outer_weight, "grp", axis=0, tiled=True),
            lax.all_gather(query_bias, "grp", axis=0, tiled=True),
            lax.all_gather(value_bias, "grp", axis=0, tiled=True),
            lax.all_gather(output_bias, "grp", axis=0, tiled=True),
            lax.all_gather(inner_bias, "grp", axis=0, tiled=True),
            lax.all_gather(outer_bias, "grp", axis=0, tiled=True),
            lax.all_gather(first_gain, "grp", axis=0, tiled=True),
            lax.all_gather(first_shift, "grp", axis=0, tiled=True),
            lax.all_gather(second_gain, "grp", axis=0, tiled=True),
            lax.all_gather(second_shift, "grp", axis=0, tiled=True),
        )
        full_query, full_key, full_value, full_output, full_inner, full_outer = gathered[:6]
        (
            bias_query,
            bias_value,
            bias_output,
            bias_inner,
            bias_outer,
            gain_first,
            shift_first,
            gain_second,
            shift_second,
        ) = [vector.astype(jnp.float32) for vector in gathered[6:]]
        queries = (
            jnp.dot(flat_tokens, full_query, preferred_element_type=jnp.float32) + bias_query
        ).astype(jnp.bfloat16)
        key_rows = jnp.dot(flat_tokens, full_key, preferred_element_type=jnp.float32).astype(
            jnp.bfloat16
        )
        value_rows = (
            jnp.dot(flat_tokens, full_value, preferred_element_type=jnp.float32) + bias_value
        ).astype(jnp.bfloat16)
        key_split = key_rows.reshape(seq_count, row_count, model_width)
        value_split = value_rows.reshape(seq_count, row_count, model_width)
        key_all, value_all = (
            lax.all_gather(key_split, "grp", axis=1, tiled=True),
            lax.all_gather(value_split, "grp", axis=1, tiled=True),
        )
        length = key_all.shape[1]
        local_segments = segment_ids[offset : offset + seq_count]
        far_segments = all_segments[offset : offset + seq_count]
        same_doc = local_segments[:, :, None] == far_segments[:, None, :]
        query_split = queries.reshape(seq_count, row_count, model_width)

        def slice_group(array, group_index):
            piece = lax.dynamic_slice_in_dim(array, group_index * group_width, group_width, 2)
            return piece.reshape(array.shape[0], array.shape[1], per_group, head_size)

        def forward_group(group_index):
            context, log_total = group_forward(
                slice_group(query_split, group_index),
                slice_group(key_all, group_index),
                slice_group(value_all, group_index),
                same_doc,
                score_scale,
            )
            return (context.reshape(seq_count, row_count, group_width), log_total)

        context_groups, log_totals = lax.map(forward_group, jnp.arange(group_count))
        context_rows = merge_groups(context_groups, flat_rows, model_width)
        attention = (
            jnp.dot(context_rows, full_output, preferred_element_type=jnp.float32) + bias_output
        )
        residual_one = flat_tokens.astype(jnp.float32) + attention
        hidden_one, norm_one_pullback = jax.vjp(layer_norm, residual_one, gain_first, shift_first)
        hidden_low = hidden_one.astype(jnp.bfloat16)
        inner_pre = jnp.dot(hidden_low, full_inner, preferred_element_type=jnp.float32) + bias_inner
        activation, gelu_pullback = jax.vjp(exact_gelu, inner_pre)
        active_low = activation.astype(jnp.bfloat16)
        feed = jnp.dot(active_low, full_outer, preferred_element_type=jnp.float32) + bias_outer
        output_rows, norm_two_pullback = jax.vjp(
            layer_norm, hidden_one + feed, gain_second, shift_second
        )
        outputs.append(output_rows.astype(jnp.bfloat16).reshape(seq_count, row_count, model_width))
        cotangent = (
            out_grad[offset : offset + seq_count]
            .reshape(flat_rows, model_width)
            .astype(jnp.float32)
        )
        grad_two, grad_gain_two, grad_shift_two = norm_two_pullback(cotangent)
        grad_feed = grad_two.astype(jnp.bfloat16)
        grad_active = times_transpose(grad_feed, full_outer)
        grad_inner = gelu_pullback(grad_active)[0].astype(jnp.bfloat16)
        grad_hidden = grad_two + times_transpose(grad_inner, full_inner)
        grad_one, grad_gain_one, grad_shift_one = norm_one_pullback(grad_hidden)
        grad_attention = grad_one.astype(jnp.bfloat16)
        grad_context = times_transpose(grad_attention, full_output).astype(jnp.bfloat16)
        grad_context = grad_context.reshape(seq_count, row_count, model_width)

        def backward_group(pieces):
            group_index, log_total = pieces
            grad_query, grad_key, grad_value = group_backward(
                slice_group(query_split, group_index),
                slice_group(key_all, group_index),
                slice_group(value_all, group_index),
                same_doc,
                log_total,
                slice_group(grad_context, group_index),
                score_scale,
            )
            return (
                grad_query.reshape(seq_count, row_count, group_width),
                grad_key.reshape(seq_count, length, group_width),
                grad_value.reshape(seq_count, length, group_width),
            )

        query_groups, key_groups, value_groups = lax.map(
            backward_group, (jnp.arange(group_count), log_totals)
        )
        key_owned, value_owned = (
            lax.psum_scatter(key_groups, "grp", scatter_dimension=2, tiled=True),
            lax.psum_scatter(value_groups, "grp", scatter_dimension=2, tiled=True),
        )
        grad_keys = merge_groups(key_owned, flat_rows, model_width).astype(jnp.bfloat16)
        grad_values = merge_groups(value_owned, flat_rows, model_width).astype(jnp.bfloat16)
        grad_queries = merge_groups(query_groups, flat_rows, model_width)
        grad_tokens = (
            grad_one
            + times_transpose(grad_queries, full_query)
            + times_transpose(grad_keys, full_key)
            + times_transpose(grad_values, full_value)
        )
        input_grads.append(
            grad_tokens.astype(jnp.bfloat16).reshape(seq_count, row_count, model_width)
        )
        norm_grads = (grad_gain_one, grad_shift_one, grad_gain_two, grad_shift_two)
        terms = gradient_terms(
            flat_tokens,
            context_rows,
            hidden_low,
            active_low,
            grad_queries,
            grad_keys,
            grad_values,
            grad_attention,
            grad_inner,
            grad_feed,
            norm_grads,
        )
        shares = (
            lax.psum_scatter(terms[0], "grp", scatter_dimension=0, tiled=True),
            lax.psum_scatter(terms[1], "grp", scatter_dimension=0, tiled=True),
            lax.psum_scatter(terms[2], "grp", scatter_dimension=0, tiled=True),
            lax.psum_scatter(terms[3], "grp", scatter_dimension=0, tiled=True),
            lax.psum_scatter(terms[4], "grp", scatter_dimension=0, tiled=True),
            lax.psum_scatter(terms[5], "grp", scatter_dimension=0, tiled=True),
            lax.psum_scatter(terms[6], "grp", scatter_dimension=0, tiled=True),
            lax.psum_scatter(terms[7], "grp", scatter_dimension=0, tiled=True),
            lax.psum_scatter(terms[8], "grp", scatter_dimension=0, tiled=True),
            lax.psum_scatter(terms[9], "grp", scatter_dimension=0, tiled=True),
            lax.psum_scatter(terms[10], "grp", scatter_dimension=0, tiled=True),
            lax.psum_scatter(terms[11], "grp", scatter_dimension=0, tiled=True),
            lax.psum_scatter(terms[12], "grp", scatter_dimension=0, tiled=True),
            lax.psum_scatter(terms[13], "grp", scatter_dimension=0, tiled=True),
            lax.psum_scatter(terms[14], "grp", scatter_dimension=0, tiled=True),
        )
        shares_list.append(shares)
    owned = reduce(
        lambda left_part, right_part: jax.tree.map(jnp.add, left_part, right_part), shares_list
    )
    summed = (
        lax.psum(owned[0].astype(jnp.bfloat16), "rep").astype(jnp.float32),
        lax.psum(owned[1].astype(jnp.bfloat16), "rep").astype(jnp.float32),
        lax.psum(owned[2].astype(jnp.bfloat16), "rep").astype(jnp.float32),
        lax.psum(owned[3].astype(jnp.bfloat16), "rep").astype(jnp.float32),
        lax.psum(owned[4].astype(jnp.bfloat16), "rep").astype(jnp.float32),
        lax.psum(owned[5].astype(jnp.bfloat16), "rep").astype(jnp.float32),
        lax.psum(owned[6].astype(jnp.bfloat16), "rep").astype(jnp.float32),
        lax.psum(owned[7].astype(jnp.bfloat16), "rep").astype(jnp.float32),
        lax.psum(owned[8].astype(jnp.bfloat16), "rep").astype(jnp.float32),
        lax.psum(owned[9].astype(jnp.bfloat16), "rep").astype(jnp.float32),
        lax.psum(owned[10].astype(jnp.bfloat16), "rep").astype(jnp.float32),
        lax.psum(owned[11].astype(jnp.bfloat16), "rep").astype(jnp.float32),
        lax.psum(owned[12].astype(jnp.bfloat16), "rep").astype(jnp.float32),
        lax.psum(owned[13].astype(jnp.bfloat16), "rep").astype(jnp.float32),
        lax.psum(owned[14].astype(jnp.bfloat16), "rep").astype(jnp.float32),
    )
    return (
        jnp.concatenate(outputs, axis=0),
        jnp.concatenate(input_grads, axis=0),
        summed[0],
        summed[1],
        summed[2],
        summed[3],
        summed[4],
        summed[5],
        summed[6],
        summed[7],
        summed[8],
        summed[9],
        summed[10],
        summed[11],
        summed[12],
        summed[13],
        summed[14],
    )


HEAD = 32
LANES = 128
QB = 256
AWAY = 2.0 ** 100
LIMIT = 100.0
LONG = 17
MESH = pl.DeviceIdType.MESH
BIG = 62 * 1024 * 1024
SCALE = HEAD ** -0.5 * 1.4426950408889634


def halves(value):
    first = value.astype(jnp.bfloat16).astype(jnp.float32)
    rest = value - first
    second = rest.astype(jnp.bfloat16).astype(jnp.float32)
    third = (rest - second).astype(jnp.bfloat16).astype(jnp.float32)
    return first, second, third


def dot(left, right):
    return jnp.dot(left, right, preferred_element_type=jnp.float32)


def zeros_for(rank, *grid):
    return (0,) * rank


def whole_spec(array):
    return pl.BlockSpec(array.shape, functools.partial(zeros_for, array.ndim), pipeline_mode=pl.Buffered(1))


def quarter_spec(w, i):
    return pl.BlockSpec((1,) + w.shape[1:], lambda *grid: (i, 0, 0, 0, 0), pipeline_mode=pl.Buffered(1))


def iota(shape, dim):
    return lax.broadcasted_iota(jnp.int32, shape, dim)


def where_am_i():
    r = lax.axis_index("rep")
    g = lax.axis_index("grp")
    return r, g, lax.div(g, 2), lax.rem(g, 2)


def remote(src, dst, send, recv, r, g):
    return pltpu.make_async_remote_copy(
        src_ref=src, dst_ref=dst, send_sem=send, recv_sem=recv, device_id=(r, g), device_id_type=MESH
    )


def greet(r, g, reps, group):
    barrier = pltpu.get_barrier_semaphore()
    for d in range(1, group):
        pl.semaphore_signal(barrier, inc=1, device_id=(r, lax.rem(g + d, group)), device_id_type=MESH)
    for d in range(1, reps):
        pl.semaphore_signal(barrier, inc=1, device_id=(lax.rem(r + d, reps), g), device_id_type=MESH)
    pl.semaphore_wait(barrier, group + reps - 2)


def vectors_of(small):
    return jnp.concatenate([small[g, 0:8, 0:48].astype(jnp.float32) for g in range(8)], axis=1)


def chip_at(z, i):
    order = ((0, 1, 2, 3), (1, 0, 2, 3), (2, 1, 3, 0), (3, 2, 1, 0))
    chip = jnp.int32(0)
    for a, row in enumerate(order):
        for k, value in enumerate(row):
            chip = jnp.where((z == a) & (i == k), value, chip)
    return chip


def gather_kernel(
    tok, wq, wk, wv, wo, wi, wu, vectors, inner, seg,
    x_out, w_out, s_out, kv_out, kt_out, vt_out, q1_out, norms,
    small, x, kv, kt, vt, q1, w0, smalls_in, wrow, wtr, mine,
    lsem, xsem, psems, tsend, trecv, psend, wsend1, wrecv1, wsend2, wrecv2, wsend3, wrecv3, ssend, srecv,
):
    r, g, z, c = where_am_i()
    reps, chips = 4, 4
    p = 2 * z + 1 - c
    heads = kv.shape[0]
    _, rows, width = x.shape
    small[0:8, :] = jnp.concatenate(
        [vectors[...].astype(jnp.float32), jnp.zeros((8, rows - 48), jnp.float32)], axis=1
    ).astype(jnp.bfloat16)
    small[8:16, :] = jnp.concatenate(
        [
            jnp.concatenate([inner[...].astype(jnp.float32), jnp.zeros((1, rows - 192), jnp.float32)], axis=1),
            seg[...].astype(jnp.float32),
            jnp.zeros((5, rows), jnp.float32),
        ],
        axis=0,
    ).astype(jnp.bfloat16)
    greet(r, g, reps, 2 * chips)
    slab = [wi.at[:, pl.ds(j * width, width)] for j in range(4)]
    quarters = (
        ((wq, 0, 48), (wk, 48, 48), (wv, 96, 48)),
        ((wo, 0, 48), (slab[0], 48, 48), (slab[1], 96, 48)),
        ((slab[2], 0, 48), (slab[3], 48, 48), (wu.at[pl.ds(0, 48), :], 96, 48)),
        ((wu.at[pl.ds(48, 144), :], 0, 144),),
    )
    swap = remote(tok.at[1 - c], x.at[g], psend, trecv.at[g], r, p)
    swap.start()
    own_x = pltpu.make_async_copy(tok.at[c], x.at[g], lsem.at[0])
    own_x.start()
    def pass_on(b, way, src=None):
        to = g + 2 if way == 0 else g - 2
        src = x.at[b] if src is None else src
        return remote(src, x.at[b], tsend.at[way, b], trecv.at[b], r, to)

    def forward(b, way, src=None):
        ok = z < chips - 1 if way == 0 else z > 0

        @pl.when(ok)
        def _():
            pass_on(b, way, src).start()

    def keep(b):
        return pltpu.make_async_copy(x.at[b], x_out.at[b], xsem.at[b])

    def arrived(b):
        remote(x.at[b], x.at[b], tsend.at[0, b], trecv.at[b], r, p).wait_recv()

    forward(g, 0, tok.at[c])
    forward(g, 1, tok.at[c])
    arrived(p)
    forward(p, 0)
    forward(p, 1)
    keep(p).start()
    for i, pieces in enumerate(quarters):
        @pl.when(r == i)
        def _():
            copies = [
                pltpu.make_async_copy(ref, mine.at[pl.ds(row, count), :], lsem.at[3 + k])
                for k, (ref, row, count) in enumerate(pieces)
            ]
            for copy in copies:
                copy.start()
            for copy in copies:
                copy.wait()

    own_w = pltpu.make_async_copy(mine, w_out.at[r, c, z], lsem.at[1])
    own_w.start()
    own_s = pltpu.make_async_copy(small, smalls_in.at[g], lsem.at[2])
    own_s.start()
    first = []
    for d in range(1, chips):
        zz = lax.rem(z + d, chips)
        copy = remote(mine, w_out.at[r, c, z], wsend1.at[d - 1], wrecv1.at[z], r, 2 * zz + c)
        copy.start()
        first.append(copy)
    smalls = []
    for d in range(1, 2 * chips):
        copy = remote(small, smalls_in.at[g], ssend.at[d - 1], srecv.at[g], r, lax.rem(g + d, 2 * chips))
        copy.start()
        smalls.append(copy)
    own_x.wait()
    keep(g).start()

    def tokens_from(d):
        for k in range(2):
            @pl.when(z >= d)
            def _():
                b = 2 * (z - d) + (c if k == 0 else 1 - c)
                arrived(b)
                forward(b, 0)
                keep(b).start()

            @pl.when(z + d < chips)
            def _():
                b = 2 * (z + d) + (c if k == 0 else 1 - c)
                arrived(b)
                forward(b, 1)
                keep(b).start()

    tokens_from(1)
    for d in range(1, chips):
        zz = lax.rem(z + d, chips)
        remote(mine, w_out.at[r, c, zz], wsend1.at[0], wrecv1.at[zz], r, p).wait_recv()
    own_w.wait()
    second = []
    for d in range(1, reps):
        copy = remote(
            w_out.at[r, c], w_out.at[r, c], wsend2.at[d - 1], wrecv2.at[r], lax.rem(r + d, reps), g
        )
        copy.start()
        second.append(copy)
    third = [remote(w_out.at[r, c], w_out.at[r, c], wsend3.at[r], wrecv3.at[r], r, p)]
    third[0].start()
    tokens_from(2)
    for d in range(1, reps):
        q = lax.rem(r + d, reps)
        remote(w_out.at[q, c], w_out.at[q, c], wsend2.at[0], wrecv2.at[q], r, p).wait_recv()
        copy = remote(w_out.at[q, c], w_out.at[q, c], wsend3.at[q], wrecv3.at[q], r, p)
        copy.start()
        third.append(copy)
    for q in range(reps):
        remote(w_out.at[q, 1 - c], w_out.at[q, 1 - c], wsend3.at[q], wrecv3.at[q], r, p).wait_recv()
    load_w = pltpu.make_async_copy(w_out.at[0], w0, lsem.at[1])
    load_w.start()
    for d in range(1, 2 * chips):
        b = lax.rem(g + d, 2 * chips)
        remote(small, smalls_in.at[b], ssend.at[0], srecv.at[b], r, p).wait_recv()
    own_s.wait()
    keep_s = pltpu.make_async_copy(smalls_in, s_out, lsem.at[2])
    keep_s.start()
    load_w.wait()

    span = heads * HEAD
    bias = vectors_of(smalls_in).astype(jnp.bfloat16)
    full = [
        jnp.concatenate([w0[i % 2, i // 2, 48 * k : 48 * k + 48, :] for i in range(8)], axis=0)
        for k in range(3)
    ]
    lane = iota((width, heads * LANES), 1)
    head, lane_in = lax.div(lane, LANES), lax.rem(lane, LANES)
    column = span * z + head * HEAD + lax.rem(lane_in, HEAD)
    hit = iota((width, heads * LANES), 0) == column
    pick_k = jnp.where(hit & (lane_in < HEAD), 1.0, 0.0).astype(jnp.bfloat16)
    pick_v = jnp.where(hit & (lane_in >= 64) & (lane_in < 96), 1.0, 0.0).astype(jnp.bfloat16)
    wrow[...] = (dot(full[1], pick_k) + dot(full[2], pick_v)).astype(jnp.bfloat16)
    row_kv = dot(bias[1:2, :], pick_v)
    pick_t = jnp.where(
        iota((span, width), 1) == span * z + iota((span, width), 0), 1.0, 0.0
    ).astype(jnp.bfloat16)

    def by_rows(left, right):
        return lax.dot_general(
            left, right, (((1,), (1,)), ((), ())), preferred_element_type=jnp.float32
        )

    for k in range(3):
        wtr[k] = by_rows(pick_t, full[k]).astype(jnp.bfloat16)
    column_bias = by_rows(pick_t, bias)
    col_q, col_v = column_bias[:, 0:1], column_bias[:, 1:2]
    one_lane = lax.rem(iota((1, heads * LANES), 1), LANES)
    row_kv = row_kv + jnp.where((one_lane >= 104) & (one_lane < 107), 1.0, 0.0)
    one = jnp.where(iota((16, rows), 0) == 0, 1.0, 0.0).astype(jnp.bfloat16)

    def stores(b):
        cols = pl.ds(pl.multiple_of(b * rows, rows), rows)
        return [
            pltpu.make_async_copy(kv.at[:, cols, :], kv_out.at[:, cols, :], psems.at[0, b])
        ] + [
            pltpu.make_async_copy(ref.at[:, :, cols], out.at[:, :, cols], psems.at[1 + i, b])
            for i, (ref, out) in enumerate(((kt, kt_out), (vt, vt_out), (q1, q1_out)))
        ]

    def project(i, most):
        half = lax.rem(i, 2)
        b = 2 * chip_at(z, lax.div(i, 2)) + c + half - 2 * c * half
        xb = x[b]
        two = smalls_in[b, 8:16, :].astype(jnp.float32)
        ids = jnp.where(c == 0, two[1:2], two[2:3])
        same = jnp.where(iota((8, rows), 0).astype(jnp.float32) == ids, 1.0, 0.0)
        hot = jnp.concatenate(
            [jnp.zeros((96, rows), jnp.float32), same, jnp.zeros((24, rows), jnp.float32)], axis=0
        ).T
        cols = pl.ds(pl.multiple_of(b * rows, rows), rows)
        flat = dot(xb, wrow[...]) + row_kv
        for h in range(heads):
            kv[h, cols, :] = (flat[:, h * LANES : (h + 1) * LANES] + hot).astype(jnp.bfloat16)
        q_t = (by_rows(wtr[0], xb) + col_q).astype(jnp.bfloat16)
        k_t = by_rows(wtr[1], xb).astype(jnp.bfloat16)
        v_t = (by_rows(wtr[2], xb) + col_v).astype(jnp.bfloat16)
        q_wide = q_t.astype(jnp.float32) * SCALE
        k_wide = k_t.astype(jnp.float32)
        sizes = []
        for n, v in enumerate((q_wide, k_wide)):
            size = most[n]
            for h in range(heads):
                size = jnp.maximum(
                    size, jnp.sum(v[h * HEAD : (h + 1) * HEAD] ** 2, axis=0, keepdims=True)
                )
            sizes.append(size)
        for h in range(heads):
            part = slice(h * HEAD, (h + 1) * HEAD)
            kt[h, :, cols] = k_t[part]
            q1[h, :, cols] = q_t[part]
            vt[h, 0:32, cols] = v_t[part]
            vt[h, 32:48, cols] = one
        for copy in stores(b):
            copy.start()
        return tuple(sizes)

    zero = jnp.zeros((1, rows), jnp.float32)
    most = lax.fori_loop(0, 6, project, (zero, zero))
    tokens_from(3)
    most = lax.fori_loop(6, 8, project, most)
    norms[0:1, :] = most[0]
    norms[1:2, :] = most[1]

    def settle(b, none):
        keep(b).wait()
        for copy in stores(b):
            copy.wait()
        return none

    swap.wait_send()
    for copy in first + smalls + second + third:
        copy.wait_send()
    for b in range(2 * chips):
        @pl.when((z < chips - 1) & (b < 2 * z + 2))
        def _():
            pass_on(b, 0).wait_send()

        @pl.when((z > 0) & (b >= 2 * z))
        def _():
            pass_on(b, 1).wait_send()

    keep_s.wait()
    lax.fori_loop(0, 2 * chips, settle, 0)


def gather(tokens, weights, vectors, inner, seg):
    dma = pltpu.SemaphoreType.DMA
    anywhere = pl.BlockSpec(memory_space=pltpu.HBM)
    vm = pl.BlockSpec(memory_space=pltpu.VMEM)
    rows, width = tokens.shape[1:]
    bf, f4 = jnp.bfloat16, jnp.float32
    heads, length = 3, 8 * rows
    made = [
        (heads, length, LANES), (heads, HEAD, length), (heads, 48, length), (heads, HEAD, length)
    ]
    return pl.pallas_call(
        gather_kernel,
        name="gather",
        out_shape=(
            jax.ShapeDtypeStruct((8, rows, width), bf),
            jax.ShapeDtypeStruct((4, 2, 4, 144, width), bf),
            jax.ShapeDtypeStruct((8, 16, rows), bf),
        )
        + tuple(jax.ShapeDtypeStruct(shape, bf) for shape in made)
        + (jax.ShapeDtypeStruct((2, rows), f4),),
        in_specs=[anywhere] * 7 + [vm] * 3,
        out_specs=[anywhere] * 7 + [vm],
        scratch_shapes=[
            pltpu.VMEM((16, rows), bf),
            pltpu.VMEM((8, rows, width), bf),
        ]
        + [pltpu.VMEM(shape, bf) for shape in made]
        + [
            pltpu.VMEM((2, 4, 144, width), bf),
            pltpu.VMEM((8, 16, rows), bf),
            pltpu.VMEM((width, heads * LANES), bf),
            pltpu.VMEM((3, heads * HEAD, width), bf),
            pltpu.VMEM((144, width), bf),
            dma((6,)), dma((8,)), dma((4, 8)), dma((2, 8)), dma((8,)), dma, dma((3,)), dma((4,)), dma((3,)), dma((4,)),
            dma((4,)), dma((4,)), dma((7,)), dma((8,)),
        ],
        compiler_params=pltpu.CompilerParams(
            collective_id=1, has_side_effects=True, vmem_limit_bytes=BIG
        ),
    )(tokens, *weights, vectors, inner, seg)


def span_of(starts, q0, docs):
    low = jnp.int32(0)
    high = starts[docs]
    for d in range(docs):
        low = jnp.where(starts[d] <= q0, jnp.maximum(low, starts[d]), low)
        high = jnp.where(starts[d + 1] >= q0 + QB, jnp.minimum(high, starts[d + 1]), high)
    first = lax.div(low, LANES)
    return first, lax.div(high + LANES - 1, LANES) - first


def in_groups(first, count, total, body):
    def at(i):
        return pl.multiple_of(i * LANES, LANES)

    big = count >= LONG - 1

    @pl.when(big)
    def _():
        body(pl.ds(at(jnp.minimum(first, total - LONG)), LONG * LANES))

    first = jnp.where(big, first + LONG, first)
    count = jnp.where(big, jnp.maximum(count - LONG, 0), count)
    many = jnp.maximum(lax.div(count, 4) - 1, 0)

    def group(i, none):
        body(pl.ds(at(first + 4 * i), 4 * LANES))
        return none

    lax.fori_loop(0, many, group, 0)
    left = count - 4 * many
    for k in range(1, 8):
        @pl.when(left == k)
        def _():
            body(pl.ds(at(first + 4 * many), k * LANES))


def attend_kernel(
    place, kv_hbm, q1, vt_hbm, small, norms, ctx, tail_out, spans, qt, acc, tall, seg, starts, kv, vt, sems,
):
    heads, length, _ = kv.shape
    blocks, hw, rows = ctx.shape
    docs = 8
    c = place[1]
    loads = [
        pltpu.make_async_copy(kv_hbm, kv, sems.at[0]),
        pltpu.make_async_copy(q1, qt.at[:, pl.ds(0, HEAD), :], sems.at[1]),
        pltpu.make_async_copy(vt_hbm, vt, sems.at[2]),
    ]
    for load in loads:
        load.start()
    for g in range(8):
        two = small[g, 8:16, :].astype(jnp.float32)
        seg[g : g + 1, :] = jnp.where(c == 0, two[1:2], two[2:3]).astype(jnp.int32)
    ids = seg[...]
    starts[0] = jnp.int32(0)
    for d in range(1, docs):
        starts[d] = jnp.sum(jnp.where(ids < d, 1.0, 0.0)).astype(jnp.int32)
    starts[docs] = jnp.int32(length)

    def far(same):
        return (same - 1.0) * AWAY

    def fill(b, none):
        cols = pl.ds(pl.multiple_of(b * rows, rows), rows)
        same = jnp.where(iota((8, rows), 0) == seg[pl.ds(b, 1), :], 1.0, 0.0)
        low = jnp.concatenate([far(same), jnp.zeros((8, rows), jnp.float32)], axis=0)
        for h in range(heads):
            qt[h, HEAD:96, cols] = jnp.zeros((96 - HEAD, rows), jnp.bfloat16)
            qt[h, 96:112, cols] = low.astype(jnp.bfloat16)
            qt[h, 112:128, cols] = jnp.zeros((16, rows), jnp.bfloat16)
        return none

    lax.fori_loop(0, blocks, fill, 0)
    bounded = jnp.max(norms[0:1, :]) * jnp.max(norms[1:2, :]) < LIMIT * LIMIT
    for load in loads:
        load.wait()

    per = rows // QB

    def query_block(b, carry):
        q0 = pl.multiple_of(b * QB, QB)
        first, count = span_of(starts, q0, docs)
        spans[0, b] = first
        spans[1, b] = count
        acc[...] = jnp.zeros_like(acc)

        def key_block(i, tops):
            keys = pl.ds(pl.multiple_of((first + i) * LANES, LANES), LANES)
            s = [dot(kv[h, keys, :], qt[h, :, pl.ds(q0, QB)]) for h in range(heads)]
            new = [jnp.maximum(tops[h], jnp.max(s[h], axis=0, keepdims=True)) for h in range(heads)]
            p = [jnp.exp2((s[h] - new[h]) * SCALE).astype(jnp.bfloat16) for h in range(heads)]
            for h in range(heads):
                acc[h] = acc[h] * jnp.exp2((tops[h] - new[h]) * SCALE) + dot(vt[h, :, keys], p[h])
            return tuple(new)

        def plain_block(keys):
            s = [dot(kv[h, keys, :], qt[h, :, pl.ds(q0, QB)]) for h in range(heads)]
            p = [jnp.exp2(v * SCALE).astype(jnp.bfloat16) for v in s]
            for h in range(heads):
                acc[h] += dot(vt[h, :, keys], p[h])

        @pl.when(bounded)
        def _():
            in_groups(first, count, length // LANES, plain_block)
            tall[...] = jnp.zeros_like(tall)

        @pl.when(jnp.logical_not(bounded))
        def _():
            lowest = jnp.full((1, QB), -3e38, jnp.float32)
            tops = lax.fori_loop(0, count, key_block, (lowest,) * heads)
            for h in range(heads):
                tall[h] = tops[h]

        g = lax.div(b, per)
        off = pl.multiple_of(lax.rem(b, per) * QB, QB)
        same = jnp.where(iota((8, QB), 0) == seg[pl.ds(g, 1), pl.ds(off, QB)], 1.0, 0.0)
        for h in range(heads):
            total = acc[h, 32:33, :]
            out = acc[h, 0:32, :] / total
            ctx[g, h * HEAD : (h + 1) * HEAD, pl.ds(off, QB)] = out.astype(jnp.bfloat16)
            parts = halves(-(tall[h] + jnp.log2(total) / SCALE))
            tail = jnp.concatenate([far(same), *parts, jnp.zeros((5, QB), jnp.float32)], axis=0)
            tail_out[h, :, pl.ds(q0, QB)] = tail.astype(jnp.bfloat16)
        return carry

    lax.fori_loop(0, length // QB, query_block, 0)


def attend(place, kv, q1, vt, small, norms):
    heads, length, _ = kv.shape
    blocks, _, rows = small.shape
    sm = pl.BlockSpec(memory_space=pltpu.SMEM)
    anywhere = pl.BlockSpec(memory_space=pltpu.HBM)
    bf, f4 = jnp.bfloat16, jnp.float32
    shapes = (
        jax.ShapeDtypeStruct((blocks, heads * HEAD, rows), bf),
        jax.ShapeDtypeStruct((heads, 16, length), bf),
    )
    return pl.pallas_call(
        attend_kernel,
        name="attend",
        grid=(1,),
        out_shape=shapes + (jax.ShapeDtypeStruct((2, length // QB), jnp.int32),),
        in_specs=[sm, anywhere, anywhere, anywhere, whole_spec(small), whole_spec(norms)],
        out_specs=[whole_spec(v) for v in shapes] + [sm],
        scratch_shapes=[
            pltpu.VMEM((heads, LANES, length), bf),
            pltpu.VMEM((heads, 48, QB), f4),
            pltpu.VMEM((heads, 1, QB), f4),
            pltpu.VMEM((8, rows), jnp.int32),
            pltpu.SMEM((16,), jnp.int32),
            pltpu.VMEM(kv.shape, bf),
            pltpu.VMEM(vt.shape, bf),
            pltpu.SemaphoreType.DMA((3,)),
        ],
        compiler_params=pltpu.CompilerParams(vmem_limit_bytes=BIG),
    )(place, kv, q1, vt, small, norms)


PIECE = 128


def middle_kernel(
    ctx, tok_hbm, og_hbm, w_hbm, small,
    layer_hbm, grad_hbm, gctx_out, pr,
    wo, wi, wu, gwo, gwi, gwu, sums, inner_sum, ctx_in, gctx, pg, pg_in,
    tok, og, w, layer_out, grad_one_out, insems, outsems, lsem, send, recv, gsend, grecv, glocal, psend, precv,
):
    seqs, rows, width = tok.shape
    slabs = wi.shape[0]
    pieces = rows // PIECE
    r, g, z, c = where_am_i()
    loads = [
        pltpu.make_async_copy(w_hbm, w, insems.at[0]),
        pltpu.make_async_copy(tok_hbm, tok, insems.at[1]),
        pltpu.make_async_copy(og_hbm, og, insems.at[2]),
    ]
    for load in loads:
        load.start()
    greet(r, g, 1, 8)

    def fetch(q):
        cols = pl.ds(pl.multiple_of(q * PIECE, PIECE), PIECE)
        for d in (4, 3, 5, 2, 6, 1, 7):
            to = lax.rem(g + d, 8)
            remote(
                ctx.at[to, :, cols], ctx_in.at[c, z, :, cols], send.at[q, d - 1], recv.at[q, g], r, to
            ).start()

    own = pltpu.make_async_copy(ctx.at[g], ctx_in.at[c, z], lsem)
    own.start()
    fetch(0)
    fetch(1)
    loads[0].wait()
    for i in range(8):
        cc, zz = i % 2, i // 2
        wo[48 * i : 48 * i + 48, :] = w[1, cc, zz, 0:48, :]
        wi[0, 48 * i : 48 * i + 48, :] = w[1, cc, zz, 48:96, :]
        wi[1, 48 * i : 48 * i + 48, :] = w[1, cc, zz, 96:144, :]
        wi[2, 48 * i : 48 * i + 48, :] = w[2, cc, zz, 0:48, :]
        wi[3, 48 * i : 48 * i + 48, :] = w[2, cc, zz, 48:96, :]
        wu[zz, 192 * cc : 192 * cc + 48, :] = w[2, cc, zz, 96:144, :]
        wu[zz, 192 * cc + 48 : 192 * cc + 192, :] = w[3, cc, zz, :, :]
    for ref in (gwo, gwi, gwu, sums, inner_sum):
        ref[...] = jnp.zeros_like(ref)
    fetch(2)
    fetch(3)

    vec = vectors_of(small)
    inner_bias = jnp.concatenate(
        [small[i, 8:16, 0:192].astype(jnp.float32)[0:1] for i in range(8)], axis=1
    )
    out_bias, outer_bias = vec[2:3, :], vec[3:4, :]
    gain_one, shift_one = vec[4:5, :], vec[5:6, :]
    gain_two, shift_two = vec[6:7, :], vec[7:8, :]

    def normal(value):
        centre = value - jnp.mean(value, axis=-1, keepdims=True)
        rate = lax.rsqrt(jnp.mean(centre * centre, axis=-1, keepdims=True) + norm_epsilon)
        return centre * rate, rate

    def normal_back(grad, gain, n, rate):
        u = grad * gain
        return rate * (
            u - jnp.mean(u, axis=-1, keepdims=True) - n * jnp.mean(u * n, axis=-1, keepdims=True)
        )

    def total(value):
        return jnp.sum(value, axis=0, keepdims=True)

    def dot_turn(left, right):
        return lax.dot_general(
            left, right, (((1,), (1,)), ((), ())), preferred_element_type=jnp.float32
        )

    def arrived(q, cols):
        for d in range(1, 8):
            b = lax.rem(g + d, 8)
            remote(
                ctx.at[g, :, cols], ctx_in.at[lax.rem(b, 2), lax.div(b, 2), :, cols],
                send.at[q, 0], recv.at[q, b], r, b,
            ).wait_recv()

    def return_piece(q, cols, d):
        to = lax.rem(g + d, 8)
        return remote(
            gctx.at[lax.rem(to, 2), lax.div(to, 2), :, cols], gctx_out.at[g, :, cols],
            gsend.at[q, d - 1], grecv.at[q, g], r, to,
        )

    def keep_piece(q, cols):
        return pltpu.make_async_copy(gctx.at[c, z, :, cols], gctx_out.at[g, :, cols], glocal.at[q])

    own.wait()
    loads[1].wait()
    loads[2].wait()

    def results(q):
        here = pl.ds(pl.multiple_of(q * PIECE, PIECE), PIECE)
        return [
            pltpu.make_async_copy(ref.at[:, here, :], out.at[:, here, :], outsems.at[k, q])
            for k, (ref, out) in enumerate(((layer_out, layer_hbm), (grad_one_out, grad_hbm)))
        ]

    def one(q, carry):
        r0 = pl.multiple_of(q * PIECE, PIECE)
        here = pl.ds(r0, PIECE)
        arrived(q, here)

        def both(ref):
            return jnp.concatenate([ref[s, here, :] for s in range(seqs)], axis=0)

        def split(ref, value):
            for s in range(seqs):
                ref[s, here, :] = value[s * PIECE : (s + 1) * PIECE].astype(ref.dtype)

        ctx_t = jnp.concatenate(
            [jnp.concatenate([ctx_in[s, zz, :, here] for zz in range(4)], axis=0) for s in range(seqs)],
            axis=1,
        )
        context = ctx_t.astype(jnp.float32).T.astype(jnp.bfloat16)
        x = both(tok).astype(jnp.float32)
        n_one, rate_one = normal(x + (dot(context, wo[...]) + out_bias))
        hidden = n_one * gain_one + shift_one
        low = hidden.astype(jnp.bfloat16)
        low_t = hidden.T.astype(jnp.bfloat16)
        feed = jnp.zeros(hidden.shape, jnp.float32)
        slopes, actives = [], []
        for j in range(slabs):
            inner = dot(low, wi[j]) + inner_bias[:, j * width : (j + 1) * width]
            cdf = 0.5 + 0.5 * lax.erf(inner * (0.5 ** 0.5))
            pdf = jnp.exp(inner * inner * -0.5) * 0.3989422804014327
            slopes.append(cdf + inner * pdf)
            active = inner * cdf
            actives.append(active)
            feed = feed + dot(active.astype(jnp.bfloat16), wu[j])
        n_two, rate_two = normal(hidden + (feed + outer_bias))
        split(layer_out, n_two * gain_two + shift_two)
        grad = both(og).astype(jnp.float32)
        grad_two = normal_back(grad, gain_two, n_two, rate_two)
        grad_feed = grad_two.astype(jnp.bfloat16)
        grad_hidden = grad_two
        for j in range(slabs):
            grad_inner = (dot_turn(grad_feed, wu[j]) * slopes[j]).astype(jnp.bfloat16)
            inner_sum[:, j * width : (j + 1) * width] += total(grad_inner.astype(jnp.float32))
            grad_hidden = grad_hidden + dot_turn(grad_inner, wi[j])
            gwi[j] += dot(low_t, grad_inner)
            gwu[j] += dot(actives[j].T.astype(jnp.bfloat16), grad_feed)
        grad_one = normal_back(grad_hidden, gain_one, n_one, rate_one)
        split(grad_one_out, grad_one)
        grad_att = grad_one.astype(jnp.bfloat16)
        back = dot_turn(wo[...], grad_att).astype(jnp.bfloat16)
        for s in range(seqs):
            for zz in range(4):
                gctx[s, zz, :, here] = back[96 * zz : 96 * zz + 96, s * PIECE : (s + 1) * PIECE]
        for d in (4, 3, 5, 2, 6, 1, 7):
            return_piece(q, here, d).start()
        keep_piece(q, here).start()
        for copy in results(q):
            copy.start()
        gwo[...] += dot(ctx_t, grad_att)
        sums[0:1, :] += total(grad_att.astype(jnp.float32))
        sums[1:2, :] += total(grad_feed.astype(jnp.float32))
        sums[2:3, :] += total(grad_hidden * n_one)
        sums[3:4, :] += total(grad_hidden)
        sums[4:5, :] += total(grad * n_two)
        sums[5:6, :] += total(grad)
        return carry

    lax.fori_loop(0, pieces, one, 0)
    rows_of_sums = jnp.concatenate(
        [sums[...]]
        + [inner_sum[:, j * width : (j + 1) * width] for j in range(slabs)]
        + [jnp.zeros((6, width), jnp.float32)],
        axis=0,
    ).astype(jnp.bfloat16)
    for i in range(8):
        cc, zz = i % 2, i // 2
        mine = slice(48 * i, 48 * i + 48)
        pg[cc, zz, 0, 0:48, :] = gwo[mine, :].astype(jnp.bfloat16)
        pg[cc, zz, 0, 48:96, :] = gwi[0, mine, :].astype(jnp.bfloat16)
        pg[cc, zz, 1, 0:48, :] = gwi[1, mine, :].astype(jnp.bfloat16)
        pg[cc, zz, 1, 48:96, :] = gwi[2, mine, :].astype(jnp.bfloat16)
        pg[cc, zz, 2, 0:48, :] = gwi[3, mine, :].astype(jnp.bfloat16)
        base = 192 * cc
        pg[cc, zz, 0, 96:112, :] = gwu[zz, base : base + 16, :].astype(jnp.bfloat16)
        pg[cc, zz, 1, 96:112, :] = gwu[zz, base + 16 : base + 32, :].astype(jnp.bfloat16)
        pg[cc, zz, 2, 48:112, :] = gwu[zz, base + 32 : base + 96, :].astype(jnp.bfloat16)
        pg[cc, zz, 3, 0:96, :] = gwu[zz, base + 96 : base + 192, :].astype(jnp.bfloat16)
        pg[cc, zz, 3, 96:112, :] = rows_of_sums
    pair = remote(pg.at[1 - c], pg_in, psend, precv, r, 2 * z + 1 - c)
    pair.start()

    def settle(q, carry):
        cols = pl.ds(pl.multiple_of(q * PIECE, PIECE), PIECE)
        for d in range(1, 8):
            b = lax.rem(g + d, 8)
            remote(
                gctx.at[c, z, :, cols], gctx_out.at[b, :, cols], gsend.at[q, 0], grecv.at[q, b], r, b
            ).wait_recv()
            return_piece(q, cols, d).wait_send()
            to = lax.rem(g + d, 8)
            remote(
                ctx.at[to, :, cols], ctx_in.at[c, z, :, cols], send.at[q, d - 1], recv.at[q, g], r, to
            ).wait_send()
        keep_piece(q, cols).wait()
        for copy in results(q):
            copy.wait()
        return carry

    pair.wait_recv()
    for i in range(4):
        pr[i] = (pg[c, i].astype(jnp.float32) + pg_in[i].astype(jnp.float32)).astype(jnp.bfloat16)
    lax.fori_loop(0, pieces, settle, 0)
    pair.wait_send()


def middle(ctx, tok, og, w, small):
    seqs, rows, width = tok.shape
    vm = pl.BlockSpec(memory_space=pltpu.VMEM)
    anywhere = pl.BlockSpec(memory_space=pltpu.HBM)
    dma = pltpu.SemaphoreType.DMA
    bf, f4 = jnp.bfloat16, jnp.float32
    pieces = rows // PIECE
    return pl.pallas_call(
        middle_kernel,
        name="middle",
        out_shape=(
            jax.ShapeDtypeStruct((seqs, rows, width), bf),
            jax.ShapeDtypeStruct((seqs, rows, width), f4),
            jax.ShapeDtypeStruct(ctx.shape, bf),
            jax.ShapeDtypeStruct((4, 4, 112, width), bf),
        ),
        in_specs=[anywhere] * 4 + [vm],
        out_specs=[anywhere, anywhere, anywhere, vm],
        scratch_shapes=[
            pltpu.VMEM((width, width), bf),
            pltpu.VMEM((4, width, width), bf),
            pltpu.VMEM((4, width, width), bf),
            pltpu.VMEM((width, width), f4),
            pltpu.VMEM((4, width, width), f4),
            pltpu.VMEM((4, width, width), f4),
            pltpu.VMEM((6, width), f4),
            pltpu.VMEM((1, 4 * width), f4),
            pltpu.VMEM((2, 4) + ctx.shape[1:], bf),
            pltpu.VMEM((2, 4) + ctx.shape[1:], bf),
            pltpu.VMEM((2, 4, 4, 112, width), bf),
            pltpu.VMEM((4, 4, 112, width), bf),
            pltpu.VMEM((seqs, rows, width), bf),
            pltpu.VMEM((seqs, rows, width), bf),
            pltpu.VMEM(w.shape, bf),
            pltpu.VMEM((seqs, rows, width), bf),
            pltpu.VMEM((seqs, rows, width), f4),
            dma((3,)), dma((2, pieces)), dma, dma((pieces, 7)), dma((pieces, 8)), dma((pieces, 7)), dma((pieces, 8)), dma((pieces,)), dma, dma,
        ],
        compiler_params=pltpu.CompilerParams(
            collective_id=2, has_side_effects=True, vmem_limit_bytes=BIG
        ),
    )(ctx, tok, og, w, small)


def attend_back_kernel(
    last, index, place, spans, x_hbm, q_hbm, tail, kv_hbm, kt_hbm, q1, gctx, ctx, *refs,
):
    heads = q1.shape[0]
    span = heads * HEAD
    if last:
        grads_in, out, gq, dt, do, acc, dq, qt, x, kv, kt, sems = refs
    else:
        out, grads_out, dt, do, acc, dq, qt, x, kv, kt, sems = refs
    length, width = x.shape
    mine = pl.ds(index * heads, heads)
    loads = [
        pltpu.make_async_copy(q_hbm.at[mine], qt.at[:, pl.ds(0, HEAD), :], sems.at[0]),
        pltpu.make_async_copy(tail.at[mine], qt.at[:, pl.ds(96, 16), :], sems.at[1]),
        pltpu.make_async_copy(kv_hbm.at[mine], kv, sems.at[3]),
        pltpu.make_async_copy(kt_hbm.at[mine], kt, sems.at[4]),
        pltpu.make_async_copy(x_hbm, x, sems.at[2]),
    ]
    for load in loads:
        load.start()
    blocks, _, rows = gctx.shape
    z = place[0]
    c = place[1]
    scale = HEAD ** -0.5

    def prepare(g, carry):
        r0 = pl.multiple_of(g * rows, rows)
        cols = pl.ds(r0, rows)
        for h in range(heads):
            part = slice(h * HEAD, (h + 1) * HEAD)
            grad = gctx[g, part, :]
            wide = grad.astype(jnp.float32)
            delta = -jnp.sum(wide * ctx[g, part, :].astype(jnp.float32), axis=0, keepdims=True)
            dt[h, 0:64, cols] = jnp.zeros((64, rows), jnp.bfloat16)
            dt[h, 64:96, cols] = grad
            qt[h, HEAD:96, cols] = jnp.zeros((96 - HEAD, rows), jnp.bfloat16)
            qt[h, 112:128, cols] = jnp.zeros((16, rows), jnp.bfloat16)
            tail = jnp.concatenate(
                [jnp.zeros((8, rows), jnp.float32), *halves(delta), jnp.zeros((21, rows), jnp.float32)],
                axis=0,
            )
            dt[h, 96:128, cols] = tail.astype(jnp.bfloat16)
            turned = jnp.concatenate(
                [wide, q1[h, :, cols].astype(jnp.float32), jnp.zeros((64, rows), jnp.float32)], axis=0
            ).T
            lane = iota((rows, LANES), 1)
            grad_rows = jnp.where(lane < HEAD, turned, 0.0).astype(jnp.bfloat16)
            query_rows = jnp.where(lane < HEAD, 0.0, turned).astype(jnp.bfloat16)
            for j in range(rows // QB):
                r1 = pl.multiple_of(2 * r0 + 2 * j * QB, QB)
                do[h, pl.ds(r1, QB), :] = grad_rows[j * QB : (j + 1) * QB]
                do[h, pl.ds(r1 + QB, QB), :] = query_rows[j * QB : (j + 1) * QB]
        return carry

    lax.fori_loop(0, blocks, prepare, 0)
    acc[...] = jnp.zeros_like(acc)
    per = rows // QB
    for load in loads[:4]:
        load.wait()

    def query_block(b, carry):
        q0 = pl.multiple_of(b * QB, QB)
        dq[...] = jnp.zeros_like(dq)

        def key_block(keys):
            s = [dot(kv[h, keys, :], qt[h, :, pl.ds(q0, QB)]) for h in range(heads)]
            d = [dot(kv[h, keys, :], dt[h, :, pl.ds(q0, QB)]) for h in range(heads)]
            p = [jnp.exp2(v * SCALE) for v in s]
            both = [
                jnp.concatenate([u.astype(jnp.bfloat16), (u * v).astype(jnp.bfloat16)], axis=1)
                for u, v in zip(p, d)
            ]
            for h in range(heads):
                acc[h, keys, :] += dot(both[h], do[h, pl.ds(2 * q0, 2 * QB), :])
            for h in range(heads):
                dq[h] += dot(kt[h, :, keys], both[h][:, QB:])

        in_groups(spans[0, b], spans[1, b], length // LANES, key_block)
        g = lax.div(b, per)
        off = pl.multiple_of(lax.rem(b, per) * QB, QB)
        for h in range(heads):
            out[g, h * HEAD : (h + 1) * HEAD, pl.ds(off, QB)] = (dq[h] * scale).astype(jnp.bfloat16)
        return carry

    lax.fori_loop(0, length // QB, query_block, 0)

    loads[4].wait()

    def finish_block(g, totals):
        r0 = pl.multiple_of(g * rows, rows)
        cols = pl.ds(r0, rows)
        for h in range(heads):
            both = acc[h, cols, :].T
            row = h * HEAD
            out[g, 2 * span + row : 2 * span + row + HEAD, :] = both[0:32].astype(jnp.bfloat16)
            out[g, span + row : span + row + HEAD, :] = (both[32:64] * scale).astype(jnp.bfloat16)
        piece = out[g]
        grad = dot(piece, x[cols, :])
        summed = jnp.sum(piece.astype(jnp.float32), axis=1, keepdims=True)
        return totals[0] + grad, totals[1] + summed

    grads, summed = lax.fori_loop(
        0,
        blocks,
        finish_block,
        (jnp.zeros((3 * span, width), jnp.float32), jnp.zeros((3 * span, 1), jnp.float32)),
    )
    if not last:
        grads_out[:, 0:width] = grads
        grads_out[:, width:] = jnp.broadcast_to(summed, (3 * span, LANES))
        return
    gq[...] = jnp.zeros_like(gq)
    before = grads_in.shape[0] // 3

    def joined(i, old, new):
        return [old[i * before : (i + 1) * before], new[i * span : (i + 1) * span]]

    old = grads_in[:, 0:width]
    whole = jnp.concatenate([v for i in range(3) for v in joined(i, old, grads)], axis=0).T
    total = 3 * (before + span)
    for g in range(8):
        gq[g % 2, g // 2, :, 0:total] = whole[48 * g : 48 * g + 48, :].astype(jnp.bfloat16)
    old = grads_in[:, width : width + 1]
    of_q = jnp.concatenate(joined(0, old, summed), axis=0)
    of_v = jnp.concatenate(joined(2, old, summed), axis=0)
    for cc in range(2):
        mine = jnp.concatenate(
            [
                of_q[48 * cc : 48 * cc + 48, :],
                of_v[48 * cc : 48 * cc + 48, :],
                jnp.zeros((48, 94), jnp.float32),
            ],
            axis=1,
        )
        gq[cc, z, :, total:] = mine.astype(jnp.bfloat16)


def attend_back(heads, index, place, spans, x, tail, kv, kt, q1, gctx, ctx, grads=None):
    blocks, rows, width = x.shape
    length = blocks * rows
    last = grads is not None
    rest = (grads,) if last else ()
    sm = pl.BlockSpec(memory_space=pltpu.SMEM)
    bf, f4 = jnp.bfloat16, jnp.float32
    once = pl.Buffered(1)
    span = heads * HEAD

    def some_heads(array):
        return pl.BlockSpec((heads,) + array.shape[1:], lambda i: (index, 0, 0), pipeline_mode=once)

    def head_rows(array):
        return pl.BlockSpec((blocks, span, rows), lambda i: (0, index, 0), pipeline_mode=once)

    flat = x.reshape(length, width)
    shapes = (
        jax.ShapeDtypeStruct((blocks, 3 * span, rows), bf),
        jax.ShapeDtypeStruct((2, 4, 48, width), bf)
        if last
        else jax.ShapeDtypeStruct((3 * span, width + LANES), f4),
    )
    return pl.pallas_call(
        functools.partial(attend_back_kernel, last, index),
        name="attend_back",
        grid=(1,),
        out_shape=shapes,
        in_specs=[sm, sm] + [pl.BlockSpec(memory_space=pltpu.HBM)] * 5
        + [some_heads(q1)]
        + [head_rows(v) for v in (gctx, ctx)]
        + [whole_spec(v) for v in rest],
        out_specs=[whole_spec(v) for v in shapes],
        scratch_shapes=[
            pltpu.VMEM((heads, LANES, length), bf),
            pltpu.VMEM((heads, 2 * length, LANES), bf),
            pltpu.VMEM((heads, length, LANES), f4),
            pltpu.VMEM((heads, HEAD, QB), f4),
            pltpu.VMEM((heads, LANES, length), bf),
            pltpu.VMEM((length, width), bf),
            pltpu.VMEM((heads,) + kv.shape[1:], bf),
            pltpu.VMEM((heads,) + kt.shape[1:], bf),
            pltpu.SemaphoreType.DMA((5,)),
        ],
        compiler_params=pltpu.CompilerParams(vmem_limit_bytes=BIG),
        cost_estimate=pl.CostEstimate(
            flops=heads * 20 * 10 ** 9, bytes_accessed=heads * 8 * 10 ** 6, transcendentals=heads * 6 * 10 ** 6
        ),
    )(place, spans, flat, q1, tail, kv, kt, q1, gctx, ctx, *rest)


def reduce_kernel(
    src, gq, pz, dst, p_out, q_out,
    gq_in, gq_sum, qa_in, qa_sum, qb_in, pz_in, p_line, pa_in, p_own, gq_own,
    lsem, send, recv, gsend, grecv, qasend, qarecv, qbsend, qbrecv, qcsend, qcrecv,
    pasend, parecv, pcsend, pcrecv,
):
    r, g, z, c = where_am_i()
    greet(r, g, 4, 8)
    waits = []
    pair = remote(gq.at[1 - c], gq_in, gsend, grecv, r, 2 * z + 1 - c)
    pair.start()
    load_g = pltpu.make_async_copy(gq.at[c], gq_own, lsem.at[1])
    load_g.start()
    load_p = pltpu.make_async_copy(pz, pz_in, lsem.at[2])
    load_p.start()
    own = pltpu.make_async_copy(src.at[g], dst.at[g], lsem.at[0])
    own.start()

    def send_to(d):
        to = lax.rem(g + d, 8)
        copy = remote(src.at[to], dst.at[g], send.at[d - 1], recv.at[g], r, to)
        copy.start()
        waits.append(copy)

    def f32(value):
        return value.astype(jnp.float32)

    load_g.wait()
    pair.wait_recv()
    gq_sum[...] = (f32(gq_own[...]) + f32(gq_in[...])).astype(jnp.bfloat16)
    for d in range(1, 4):
        rr = lax.rem(r + d, 4)
        copy = remote(gq_sum.at[rr], qa_in.at[r], qasend.at[d - 1], qarecv.at[r], rr, g)
        copy.start()
        waits.append(copy)
    load_p.wait()
    total = f32(pz_in[0])
    for i in range(1, 4):
        total = total + f32(pz_in[i])
    p_line[...] = total.astype(jnp.bfloat16)
    for d in range(1, 4):
        rr = lax.rem(r + d, 4)
        copy = remote(p_line.at[rr], pa_in.at[r], pasend.at[d - 1], parecv.at[r], rr, g)
        copy.start()
        waits.append(copy)
    for d in range(1, 4):
        b = lax.rem(r + d, 4)
        remote(gq_sum.at[r], qa_in.at[b], qasend.at[0], qarecv.at[b], b, g).wait_recv()
    total = f32(gq_sum[r])
    for d in range(1, 4):
        total = total + f32(qa_in[lax.rem(r + d, 4)])
    qa_sum[...] = total.astype(jnp.bfloat16)

    @pl.when(z != r)
    def _():
        remote(qa_sum, qb_in.at[z], qbsend, qbrecv.at[z], r, 2 * r + c).start()

    for d in (4, 3, 5, 2, 6, 1, 7):
        send_to(d)
    for d in range(1, 4):
        b = lax.rem(r + d, 4)
        remote(p_line.at[r], pa_in.at[b], pasend.at[0], parecv.at[b], b, g).wait_recv()
    total = f32(p_line[r])
    for d in range(1, 4):
        total = total + f32(pa_in[lax.rem(r + d, 4)])
    p_own[...] = total.astype(jnp.bfloat16)
    keep_p = pltpu.make_async_copy(p_own, p_out.at[r], lsem.at[3])
    keep_p.start()
    for d in range(1, 4):
        rr = lax.rem(r + d, 4)
        copy = remote(p_own, p_out.at[r], pcsend.at[d - 1], pcrecv.at[r], rr, g)
        copy.start()
        waits.append(copy)

    @pl.when(z == r)
    def _():
        for d in range(1, 4):
            b = lax.rem(z + d, 4)
            remote(qa_sum, qb_in.at[b], qbsend, qbrecv.at[b], r, g).wait_recv()
        qb_in[z] = qa_sum[...]
        keep = pltpu.make_async_copy(qb_in, q_out, lsem.at[4])
        keep.start()
        for d in range(1, 4):
            remote(qb_in, q_out, qcsend.at[d - 1], qcrecv, lax.rem(r + d, 4), g).start()
        keep.wait()
        for d in range(1, 4):
            remote(qb_in, q_out, qcsend.at[d - 1], qcrecv, lax.rem(r + d, 4), g).wait_send()

    @pl.when(z != r)
    def _():
        remote(qb_in, q_out, qcsend.at[0], qcrecv, r, g).wait_recv()
        remote(qa_sum, qb_in.at[z], qbsend, qbrecv.at[z], r, 2 * r + c).wait_send()

    for d in range(1, 4):
        b = lax.rem(r + d, 4)
        remote(p_own, p_out.at[b], pcsend.at[0], pcrecv.at[b], b, g).wait_recv()
    for d in range(1, 8):
        b = lax.rem(g + d, 8)
        remote(src.at[g], dst.at[b], send.at[0], recv.at[b], r, b).wait_recv()
    pair.wait_send()
    for copy in waits:
        copy.wait_send()
    keep_p.wait()
    own.wait()


def reduce_all(src, gq, pz):
    dma = pltpu.SemaphoreType.DMA
    anywhere = pl.BlockSpec(memory_space=pltpu.HBM)
    bf = jnp.bfloat16
    width = gq.shape[-1]
    part = (4, 48, width)
    return pl.pallas_call(
        reduce_kernel,
        name="reduce",
        out_shape=(
            jax.ShapeDtypeStruct(src.shape, bf),
            jax.ShapeDtypeStruct((4, 112, width), bf),
            jax.ShapeDtypeStruct(part, bf),
        ),
        in_specs=[anywhere] * 3,
        out_specs=[anywhere] * 3,
        scratch_shapes=[
            pltpu.VMEM(part, bf),
            pltpu.VMEM(part, bf),
            pltpu.VMEM(part, bf),
            pltpu.VMEM((48, width), bf),
            pltpu.VMEM(part, bf),
            pltpu.VMEM((4, 4, 112, width), bf),
            pltpu.VMEM((4, 112, width), bf),
            pltpu.VMEM((4, 112, width), bf),
            pltpu.VMEM((112, width), bf),
            pltpu.VMEM(part, bf),
            dma((5,)), dma((7,)), dma((8,)), dma, dma, dma((3,)), dma((4,)), dma, dma((4,)), dma((3,)), dma,
            dma((3,)), dma((4,)), dma((3,)), dma((4,)),
        ],
        compiler_params=pltpu.CompilerParams(
            collective_id=4, has_side_effects=True, vmem_limit_bytes=BIG
        ),
    )(src, gq, pz)


def finish_kernel(
    place, layer_in, in_0, in_1, grad_one, w, p_in, q_in,
    layer_out, out, g_q, g_k, g_v, g_o, g_in, g_up, rows_out, inner_out, wq, held, sems,
):
    width = w.shape[-1]
    span = 96
    step = pl.program_id(0)
    z = place[0]
    c = place[1]
    load = pltpu.make_async_copy(layer_in, held, sems.at[0])
    store = pltpu.make_async_copy(held, layer_out, sems.at[1])

    @pl.when(step == 0)
    def _():
        load.start()
        for i in range(3):
            for g in range(8):
                wq[i, 48 * g : 48 * g + 48, :] = w[0, g % 2, g // 2, 48 * i : 48 * i + 48, :]

    total = grad_one[0]
    for i in range(3):
        turned = jnp.concatenate(
            [
                ref[zz, 0, i * count : (i + 1) * count, :]
                for zz in range(4)
                for ref, count in ((in_0, in_0.shape[2] // 3), (in_1, in_1.shape[2] // 3))
            ],
            axis=0,
        )
        back = turned.astype(jnp.float32).T.astype(jnp.bfloat16)
        total = total + lax.dot_general(
            back, wq[i], (((1,), (1,)), ((), ())), preferred_element_type=jnp.float32
        )
    out[0] = total.astype(jnp.bfloat16)

    @pl.when(step == 0)
    def _():
        load.wait()
        store.start()
        wide = [q_in[zz].astype(jnp.float32) for zz in range(4)]
        for i, ref in enumerate((g_q, g_k, g_v)):
            ref[...] = jnp.concatenate([v[:, i * span : (i + 1) * span] for v in wide], axis=1)
        sums = p_in[3, 96:112, :]
        pick = jnp.where(
            iota((width, 48), 0) == 48 * (2 * z + c) + iota((width, 48), 1), 1.0, 0.0
        ).astype(jnp.bfloat16)
        rows_out[8:24, :] = dot(sums, pick)
        both = q_in[z].astype(jnp.float32)[:, 3 * span :].T
        rows_out[0:8, :] = both[0:8, :]
        pick = jnp.where(
            iota((width, 192), 0) == 192 * c + iota((width, 192), 1), 1.0, 0.0
        ).astype(jnp.bfloat16)
        inner = dot(sums, pick)
        inner_out[...] = jnp.sum(
            jnp.where(iota((16, 192), 0) == 6 + z, inner, 0.0), axis=0, keepdims=True
        )
        g_o[...] = p_in[0, 0:48, :].astype(jnp.float32)
        g_in[:, 0:384] = p_in[0, 48:96, :].astype(jnp.float32)
        g_in[:, 384:768] = p_in[1, 0:48, :].astype(jnp.float32)
        g_in[:, 768:1152] = p_in[1, 48:96, :].astype(jnp.float32)
        g_in[:, 1152:1536] = p_in[2, 0:48, :].astype(jnp.float32)
        g_up[0:16, :] = p_in[0, 96:112, :].astype(jnp.float32)
        g_up[16:32, :] = p_in[1, 96:112, :].astype(jnp.float32)
        g_up[32:96, :] = p_in[2, 48:112, :].astype(jnp.float32)
        g_up[96:192, :] = p_in[3, 0:96, :].astype(jnp.float32)

    @pl.when(step == 1)
    def _():
        store.wait()


def finish(place, layer_in, in_0, in_1, grad_one, w, p_in, q_in):
    seqs, rows, width = grad_one.shape
    sm = pl.BlockSpec(memory_space=pltpu.SMEM)
    hbm = pl.BlockSpec(memory_space=pltpu.HBM)
    bf, f4 = jnp.bfloat16, jnp.float32
    shapes = ((48, width),) * 4 + ((48, 4 * width), (192, width), (24, 48), (1, 192))
    in_0, in_1 = (v.reshape((4, 2) + v.shape[1:]) for v in (in_0, in_1))

    def of_sequence(v):
        return pl.BlockSpec((4, 1) + v.shape[2:], lambda i: (0, i, 0, 0))

    one = pl.BlockSpec((1, rows, width), lambda i: (i, 0, 0))
    return pl.pallas_call(
        finish_kernel,
        name="finish",
        grid=(seqs,),
        out_shape=(jax.ShapeDtypeStruct((seqs, rows, width), bf),) * 2
        + tuple(jax.ShapeDtypeStruct(shape, f4) for shape in shapes),
        in_specs=[
            sm, hbm, of_sequence(in_0), of_sequence(in_1), one,
            quarter_spec(w, 0), whole_spec(p_in), whole_spec(q_in),
        ],
        out_specs=[hbm, one]
        + [pl.BlockSpec(shape, functools.partial(zeros_for, len(shape))) for shape in shapes],
        scratch_shapes=[
            pltpu.VMEM((3, width, width), bf),
            pltpu.VMEM((seqs, rows, width), bf),
            pltpu.SemaphoreType.DMA((2,)),
        ],
        compiler_params=pltpu.CompilerParams(vmem_limit_bytes=BIG - 1600 * 1024),
    )(place, layer_in, in_0, in_1, grad_one, w, p_in, q_in)


def line_of_chips(
    tokens, segment_ids, out_grad, query_weight, key_weight, value_weight, output_weight,
    inner_weight, outer_weight, query_bias, value_bias, output_bias, inner_bias, outer_bias,
    first_gain, first_shift, second_gain, second_shift,
):
    bf = jnp.bfloat16
    width = tokens.shape[2]
    g = lax.axis_index("grp")
    z, c = lax.div(g, 2), lax.rem(g, 2)
    place = jnp.stack([z, c]).astype(jnp.int32)
    weights = (query_weight, key_weight, value_weight, output_weight, inner_weight, outer_weight)
    vectors = jnp.concatenate(
        [
            v[None]
            for v in (
                query_bias, value_bias, output_bias, outer_bias,
                first_gain, first_shift, second_gain, second_shift,
            )
        ],
        axis=0,
    )
    x, w, small, kv, kt, vt, q1, norms = gather(
        tokens, weights, vectors, inner_bias[None], segment_ids
    )
    ctx, tail, spans = attend(place, kv, q1, vt, small, norms)
    layer_out, grad_one, gctx_in, pr = middle(ctx, tokens, out_grad, w, small)
    same_core = [[i + j for i in range(0, 8, 2)] for j in range(2)]
    pz = lax.all_to_all(pr, "grp", 0, 0, axis_index_groups=same_core, tiled=True)
    back = functools.partial(
        attend_back, place=place, spans=spans, x=x, tail=tail, kv=kv, kt=kt, q1=q1,
        gctx=gctx_in, ctx=ctx,
    )
    parts_0, grads_0 = back(2, 0)
    in_0 = lax.all_to_all(parts_0, "grp", 0, 0, tiled=True)
    parts_1, gq = back(1, 2, grads=grads_0)
    in_1, p_in, q_in = reduce_all(parts_1, gq, pz)
    layer_out, input_grad, g_q, g_k, g_v, g_o, g_in, g_up, rows, inner_row = finish(
        place, layer_out, in_0, in_1, grad_one, w, p_in, q_in
    )
    return (
        layer_out, input_grad, g_q, g_k, g_v, g_o, g_in, g_up,
        rows[0], rows[1], rows[8], inner_row[0], rows[9], rows[10], rows[11], rows[12], rows[13],
    )


def solution(mesh):
    in_specs = (
        P("rep", "grp", None),
        P("rep", "grp"),
        P("rep", "grp", None),
        P("grp", None),
        P("grp", None),
        P("grp", None),
        P("grp", None),
        P("grp", None),
        P("grp", None),
        P("grp"),
        P("grp"),
        P("grp"),
        P("grp"),
        P("grp"),
        P("grp"),
        P("grp"),
        P("grp"),
        P("grp"),
    )
    out_specs = (
        P("rep", "grp", None),
        P("rep", "grp", None),
        P("grp", None),
        P("grp", None),
        P("grp", None),
        P("grp", None),
        P("grp", None),
        P("grp", None),
        P("grp"),
        P("grp"),
        P("grp"),
        P("grp"),
        P("grp"),
        P("grp"),
        P("grp"),
        P("grp"),
        P("grp"),
    )
    whole_line = mesh.shape["grp"] == 8 and mesh.shape["rep"] == 4
    return jax.shard_map(
        line_of_chips if whole_line else on_device, mesh=mesh, in_specs=in_specs, out_specs=out_specs, check_vma=False
    )
```

```python
import functools
from functools import reduce

import jax
import jax.numpy as jnp
from jax import lax
from jax.experimental import pallas as pl
from jax.experimental.pallas import tpu as pltpu
from jax.sharding import PartitionSpec as P

H = 12
MICRO = 2
SEQ_MB = 1


norm_epsilon = 1e-05
masked_score = -1000000000.0


def layer_norm(inputs, norm_gain, norm_shift):
    center = inputs - jnp.mean(inputs, axis=-1, keepdims=True)
    spread = jnp.mean(center * center, axis=-1, keepdims=True)
    return center * lax.rsqrt(spread + norm_epsilon) * norm_gain + norm_shift


def exact_gelu(inputs):
    return jax.nn.gelu(inputs, approximate=False)


def times_transpose(left, right):
    return lax.dot_general(
        left, right, (((1,), (1,)), ((), ())), preferred_element_type=jnp.float32
    )


def transpose_times(left, right):
    return lax.dot_general(
        left, right, (((0,), (0,)), ((), ())), preferred_element_type=jnp.float32
    )


def column_total(inputs):
    return jnp.sum(inputs.astype(jnp.float32), axis=0)


def masked_scores(query_group, key_group, same_doc, score_scale):
    scores = (
        jnp.einsum("bqhd,bkhd->bhqk", query_group, key_group, preferred_element_type=jnp.float32)
        * score_scale
    )
    return jnp.where(same_doc[:, None], scores, masked_score)


def group_forward(query_group, key_group, value_group, same_doc, score_scale):
    scores = masked_scores(query_group, key_group, same_doc, score_scale)
    highest = jnp.max(scores, axis=-1, keepdims=True)
    log_total = highest + jnp.log(jnp.sum(jnp.exp(scores - highest), axis=-1, keepdims=True))
    weights_low = jnp.exp(scores - log_total).astype(jnp.bfloat16)
    context = jnp.einsum(
        "bhqk,bkhd->bqhd", weights_low, value_group, preferred_element_type=jnp.float32
    )
    return (context.astype(jnp.bfloat16), log_total)


def group_backward(
    query_group, key_group, value_group, same_doc, log_total, grad_context, score_scale
):
    attn_weights = jnp.exp(masked_scores(query_group, key_group, same_doc, score_scale) - log_total)
    weights_low = attn_weights.astype(jnp.bfloat16)
    grad_weights = jnp.einsum(
        "bqhd,bkhd->bhqk", grad_context, value_group, preferred_element_type=jnp.float32
    )
    centre = jnp.sum(attn_weights * grad_weights, axis=-1, keepdims=True)
    grad_scores = (attn_weights * (grad_weights - centre)).astype(jnp.bfloat16)
    grad_query = jnp.einsum(
        "bhqk,bkhd->bqhd", grad_scores, key_group, preferred_element_type=jnp.float32
    )
    grad_query = (grad_query * score_scale).astype(jnp.bfloat16)
    grad_key = (
        jnp.einsum("bhqk,bqhd->bkhd", grad_scores, query_group, preferred_element_type=jnp.float32)
        * score_scale
    )
    grad_value = jnp.einsum(
        "bhqk,bqhd->bkhd", weights_low, grad_context, preferred_element_type=jnp.float32
    )
    return (grad_query, grad_key, grad_value)


def merge_groups(stacked, row_total, model_width):
    return jnp.moveaxis(stacked, 0, 2).reshape(row_total, model_width)


def gradient_terms(
    token_rows,
    context_rows,
    hidden_rows,
    active_rows,
    grad_queries,
    grad_keys,
    grad_values,
    grad_attention,
    grad_inner,
    grad_feed,
    norm_grads,
):
    return (
        transpose_times(token_rows, grad_queries),
        transpose_times(token_rows, grad_keys),
        transpose_times(token_rows, grad_values),
        transpose_times(context_rows, grad_attention),
        transpose_times(hidden_rows, grad_inner),
        transpose_times(active_rows, grad_feed),
        column_total(grad_queries),
        column_total(grad_values),
        column_total(grad_attention),
        column_total(grad_inner),
        column_total(grad_feed),
        norm_grads[0],
        norm_grads[1],
        norm_grads[2],
        norm_grads[3],
    )


def on_device(
    tokens,
    segment_ids,
    out_grad,
    query_weight,
    key_weight,
    value_weight,
    output_weight,
    inner_weight,
    outer_weight,
    query_bias,
    value_bias,
    output_bias,
    inner_bias,
    outer_bias,
    first_gain,
    first_shift,
    second_gain,
    second_shift,
):
    row_count = tokens.shape[1]
    model_width = tokens.shape[2]
    head_count = H
    head_size = model_width // head_count
    per_group = max(1, min(head_count, 128 // head_size))
    group_width = per_group * head_size
    group_count = head_count // per_group
    score_scale = head_size ** (-0.5)
    seq_count = SEQ_MB
    flat_rows = seq_count * row_count
    all_segments = lax.all_gather(segment_ids, "grp", axis=1, tiled=True)
    outputs = []
    input_grads = []
    shares_list = []
    for batch_index in range(MICRO):
        offset = batch_index * seq_count
        local_tokens = tokens[offset : offset + seq_count]
        flat_tokens = local_tokens.reshape(flat_rows, model_width)
        gathered = (
            lax.all_gather(query_weight, "grp", axis=0, tiled=True),
            lax.all_gather(key_weight, "grp", axis=0, tiled=True),
            lax.all_gather(value_weight, "grp", axis=0, tiled=True),
            lax.all_gather(output_weight, "grp", axis=0, tiled=True),
            lax.all_gather(inner_weight, "grp", axis=0, tiled=True),
            lax.all_gather(outer_weight, "grp", axis=0, tiled=True),
            lax.all_gather(query_bias, "grp", axis=0, tiled=True),
            lax.all_gather(value_bias, "grp", axis=0, tiled=True),
            lax.all_gather(output_bias, "grp", axis=0, tiled=True),
            lax.all_gather(inner_bias, "grp", axis=0, tiled=True),
            lax.all_gather(outer_bias, "grp", axis=0, tiled=True),
            lax.all_gather(first_gain, "grp", axis=0, tiled=True),
            lax.all_gather(first_shift, "grp", axis=0, tiled=True),
            lax.all_gather(second_gain, "grp", axis=0, tiled=True),
            lax.all_gather(second_shift, "grp", axis=0, tiled=True),
        )
        full_query, full_key, full_value, full_output, full_inner, full_outer = gathered[:6]
        (
            bias_query,
            bias_value,
            bias_output,
            bias_inner,
            bias_outer,
            gain_first,
            shift_first,
            gain_second,
            shift_second,
        ) = [vector.astype(jnp.float32) for vector in gathered[6:]]
        queries = (
            jnp.dot(flat_tokens, full_query, preferred_element_type=jnp.float32) + bias_query
        ).astype(jnp.bfloat16)
        key_rows = jnp.dot(flat_tokens, full_key, preferred_element_type=jnp.float32).astype(
            jnp.bfloat16
        )
        value_rows = (
            jnp.dot(flat_tokens, full_value, preferred_element_type=jnp.float32) + bias_value
        ).astype(jnp.bfloat16)
        key_split = key_rows.reshape(seq_count, row_count, model_width)
        value_split = value_rows.reshape(seq_count, row_count, model_width)
        key_all, value_all = (
            lax.all_gather(key_split, "grp", axis=1, tiled=True),
            lax.all_gather(value_split, "grp", axis=1, tiled=True),
        )
        length = key_all.shape[1]
        local_segments = segment_ids[offset : offset + seq_count]
        far_segments = all_segments[offset : offset + seq_count]
        same_doc = local_segments[:, :, None] == far_segments[:, None, :]
        query_split = queries.reshape(seq_count, row_count, model_width)

        def slice_group(array, group_index):
            piece = lax.dynamic_slice_in_dim(array, group_index * group_width, group_width, 2)
            return piece.reshape(array.shape[0], array.shape[1], per_group, head_size)

        def forward_group(group_index):
            context, log_total = group_forward(
                slice_group(query_split, group_index),
                slice_group(key_all, group_index),
                slice_group(value_all, group_index),
                same_doc,
                score_scale,
            )
            return (context.reshape(seq_count, row_count, group_width), log_total)

        context_groups, log_totals = lax.map(forward_group, jnp.arange(group_count))
        context_rows = merge_groups(context_groups, flat_rows, model_width)
        attention = (
            jnp.dot(context_rows, full_output, preferred_element_type=jnp.float32) + bias_output
        )
        residual_one = flat_tokens.astype(jnp.float32) + attention
        hidden_one, norm_one_pullback = jax.vjp(layer_norm, residual_one, gain_first, shift_first)
        hidden_low = hidden_one.astype(jnp.bfloat16)
        inner_pre = jnp.dot(hidden_low, full_inner, preferred_element_type=jnp.float32) + bias_inner
        activation, gelu_pullback = jax.vjp(exact_gelu, inner_pre)
        active_low = activation.astype(jnp.bfloat16)
        feed = jnp.dot(active_low, full_outer, preferred_element_type=jnp.float32) + bias_outer
        output_rows, norm_two_pullback = jax.vjp(
            layer_norm, hidden_one + feed, gain_second, shift_second
        )
        outputs.append(output_rows.astype(jnp.bfloat16).reshape(seq_count, row_count, model_width))
        cotangent = (
            out_grad[offset : offset + seq_count]
            .reshape(flat_rows, model_width)
            .astype(jnp.float32)
        )
        grad_two, grad_gain_two, grad_shift_two = norm_two_pullback(cotangent)
        grad_feed = grad_two.astype(jnp.bfloat16)
        grad_active = times_transpose(grad_feed, full_outer)
        grad_inner = gelu_pullback(grad_active)[0].astype(jnp.bfloat16)
        grad_hidden = grad_two + times_transpose(grad_inner, full_inner)
        grad_one, grad_gain_one, grad_shift_one = norm_one_pullback(grad_hidden)
        grad_attention = grad_one.astype(jnp.bfloat16)
        grad_context = times_transpose(grad_attention, full_output).astype(jnp.bfloat16)
        grad_context = grad_context.reshape(seq_count, row_count, model_width)

        def backward_group(pieces):
            group_index, log_total = pieces
            grad_query, grad_key, grad_value = group_backward(
                slice_group(query_split, group_index),
                slice_group(key_all, group_index),
                slice_group(value_all, group_index),
                same_doc,
                log_total,
                slice_group(grad_context, group_index),
                score_scale,
            )
            return (
                grad_query.reshape(seq_count, row_count, group_width),
                grad_key.reshape(seq_count, length, group_width),
                grad_value.reshape(seq_count, length, group_width),
            )

        query_groups, key_groups, value_groups = lax.map(
            backward_group, (jnp.arange(group_count), log_totals)
        )
        key_owned, value_owned = (
            lax.psum_scatter(key_groups, "grp", scatter_dimension=2, tiled=True),
            lax.psum_scatter(value_groups, "grp", scatter_dimension=2, tiled=True),
        )
        grad_keys = merge_groups(key_owned, flat_rows, model_width).astype(jnp.bfloat16)
        grad_values = merge_groups(value_owned, flat_rows, model_width).astype(jnp.bfloat16)
        grad_queries = merge_groups(query_groups, flat_rows, model_width)
        grad_tokens = (
            grad_one
            + times_transpose(grad_queries, full_query)
            + times_transpose(grad_keys, full_key)
            + times_transpose(grad_values, full_value)
        )
        input_grads.append(
            grad_tokens.astype(jnp.bfloat16).reshape(seq_count, row_count, model_width)
        )
        norm_grads = (grad_gain_one, grad_shift_one, grad_gain_two, grad_shift_two)
        terms = gradient_terms(
            flat_tokens,
            context_rows,
            hidden_low,
            active_low,
            grad_queries,
            grad_keys,
            grad_values,
            grad_attention,
            grad_inner,
            grad_feed,
            norm_grads,
        )
        shares = (
            lax.psum_scatter(terms[0], "grp", scatter_dimension=0, tiled=True),
            lax.psum_scatter(terms[1], "grp", scatter_dimension=0, tiled=True),
            lax.psum_scatter(terms[2], "grp", scatter_dimension=0, tiled=True),
            lax.psum_scatter(terms[3], "grp", scatter_dimension=0, tiled=True),
            lax.psum_scatter(terms[4], "grp", scatter_dimension=0, tiled=True),
            lax.psum_scatter(terms[5], "grp", scatter_dimension=0, tiled=True),
            lax.psum_scatter(terms[6], "grp", scatter_dimension=0, tiled=True),
            lax.psum_scatter(terms[7], "grp", scatter_dimension=0, tiled=True),
            lax.psum_scatter(terms[8], "grp", scatter_dimension=0, tiled=True),
            lax.psum_scatter(terms[9], "grp", scatter_dimension=0, tiled=True),
            lax.psum_scatter(terms[10], "grp", scatter_dimension=0, tiled=True),
            lax.psum_scatter(terms[11], "grp", scatter_dimension=0, tiled=True),
            lax.psum_scatter(terms[12], "grp", scatter_dimension=0, tiled=True),
            lax.psum_scatter(terms[13], "grp", scatter_dimension=0, tiled=True),
            lax.psum_scatter(terms[14], "grp", scatter_dimension=0, tiled=True),
        )
        shares_list.append(shares)
    owned = reduce(
        lambda left_part, right_part: jax.tree.map(jnp.add, left_part, right_part), shares_list
    )
    summed = (
        lax.psum(owned[0].astype(jnp.bfloat16), "rep").astype(jnp.float32),
        lax.psum(owned[1].astype(jnp.bfloat16), "rep").astype(jnp.float32),
        lax.psum(owned[2].astype(jnp.bfloat16), "rep").astype(jnp.float32),
        lax.psum(owned[3].astype(jnp.bfloat16), "rep").astype(jnp.float32),
        lax.psum(owned[4].astype(jnp.bfloat16), "rep").astype(jnp.float32),
        lax.psum(owned[5].astype(jnp.bfloat16), "rep").astype(jnp.float32),
        lax.psum(owned[6].astype(jnp.bfloat16), "rep").astype(jnp.float32),
        lax.psum(owned[7].astype(jnp.bfloat16), "rep").astype(jnp.float32),
        lax.psum(owned[8].astype(jnp.bfloat16), "rep").astype(jnp.float32),
        lax.psum(owned[9].astype(jnp.bfloat16), "rep").astype(jnp.float32),
        lax.psum(owned[10].astype(jnp.bfloat16), "rep").astype(jnp.float32),
        lax.psum(owned[11].astype(jnp.bfloat16), "rep").astype(jnp.float32),
        lax.psum(owned[12].astype(jnp.bfloat16), "rep").astype(jnp.float32),
        lax.psum(owned[13].astype(jnp.bfloat16), "rep").astype(jnp.float32),
        lax.psum(owned[14].astype(jnp.bfloat16), "rep").astype(jnp.float32),
    )
    return (
        jnp.concatenate(outputs, axis=0),
        jnp.concatenate(input_grads, axis=0),
        summed[0],
        summed[1],
        summed[2],
        summed[3],
        summed[4],
        summed[5],
        summed[6],
        summed[7],
        summed[8],
        summed[9],
        summed[10],
        summed[11],
        summed[12],
        summed[13],
        summed[14],
    )


HEAD = 32
LANES = 128
QB = 256
AWAY = 2.0 ** 100
LIMIT = 100.0
LONG = 17
MESH = pl.DeviceIdType.MESH
BIG = 62 * 1024 * 1024
SCALE = HEAD ** -0.5 * 1.4426950408889634


def halves(value):
    first = value.astype(jnp.bfloat16).astype(jnp.float32)
    rest = value - first
    second = rest.astype(jnp.bfloat16).astype(jnp.float32)
    third = (rest - second).astype(jnp.bfloat16).astype(jnp.float32)
    return first, second, third


def dot(left, right):
    return jnp.dot(left, right, preferred_element_type=jnp.float32)


def zeros_for(rank, *grid):
    return (0,) * rank


def whole_spec(array):
    return pl.BlockSpec(array.shape, functools.partial(zeros_for, array.ndim), pipeline_mode=pl.Buffered(1))


def quarter_spec(w, i):
    return pl.BlockSpec((1,) + w.shape[1:], lambda *grid: (i, 0, 0, 0, 0), pipeline_mode=pl.Buffered(1))


def iota(shape, dim):
    return lax.broadcasted_iota(jnp.int32, shape, dim)


def where_am_i():
    r = lax.axis_index("rep")
    g = lax.axis_index("grp")
    return r, g, lax.div(g, 2), lax.rem(g, 2)


def remote(src, dst, send, recv, r, g):
    return pltpu.make_async_remote_copy(
        src_ref=src, dst_ref=dst, send_sem=send, recv_sem=recv, device_id=(r, g), device_id_type=MESH
    )


def greet(r, g, reps, group):
    barrier = pltpu.get_barrier_semaphore()
    for d in range(1, group):
        pl.semaphore_signal(barrier, inc=1, device_id=(r, lax.rem(g + d, group)), device_id_type=MESH)
    for d in range(1, reps):
        pl.semaphore_signal(barrier, inc=1, device_id=(lax.rem(r + d, reps), g), device_id_type=MESH)
    pl.semaphore_wait(barrier, group + reps - 2)


def vectors_of(small):
    return jnp.concatenate([small[g, 0:8, 0:48].astype(jnp.float32) for g in range(8)], axis=1)


def chip_at(z, i):
    order = ((0, 1, 2, 3), (1, 0, 2, 3), (2, 1, 3, 0), (3, 2, 1, 0))
    chip = jnp.int32(0)
    for a, row in enumerate(order):
        for k, value in enumerate(row):
            chip = jnp.where((z == a) & (i == k), value, chip)
    return chip


def gather_kernel(
    tok, wq, wk, wv, wo, wi, wu, vectors, inner, seg,
    x_out, w_out, s_out, kv_out, kt_out, vt_out, q1_out, norms,
    small, x, kv, kt, vt, q1, w0, smalls_in, wrow, wtr, mine,
    lsem, xsem, psems, tsend, trecv, psend, wsend1, wrecv1, wsend2, wrecv2, wsend3, wrecv3, ssend, srecv,
):
    r, g, z, c = where_am_i()
    reps, chips = 4, 4
    p = 2 * z + 1 - c
    heads = kv.shape[0]
    _, rows, width = x.shape
    small[0:8, :] = jnp.concatenate(
        [vectors[...].astype(jnp.float32), jnp.zeros((8, rows - 48), jnp.float32)], axis=1
    ).astype(jnp.bfloat16)
    small[8:16, :] = jnp.concatenate(
        [
            jnp.concatenate([inner[...].astype(jnp.float32), jnp.zeros((1, rows - 192), jnp.float32)], axis=1),
            seg[...].astype(jnp.float32),
            jnp.zeros((5, rows), jnp.float32),
        ],
        axis=0,
    ).astype(jnp.bfloat16)
    greet(r, g, reps, 2 * chips)
    slab = [wi.at[:, pl.ds(j * width, width)] for j in range(4)]
    quarters = (
        ((wq, 0, 48), (wk, 48, 48), (wv, 96, 48)),
        ((wo, 0, 48), (slab[0], 48, 48), (slab[1], 96, 48)),
        ((slab[2], 0, 48), (slab[3], 48, 48), (wu.at[pl.ds(0, 48), :], 96, 48)),
        ((wu.at[pl.ds(48, 144), :], 0, 144),),
    )
    swap = remote(tok.at[1 - c], x.at[g], psend, trecv.at[g], r, p)
    swap.start()
    own_x = pltpu.make_async_copy(tok.at[c], x.at[g], lsem.at[0])
    own_x.start()
    def pass_on(b, way, src=None):
        to = g + 2 if way == 0 else g - 2
        src = x.at[b] if src is None else src
        return remote(src, x.at[b], tsend.at[way, b], trecv.at[b], r, to)

    def forward(b, way, src=None):
        ok = z < chips - 1 if way == 0 else z > 0

        @pl.when(ok)
        def _():
            pass_on(b, way, src).start()

    def keep(b):
        return pltpu.make_async_copy(x.at[b], x_out.at[b], xsem.at[b])

    def arrived(b):
        remote(x.at[b], x.at[b], tsend.at[0, b], trecv.at[b], r, p).wait_recv()

    forward(g, 0, tok.at[c])
    forward(g, 1, tok.at[c])
    arrived(p)
    forward(p, 0)
    forward(p, 1)
    keep(p).start()
    for i, pieces in enumerate(quarters):
        @pl.when(r == i)
        def _():
            copies = [
                pltpu.make_async_copy(ref, mine.at[pl.ds(row, count), :], lsem.at[3 + k])
                for k, (ref, row, count) in enumerate(pieces)
            ]
            for copy in copies:
                copy.start()
            for copy in copies:
                copy.wait()

    own_w = pltpu.make_async_copy(mine, w_out.at[r, c, z], lsem.at[1])
    own_w.start()
    own_s = pltpu.make_async_copy(small, smalls_in.at[g], lsem.at[2])
    own_s.start()
    first = []
    for d in range(1, chips):
        zz = lax.rem(z + d, chips)
        copy = remote(mine, w_out.at[r, c, z], wsend1.at[d - 1], wrecv1.at[z], r, 2 * zz + c)
        copy.start()
        first.append(copy)
    smalls = []
    for d in range(1, 2 * chips):
        copy = remote(small, smalls_in.at[g], ssend.at[d - 1], srecv.at[g], r, lax.rem(g + d, 2 * chips))
        copy.start()
        smalls.append(copy)
    own_x.wait()
    keep(g).start()

    def tokens_from(d):
        for k in range(2):
            @pl.when(z >= d)
            def _():
                b = 2 * (z - d) + (c if k == 0 else 1 - c)
                arrived(b)
                forward(b, 0)
                keep(b).start()

            @pl.when(z + d < chips)
            def _():
                b = 2 * (z + d) + (c if k == 0 else 1 - c)
                arrived(b)
                forward(b, 1)
                keep(b).start()

    tokens_from(1)
    for d in range(1, chips):
        zz = lax.rem(z + d, chips)
        remote(mine, w_out.at[r, c, zz], wsend1.at[0], wrecv1.at[zz], r, p).wait_recv()
    own_w.wait()
    second = []
    for d in range(1, reps):
        copy = remote(
            w_out.at[r, c], w_out.at[r, c], wsend2.at[d - 1], wrecv2.at[r], lax.rem(r + d, reps), g
        )
        copy.start()
        second.append(copy)
    third = [remote(w_out.at[r, c], w_out.at[r, c], wsend3.at[r], wrecv3.at[r], r, p)]
    third[0].start()
    tokens_from(2)
    for d in range(1, reps):
        q = lax.rem(r + d, reps)
        remote(w_out.at[q, c], w_out.at[q, c], wsend2.at[0], wrecv2.at[q], r, p).wait_recv()
        copy = remote(w_out.at[q, c], w_out.at[q, c], wsend3.at[q], wrecv3.at[q], r, p)
        copy.start()
        third.append(copy)
    for q in range(reps):
        remote(w_out.at[q, 1 - c], w_out.at[q, 1 - c], wsend3.at[q], wrecv3.at[q], r, p).wait_recv()
    load_w = pltpu.make_async_copy(w_out.at[0], w0, lsem.at[1])
    load_w.start()
    for d in range(1, 2 * chips):
        b = lax.rem(g + d, 2 * chips)
        remote(small, smalls_in.at[b], ssend.at[0], srecv.at[b], r, p).wait_recv()
    own_s.wait()
    keep_s = pltpu.make_async_copy(smalls_in, s_out, lsem.at[2])
    keep_s.start()
    load_w.wait()

    span = heads * HEAD
    bias = vectors_of(smalls_in).astype(jnp.bfloat16)
    full = [
        jnp.concatenate([w0[i % 2, i // 2, 48 * k : 48 * k + 48, :] for i in range(8)], axis=0)
        for k in range(3)
    ]
    lane = iota((width, heads * LANES), 1)
    head, lane_in = lax.div(lane, LANES), lax.rem(lane, LANES)
    column = span * z + head * HEAD + lax.rem(lane_in, HEAD)
    hit = iota((width, heads * LANES), 0) == column
    pick_k = jnp.where(hit & (lane_in < HEAD), 1.0, 0.0).astype(jnp.bfloat16)
    pick_v = jnp.where(hit & (lane_in >= 64) & (lane_in < 96), 1.0, 0.0).astype(jnp.bfloat16)
    wrow[...] = (dot(full[1], pick_k) + dot(full[2], pick_v)).astype(jnp.bfloat16)
    row_kv = dot(bias[1:2, :], pick_v)
    pick_t = jnp.where(
        iota((span, width), 1) == span * z + iota((span, width), 0), 1.0, 0.0
    ).astype(jnp.bfloat16)

    def by_rows(left, right):
        return lax.dot_general(
            left, right, (((1,), (1,)), ((), ())), preferred_element_type=jnp.float32
        )

    for k in range(3):
        wtr[k] = by_rows(pick_t, full[k]).astype(jnp.bfloat16)
    column_bias = by_rows(pick_t, bias)
    col_q, col_v = column_bias[:, 0:1], column_bias[:, 1:2]
    one_lane = lax.rem(iota((1, heads * LANES), 1), LANES)
    row_kv = row_kv + jnp.where((one_lane >= 104) & (one_lane < 107), 1.0, 0.0)
    one = jnp.where(iota((16, rows), 0) == 0, 1.0, 0.0).astype(jnp.bfloat16)

    def stores(b):
        cols = pl.ds(pl.multiple_of(b * rows, rows), rows)
        return [
            pltpu.make_async_copy(kv.at[:, cols, :], kv_out.at[:, cols, :], psems.at[0, b])
        ] + [
            pltpu.make_async_copy(ref.at[:, :, cols], out.at[:, :, cols], psems.at[1 + i, b])
            for i, (ref, out) in enumerate(((kt, kt_out), (vt, vt_out), (q1, q1_out)))
        ]

    def project(i, most):
        half = lax.rem(i, 2)
        b = 2 * chip_at(z, lax.div(i, 2)) + c + half - 2 * c * half
        xb = x[b]
        two = smalls_in[b, 8:16, :].astype(jnp.float32)
        ids = jnp.where(c == 0, two[1:2], two[2:3])
        same = jnp.where(iota((8, rows), 0).astype(jnp.float32) == ids, 1.0, 0.0)
        hot = jnp.concatenate(
            [jnp.zeros((96, rows), jnp.float32), same, jnp.zeros((24, rows), jnp.float32)], axis=0
        ).T
        cols = pl.ds(pl.multiple_of(b * rows, rows), rows)
        flat = dot(xb, wrow[...]) + row_kv
        for h in range(heads):
            kv[h, cols, :] = (flat[:, h * LANES : (h + 1) * LANES] + hot).astype(jnp.bfloat16)
        q_t = (by_rows(wtr[0], xb) + col_q).astype(jnp.bfloat16)
        k_t = by_rows(wtr[1], xb).astype(jnp.bfloat16)
        v_t = (by_rows(wtr[2], xb) + col_v).astype(jnp.bfloat16)
        q_wide = q_t.astype(jnp.float32) * SCALE
        k_wide = k_t.astype(jnp.float32)
        sizes = []
        for n, v in enumerate((q_wide, k_wide)):
            size = most[n]
            for h in range(heads):
                size = jnp.maximum(
                    size, jnp.sum(v[h * HEAD : (h + 1) * HEAD] ** 2, axis=0, keepdims=True)
                )
            sizes.append(size)
        for h in range(heads):
            part = slice(h * HEAD, (h + 1) * HEAD)
            kt[h, :, cols] = k_t[part]
            q1[h, :, cols] = q_t[part]
            vt[h, 0:32, cols] = v_t[part]
            vt[h, 32:48, cols] = one
        for copy in stores(b):
            copy.start()
        return tuple(sizes)

    zero = jnp.zeros((1, rows), jnp.float32)
    most = lax.fori_loop(0, 6, project, (zero, zero))
    tokens_from(3)
    most = lax.fori_loop(6, 8, project, most)
    norms[0:1, :] = most[0]
    norms[1:2, :] = most[1]

    def settle(b, none):
        keep(b).wait()
        for copy in stores(b):
            copy.wait()
        return none

    swap.wait_send()
    for copy in first + smalls + second + third:
        copy.wait_send()
    for b in range(2 * chips):
        @pl.when((z < chips - 1) & (b < 2 * z + 2))
        def _():
            pass_on(b, 0).wait_send()

        @pl.when((z > 0) & (b >= 2 * z))
        def _():
            pass_on(b, 1).wait_send()

    keep_s.wait()
    lax.fori_loop(0, 2 * chips, settle, 0)


def gather(tokens, weights, vectors, inner, seg):
    dma = pltpu.SemaphoreType.DMA
    anywhere = pl.BlockSpec(memory_space=pltpu.HBM)
    vm = pl.BlockSpec(memory_space=pltpu.VMEM)
    rows, width = tokens.shape[1:]
    bf, f4 = jnp.bfloat16, jnp.float32
    heads, length = 3, 8 * rows
    made = [
        (heads, length, LANES), (heads, HEAD, length), (heads, 48, length), (heads, HEAD, length)
    ]
    return pl.pallas_call(
        gather_kernel,
        name="gather",
        out_shape=(
            jax.ShapeDtypeStruct((8, rows, width), bf),
            jax.ShapeDtypeStruct((4, 2, 4, 144, width), bf),
            jax.ShapeDtypeStruct((8, 16, rows), bf),
        )
        + tuple(jax.ShapeDtypeStruct(shape, bf) for shape in made)
        + (jax.ShapeDtypeStruct((2, rows), f4),),
        in_specs=[anywhere] * 7 + [vm] * 3,
        out_specs=[anywhere] * 7 + [vm],
        scratch_shapes=[
            pltpu.VMEM((16, rows), bf),
            pltpu.VMEM((8, rows, width), bf),
        ]
        + [pltpu.VMEM(shape, bf) for shape in made]
        + [
            pltpu.VMEM((2, 4, 144, width), bf),
            pltpu.VMEM((8, 16, rows), bf),
            pltpu.VMEM((width, heads * LANES), bf),
            pltpu.VMEM((3, heads * HEAD, width), bf),
            pltpu.VMEM((144, width), bf),
            dma((6,)), dma((8,)), dma((4, 8)), dma((2, 8)), dma((8,)), dma, dma((3,)), dma((4,)), dma((3,)), dma((4,)),
            dma((4,)), dma((4,)), dma((7,)), dma((8,)),
        ],
        compiler_params=pltpu.CompilerParams(
            collective_id=1, has_side_effects=True, vmem_limit_bytes=BIG
        ),
    )(tokens, *weights, vectors, inner, seg)


def span_of(starts, q0, docs):
    low = jnp.int32(0)
    high = starts[docs]
    for d in range(docs):
        low = jnp.where(starts[d] <= q0, jnp.maximum(low, starts[d]), low)
        high = jnp.where(starts[d + 1] >= q0 + QB, jnp.minimum(high, starts[d + 1]), high)
    first = lax.div(low, LANES)
    return first, lax.div(high + LANES - 1, LANES) - first


def in_groups(first, count, total, body):
    def at(i):
        return pl.multiple_of(i * LANES, LANES)

    big = count >= LONG - 1

    @pl.when(big)
    def _():
        body(pl.ds(at(jnp.minimum(first, total - LONG)), LONG * LANES))

    first = jnp.where(big, first + LONG, first)
    count = jnp.where(big, jnp.maximum(count - LONG, 0), count)
    many = jnp.maximum(lax.div(count, 4) - 1, 0)

    def group(i, none):
        body(pl.ds(at(first + 4 * i), 4 * LANES))
        return none

    lax.fori_loop(0, many, group, 0)
    left = count - 4 * many
    for k in range(1, 8):
        @pl.when(left == k)
        def _():
            body(pl.ds(at(first + 4 * many), k * LANES))


def attend_kernel(
    kv_hbm, q1, vt_hbm, small, norms, ctx, tail_out, spans, qt, acc, tall, seg, starts, kv, vt, sems,
):
    heads, length, _ = kv.shape
    blocks, hw, rows = ctx.shape
    docs = 8
    c = where_am_i()[3]
    loads = [
        pltpu.make_async_copy(kv_hbm, kv, sems.at[0]),
        pltpu.make_async_copy(q1, qt.at[:, pl.ds(0, HEAD), :], sems.at[1]),
        pltpu.make_async_copy(vt_hbm, vt, sems.at[2]),
    ]
    for load in loads:
        load.start()
    for g in range(8):
        two = small[g, 8:16, :].astype(jnp.float32)
        seg[g : g + 1, :] = jnp.where(c == 0, two[1:2], two[2:3]).astype(jnp.int32)
    ids = seg[...]
    starts[0] = jnp.int32(0)
    for d in range(1, docs):
        starts[d] = jnp.sum(jnp.where(ids < d, 1.0, 0.0)).astype(jnp.int32)
    starts[docs] = jnp.int32(length)

    def far(same):
        return (same - 1.0) * AWAY

    def fill(b, none):
        cols = pl.ds(pl.multiple_of(b * rows, rows), rows)
        same = jnp.where(iota((8, rows), 0) == seg[pl.ds(b, 1), :], 1.0, 0.0)
        low = jnp.concatenate([far(same), jnp.zeros((8, rows), jnp.float32)], axis=0)
        for h in range(heads):
            qt[h, HEAD:96, cols] = jnp.zeros((96 - HEAD, rows), jnp.bfloat16)
            qt[h, 96:112, cols] = low.astype(jnp.bfloat16)
            qt[h, 112:128, cols] = jnp.zeros((16, rows), jnp.bfloat16)
        return none

    lax.fori_loop(0, blocks, fill, 0)
    bounded = jnp.max(norms[0:1, :]) * jnp.max(norms[1:2, :]) < LIMIT * LIMIT
    for load in loads:
        load.wait()

    per = rows // QB

    def query_block(b, carry):
        q0 = pl.multiple_of(b * QB, QB)
        first, count = span_of(starts, q0, docs)
        spans[0, b] = first
        spans[1, b] = count
        acc[...] = jnp.zeros_like(acc)

        def key_block(i, tops):
            keys = pl.ds(pl.multiple_of((first + i) * LANES, LANES), LANES)
            s = [dot(kv[h, keys, :], qt[h, :, pl.ds(q0, QB)]) for h in range(heads)]
            new = [jnp.maximum(tops[h], jnp.max(s[h], axis=0, keepdims=True)) for h in range(heads)]
            p = [jnp.exp2((s[h] - new[h]) * SCALE).astype(jnp.bfloat16) for h in range(heads)]
            for h in range(heads):
                acc[h] = acc[h] * jnp.exp2((tops[h] - new[h]) * SCALE) + dot(vt[h, :, keys], p[h])
            return tuple(new)

        def plain_block(keys):
            s = [dot(kv[h, keys, :], qt[h, :, pl.ds(q0, QB)]) for h in range(heads)]
            p = [jnp.exp2(v * SCALE).astype(jnp.bfloat16) for v in s]
            for h in range(heads):
                acc[h] += dot(vt[h, :, keys], p[h])

        @pl.when(bounded)
        def _():
            in_groups(first, count, length // LANES, plain_block)
            tall[...] = jnp.zeros_like(tall)

        @pl.when(jnp.logical_not(bounded))
        def _():
            lowest = jnp.full((1, QB), -3e38, jnp.float32)
            tops = lax.fori_loop(0, count, key_block, (lowest,) * heads)
            for h in range(heads):
                tall[h] = tops[h]

        g = lax.div(b, per)
        off = pl.multiple_of(lax.rem(b, per) * QB, QB)
        same = jnp.where(iota((8, QB), 0) == seg[pl.ds(g, 1), pl.ds(off, QB)], 1.0, 0.0)
        for h in range(heads):
            total = acc[h, 32:33, :]
            out = acc[h, 0:32, :] / total
            ctx[g, h * HEAD : (h + 1) * HEAD, pl.ds(off, QB)] = out.astype(jnp.bfloat16)
            parts = halves(-(tall[h] + jnp.log2(total) / SCALE))
            tail = jnp.concatenate([far(same), *parts, jnp.zeros((5, QB), jnp.float32)], axis=0)
            tail_out[h, :, pl.ds(q0, QB)] = tail.astype(jnp.bfloat16)
        return carry

    lax.fori_loop(0, length // QB, query_block, 0)


def attend(kv, q1, vt, small, norms):
    heads, length, _ = kv.shape
    blocks, _, rows = small.shape
    sm = pl.BlockSpec(memory_space=pltpu.SMEM)
    anywhere = pl.BlockSpec(memory_space=pltpu.HBM)
    bf, f4 = jnp.bfloat16, jnp.float32
    shapes = (
        jax.ShapeDtypeStruct((blocks, heads * HEAD, rows), bf),
        jax.ShapeDtypeStruct((heads, 16, length), bf),
    )
    return pl.pallas_call(
        attend_kernel,
        name="attend",
        grid=(1,),
        out_shape=shapes + (jax.ShapeDtypeStruct((2, length // QB), jnp.int32),),
        in_specs=[anywhere, anywhere, anywhere, whole_spec(small), whole_spec(norms)],
        out_specs=[whole_spec(v) for v in shapes] + [sm],
        scratch_shapes=[
            pltpu.VMEM((heads, LANES, length), bf),
            pltpu.VMEM((heads, 48, QB), f4),
            pltpu.VMEM((heads, 1, QB), f4),
            pltpu.VMEM((8, rows), jnp.int32),
            pltpu.SMEM((16,), jnp.int32),
            pltpu.VMEM(kv.shape, bf),
            pltpu.VMEM(vt.shape, bf),
            pltpu.SemaphoreType.DMA((3,)),
        ],
        compiler_params=pltpu.CompilerParams(vmem_limit_bytes=BIG),
    )(kv, q1, vt, small, norms)


PIECE = 128


def middle_kernel(
    ctx, tok_hbm, og_hbm, w_hbm, small,
    layer_hbm, grad_hbm, gctx_out, pr,
    wo, wi, wu, gwo, gwi, gwu, sums, inner_sum, ctx_in, gctx, pg, pg_in,
    tok, og, w, layer_out, grad_one_out, insems, outsems, lsem, send, recv, gsend, grecv, glocal, psend, precv,
):
    seqs, rows, width = tok.shape
    slabs = wi.shape[0]
    pieces = rows // PIECE
    r, g, z, c = where_am_i()
    loads = [
        pltpu.make_async_copy(w_hbm, w, insems.at[0]),
        pltpu.make_async_copy(tok_hbm, tok, insems.at[1]),
        pltpu.make_async_copy(og_hbm, og, insems.at[2]),
    ]
    for load in loads:
        load.start()
    greet(r, g, 1, 8)

    def fetch(q):
        cols = pl.ds(pl.multiple_of(q * PIECE, PIECE), PIECE)
        for d in (4, 3, 5, 2, 6, 1, 7):
            to = lax.rem(g + d, 8)
            remote(
                ctx.at[to, :, cols], ctx_in.at[c, z, :, cols], send.at[q, d - 1], recv.at[q, g], r, to
            ).start()

    own = pltpu.make_async_copy(ctx.at[g], ctx_in.at[c, z], lsem)
    own.start()
    fetch(0)
    fetch(1)
    loads[0].wait()
    for i in range(8):
        cc, zz = i % 2, i // 2
        wo[48 * i : 48 * i + 48, :] = w[1, cc, zz, 0:48, :]
        wi[0, 48 * i : 48 * i + 48, :] = w[1, cc, zz, 48:96, :]
        wi[1, 48 * i : 48 * i + 48, :] = w[1, cc, zz, 96:144, :]
        wi[2, 48 * i : 48 * i + 48, :] = w[2, cc, zz, 0:48, :]
        wi[3, 48 * i : 48 * i + 48, :] = w[2, cc, zz, 48:96, :]
        wu[zz, 192 * cc : 192 * cc + 48, :] = w[2, cc, zz, 96:144, :]
        wu[zz, 192 * cc + 48 : 192 * cc + 192, :] = w[3, cc, zz, :, :]
    for ref in (gwo, gwi, gwu, sums, inner_sum):
        ref[...] = jnp.zeros_like(ref)
    fetch(2)
    fetch(3)

    vec = vectors_of(small)
    inner_bias = jnp.concatenate(
        [small[i, 8:16, 0:192].astype(jnp.float32)[0:1] for i in range(8)], axis=1
    )
    out_bias, outer_bias = vec[2:3, :], vec[3:4, :]
    gain_one, shift_one = vec[4:5, :], vec[5:6, :]
    gain_two, shift_two = vec[6:7, :], vec[7:8, :]

    def normal(value):
        centre = value - jnp.mean(value, axis=-1, keepdims=True)
        rate = lax.rsqrt(jnp.mean(centre * centre, axis=-1, keepdims=True) + norm_epsilon)
        return centre * rate, rate

    def normal_back(grad, gain, n, rate):
        u = grad * gain
        return rate * (
            u - jnp.mean(u, axis=-1, keepdims=True) - n * jnp.mean(u * n, axis=-1, keepdims=True)
        )

    def total(value):
        return jnp.sum(value, axis=0, keepdims=True)

    def dot_turn(left, right):
        return lax.dot_general(
            left, right, (((1,), (1,)), ((), ())), preferred_element_type=jnp.float32
        )

    def arrived(q, cols):
        for d in range(1, 8):
            b = lax.rem(g + d, 8)
            remote(
                ctx.at[g, :, cols], ctx_in.at[lax.rem(b, 2), lax.div(b, 2), :, cols],
                send.at[q, 0], recv.at[q, b], r, b,
            ).wait_recv()

    def return_piece(q, cols, d):
        to = lax.rem(g + d, 8)
        return remote(
            gctx.at[lax.rem(to, 2), lax.div(to, 2), :, cols], gctx_out.at[g, :, cols],
            gsend.at[q, d - 1], grecv.at[q, g], r, to,
        )

    def keep_piece(q, cols):
        return pltpu.make_async_copy(gctx.at[c, z, :, cols], gctx_out.at[g, :, cols], glocal.at[q])

    own.wait()
    loads[1].wait()
    loads[2].wait()

    def results(q):
        here = pl.ds(pl.multiple_of(q * PIECE, PIECE), PIECE)
        return [
            pltpu.make_async_copy(ref.at[:, here, :], out.at[:, here, :], outsems.at[k, q])
            for k, (ref, out) in enumerate(((layer_out, layer_hbm), (grad_one_out, grad_hbm)))
        ]

    def one(q, carry):
        r0 = pl.multiple_of(q * PIECE, PIECE)
        here = pl.ds(r0, PIECE)
        arrived(q, here)

        def both(ref):
            return jnp.concatenate([ref[s, here, :] for s in range(seqs)], axis=0)

        def split(ref, value):
            for s in range(seqs):
                ref[s, here, :] = value[s * PIECE : (s + 1) * PIECE].astype(ref.dtype)

        ctx_t = jnp.concatenate(
            [jnp.concatenate([ctx_in[s, zz, :, here] for zz in range(4)], axis=0) for s in range(seqs)],
            axis=1,
        )
        context = ctx_t.astype(jnp.float32).T.astype(jnp.bfloat16)
        x = both(tok).astype(jnp.float32)
        n_one, rate_one = normal(x + (dot(context, wo[...]) + out_bias))
        hidden = n_one * gain_one + shift_one
        low = hidden.astype(jnp.bfloat16)
        low_t = hidden.T.astype(jnp.bfloat16)
        feed = jnp.zeros(hidden.shape, jnp.float32)
        slopes, actives = [], []
        for j in range(slabs):
            inner = dot(low, wi[j]) + inner_bias[:, j * width : (j + 1) * width]
            cdf = 0.5 + 0.5 * lax.erf(inner * (0.5 ** 0.5))
            pdf = jnp.exp(inner * inner * -0.5) * 0.3989422804014327
            slopes.append(cdf + inner * pdf)
            active = inner * cdf
            actives.append(active)
            feed = feed + dot(active.astype(jnp.bfloat16), wu[j])
        n_two, rate_two = normal(hidden + (feed + outer_bias))
        split(layer_out, n_two * gain_two + shift_two)
        grad = both(og).astype(jnp.float32)
        grad_two = normal_back(grad, gain_two, n_two, rate_two)
        grad_feed = grad_two.astype(jnp.bfloat16)
        grad_hidden = grad_two
        for j in range(slabs):
            grad_inner = (dot_turn(grad_feed, wu[j]) * slopes[j]).astype(jnp.bfloat16)
            inner_sum[:, j * width : (j + 1) * width] += total(grad_inner.astype(jnp.float32))
            grad_hidden = grad_hidden + dot_turn(grad_inner, wi[j])
            gwi[j] += dot(low_t, grad_inner)
            gwu[j] += dot(actives[j].T.astype(jnp.bfloat16), grad_feed)
        grad_one = normal_back(grad_hidden, gain_one, n_one, rate_one)
        split(grad_one_out, grad_one)
        grad_att = grad_one.astype(jnp.bfloat16)
        back = dot_turn(wo[...], grad_att).astype(jnp.bfloat16)
        for s in range(seqs):
            for zz in range(4):
                gctx[s, zz, :, here] = back[96 * zz : 96 * zz + 96, s * PIECE : (s + 1) * PIECE]
        for d in (4, 3, 5, 2, 6, 1, 7):
            return_piece(q, here, d).start()
        keep_piece(q, here).start()
        for copy in results(q):
            copy.start()
        gwo[...] += dot(ctx_t, grad_att)
        sums[0:1, :] += total(grad_att.astype(jnp.float32))
        sums[1:2, :] += total(grad_feed.astype(jnp.float32))
        sums[2:3, :] += total(grad_hidden * n_one)
        sums[3:4, :] += total(grad_hidden)
        sums[4:5, :] += total(grad * n_two)
        sums[5:6, :] += total(grad)
        return carry

    lax.fori_loop(0, pieces, one, 0)
    rows_of_sums = jnp.concatenate(
        [sums[...]]
        + [inner_sum[:, j * width : (j + 1) * width] for j in range(slabs)]
        + [jnp.zeros((6, width), jnp.float32)],
        axis=0,
    ).astype(jnp.bfloat16)
    for i in range(8):
        cc, zz = i % 2, i // 2
        mine = slice(48 * i, 48 * i + 48)
        pg[cc, zz, 0, 0:48, :] = gwo[mine, :].astype(jnp.bfloat16)
        pg[cc, zz, 0, 48:96, :] = gwi[0, mine, :].astype(jnp.bfloat16)
        pg[cc, zz, 1, 0:48, :] = gwi[1, mine, :].astype(jnp.bfloat16)
        pg[cc, zz, 1, 48:96, :] = gwi[2, mine, :].astype(jnp.bfloat16)
        pg[cc, zz, 2, 0:48, :] = gwi[3, mine, :].astype(jnp.bfloat16)
        base = 192 * cc
        pg[cc, zz, 0, 96:112, :] = gwu[zz, base : base + 16, :].astype(jnp.bfloat16)
        pg[cc, zz, 1, 96:112, :] = gwu[zz, base + 16 : base + 32, :].astype(jnp.bfloat16)
        pg[cc, zz, 2, 48:112, :] = gwu[zz, base + 32 : base + 96, :].astype(jnp.bfloat16)
        pg[cc, zz, 3, 0:96, :] = gwu[zz, base + 96 : base + 192, :].astype(jnp.bfloat16)
        pg[cc, zz, 3, 96:112, :] = rows_of_sums
    pair = remote(pg.at[1 - c], pg_in, psend, precv, r, 2 * z + 1 - c)
    pair.start()

    def settle(q, carry):
        cols = pl.ds(pl.multiple_of(q * PIECE, PIECE), PIECE)
        for d in range(1, 8):
            b = lax.rem(g + d, 8)
            remote(
                gctx.at[c, z, :, cols], gctx_out.at[b, :, cols], gsend.at[q, 0], grecv.at[q, b], r, b
            ).wait_recv()
            return_piece(q, cols, d).wait_send()
            to = lax.rem(g + d, 8)
            remote(
                ctx.at[to, :, cols], ctx_in.at[c, z, :, cols], send.at[q, d - 1], recv.at[q, g], r, to
            ).wait_send()
        keep_piece(q, cols).wait()
        for copy in results(q):
            copy.wait()
        return carry

    pair.wait_recv()
    for i in range(4):
        pr[i] = (pg[c, i].astype(jnp.float32) + pg_in[i].astype(jnp.float32)).astype(jnp.bfloat16)
    lax.fori_loop(0, pieces, settle, 0)
    pair.wait_send()


def middle(ctx, tok, og, w, small):
    seqs, rows, width = tok.shape
    vm = pl.BlockSpec(memory_space=pltpu.VMEM)
    anywhere = pl.BlockSpec(memory_space=pltpu.HBM)
    dma = pltpu.SemaphoreType.DMA
    bf, f4 = jnp.bfloat16, jnp.float32
    pieces = rows // PIECE
    return pl.pallas_call(
        middle_kernel,
        name="middle",
        out_shape=(
            jax.ShapeDtypeStruct((seqs, rows, width), bf),
            jax.ShapeDtypeStruct((seqs, rows, width), f4),
            jax.ShapeDtypeStruct(ctx.shape, bf),
            jax.ShapeDtypeStruct((4, 4, 112, width), bf),
        ),
        in_specs=[anywhere] * 4 + [vm],
        out_specs=[anywhere, anywhere, anywhere, vm],
        scratch_shapes=[
            pltpu.VMEM((width, width), bf),
            pltpu.VMEM((4, width, width), bf),
            pltpu.VMEM((4, width, width), bf),
            pltpu.VMEM((width, width), f4),
            pltpu.VMEM((4, width, width), f4),
            pltpu.VMEM((4, width, width), f4),
            pltpu.VMEM((6, width), f4),
            pltpu.VMEM((1, 4 * width), f4),
            pltpu.VMEM((2, 4) + ctx.shape[1:], bf),
            pltpu.VMEM((2, 4) + ctx.shape[1:], bf),
            pltpu.VMEM((2, 4, 4, 112, width), bf),
            pltpu.VMEM((4, 4, 112, width), bf),
            pltpu.VMEM((seqs, rows, width), bf),
            pltpu.VMEM((seqs, rows, width), bf),
            pltpu.VMEM(w.shape, bf),
            pltpu.VMEM((seqs, rows, width), bf),
            pltpu.VMEM((seqs, rows, width), f4),
            dma((3,)), dma((2, pieces)), dma, dma((pieces, 7)), dma((pieces, 8)), dma((pieces, 7)), dma((pieces, 8)), dma((pieces,)), dma, dma,
        ],
        compiler_params=pltpu.CompilerParams(
            collective_id=2, has_side_effects=True, vmem_limit_bytes=BIG
        ),
    )(ctx, tok, og, w, small)


def attend_back_kernel(
    last, index, spans, x_hbm, q_hbm, tail, kv_hbm, kt_hbm, q1, gctx, ctx, *refs,
):
    heads = q1.shape[0]
    span = heads * HEAD
    if last:
        grads_in, out, gq, dt, do, acc, dq, qt, x, kv, kt, sems = refs
    else:
        out, grads_out, dt, do, acc, dq, qt, x, kv, kt, sems = refs
    length, width = x.shape
    mine = pl.ds(index * heads, heads)
    loads = [
        pltpu.make_async_copy(q_hbm.at[mine], qt.at[:, pl.ds(0, HEAD), :], sems.at[0]),
        pltpu.make_async_copy(tail.at[mine], qt.at[:, pl.ds(96, 16), :], sems.at[1]),
        pltpu.make_async_copy(kv_hbm.at[mine], kv, sems.at[3]),
        pltpu.make_async_copy(kt_hbm.at[mine], kt, sems.at[4]),
        pltpu.make_async_copy(x_hbm, x, sems.at[2]),
    ]
    for load in loads:
        load.start()
    blocks, _, rows = gctx.shape
    z = where_am_i()[2]
    scale = HEAD ** -0.5

    def prepare(g, carry):
        r0 = pl.multiple_of(g * rows, rows)
        cols = pl.ds(r0, rows)
        for h in range(heads):
            part = slice(h * HEAD, (h + 1) * HEAD)
            grad = gctx[g, part, :]
            wide = grad.astype(jnp.float32)
            delta = -jnp.sum(wide * ctx[g, part, :].astype(jnp.float32), axis=0, keepdims=True)
            dt[h, 0:64, cols] = jnp.zeros((64, rows), jnp.bfloat16)
            dt[h, 64:96, cols] = grad
            qt[h, HEAD:96, cols] = jnp.zeros((96 - HEAD, rows), jnp.bfloat16)
            qt[h, 112:128, cols] = jnp.zeros((16, rows), jnp.bfloat16)
            tail = jnp.concatenate(
                [jnp.zeros((8, rows), jnp.float32), *halves(delta), jnp.zeros((21, rows), jnp.float32)],
                axis=0,
            )
            dt[h, 96:128, cols] = tail.astype(jnp.bfloat16)
            turned = jnp.concatenate(
                [wide, q1[h, :, cols].astype(jnp.float32), jnp.zeros((64, rows), jnp.float32)], axis=0
            ).T
            lane = iota((rows, LANES), 1)
            grad_rows = jnp.where(lane < HEAD, turned, 0.0).astype(jnp.bfloat16)
            query_rows = jnp.where(lane < HEAD, 0.0, turned).astype(jnp.bfloat16)
            for j in range(rows // QB):
                r1 = pl.multiple_of(2 * r0 + 2 * j * QB, QB)
                do[h, pl.ds(r1, QB), :] = grad_rows[j * QB : (j + 1) * QB]
                do[h, pl.ds(r1 + QB, QB), :] = query_rows[j * QB : (j + 1) * QB]
        return carry

    lax.fori_loop(0, blocks, prepare, 0)
    acc[...] = jnp.zeros_like(acc)
    per = rows // QB
    for load in loads[:4]:
        load.wait()

    def query_block(b, carry):
        q0 = pl.multiple_of(b * QB, QB)
        dq[...] = jnp.zeros_like(dq)

        def key_block(keys):
            s = [dot(kv[h, keys, :], qt[h, :, pl.ds(q0, QB)]) for h in range(heads)]
            d = [dot(kv[h, keys, :], dt[h, :, pl.ds(q0, QB)]) for h in range(heads)]
            p = [jnp.exp2(v * SCALE) for v in s]
            both = [
                jnp.concatenate([u.astype(jnp.bfloat16), (u * v).astype(jnp.bfloat16)], axis=1)
                for u, v in zip(p, d)
            ]
            for h in range(heads):
                acc[h, keys, :] += dot(both[h], do[h, pl.ds(2 * q0, 2 * QB), :])
            for h in range(heads):
                dq[h] += dot(kt[h, :, keys], both[h][:, QB:])

        in_groups(spans[0, b], spans[1, b], length // LANES, key_block)
        g = lax.div(b, per)
        off = pl.multiple_of(lax.rem(b, per) * QB, QB)
        for h in range(heads):
            out[g, h * HEAD : (h + 1) * HEAD, pl.ds(off, QB)] = (dq[h] * scale).astype(jnp.bfloat16)
        return carry

    lax.fori_loop(0, length // QB, query_block, 0)

    loads[4].wait()

    def finish_block(g, totals):
        r0 = pl.multiple_of(g * rows, rows)
        cols = pl.ds(r0, rows)
        for h in range(heads):
            both = acc[h, cols, :].T
            row = h * HEAD
            out[g, 2 * span + row : 2 * span + row + HEAD, :] = both[0:32].astype(jnp.bfloat16)
            out[g, span + row : span + row + HEAD, :] = (both[32:64] * scale).astype(jnp.bfloat16)
        piece = out[g]
        grad = dot(piece, x[cols, :])
        summed = jnp.sum(piece.astype(jnp.float32), axis=1, keepdims=True)
        return totals[0] + grad, totals[1] + summed

    grads, summed = lax.fori_loop(
        0,
        blocks,
        finish_block,
        (jnp.zeros((3 * span, width), jnp.float32), jnp.zeros((3 * span, 1), jnp.float32)),
    )
    if not last:
        grads_out[:, 0:width] = grads
        grads_out[:, width:] = jnp.broadcast_to(summed, (3 * span, LANES))
        return
    gq[...] = jnp.zeros_like(gq)
    before = grads_in.shape[0] // 3

    def joined(i, old, new):
        return [old[i * before : (i + 1) * before], new[i * span : (i + 1) * span]]

    old = grads_in[:, 0:width]
    whole = jnp.concatenate([v for i in range(3) for v in joined(i, old, grads)], axis=0).T
    total = 3 * (before + span)
    for g in range(8):
        gq[g % 2, g // 2, :, 0:total] = whole[48 * g : 48 * g + 48, :].astype(jnp.bfloat16)
    old = grads_in[:, width : width + 1]
    of_q = jnp.concatenate(joined(0, old, summed), axis=0)
    of_v = jnp.concatenate(joined(2, old, summed), axis=0)
    for cc in range(2):
        mine = jnp.concatenate(
            [
                of_q[48 * cc : 48 * cc + 48, :],
                of_v[48 * cc : 48 * cc + 48, :],
                jnp.zeros((48, 94), jnp.float32),
            ],
            axis=1,
        )
        gq[cc, z, :, total:] = mine.astype(jnp.bfloat16)


def attend_back(heads, index, spans, x, tail, kv, kt, q1, gctx, ctx, grads=None):
    blocks, rows, width = x.shape
    length = blocks * rows
    last = grads is not None
    rest = (grads,) if last else ()
    sm = pl.BlockSpec(memory_space=pltpu.SMEM)
    bf, f4 = jnp.bfloat16, jnp.float32
    once = pl.Buffered(1)
    span = heads * HEAD

    def some_heads(array):
        return pl.BlockSpec((heads,) + array.shape[1:], lambda i: (index, 0, 0), pipeline_mode=once)

    def head_rows(array):
        return pl.BlockSpec((blocks, span, rows), lambda i: (0, index, 0), pipeline_mode=once)

    flat = x.reshape(length, width)
    shapes = (
        jax.ShapeDtypeStruct((blocks, 3 * span, rows), bf),
        jax.ShapeDtypeStruct((2, 4, 48, width), bf)
        if last
        else jax.ShapeDtypeStruct((3 * span, width + LANES), f4),
    )
    return pl.pallas_call(
        functools.partial(attend_back_kernel, last, index),
        name="attend_back",
        grid=(1,),
        out_shape=shapes,
        in_specs=[sm] + [pl.BlockSpec(memory_space=pltpu.HBM)] * 5
        + [some_heads(q1)]
        + [head_rows(v) for v in (gctx, ctx)]
        + [whole_spec(v) for v in rest],
        out_specs=[whole_spec(v) for v in shapes],
        scratch_shapes=[
            pltpu.VMEM((heads, LANES, length), bf),
            pltpu.VMEM((heads, 2 * length, LANES), bf),
            pltpu.VMEM((heads, length, LANES), f4),
            pltpu.VMEM((heads, HEAD, QB), f4),
            pltpu.VMEM((heads, LANES, length), bf),
            pltpu.VMEM((length, width), bf),
            pltpu.VMEM((heads,) + kv.shape[1:], bf),
            pltpu.VMEM((heads,) + kt.shape[1:], bf),
            pltpu.SemaphoreType.DMA((5,)),
        ],
        compiler_params=pltpu.CompilerParams(vmem_limit_bytes=BIG),
        cost_estimate=pl.CostEstimate(
            flops=heads * 20 * 10 ** 9, bytes_accessed=heads * 8 * 10 ** 6, transcendentals=heads * 6 * 10 ** 6
        ),
    )(spans, flat, q1, tail, kv, kt, q1, gctx, ctx, *rest)


def reduce_kernel(
    src, gq, pz, dst, p_out, q_out,
    gq_in, gq_sum, qa_in, qa_sum, qb_in, pz_in, p_line, pa_in, p_own, gq_own,
    lsem, send, recv, gsend, grecv, qasend, qarecv, qbsend, qbrecv, qcsend, qcrecv,
    pasend, parecv, pcsend, pcrecv,
):
    r, g, z, c = where_am_i()
    greet(r, g, 4, 8)
    waits = []
    pair = remote(gq.at[1 - c], gq_in, gsend, grecv, r, 2 * z + 1 - c)
    pair.start()
    load_g = pltpu.make_async_copy(gq.at[c], gq_own, lsem.at[1])
    load_g.start()
    load_p = pltpu.make_async_copy(pz, pz_in, lsem.at[2])
    load_p.start()
    own = pltpu.make_async_copy(src.at[g], dst.at[g], lsem.at[0])
    own.start()

    def send_to(d):
        to = lax.rem(g + d, 8)
        copy = remote(src.at[to], dst.at[g], send.at[d - 1], recv.at[g], r, to)
        copy.start()
        waits.append(copy)

    def f32(value):
        return value.astype(jnp.float32)

    load_g.wait()
    pair.wait_recv()
    gq_sum[...] = (f32(gq_own[...]) + f32(gq_in[...])).astype(jnp.bfloat16)
    for d in range(1, 4):
        rr = lax.rem(r + d, 4)
        copy = remote(gq_sum.at[rr], qa_in.at[r], qasend.at[d - 1], qarecv.at[r], rr, g)
        copy.start()
        waits.append(copy)
    load_p.wait()
    total = f32(pz_in[0])
    for i in range(1, 4):
        total = total + f32(pz_in[i])
    p_line[...] = total.astype(jnp.bfloat16)
    for d in range(1, 4):
        rr = lax.rem(r + d, 4)
        copy = remote(p_line.at[rr], pa_in.at[r], pasend.at[d - 1], parecv.at[r], rr, g)
        copy.start()
        waits.append(copy)
    for d in range(1, 4):
        b = lax.rem(r + d, 4)
        remote(gq_sum.at[r], qa_in.at[b], qasend.at[0], qarecv.at[b], b, g).wait_recv()
    total = f32(gq_sum[r])
    for d in range(1, 4):
        total = total + f32(qa_in[lax.rem(r + d, 4)])
    qa_sum[...] = total.astype(jnp.bfloat16)

    @pl.when(z != r)
    def _():
        remote(qa_sum, qb_in.at[z], qbsend, qbrecv.at[z], r, 2 * r + c).start()

    for d in (4, 3, 5, 2, 6, 1, 7):
        send_to(d)
    for d in range(1, 4):
        b = lax.rem(r + d, 4)
        remote(p_line.at[r], pa_in.at[b], pasend.at[0], parecv.at[b], b, g).wait_recv()
    total = f32(p_line[r])
    for d in range(1, 4):
        total = total + f32(pa_in[lax.rem(r + d, 4)])
    p_own[...] = total.astype(jnp.bfloat16)
    keep_p = pltpu.make_async_copy(p_own, p_out.at[r], lsem.at[3])
    keep_p.start()
    for d in range(1, 4):
        rr = lax.rem(r + d, 4)
        copy = remote(p_own, p_out.at[r], pcsend.at[d - 1], pcrecv.at[r], rr, g)
        copy.start()
        waits.append(copy)

    @pl.when(z == r)
    def _():
        for d in range(1, 4):
            b = lax.rem(z + d, 4)
            remote(qa_sum, qb_in.at[b], qbsend, qbrecv.at[b], r, g).wait_recv()
        qb_in[z] = qa_sum[...]
        keep = pltpu.make_async_copy(qb_in, q_out, lsem.at[4])
        keep.start()
        for d in range(1, 4):
            remote(qb_in, q_out, qcsend.at[d - 1], qcrecv, lax.rem(r + d, 4), g).start()
        keep.wait()
        for d in range(1, 4):
            remote(qb_in, q_out, qcsend.at[d - 1], qcrecv, lax.rem(r + d, 4), g).wait_send()

    @pl.when(z != r)
    def _():
        remote(qb_in, q_out, qcsend.at[0], qcrecv, r, g).wait_recv()
        remote(qa_sum, qb_in.at[z], qbsend, qbrecv.at[z], r, 2 * r + c).wait_send()

    for d in range(1, 4):
        b = lax.rem(r + d, 4)
        remote(p_own, p_out.at[b], pcsend.at[0], pcrecv.at[b], b, g).wait_recv()
    for d in range(1, 8):
        b = lax.rem(g + d, 8)
        remote(src.at[g], dst.at[b], send.at[0], recv.at[b], r, b).wait_recv()
    pair.wait_send()
    for copy in waits:
        copy.wait_send()
    keep_p.wait()
    own.wait()


def reduce_all(src, gq, pz):
    dma = pltpu.SemaphoreType.DMA
    anywhere = pl.BlockSpec(memory_space=pltpu.HBM)
    bf = jnp.bfloat16
    width = gq.shape[-1]
    part = (4, 48, width)
    return pl.pallas_call(
        reduce_kernel,
        name="reduce",
        out_shape=(
            jax.ShapeDtypeStruct(src.shape, bf),
            jax.ShapeDtypeStruct((4, 112, width), bf),
            jax.ShapeDtypeStruct(part, bf),
        ),
        in_specs=[anywhere] * 3,
        out_specs=[anywhere] * 3,
        scratch_shapes=[
            pltpu.VMEM(part, bf),
            pltpu.VMEM(part, bf),
            pltpu.VMEM(part, bf),
            pltpu.VMEM((48, width), bf),
            pltpu.VMEM(part, bf),
            pltpu.VMEM((4, 4, 112, width), bf),
            pltpu.VMEM((4, 112, width), bf),
            pltpu.VMEM((4, 112, width), bf),
            pltpu.VMEM((112, width), bf),
            pltpu.VMEM(part, bf),
            dma((5,)), dma((7,)), dma((8,)), dma, dma, dma((3,)), dma((4,)), dma, dma((4,)), dma((3,)), dma,
            dma((3,)), dma((4,)), dma((3,)), dma((4,)),
        ],
        compiler_params=pltpu.CompilerParams(
            collective_id=4, has_side_effects=True, vmem_limit_bytes=BIG
        ),
    )(src, gq, pz)


def finish_kernel(
    layer_in, in_0, in_1, grad_one, w, p_in, q_in,
    layer_out, out, g_q, g_k, g_v, g_o, g_in, g_up, rows_out, inner_out, wq, held, sems,
):
    width = w.shape[-1]
    span = 96
    step = pl.program_id(0)
    z, c = where_am_i()[2:]
    load = pltpu.make_async_copy(layer_in, held, sems.at[0])
    store = pltpu.make_async_copy(held, layer_out, sems.at[1])

    @pl.when(step == 0)
    def _():
        load.start()
        for i in range(3):
            for g in range(8):
                wq[i, 48 * g : 48 * g + 48, :] = w[0, g % 2, g // 2, 48 * i : 48 * i + 48, :]

    total = grad_one[0]
    for i in range(3):
        turned = jnp.concatenate(
            [
                ref[zz, 0, i * count : (i + 1) * count, :]
                for zz in range(4)
                for ref, count in ((in_0, in_0.shape[2] // 3), (in_1, in_1.shape[2] // 3))
            ],
            axis=0,
        )
        back = turned.astype(jnp.float32).T.astype(jnp.bfloat16)
        total = total + lax.dot_general(
            back, wq[i], (((1,), (1,)), ((), ())), preferred_element_type=jnp.float32
        )
    out[0] = total.astype(jnp.bfloat16)

    @pl.when(step == 0)
    def _():
        load.wait()
        store.start()
        wide = [q_in[zz].astype(jnp.float32) for zz in range(4)]
        for i, ref in enumerate((g_q, g_k, g_v)):
            ref[...] = jnp.concatenate([v[:, i * span : (i + 1) * span] for v in wide], axis=1)
        sums = p_in[3, 96:112, :]
        pick = jnp.where(
            iota((width, 48), 0) == 48 * (2 * z + c) + iota((width, 48), 1), 1.0, 0.0
        ).astype(jnp.bfloat16)
        rows_out[8:24, :] = dot(sums, pick)
        both = q_in[z].astype(jnp.float32)[:, 3 * span :].T
        rows_out[0:8, :] = both[0:8, :]
        pick = jnp.where(
            iota((width, 192), 0) == 192 * c + iota((width, 192), 1), 1.0, 0.0
        ).astype(jnp.bfloat16)
        inner = dot(sums, pick)
        inner_out[...] = jnp.sum(
            jnp.where(iota((16, 192), 0) == 6 + z, inner, 0.0), axis=0, keepdims=True
        )
        g_o[...] = p_in[0, 0:48, :].astype(jnp.float32)
        g_in[:, 0:384] = p_in[0, 48:96, :].astype(jnp.float32)
        g_in[:, 384:768] = p_in[1, 0:48, :].astype(jnp.float32)
        g_in[:, 768:1152] = p_in[1, 48:96, :].astype(jnp.float32)
        g_in[:, 1152:1536] = p_in[2, 0:48, :].astype(jnp.float32)
        g_up[0:16, :] = p_in[0, 96:112, :].astype(jnp.float32)
        g_up[16:32, :] = p_in[1, 96:112, :].astype(jnp.float32)
        g_up[32:96, :] = p_in[2, 48:112, :].astype(jnp.float32)
        g_up[96:192, :] = p_in[3, 0:96, :].astype(jnp.float32)

    @pl.when(step == 1)
    def _():
        store.wait()


def finish(layer_in, in_0, in_1, grad_one, w, p_in, q_in):
    seqs, rows, width = grad_one.shape
    sm = pl.BlockSpec(memory_space=pltpu.SMEM)
    hbm = pl.BlockSpec(memory_space=pltpu.HBM)
    bf, f4 = jnp.bfloat16, jnp.float32
    shapes = ((48, width),) * 4 + ((48, 4 * width), (192, width), (24, 48), (1, 192))
    in_0, in_1 = (v.reshape((4, 2) + v.shape[1:]) for v in (in_0, in_1))

    def of_sequence(v):
        return pl.BlockSpec((4, 1) + v.shape[2:], lambda i: (0, i, 0, 0))

    one = pl.BlockSpec((1, rows, width), lambda i: (i, 0, 0))
    return pl.pallas_call(
        finish_kernel,
        name="finish",
        grid=(seqs,),
        out_shape=(jax.ShapeDtypeStruct((seqs, rows, width), bf),) * 2
        + tuple(jax.ShapeDtypeStruct(shape, f4) for shape in shapes),
        in_specs=[
            hbm, of_sequence(in_0), of_sequence(in_1), one,
            quarter_spec(w, 0), whole_spec(p_in), whole_spec(q_in),
        ],
        out_specs=[hbm, one]
        + [pl.BlockSpec(shape, functools.partial(zeros_for, len(shape))) for shape in shapes],
        scratch_shapes=[
            pltpu.VMEM((3, width, width), bf),
            pltpu.VMEM((seqs, rows, width), bf),
            pltpu.SemaphoreType.DMA((2,)),
        ],
        compiler_params=pltpu.CompilerParams(vmem_limit_bytes=BIG - 1600 * 1024),
    )(layer_in, in_0, in_1, grad_one, w, p_in, q_in)


def line_of_chips(
    tokens, segment_ids, out_grad, query_weight, key_weight, value_weight, output_weight,
    inner_weight, outer_weight, query_bias, value_bias, output_bias, inner_bias, outer_bias,
    first_gain, first_shift, second_gain, second_shift,
):
    bf = jnp.bfloat16
    width = tokens.shape[2]
    weights = (query_weight, key_weight, value_weight, output_weight, inner_weight, outer_weight)
    vectors = jnp.concatenate(
        [
            v[None]
            for v in (
                query_bias, value_bias, output_bias, outer_bias,
                first_gain, first_shift, second_gain, second_shift,
            )
        ],
        axis=0,
    )
    x, w, small, kv, kt, vt, q1, norms = gather(
        tokens, weights, vectors, inner_bias[None], segment_ids
    )
    ctx, tail, spans = attend(kv, q1, vt, small, norms)
    layer_out, grad_one, gctx_in, pr = middle(ctx, tokens, out_grad, w, small)
    same_core = [[i + j for i in range(0, 8, 2)] for j in range(2)]
    pz = lax.all_to_all(pr, "grp", 0, 0, axis_index_groups=same_core, tiled=True)
    back = functools.partial(
        attend_back, spans=spans, x=x, tail=tail, kv=kv, kt=kt, q1=q1,
        gctx=gctx_in, ctx=ctx,
    )
    parts_0, grads_0 = back(2, 0)
    in_0 = lax.all_to_all(parts_0, "grp", 0, 0, tiled=True)
    parts_1, gq = back(1, 2, grads=grads_0)
    in_1, p_in, q_in = reduce_all(parts_1, gq, pz)
    layer_out, input_grad, g_q, g_k, g_v, g_o, g_in, g_up, rows, inner_row = finish(
        layer_out, in_0, in_1, grad_one, w, p_in, q_in
    )
    return (
        layer_out, input_grad, g_q, g_k, g_v, g_o, g_in, g_up,
        rows[0], rows[1], rows[8], inner_row[0], rows[9], rows[10], rows[11], rows[12], rows[13],
    )


def solution(mesh):
    in_specs = (
        P("rep", "grp", None),
        P("rep", "grp"),
        P("rep", "grp", None),
        P("grp", None),
        P("grp", None),
        P("grp", None),
        P("grp", None),
        P("grp", None),
        P("grp", None),
        P("grp"),
        P("grp"),
        P("grp"),
        P("grp"),
        P("grp"),
        P("grp"),
        P("grp"),
        P("grp"),
        P("grp"),
    )
    out_specs = (
        P("rep", "grp", None),
        P("rep", "grp", None),
        P("grp", None),
        P("grp", None),
        P("grp", None),
        P("grp", None),
        P("grp", None),
        P("grp", None),
        P("grp"),
        P("grp"),
        P("grp"),
        P("grp"),
        P("grp"),
        P("grp"),
        P("grp"),
        P("grp"),
        P("grp"),
    )
    whole_line = mesh.shape["grp"] == 8 and mesh.shape["rep"] == 4
    return jax.shard_map(
        line_of_chips if whole_line else on_device, mesh=mesh, in_specs=in_specs, out_specs=out_specs, check_vma=False
    )
```
